128 devices in a mesh: dp: 64 (over y, z_hi, x, core), mod: 2 (over z_lo).
Axes of the slice: x: 4, y: 4, z: 4 (z_hi: 2, z_lo: 2; z = z_hi * 2 + z_lo), core: 2. Of those that a mesh axis runs over, the one named last changes fastest.
Arguments:
- tokens: bfloat16 [256, 256, 1024], P(('dp', 'mod')), may hold values from -6 to 6
- condition: bfloat16 [256, 1024], P(('dp', 'mod')), may hold values from -6 to 6
- occupied: int32 [256], P(('dp', 'mod')), may hold values from 0 to 1, as said below
- modulation_weight: bfloat16 [1024, 6144], P(None, 'mod'), may hold values from -0.1875 to 0.1875
- modulation_bias: float32 [6, 1024], P('mod'), may hold values from -3 to 3
- input_weight: bfloat16 [1024, 3072], replicated, may hold values from -0.1875 to 0.1875
- query_bias: float32 [1024], replicated, may hold values from -3 to 3
- value_bias: float32 [1024], replicated, may hold values from -3 to 3
- output_weight: bfloat16 [1024, 1024], replicated, may hold values from -1.5 to 1.5
- output_bias: float32 [1024], replicated, may hold values from -3 to 3
- expand_weight: bfloat16 [1024, 4096], replicated, may hold values from -0.1875 to 0.1875
- expand_bias: float32 [4096], replicated, may hold values from -3 to 3
- contract_weight: bfloat16 [4096, 1024], replicated, may hold values from -0.1875 to 0.1875
- contract_bias: float32 [1024], replicated, may hold values from -3 to 3
- cotangent: bfloat16 [256, 256, 1024], P(('dp', 'mod')), may hold values from -6 to 6
Outputs:
- layer_out: float32 [256, 256, 1024], P(('dp', 'mod'))
- tokens_grad: float32 [256, 256, 1024], P(('dp', 'mod'))
- condition_grad: float32 [256, 1024], P(('dp', 'mod'))
- modulation_weight_grad: float32 [1024, 6144], P('dp', 'mod')
- modulation_bias_grad: float32 [6, 1024], P('mod', 'dp')
- input_weight_grad: float32 [1024, 3072], P(('dp', 'mod'))
- query_bias_grad: float32 [1024], P(('dp', 'mod'))
- value_bias_grad: float32 [1024], P(('dp', 'mod'))
- output_weight_grad: float32 [1024, 1024], P(('dp', 'mod'))
- output_bias_grad: float32 [1024], P(('dp', 'mod'))
- expand_weight_grad: float32 [1024, 4096], P(('dp', 'mod'))
- expand_bias_grad: float32 [4096], P(('dp', 'mod'))
- contract_weight_grad: float32 [4096, 1024], P(('dp', 'mod'))
- contract_bias_grad: float32 [1024], P(('dp', 'mod'))
The draws below stay inside these ranges and needn't reach their ends.
Inputs may be any that keep to these rules, and one draw needn't show every extreme that they name: Slots come in aligned groups of 2 held by one device; the images of a group with occupied = 1 are its first 1 to 2 slots, every group has one, and some group has all 2.
All inputs are finite; a program needn't handle non-finite values.
Results may differ from the reference program's by a relative error of at most 0.017.
The reference program's roundings to bfloat16 on the way count: a program that leaves them out, or rounds other values in their place, can miss the bound.
Values may be sent and summed in bfloat16 or wider, within the bound.
No kernel may reach another device: no remote copies, remote signals or barrier semaphores. Data moves between devices by JAX's collectives and lax.ppermute only.
A program may use at most 256 MiB of HBM per device.

```python
import math
import jax
import jax.numpy as jnp
from jax import lax

D = 1024
HEAD_DIM = 64
FF = 4096
S = 256
CAP = 2
IMAGES = 256


def draw_occupied(key, part):
    groups = IMAGES // CAP
    key_count, key_full = jax.random.split(key)
    counts = jax.random.randint(key_count, (groups,), 1, CAP + 1)
    fullest = jax.random.randint(key_full, (), 0, groups)
    counts = jnp.where(jnp.arange(groups) == fullest, CAP, counts)
    slots = jnp.arange(CAP)
    return (slots[None, :] < counts[:, None]).reshape(-1).astype(jnp.int32)


def level_of(own_key, shape, cuts, least, largest):
    def one(axis_at, shards_of):
        draws = jax.random.uniform(jax.random.fold_in(jax.random.fold_in(own_key, 6), axis_at), (shards_of,), jnp.float32, least / len(cuts), largest / len(cuts))
        return jnp.repeat(jnp.exp(draws), shape[axis_at] // shards_of).reshape((-1,) + (1,) * (len(shape) - axis_at - 1))

    loudness = one(*cuts[0])
    for cut in cuts[1:]:
        loudness = loudness * one(*cut)
    return loudness


def bell_draw(own_key, dims, scale, bound, cuts=(), dtype=jnp.bfloat16):
    result = jax.random.normal(own_key, dims, jnp.float32) * scale
    if len(cuts) > 0:
        result = level_of(own_key, dims, cuts, -0.22, 0.18) * result
    return jnp.clip(result, min=-bound, max=bound).astype(dtype)


def setup_inputs(seed: int = 0) -> dict:
    arg_keys = jax.random.split(jax.random.key(seed), 16)
    tokens = bell_draw(arg_keys[0], (IMAGES, S, D), 1.0, 6.0, ((0, 128),))
    condition = bell_draw(arg_keys[1], (IMAGES, D), 1.0, 6.0, ((0, 128),))
    occupied = draw_occupied(jax.random.fold_in(arg_keys[15], 71), 0)
    modulation_weight = bell_draw(arg_keys[3], (D, 6 * D), D ** -0.5, 0.1875, ((1, 2),))
    modulation_bias = bell_draw(arg_keys[4], (6, D), 0.5, 3.0, ((0, 2),), jnp.float32)
    input_weight = bell_draw(arg_keys[5], (D, 3 * D), D ** -0.5, 0.1875)
    query_bias = bell_draw(arg_keys[6], (D,), 0.5, 3.0, (), jnp.float32)
    value_bias = bell_draw(arg_keys[7], (D,), 0.5, 3.0, (), jnp.float32)
    output_weight = bell_draw(arg_keys[8], (D, D), (D // 64) ** -0.5, 1.5)
    output_bias = bell_draw(arg_keys[9], (D,), 0.5, 3.0, (), jnp.float32)
    expand_weight = bell_draw(arg_keys[10], (D, FF), D ** -0.5, 0.1875)
    expand_bias = bell_draw(arg_keys[11], (FF,), 0.5, 3.0, (), jnp.float32)
    contract_weight = bell_draw(arg_keys[12], (FF, D), (FF // 4) ** -0.5, 0.1875)
    contract_bias = bell_draw(arg_keys[13], (D,), 0.5, 3.0, (), jnp.float32)
    cotangent = bell_draw(arg_keys[14], (IMAGES, S, D), 1.0, 6.0, ((0, 128),))
    return {"tokens": tokens, "condition": condition, "occupied": occupied, "modulation_weight": modulation_weight, "modulation_bias": modulation_bias, "input_weight": input_weight, "query_bias": query_bias, "value_bias": value_bias, "output_weight": output_weight, "output_bias": output_bias, "expand_weight": expand_weight, "expand_bias": expand_bias, "contract_weight": contract_weight, "contract_bias": contract_bias, "cotangent": cotangent}


@jax.custom_vjp
def low(v):
    return lax.optimization_barrier(v.astype(jnp.bfloat16)).astype(jnp.float32)

@jax.custom_vjp
def low_back(v):
    return v

def low_keep(v):
    return (low(v), None)

def low_pass(kept, grad):
    return (grad,)

def back_keep(v):
    return (v, None)

def back_low(kept, grad):
    return (low(grad),)
low.defvjp(low_keep, low_pass)
low_back.defvjp(back_keep, back_low)
EPS = 1e-06
HIGH = lax.Precision.HIGHEST
GELU_C = 0.7978845608028654

def rounded_both(values):
    return low(low_back(values))

def normalize(values):
    centre = values - lax.optimization_barrier(jnp.mean(values, axis=-1, keepdims=True))
    variance = lax.optimization_barrier(jnp.mean(centre * centre, axis=-1, keepdims=True))
    return centre * lax.rsqrt(variance + EPS)

def block(inputs, condition, alive, modulation_weight, modulation_bias, input_weight, query_bias, value_bias, output_weight, output_bias, expand_weight, expand_bias, contract_weight, contract_bias):
    images, length, width = inputs.shape
    heads = width // HEAD_DIM
    silu_c = low(jax.nn.silu(condition))
    modulation = low_back(jnp.einsum('gd,de->ge', silu_c, modulation_weight, precision=HIGH) + modulation_bias.reshape(-1))
    pieces = jnp.split(modulation[:, None, :], 6, axis=-1)
    shift_a, scale_a, gate_a, shift_b, scale_b, gate_b = pieces
    mod_a = low(normalize(inputs) * (1.0 + scale_a) + shift_a)
    qkv_bias = jnp.concatenate([query_bias, jnp.zeros_like(query_bias), value_bias])
    qkv = rounded_both(jnp.einsum('gsd,de->gse', mod_a, input_weight, precision=HIGH) + qkv_bias)
    queries, keys, values = jnp.split(qkv, 3, axis=-1)
    queries = queries.reshape(images, length, heads, HEAD_DIM)
    keys = keys.reshape(images, length, heads, HEAD_DIM)
    values = values.reshape(images, length, heads, HEAD_DIM)
    scores = low_back(jnp.einsum('gqhe,gkhe->ghqk', queries, keys, precision=HIGH) * HEAD_DIM ** (-0.5))
    probs = low(jax.nn.softmax(scores, axis=-1))
    attended = jnp.einsum('ghqk,gkhe->gqhe', probs, values, precision=HIGH).reshape(images, length, width)
    attended = rounded_both(attended)
    branch_a = low_back(jnp.einsum('gsd,de->gse', attended, output_weight, precision=HIGH) + output_bias)
    middle = inputs + gate_a * branch_a
    mod_b = low(normalize(middle) * (1.0 + scale_b) + shift_b)
    expanded = low_back(jnp.einsum('gsd,df->gsf', mod_b, expand_weight, precision=HIGH) + expand_bias)
    activated = low(0.5 * expanded * (1.0 + jnp.tanh(GELU_C * (expanded + 0.044715 * expanded * expanded * expanded))))
    branch_b = low_back(jnp.einsum('gsf,fd->gsd', activated, contract_weight, precision=HIGH) + contract_bias)
    return (middle + gate_b * branch_b) * alive[:, None, None]

def reference(tokens, condition, occupied, modulation_weight, modulation_bias, input_weight, query_bias, value_bias, output_weight, output_bias, expand_weight, expand_bias, contract_weight, contract_bias, cotangent):
    params = tuple((p.astype(jnp.float32) for p in (modulation_weight, modulation_bias, input_weight, query_bias, value_bias, output_weight, output_bias, expand_weight, expand_bias, contract_weight, contract_bias)))
    group = math.gcd(IMAGES, 16)
    count = IMAGES // group
    token_groups = tokens.astype(jnp.float32).reshape(count, group, S, D)
    cond_groups = condition.astype(jnp.float32).reshape(count, group, D)
    alive_groups = occupied.astype(jnp.float32).reshape(count, group)
    cot_groups = cotangent.astype(jnp.float32).reshape(count, group, S, D)

    def step(totals, item):
        token_part, cond_part, alive_part, cot_part = item

        def forward(token_arg, cond_arg, *param_args):
            return block(token_arg, cond_arg, alive_part, *param_args)
        output, pullback = jax.vjp(forward, token_part, cond_part, *params)
        grads = pullback(cot_part)
        summed = tuple((a + b for a, b in zip(totals, grads[2:])))
        return (summed, (output, grads[0], grads[1]))
    zeros = tuple((jnp.zeros_like(p) for p in params))
    totals, stacked = lax.scan(step, zeros, (token_groups, cond_groups, alive_groups, cot_groups))
    outputs, token_grads, cond_grads = stacked
    return (outputs.reshape(IMAGES, S, D), token_grads.reshape(IMAGES, S, D), cond_grads.reshape(IMAGES, D), totals[0], totals[1], totals[2], totals[3], totals[4], totals[5], totals[6], totals[7], totals[8], totals[9], totals[10])
```

```python
import jax
import jax.numpy as jnp
import numpy as np
from jax import lax
from jax.sharding import Mesh
from jax.sharding import PartitionSpec as P

HEAD_DIM = 64


EPS = 1e-06
GELU_C = 0.7978845608028654

AXES = ("y", "zh", "x", "c", "zl")
DP = ("y", "zh", "x", "c")
STAGES = ("c", "x", "y", "zh", "zl")


def matmul(left, right):
    return jnp.dot(left, right, preferred_element_type=jnp.float32)


def left_trans(left, right):
    return lax.dot_general(
        left, right, (((0,), (0,)), ((), ())), preferred_element_type=jnp.float32
    )


def right_trans(left, right):
    return lax.dot_general(
        left, right, (((1,), (1,)), ((), ())), preferred_element_type=jnp.float32
    )


def normalize(values):
    centre = values - jnp.mean(values, axis=-1, keepdims=True)
    inverse = lax.rsqrt(jnp.mean(centre * centre, axis=-1, keepdims=True) + EPS)
    return (centre * inverse, inverse)


def norm_back(grad, normed, inverse):
    return inverse * (
        grad
        - jnp.mean(grad, axis=-1, keepdims=True)
        - normed * jnp.mean(grad * normed, axis=-1, keepdims=True)
    )


def reduce_packed(pieces, sizes):
    blocks = 1
    for a in AXES:
        blocks *= sizes[a]
    flat = []
    for piece in pieces:
        flat.append(piece.reshape(blocks, -1))
    widths = [f.shape[1] for f in flat]
    packed = jnp.concatenate(flat, axis=1).astype(jnp.bfloat16)
    shape = [sizes[a] for a in AXES]
    packed = packed.reshape(*shape, -1)
    packed = jnp.transpose(packed, [AXES.index(a) for a in STAGES] + [len(AXES)])
    packed = packed.reshape(blocks, -1)
    for a in STAGES:
        packed = lax.psum_scatter(packed, a, scatter_dimension=0, tiled=True)
    packed = packed.astype(jnp.float32).reshape(-1)
    outs = []
    start = 0
    for piece, w in zip(pieces, widths):
        outs.append(packed[start : start + w].reshape((piece.shape[0] // blocks,) + piece.shape[1:]))
        start += w
    return outs


def gather_dp(values):
    for a in ("c", "x", "zh", "y"):
        values = lax.all_gather(values, a, axis=0, tiled=True)
    return values


def per_device(
    sizes,
    tokens,
    condition,
    occupied,
    modulation_weight,
    modulation_bias,
    input_weight,
    query_bias,
    value_bias,
    output_weight,
    output_bias,
    expand_weight,
    expand_bias,
    contract_weight,
    contract_bias,
    cotangent,
):
    images, rows, width = tokens.shape
    heads = width // HEAD_DIM
    flat = images * rows
    factor = HEAD_DIM ** (-0.5)
    cond_full = condition.astype(jnp.float32)
    sigmoid = jax.nn.sigmoid(cond_full)
    silu_b = (cond_full * sigmoid).astype(jnp.bfloat16)
    silu_pair = lax.all_gather(silu_b, "zl", axis=0, tiled=True)
    mod_cols = matmul(silu_pair, modulation_weight) + modulation_bias.reshape(1, -1)
    modulation = lax.all_to_all(mod_cols, "zl", split_axis=0, concat_axis=1, tiled=True).reshape(
        images, 6, 1, width
    )
    shift_a = modulation[:, 0]
    scale_a = modulation[:, 1]
    gate_a = modulation[:, 2]
    shift_b = modulation[:, 3]
    scale_b = modulation[:, 4]
    gate_b = modulation[:, 5]
    inputs = tokens.astype(jnp.float32)
    normed_a, inverse_a = normalize(inputs)
    mod_a = (normed_a * (1.0 + scale_a) + shift_a).astype(jnp.bfloat16).reshape(flat, width)
    qkv_bias = jnp.concatenate([query_bias, jnp.zeros_like(query_bias), value_bias])
    projected = (matmul(mod_a, input_weight) + qkv_bias).astype(jnp.bfloat16)
    queries = projected[:, :width].reshape(images, rows, heads, HEAD_DIM)
    keys_all = projected[:, width : 2 * width].reshape(images, rows, heads, HEAD_DIM)
    values_all = projected[:, 2 * width :].reshape(images, rows, heads, HEAD_DIM)
    scores = (
        jnp.einsum("bqhe,bkhe->bhqk", queries, keys_all, preferred_element_type=jnp.float32)
        * factor
    )
    highest = jnp.max(scores, axis=-1, keepdims=True)
    weights = jnp.exp(scores - highest)
    probs = weights / jnp.sum(weights, axis=-1, keepdims=True)
    probs_b = probs.astype(jnp.bfloat16)
    attended = jnp.einsum(
        "bhqk,bkhe->bqhe", probs_b, values_all, preferred_element_type=jnp.float32
    )
    attended_b = attended.reshape(flat, width).astype(jnp.bfloat16)
    branch_a = (matmul(attended_b, output_weight) + output_bias).reshape(images, rows, width)
    middle = inputs + gate_a * branch_a
    normed_b, inverse_b = normalize(middle)
    mod_b = (normed_b * (1.0 + scale_b) + shift_b).astype(jnp.bfloat16).reshape(flat, width)
    expanded = matmul(mod_b, expand_weight) + expand_bias
    tanh_part = jnp.tanh(GELU_C * (expanded + 0.044715 * expanded * expanded * expanded))
    activated_b = (0.5 * expanded * (1.0 + tanh_part)).astype(jnp.bfloat16)
    branch_b = (matmul(activated_b, contract_weight) + contract_bias).reshape(images, rows, width)
    alive = occupied.astype(jnp.float32)[:, None, None]
    layer_out = (middle + gate_b * branch_b) * alive
    grad_out = cotangent.astype(jnp.float32) * alive
    grad_gate_b = jnp.sum(grad_out * branch_b, axis=1)
    grad_branch_b = (grad_out * gate_b).astype(jnp.bfloat16).reshape(flat, width)
    contract_grad = left_trans(activated_b, grad_branch_b)
    contract_bias_grad = jnp.sum(grad_branch_b.astype(jnp.float32), axis=0)
    grad_act = right_trans(grad_branch_b, contract_weight)
    slope = 0.5 * (1.0 + tanh_part) + 0.5 * expanded * (1.0 - tanh_part * tanh_part) * GELU_C * (
        1.0 + 3.0 * 0.044715 * expanded * expanded
    )
    grad_exp_b = (grad_act * slope).astype(jnp.bfloat16)
    expand_grad = left_trans(mod_b, grad_exp_b)
    expand_bias_grad = jnp.sum(grad_exp_b.astype(jnp.float32), axis=0)
    grad_mod_b = right_trans(grad_exp_b, expand_weight).reshape(images, rows, width)
    grad_shift_b = jnp.sum(grad_mod_b, axis=1)
    grad_scale_b = jnp.sum(grad_mod_b * normed_b, axis=1)
    grad_middle = grad_out + norm_back(grad_mod_b * (1.0 + scale_b), normed_b, inverse_b)
    grad_gate_a = jnp.sum(grad_middle * branch_a, axis=1)
    grad_branch_a = (grad_middle * gate_a).astype(jnp.bfloat16).reshape(flat, width)
    output_grad = left_trans(attended_b, grad_branch_a)
    output_bias_grad = jnp.sum(grad_branch_a.astype(jnp.float32), axis=0)
    grad_att_b = (
        right_trans(grad_branch_a, output_weight)
        .astype(jnp.bfloat16)
        .reshape(images, rows, heads, HEAD_DIM)
    )
    grad_probs = jnp.einsum(
        "bqhe,bkhe->bhqk", grad_att_b, values_all, preferred_element_type=jnp.float32
    )
    grad_values = jnp.einsum(
        "bhqk,bqhe->bkhe", probs_b, grad_att_b, preferred_element_type=jnp.float32
    )
    inner = jnp.sum(grad_probs * probs, axis=-1, keepdims=True)
    grad_scores_b = (probs * (grad_probs - inner)).astype(jnp.bfloat16)
    grad_queries = (
        jnp.einsum("bhqk,bkhe->bqhe", grad_scores_b, keys_all, preferred_element_type=jnp.float32)
        * factor
    )
    grad_keys = (
        jnp.einsum("bhqk,bqhe->bkhe", grad_scores_b, queries, preferred_element_type=jnp.float32)
        * factor
    )
    grad_proj_b = jnp.concatenate(
        [
            grad_queries.reshape(flat, width),
            grad_keys.reshape(flat, width),
            grad_values.reshape(flat, width),
        ],
        axis=1,
    ).astype(jnp.bfloat16)
    input_grad = left_trans(mod_a, grad_proj_b)
    bias_sums = jnp.sum(grad_proj_b.astype(jnp.float32), axis=0)
    query_bias_grad = bias_sums[:width]
    value_bias_grad = bias_sums[2 * width :]
    grad_mod_a = right_trans(grad_proj_b, input_weight).reshape(images, rows, width)
    grad_shift_a = jnp.sum(grad_mod_a, axis=1)
    grad_scale_a = jnp.sum(grad_mod_a * normed_a, axis=1)
    tokens_grad = grad_middle + norm_back(grad_mod_a * (1.0 + scale_a), normed_a, inverse_a)
    modulation_terms = jnp.stack(
        [grad_shift_a, grad_scale_a, grad_gate_a, grad_shift_b, grad_scale_b, grad_gate_b], axis=1
    ).reshape(images, 6 * width)
    modulation_own = modulation_terms.astype(jnp.bfloat16)
    modulation_cols = lax.all_to_all(modulation_own, "zl", split_axis=1, concat_axis=0, tiled=True)
    silu_terms = right_trans(modulation_cols, modulation_weight)
    silu_sums = lax.psum_scatter(silu_terms, "zl", scatter_dimension=0, tiled=True)
    condition_grad = silu_sums * sigmoid * (1.0 + cond_full * (1.0 - sigmoid))
    factors = gather_dp(jnp.concatenate([silu_pair, modulation_cols], axis=1))
    silu_all = factors[:, :width]
    mod_all = factors[:, width:]
    dp_index = lax.axis_index(DP)
    dp_count = factors.shape[0] // silu_pair.shape[0]
    row_block = width // dp_count
    silu_rows = lax.dynamic_slice_in_dim(silu_all, dp_index * row_block, row_block, axis=1)
    modulation_weight_grad = left_trans(silu_rows, mod_all)
    bias_all = jnp.sum(mod_all.astype(jnp.float32), axis=0).reshape(-1, width)
    modulation_bias_grad = lax.dynamic_slice_in_dim(bias_all, dp_index * row_block, row_block, axis=1)
    summed = reduce_packed(
        [
            input_grad,
            query_bias_grad,
            value_bias_grad,
            output_grad,
            output_bias_grad,
            expand_grad,
            expand_bias_grad,
            contract_grad,
            contract_bias_grad,
        ],
        sizes,
    )
    return (
        layer_out,
        tokens_grad,
        condition_grad,
        modulation_weight_grad,
        modulation_bias_grad,
        *summed,
    )


def solution(mesh):
    dp_size, mod_size = mesh.devices.shape
    rest = dp_size // 4
    side = int(round(rest ** 0.5))
    shape = (side, 2, rest // side, 2, mod_size)
    sizes = dict(zip(AXES, shape))
    physical = Mesh(np.asarray(mesh.devices).reshape(shape), AXES)
    ALL = AXES
    placed = (
        P(ALL, None, None),
        P(ALL, None),
        P(ALL),
        P(None, "zl"),
        P("zl", None),
        P(),
        P(),
        P(),
        P(),
        P(),
        P(),
        P(),
        P(),
        P(),
        P(ALL, None, None),
    )
    import functools

    return jax.shard_map(
        functools.partial(per_device, sizes),
        mesh=physical,
        in_specs=placed,
        out_specs=(
            P(ALL, None, None),
            P(ALL, None, None),
            P(ALL, None),
            P(DP, "zl"),
            P("zl", DP),
            P(ALL, None),
            P(ALL),
            P(ALL),
            P(ALL, None),
            P(ALL),
            P(ALL, None),
            P(ALL),
            P(ALL, None),
            P(ALL),
        ),
        check_vma=False,
    )
```

```python
import jax
import jax.numpy as jnp
import numpy as np
from jax import lax
from jax.sharding import Mesh
from jax.sharding import PartitionSpec as P

HEAD_DIM = 64


EPS = 1e-06
GELU_C = 0.7978845608028654

AXES = ("y", "zh", "x", "c", "zl")
DP = ("y", "zh", "x", "c")
STAGES = ("c", "x", "y", "zh", "zl")


def matmul(left, right):
    return jnp.dot(left, right, preferred_element_type=jnp.float32)


def left_trans(left, right):
    return lax.dot_general(
        left, right, (((0,), (0,)), ((), ())), preferred_element_type=jnp.float32
    )


def right_trans(left, right):
    return lax.dot_general(
        left, right, (((1,), (1,)), ((), ())), preferred_element_type=jnp.float32
    )


def normalize(values):
    centre = values - jnp.mean(values, axis=-1, keepdims=True)
    inverse = lax.rsqrt(jnp.mean(centre * centre, axis=-1, keepdims=True) + EPS)
    return (centre * inverse, inverse)


def norm_back(grad, normed, inverse):
    return inverse * (
        grad
        - jnp.mean(grad, axis=-1, keepdims=True)
        - normed * jnp.mean(grad * normed, axis=-1, keepdims=True)
    )


def stage_order(values, sizes, inner):
    lead = values.shape[:-1]
    shape = [sizes[a] for a in AXES]
    values = values.reshape(*lead, *shape, inner)
    n = len(lead)
    order = list(range(n)) + [n + AXES.index(a) for a in STAGES] + [n + len(AXES)]
    return jnp.transpose(values, order).reshape(*lead, -1)


def reduce_stages(packed):
    for a in STAGES:
        packed = lax.psum_scatter(packed, a, scatter_dimension=0, tiled=True)
    return packed.astype(jnp.float32)


def bias_columns(columns, rows):
    block = jnp.stack(columns, axis=1)
    return jnp.pad(block, ((0, 0), (0, 128 - block.shape[1]))).astype(jnp.bfloat16)


def gather_dp(values):
    for a in ("c", "x", "zh", "y"):
        values = lax.all_gather(values, a, axis=0, tiled=True)
    return values


def per_device(
    sizes,
    tokens,
    condition,
    occupied,
    modulation_weight,
    modulation_bias,
    input_weight,
    query_bias,
    value_bias,
    output_weight,
    output_bias,
    expand_weight,
    expand_bias,
    contract_weight,
    contract_bias,
    cotangent,
):
    images, rows, width = tokens.shape
    heads = width // HEAD_DIM
    flat = images * rows
    factor = HEAD_DIM ** (-0.5)
    cond_full = condition.astype(jnp.float32)
    sigmoid = jax.nn.sigmoid(cond_full)
    silu_b = (cond_full * sigmoid).astype(jnp.bfloat16)
    silu_pair = lax.all_gather(silu_b, "zl", axis=0, tiled=True)
    mod_cols = matmul(silu_pair, modulation_weight) + modulation_bias.reshape(1, -1)
    modulation = lax.all_to_all(mod_cols, "zl", split_axis=0, concat_axis=1, tiled=True).reshape(
        images, 6, 1, width
    )
    shift_a = modulation[:, 0]
    scale_a = modulation[:, 1]
    gate_a = modulation[:, 2]
    shift_b = modulation[:, 3]
    scale_b = modulation[:, 4]
    gate_b = modulation[:, 5]
    inputs = tokens.astype(jnp.float32)
    normed_a, inverse_a = normalize(inputs)
    mod_a = (normed_a * (1.0 + scale_a) + shift_a).astype(jnp.bfloat16).reshape(flat, width)
    qkv_bias = jnp.concatenate([query_bias, jnp.zeros_like(query_bias), value_bias])
    projected = (matmul(mod_a, input_weight) + qkv_bias).astype(jnp.bfloat16)
    queries = projected[:, :width].reshape(images, rows, heads, HEAD_DIM)
    keys_all = projected[:, width : 2 * width].reshape(images, rows, heads, HEAD_DIM)
    values_all = projected[:, 2 * width :].reshape(images, rows, heads, HEAD_DIM)
    scores = (
        jnp.einsum("bqhe,bkhe->bhqk", queries, keys_all, preferred_element_type=jnp.float32)
        * factor
    )
    highest = jnp.max(scores, axis=-1, keepdims=True)
    weights = jnp.exp(scores - highest)
    probs = weights / jnp.sum(weights, axis=-1, keepdims=True)
    probs_b = probs.astype(jnp.bfloat16)
    attended = jnp.einsum(
        "bhqk,bkhe->bqhe", probs_b, values_all, preferred_element_type=jnp.float32
    )
    attended_b = attended.reshape(flat, width).astype(jnp.bfloat16)
    branch_a = (matmul(attended_b, output_weight) + output_bias).reshape(images, rows, width)
    middle = inputs + gate_a * branch_a
    normed_b, inverse_b = normalize(middle)
    mod_b = (normed_b * (1.0 + scale_b) + shift_b).astype(jnp.bfloat16).reshape(flat, width)
    expanded = matmul(mod_b, expand_weight) + expand_bias
    tanh_part = jnp.tanh(GELU_C * (expanded + 0.044715 * expanded * expanded * expanded))
    activated_b = (0.5 * expanded * (1.0 + tanh_part)).astype(jnp.bfloat16)
    branch_b = (matmul(activated_b, contract_weight) + contract_bias).reshape(images, rows, width)
    alive = occupied.astype(jnp.float32)[:, None, None]
    layer_out = (middle + gate_b * branch_b) * alive
    grad_out = cotangent.astype(jnp.float32) * alive
    grad_gate_b = jnp.sum(grad_out * branch_b, axis=1)
    grad_branch_b = (grad_out * gate_b).astype(jnp.bfloat16).reshape(flat, width)
    blocks = 1
    for a in AXES:
        blocks *= sizes[a]
    ff = activated_b.shape[1]
    split = ff // width
    act_perm = stage_order(
        activated_b.reshape(flat, blocks, split, width // blocks)
        .transpose(0, 2, 1, 3)
        .reshape(flat, split, width),
        sizes,
        width // blocks,
    )
    contract_parts = [
        left_trans(act_perm[:, q], grad_branch_b).astype(jnp.bfloat16) for q in range(split)
    ]
    contract_bias_grad = stage_order(
        jnp.sum(grad_branch_b.astype(jnp.float32), axis=0), sizes, width // blocks
    )
    grad_act = right_trans(grad_branch_b, contract_weight)
    slope = 0.5 * (1.0 + tanh_part) + 0.5 * expanded * (1.0 - tanh_part * tanh_part) * GELU_C * (
        1.0 + 3.0 * 0.044715 * expanded * expanded
    )
    grad_exp_b = (grad_act * slope).astype(jnp.bfloat16)
    expand_grad = left_trans(stage_order(mod_b, sizes, width // blocks), grad_exp_b).astype(jnp.bfloat16)
    expand_bias_grad = stage_order(
        jnp.sum(grad_exp_b.astype(jnp.float32), axis=0)
        .reshape(blocks, split, width // blocks)
        .transpose(1, 0, 2)
        .reshape(split, width),
        sizes,
        width // blocks,
    )
    chain_a = reduce_stages(
        jnp.concatenate(
            [expand_grad]
            + contract_parts
            + [bias_columns([contract_bias_grad] + [expand_bias_grad[q] for q in range(split)], width)],
            axis=1,
        )
    )
    grad_mod_b = right_trans(grad_exp_b, expand_weight).reshape(images, rows, width)
    grad_shift_b = jnp.sum(grad_mod_b, axis=1)
    grad_scale_b = jnp.sum(grad_mod_b * normed_b, axis=1)
    grad_middle = grad_out + norm_back(grad_mod_b * (1.0 + scale_b), normed_b, inverse_b)
    grad_gate_a = jnp.sum(grad_middle * branch_a, axis=1)
    grad_branch_a = (grad_middle * gate_a).astype(jnp.bfloat16).reshape(flat, width)
    output_grad = left_trans(stage_order(attended_b, sizes, width // blocks), grad_branch_a).astype(
        jnp.bfloat16
    )
    output_bias_grad = stage_order(
        jnp.sum(grad_branch_a.astype(jnp.float32), axis=0), sizes, width // blocks
    )
    grad_att_b = (
        right_trans(grad_branch_a, output_weight)
        .astype(jnp.bfloat16)
        .reshape(images, rows, heads, HEAD_DIM)
    )
    grad_probs = jnp.einsum(
        "bqhe,bkhe->bhqk", grad_att_b, values_all, preferred_element_type=jnp.float32
    )
    grad_values = jnp.einsum(
        "bhqk,bqhe->bkhe", probs_b, grad_att_b, preferred_element_type=jnp.float32
    )
    inner = jnp.sum(grad_probs * probs, axis=-1, keepdims=True)
    grad_scores_b = (probs * (grad_probs - inner)).astype(jnp.bfloat16)
    grad_queries = (
        jnp.einsum("bhqk,bkhe->bqhe", grad_scores_b, keys_all, preferred_element_type=jnp.float32)
        * factor
    )
    grad_keys = (
        jnp.einsum("bhqk,bqhe->bkhe", grad_scores_b, queries, preferred_element_type=jnp.float32)
        * factor
    )
    grad_proj_b = jnp.concatenate(
        [
            grad_queries.reshape(flat, width),
            grad_keys.reshape(flat, width),
            grad_values.reshape(flat, width),
        ],
        axis=1,
    ).astype(jnp.bfloat16)
    input_grad = left_trans(stage_order(mod_a, sizes, width // blocks), grad_proj_b).astype(jnp.bfloat16)
    bias_sums = jnp.sum(grad_proj_b.astype(jnp.float32), axis=0)
    query_bias_grad = stage_order(bias_sums[:width], sizes, width // blocks)
    value_bias_grad = stage_order(bias_sums[2 * width :], sizes, width // blocks)
    chain_b = reduce_stages(
        jnp.concatenate(
            [
                input_grad,
                output_grad,
                bias_columns([query_bias_grad, value_bias_grad, output_bias_grad], width),
            ],
            axis=1,
        )
    )
    grad_mod_a = right_trans(grad_proj_b, input_weight).reshape(images, rows, width)
    grad_shift_a = jnp.sum(grad_mod_a, axis=1)
    grad_scale_a = jnp.sum(grad_mod_a * normed_a, axis=1)
    tokens_grad = grad_middle + norm_back(grad_mod_a * (1.0 + scale_a), normed_a, inverse_a)
    modulation_terms = jnp.stack(
        [grad_shift_a, grad_scale_a, grad_gate_a, grad_shift_b, grad_scale_b, grad_gate_b], axis=1
    ).reshape(images, 6 * width)
    modulation_own = modulation_terms.astype(jnp.bfloat16)
    modulation_cols = lax.all_to_all(modulation_own, "zl", split_axis=1, concat_axis=0, tiled=True)
    silu_terms = right_trans(modulation_cols, modulation_weight)
    silu_sums = lax.psum_scatter(silu_terms, "zl", scatter_dimension=0, tiled=True)
    condition_grad = silu_sums * sigmoid * (1.0 + cond_full * (1.0 - sigmoid))
    factors = gather_dp(jnp.concatenate([silu_pair, modulation_cols], axis=1))
    silu_all = factors[:, :width]
    mod_all = factors[:, width:]
    dp_index = lax.axis_index(DP)
    dp_count = factors.shape[0] // silu_pair.shape[0]
    row_block = width // dp_count
    silu_rows = lax.dynamic_slice_in_dim(silu_all, dp_index * row_block, row_block, axis=1)
    modulation_weight_grad = left_trans(silu_rows, mod_all)
    bias_all = jnp.sum(mod_all.astype(jnp.float32), axis=0).reshape(-1, width)
    modulation_bias_grad = lax.dynamic_slice_in_dim(bias_all, dp_index * row_block, row_block, axis=1)
    three = input_weight.shape[1]
    fw = expand_weight.shape[1]
    input_weight_grad = chain_b[:, :three]
    output_weight_grad = chain_b[:, three : three + width]
    qb_grad = chain_b[:, three + width]
    vb_grad = chain_b[:, three + width + 1]
    ob_grad = chain_b[:, three + width + 2]
    expand_weight_grad = chain_a[:, :fw]
    contract_weight_grad = chain_a[:, fw : fw + split * width].reshape(-1, split, width)
    contract_weight_grad = contract_weight_grad.transpose(1, 0, 2).reshape(-1, width)
    cb_grad = chain_a[:, fw + split * width]
    eb_grad = chain_a[:, fw + split * width + 1 : fw + split * width + 1 + split].T.reshape(-1)
    summed = (
        input_weight_grad,
        qb_grad,
        vb_grad,
        output_weight_grad,
        ob_grad,
        expand_weight_grad,
        eb_grad,
        contract_weight_grad,
        cb_grad,
    )
    return (
        layer_out,
        tokens_grad,
        condition_grad,
        modulation_weight_grad,
        modulation_bias_grad,
        *summed,
    )


def solution(mesh):
    dp_size, mod_size = mesh.devices.shape
    rest = dp_size // 4
    side = int(round(rest ** 0.5))
    shape = (side, 2, rest // side, 2, mod_size)
    sizes = dict(zip(AXES, shape))
    physical = Mesh(np.asarray(mesh.devices).reshape(shape), AXES)
    ALL = AXES
    placed = (
        P(ALL, None, None),
        P(ALL, None),
        P(ALL),
        P(None, "zl"),
        P("zl", None),
        P(),
        P(),
        P(),
        P(),
        P(),
        P(),
        P(),
        P(),
        P(),
        P(ALL, None, None),
    )
    import functools

    return jax.shard_map(
        functools.partial(per_device, sizes),
        mesh=physical,
        in_specs=placed,
        out_specs=(
            P(ALL, None, None),
            P(ALL, None, None),
            P(ALL, None),
            P(DP, "zl"),
            P("zl", DP),
            P(ALL, None),
            P(ALL),
            P(ALL),
            P(ALL, None),
            P(ALL),
            P(ALL, None),
            P(ALL),
            P(ALL, None),
            P(ALL),
        ),
        check_vma=False,
    )
```

```python
import jax
import jax.numpy as jnp
import numpy as np
from jax import lax
from jax.sharding import Mesh
from jax.sharding import PartitionSpec as P

HEAD_DIM = 64


EPS = 1e-06
GELU_C = 0.7978845608028654

AXES = ("y", "zh", "x", "c", "zl")
DP = ("y", "zh", "x", "c")
STAGES = ("c", "x", "y", "zh", "zl")


def matmul(left, right):
    return jnp.dot(left, right, preferred_element_type=jnp.float32)


def left_trans(left, right):
    return lax.dot_general(
        left, right, (((0,), (0,)), ((), ())), preferred_element_type=jnp.float32
    )


def right_trans(left, right):
    return lax.dot_general(
        left, right, (((1,), (1,)), ((), ())), preferred_element_type=jnp.float32
    )


def normalize(values):
    centre = values - jnp.mean(values, axis=-1, keepdims=True)
    inverse = lax.rsqrt(jnp.mean(centre * centre, axis=-1, keepdims=True) + EPS)
    return (centre * inverse, inverse)


def norm_back(grad, normed, inverse):
    return inverse * (
        grad
        - jnp.mean(grad, axis=-1, keepdims=True)
        - normed * jnp.mean(grad * normed, axis=-1, keepdims=True)
    )


def stage_order(values, sizes, inner):
    lead = values.shape[:-1]
    shape = [sizes[a] for a in AXES]
    values = values.reshape(*lead, *shape, inner)
    n = len(lead)
    order = list(range(n)) + [n + AXES.index(a) for a in STAGES] + [n + len(AXES)]
    return jnp.transpose(values, order).reshape(*lead, -1)


def reduce_stages(packed, stages):
    for a in stages:
        packed = lax.psum_scatter(packed, a, scatter_dimension=0, tiled=True)
    return packed


def reduce_rest(packed, axes):
    count = 1
    for a in axes:
        count *= lax.axis_size(a)
    chunks = packed.reshape(count, packed.shape[0] // count, packed.shape[1])
    chunks = lax.all_to_all(chunks, axes, 0, 0, tiled=False)
    return jnp.sum(chunks.astype(jnp.float32), axis=0)


def bias_columns(columns, rows):
    block = jnp.stack(columns, axis=1)
    return jnp.pad(block, ((0, 0), (0, 128 - block.shape[1]))).astype(jnp.bfloat16)


def gather_dp(values):
    count = 1
    for a in DP:
        count *= lax.axis_size(a)
    copies = jnp.broadcast_to(values[None], (count,) + values.shape)
    return lax.all_to_all(copies, DP, 0, 0, tiled=False).reshape(-1, values.shape[1])


def per_device(
    sizes,
    tokens,
    condition,
    occupied,
    modulation_weight,
    modulation_bias,
    input_weight,
    query_bias,
    value_bias,
    output_weight,
    output_bias,
    expand_weight,
    expand_bias,
    contract_weight,
    contract_bias,
    cotangent,
):
    images, rows, width = tokens.shape
    heads = width // HEAD_DIM
    flat = images * rows
    factor = HEAD_DIM ** (-0.5)
    cond_full = condition.astype(jnp.float32)
    sigmoid = jax.nn.sigmoid(cond_full)
    silu_b = (cond_full * sigmoid).astype(jnp.bfloat16)
    silu_pair = lax.all_gather(silu_b, "zl", axis=0, tiled=True)
    mod_cols = matmul(silu_pair, modulation_weight) + modulation_bias.reshape(1, -1)
    modulation = lax.all_to_all(mod_cols, "zl", split_axis=0, concat_axis=1, tiled=True).reshape(
        images, 6, 1, width
    )
    shift_a = modulation[:, 0]
    scale_a = modulation[:, 1]
    gate_a = modulation[:, 2]
    shift_b = modulation[:, 3]
    scale_b = modulation[:, 4]
    gate_b = modulation[:, 5]
    inputs = tokens.astype(jnp.float32)
    normed_a, inverse_a = normalize(inputs)
    mod_a = (normed_a * (1.0 + scale_a) + shift_a).astype(jnp.bfloat16).reshape(flat, width)
    qkv_bias = jnp.concatenate([query_bias, jnp.zeros_like(query_bias), value_bias])
    projected = (matmul(mod_a, input_weight) + qkv_bias).astype(jnp.bfloat16)
    queries = projected[:, :width].reshape(images, rows, heads, HEAD_DIM)
    keys_all = projected[:, width : 2 * width].reshape(images, rows, heads, HEAD_DIM)
    values_all = projected[:, 2 * width :].reshape(images, rows, heads, HEAD_DIM)
    scores = (
        jnp.einsum("bqhe,bkhe->bhqk", queries, keys_all, preferred_element_type=jnp.float32)
        * factor
    )
    highest = jnp.max(scores, axis=-1, keepdims=True)
    weights = jnp.exp(scores - highest)
    probs = weights / jnp.sum(weights, axis=-1, keepdims=True)
    probs_b = probs.astype(jnp.bfloat16)
    attended = jnp.einsum(
        "bhqk,bkhe->bqhe", probs_b, values_all, preferred_element_type=jnp.float32
    )
    attended_b = attended.reshape(flat, width).astype(jnp.bfloat16)
    branch_a = (matmul(attended_b, output_weight) + output_bias).reshape(images, rows, width)
    middle = inputs + gate_a * branch_a
    normed_b, inverse_b = normalize(middle)
    mod_b = (normed_b * (1.0 + scale_b) + shift_b).astype(jnp.bfloat16).reshape(flat, width)
    expanded = matmul(mod_b, expand_weight) + expand_bias
    tanh_part = jnp.tanh(GELU_C * (expanded + 0.044715 * expanded * expanded * expanded))
    activated_b = (0.5 * expanded * (1.0 + tanh_part)).astype(jnp.bfloat16)
    branch_b = (matmul(activated_b, contract_weight) + contract_bias).reshape(images, rows, width)
    alive = occupied.astype(jnp.float32)[:, None, None]
    layer_out = (middle + gate_b * branch_b) * alive
    grad_out = cotangent.astype(jnp.float32) * alive
    grad_gate_b = jnp.sum(grad_out * branch_b, axis=1)
    grad_branch_b = (grad_out * gate_b).astype(jnp.bfloat16).reshape(flat, width)
    blocks = 1
    for a in AXES:
        blocks *= sizes[a]
    ff = activated_b.shape[1]
    split = ff // width
    act_perm = stage_order(
        activated_b.reshape(flat, blocks, split, width // blocks)
        .transpose(0, 2, 1, 3)
        .reshape(flat, split, width),
        sizes,
        width // blocks,
    )
    contract_parts = [
        left_trans(act_perm[:, q], grad_branch_b).astype(jnp.bfloat16) for q in range(split)
    ]
    contract_bias_grad = stage_order(
        jnp.sum(grad_branch_b.astype(jnp.float32), axis=0), sizes, width // blocks
    )
    grad_act = right_trans(grad_branch_b, contract_weight)
    slope = 0.5 * (1.0 + tanh_part) + 0.5 * expanded * (1.0 - tanh_part * tanh_part) * GELU_C * (
        1.0 + 3.0 * 0.044715 * expanded * expanded
    )
    grad_exp_b = (grad_act * slope).astype(jnp.bfloat16)
    expand_grad = left_trans(stage_order(mod_b, sizes, width // blocks), grad_exp_b).astype(jnp.bfloat16)
    expand_bias_grad = stage_order(
        jnp.sum(grad_exp_b.astype(jnp.float32), axis=0)
        .reshape(blocks, split, width // blocks)
        .transpose(1, 0, 2)
        .reshape(split, width),
        sizes,
        width // blocks,
    )
    chain_a = reduce_stages(
        jnp.concatenate(
            [expand_grad]
            + contract_parts
            + [bias_columns([contract_bias_grad] + [expand_bias_grad[q] for q in range(split)], width)],
            axis=1,
        ),
        STAGES[:2],
    )
    grad_mod_b = right_trans(grad_exp_b, expand_weight).reshape(images, rows, width)
    grad_shift_b = jnp.sum(grad_mod_b, axis=1)
    grad_scale_b = jnp.sum(grad_mod_b * normed_b, axis=1)
    grad_middle = grad_out + norm_back(grad_mod_b * (1.0 + scale_b), normed_b, inverse_b)
    grad_gate_a = jnp.sum(grad_middle * branch_a, axis=1)
    grad_branch_a = (grad_middle * gate_a).astype(jnp.bfloat16).reshape(flat, width)
    output_grad = left_trans(stage_order(attended_b, sizes, width // blocks), grad_branch_a).astype(
        jnp.bfloat16
    )
    output_bias_grad = stage_order(
        jnp.sum(grad_branch_a.astype(jnp.float32), axis=0), sizes, width // blocks
    )
    grad_att_b = (
        right_trans(grad_branch_a, output_weight)
        .astype(jnp.bfloat16)
        .reshape(images, rows, heads, HEAD_DIM)
    )
    grad_probs = jnp.einsum(
        "bqhe,bkhe->bhqk", grad_att_b, values_all, preferred_element_type=jnp.float32
    )
    grad_values = jnp.einsum(
        "bhqk,bqhe->bkhe", probs_b, grad_att_b, preferred_element_type=jnp.float32
    )
    inner = jnp.sum(grad_probs * probs, axis=-1, keepdims=True)
    grad_scores_b = (probs * (grad_probs - inner)).astype(jnp.bfloat16)
    grad_queries = (
        jnp.einsum("bhqk,bkhe->bqhe", grad_scores_b, keys_all, preferred_element_type=jnp.float32)
        * factor
    )
    grad_keys = (
        jnp.einsum("bhqk,bqhe->bkhe", grad_scores_b, queries, preferred_element_type=jnp.float32)
        * factor
    )
    grad_proj_b = jnp.concatenate(
        [
            grad_queries.reshape(flat, width),
            grad_keys.reshape(flat, width),
            grad_values.reshape(flat, width),
        ],
        axis=1,
    ).astype(jnp.bfloat16)
    input_grad = left_trans(stage_order(mod_a, sizes, width // blocks), grad_proj_b).astype(jnp.bfloat16)
    bias_sums = jnp.sum(grad_proj_b.astype(jnp.float32), axis=0)
    query_bias_grad = stage_order(bias_sums[:width], sizes, width // blocks)
    value_bias_grad = stage_order(bias_sums[2 * width :], sizes, width // blocks)
    chain_b = reduce_stages(
        jnp.concatenate(
            [
                input_grad,
                output_grad,
                bias_columns([query_bias_grad, value_bias_grad, output_bias_grad], width),
            ],
            axis=1,
        ),
        STAGES[:2],
    )
    grad_mod_a = right_trans(grad_proj_b, input_weight).reshape(images, rows, width)
    grad_shift_a = jnp.sum(grad_mod_a, axis=1)
    grad_scale_a = jnp.sum(grad_mod_a * normed_a, axis=1)
    tokens_grad = grad_middle + norm_back(grad_mod_a * (1.0 + scale_a), normed_a, inverse_a)
    modulation_terms = jnp.stack(
        [grad_shift_a, grad_scale_a, grad_gate_a, grad_shift_b, grad_scale_b, grad_gate_b], axis=1
    ).reshape(images, 6 * width)
    modulation_own = modulation_terms.astype(jnp.bfloat16)
    modulation_cols = lax.all_to_all(modulation_own, "zl", split_axis=1, concat_axis=0, tiled=True)
    silu_terms = right_trans(modulation_cols, modulation_weight)
    silu_sums = lax.psum_scatter(silu_terms, "zl", scatter_dimension=0, tiled=True)
    condition_grad = silu_sums * sigmoid * (1.0 + cond_full * (1.0 - sigmoid))
    factors = gather_dp(jnp.concatenate([silu_pair, modulation_cols], axis=1))
    silu_all = factors[:, :width]
    mod_all = factors[:, width:]
    dp_index = lax.axis_index(DP)
    dp_count = factors.shape[0] // silu_pair.shape[0]
    row_block = width // dp_count
    silu_rows = lax.dynamic_slice_in_dim(silu_all, dp_index * row_block, row_block, axis=1)
    modulation_weight_grad = left_trans(silu_rows, mod_all)
    bias_all = jnp.sum(mod_all.astype(jnp.float32), axis=0).reshape(-1, width)
    modulation_bias_grad = lax.dynamic_slice_in_dim(bias_all, dp_index * row_block, row_block, axis=1)
    rest = reduce_rest(jnp.concatenate([chain_a, chain_b], axis=1), STAGES[2:])
    chain_a = rest[:, : chain_a.shape[1]]
    chain_b = rest[:, chain_a.shape[1] :]
    three = input_weight.shape[1]
    fw = expand_weight.shape[1]
    input_weight_grad = chain_b[:, :three]
    output_weight_grad = chain_b[:, three : three + width]
    qb_grad = chain_b[:, three + width]
    vb_grad = chain_b[:, three + width + 1]
    ob_grad = chain_b[:, three + width + 2]
    expand_weight_grad = chain_a[:, :fw]
    contract_weight_grad = chain_a[:, fw : fw + split * width].reshape(-1, split, width)
    contract_weight_grad = contract_weight_grad.transpose(1, 0, 2).reshape(-1, width)
    cb_grad = chain_a[:, fw + split * width]
    eb_grad = chain_a[:, fw + split * width + 1 : fw + split * width + 1 + split].T.reshape(-1)
    summed = (
        input_weight_grad,
        qb_grad,
        vb_grad,
        output_weight_grad,
        ob_grad,
        expand_weight_grad,
        eb_grad,
        contract_weight_grad,
        cb_grad,
    )
    return (
        layer_out,
        tokens_grad,
        condition_grad,
        modulation_weight_grad,
        modulation_bias_grad,
        *summed,
    )


def solution(mesh):
    dp_size, mod_size = mesh.devices.shape
    rest = dp_size // 4
    side = int(round(rest ** 0.5))
    shape = (side, 2, rest // side, 2, mod_size)
    sizes = dict(zip(AXES, shape))
    physical = Mesh(np.asarray(mesh.devices).reshape(shape), AXES)
    ALL = AXES
    placed = (
        P(ALL, None, None),
        P(ALL, None),
        P(ALL),
        P(None, "zl"),
        P("zl", None),
        P(),
        P(),
        P(),
        P(),
        P(),
        P(),
        P(),
        P(),
        P(),
        P(ALL, None, None),
    )
    import functools

    return jax.shard_map(
        functools.partial(per_device, sizes),
        mesh=physical,
        in_specs=placed,
        out_specs=(
            P(ALL, None, None),
            P(ALL, None, None),
            P(ALL, None),
            P(DP, "zl"),
            P("zl", DP),
            P(ALL, None),
            P(ALL),
            P(ALL),
            P(ALL, None),
            P(ALL),
            P(ALL, None),
            P(ALL),
            P(ALL, None),
            P(ALL),
        ),
        check_vma=False,
    )
```

```python
import jax
import jax.numpy as jnp
import numpy as np
from jax import lax
from jax.sharding import Mesh
from jax.sharding import PartitionSpec as P

HEAD_DIM = 64


EPS = 1e-06
GELU_C = 0.7978845608028654

AXES = ("y", "zh", "x", "c", "zl")
DP = ("y", "zh", "x", "c")
STAGES = ("c", "x", "y", "zh", "zl")
STAGES_B = ("c", "y", "x", "zh", "zl")


def matmul(left, right):
    return jnp.dot(left, right, preferred_element_type=jnp.float32)


def left_trans(left, right):
    return lax.dot_general(
        left, right, (((0,), (0,)), ((), ())), preferred_element_type=jnp.float32
    )


def right_trans(left, right):
    return lax.dot_general(
        left, right, (((1,), (1,)), ((), ())), preferred_element_type=jnp.float32
    )


def normalize(values):
    centre = values - jnp.mean(values, axis=-1, keepdims=True)
    inverse = lax.rsqrt(jnp.mean(centre * centre, axis=-1, keepdims=True) + EPS)
    return (centre * inverse, inverse)


def norm_back(grad, normed, inverse):
    return inverse * (
        grad
        - jnp.mean(grad, axis=-1, keepdims=True)
        - normed * jnp.mean(grad * normed, axis=-1, keepdims=True)
    )


def stage_order(values, sizes, inner, stages=STAGES):
    lead = values.shape[:-1]
    shape = [sizes[a] for a in AXES]
    values = values.reshape(*lead, *shape, inner)
    n = len(lead)
    order = list(range(n)) + [n + AXES.index(a) for a in stages] + [n + len(AXES)]
    return jnp.transpose(values, order).reshape(*lead, -1)


def reduce_stages(packed, stages):
    for a in stages:
        packed = lax.psum_scatter(packed, a, scatter_dimension=0, tiled=True)
    return packed


def reduce_rest(packed, axes):
    count = 1
    for a in axes:
        count *= lax.axis_size(a)
    chunks = packed.reshape(count, packed.shape[0] // count, packed.shape[1])
    chunks = lax.all_to_all(chunks, axes, 0, 0, tiled=False)
    return jnp.sum(chunks.astype(jnp.float32), axis=0)


def bias_columns(columns, rows):
    block = jnp.stack(columns, axis=1)
    return jnp.pad(block, ((0, 0), (0, 128 - block.shape[1]))).astype(jnp.bfloat16)


def gather_dp(values):
    count = 1
    for a in DP:
        count *= lax.axis_size(a)
    copies = jnp.broadcast_to(values[None], (count,) + values.shape)
    return lax.all_to_all(copies, DP, 0, 0, tiled=False).reshape(-1, values.shape[1])


def per_device(
    sizes,
    tokens,
    condition,
    occupied,
    modulation_weight,
    modulation_bias,
    input_weight,
    query_bias,
    value_bias,
    output_weight,
    output_bias,
    expand_weight,
    expand_bias,
    contract_weight,
    contract_bias,
    cotangent,
):
    images, rows, width = tokens.shape
    heads = width // HEAD_DIM
    flat = images * rows
    factor = HEAD_DIM ** (-0.5)
    cond_full = condition.astype(jnp.float32)
    sigmoid = jax.nn.sigmoid(cond_full)
    silu_b = (cond_full * sigmoid).astype(jnp.bfloat16)
    silu_pair = lax.all_gather(silu_b, "zl", axis=0, tiled=True)
    mod_cols = matmul(silu_pair, modulation_weight) + modulation_bias.reshape(1, -1)
    modulation = lax.all_to_all(mod_cols, "zl", split_axis=0, concat_axis=1, tiled=True).reshape(
        images, 6, 1, width
    )
    shift_a = modulation[:, 0]
    scale_a = modulation[:, 1]
    gate_a = modulation[:, 2]
    shift_b = modulation[:, 3]
    scale_b = modulation[:, 4]
    gate_b = modulation[:, 5]
    inputs = tokens.astype(jnp.float32)
    normed_a, inverse_a = normalize(inputs)
    mod_a = (normed_a * (1.0 + scale_a) + shift_a).astype(jnp.bfloat16).reshape(flat, width)
    qkv_bias = jnp.concatenate([query_bias, jnp.zeros_like(query_bias), value_bias])
    projected = (matmul(mod_a, input_weight) + qkv_bias).astype(jnp.bfloat16)
    queries = projected[:, :width].reshape(images, rows, heads, HEAD_DIM)
    keys_all = projected[:, width : 2 * width].reshape(images, rows, heads, HEAD_DIM)
    values_all = projected[:, 2 * width :].reshape(images, rows, heads, HEAD_DIM)
    scores = (
        jnp.einsum("bqhe,bkhe->bhqk", queries, keys_all, preferred_element_type=jnp.float32)
        * factor
    )
    highest = jnp.max(scores, axis=-1, keepdims=True)
    weights = jnp.exp(scores - highest)
    probs = weights / jnp.sum(weights, axis=-1, keepdims=True)
    probs_b = probs.astype(jnp.bfloat16)
    attended = jnp.einsum(
        "bhqk,bkhe->bqhe", probs_b, values_all, preferred_element_type=jnp.float32
    )
    attended_b = attended.reshape(flat, width).astype(jnp.bfloat16)
    branch_a = (matmul(attended_b, output_weight) + output_bias).reshape(images, rows, width)
    middle = inputs + gate_a * branch_a
    normed_b, inverse_b = normalize(middle)
    mod_b = (normed_b * (1.0 + scale_b) + shift_b).astype(jnp.bfloat16).reshape(flat, width)
    expanded = matmul(mod_b, expand_weight) + expand_bias
    tanh_part = jnp.tanh(GELU_C * (expanded + 0.044715 * expanded * expanded * expanded))
    activated_b = (0.5 * expanded * (1.0 + tanh_part)).astype(jnp.bfloat16)
    branch_b = (matmul(activated_b, contract_weight) + contract_bias).reshape(images, rows, width)
    alive = occupied.astype(jnp.float32)[:, None, None]
    layer_out = (middle + gate_b * branch_b) * alive
    grad_out = cotangent.astype(jnp.float32) * alive
    grad_gate_b = jnp.sum(grad_out * branch_b, axis=1)
    grad_branch_b = (grad_out * gate_b).astype(jnp.bfloat16).reshape(flat, width)
    blocks = 1
    for a in AXES:
        blocks *= sizes[a]
    ff = activated_b.shape[1]
    split = ff // width
    act_perm = stage_order(
        activated_b.reshape(flat, blocks, split, width // blocks)
        .transpose(0, 2, 1, 3)
        .reshape(flat, split, width),
        sizes,
        width // blocks,
    )
    contract_parts = [
        left_trans(act_perm[:, q], grad_branch_b).astype(jnp.bfloat16) for q in range(split)
    ]
    contract_bias_grad = stage_order(
        jnp.sum(grad_branch_b.astype(jnp.float32), axis=0), sizes, width // blocks
    )
    grad_act = right_trans(grad_branch_b, contract_weight)
    slope = 0.5 * (1.0 + tanh_part) + 0.5 * expanded * (1.0 - tanh_part * tanh_part) * GELU_C * (
        1.0 + 3.0 * 0.044715 * expanded * expanded
    )
    grad_exp_b = (grad_act * slope).astype(jnp.bfloat16)
    expand_grad = left_trans(stage_order(mod_b, sizes, width // blocks), grad_exp_b).astype(jnp.bfloat16)
    expand_bias_grad = stage_order(
        jnp.sum(grad_exp_b.astype(jnp.float32), axis=0)
        .reshape(blocks, split, width // blocks)
        .transpose(1, 0, 2)
        .reshape(split, width),
        sizes,
        width // blocks,
    )
    packed_a = jnp.concatenate(
        [expand_grad]
        + contract_parts
        + [bias_columns([contract_bias_grad] + [expand_bias_grad[q] for q in range(split)], width)],
        axis=1,
    )
    packed_a, grad_exp_b = lax.optimization_barrier((packed_a, grad_exp_b))
    chain_a = reduce_stages(packed_a, STAGES[:2])
    grad_mod_b = right_trans(grad_exp_b, expand_weight).reshape(images, rows, width)
    grad_shift_b = jnp.sum(grad_mod_b, axis=1)
    grad_scale_b = jnp.sum(grad_mod_b * normed_b, axis=1)
    grad_middle = grad_out + norm_back(grad_mod_b * (1.0 + scale_b), normed_b, inverse_b)
    grad_gate_a = jnp.sum(grad_middle * branch_a, axis=1)
    grad_branch_a = (grad_middle * gate_a).astype(jnp.bfloat16).reshape(flat, width)
    output_grad = left_trans(stage_order(attended_b, sizes, width // blocks, STAGES_B), grad_branch_a).astype(
        jnp.bfloat16
    )
    output_bias_grad = stage_order(
        jnp.sum(grad_branch_a.astype(jnp.float32), axis=0), sizes, width // blocks, STAGES_B
    )
    grad_att_b = (
        right_trans(grad_branch_a, output_weight)
        .astype(jnp.bfloat16)
        .reshape(images, rows, heads, HEAD_DIM)
    )
    grad_probs = jnp.einsum(
        "bqhe,bkhe->bhqk", grad_att_b, values_all, preferred_element_type=jnp.float32
    )
    grad_values = jnp.einsum(
        "bhqk,bqhe->bkhe", probs_b, grad_att_b, preferred_element_type=jnp.float32
    )
    inner = jnp.sum(grad_probs * probs, axis=-1, keepdims=True)
    grad_scores_b = (probs * (grad_probs - inner)).astype(jnp.bfloat16)
    grad_queries = (
        jnp.einsum("bhqk,bkhe->bqhe", grad_scores_b, keys_all, preferred_element_type=jnp.float32)
        * factor
    )
    grad_keys = (
        jnp.einsum("bhqk,bqhe->bkhe", grad_scores_b, queries, preferred_element_type=jnp.float32)
        * factor
    )
    grad_proj_b = jnp.concatenate(
        [
            grad_queries.reshape(flat, width),
            grad_keys.reshape(flat, width),
            grad_values.reshape(flat, width),
        ],
        axis=1,
    ).astype(jnp.bfloat16)
    input_grad = left_trans(stage_order(mod_a, sizes, width // blocks, STAGES_B), grad_proj_b).astype(
        jnp.bfloat16
    )
    bias_sums = jnp.sum(grad_proj_b.astype(jnp.float32), axis=0)
    query_bias_grad = stage_order(bias_sums[:width], sizes, width // blocks, STAGES_B)
    value_bias_grad = stage_order(bias_sums[2 * width :], sizes, width // blocks, STAGES_B)
    chain_b = reduce_stages(
        jnp.concatenate(
            [
                input_grad,
                output_grad,
                bias_columns([query_bias_grad, value_bias_grad, output_bias_grad], width),
            ],
            axis=1,
        ),
        STAGES_B[:1],
    )
    chain_b = reduce_rest(chain_b, STAGES_B[1:2]).astype(jnp.bfloat16)
    grad_mod_a = right_trans(grad_proj_b, input_weight).reshape(images, rows, width)
    grad_shift_a = jnp.sum(grad_mod_a, axis=1)
    grad_scale_a = jnp.sum(grad_mod_a * normed_a, axis=1)
    tokens_grad = grad_middle + norm_back(grad_mod_a * (1.0 + scale_a), normed_a, inverse_a)
    modulation_terms = jnp.stack(
        [grad_shift_a, grad_scale_a, grad_gate_a, grad_shift_b, grad_scale_b, grad_gate_b], axis=1
    ).reshape(images, 6 * width)
    modulation_own = modulation_terms.astype(jnp.bfloat16)
    modulation_cols = lax.all_to_all(modulation_own, "zl", split_axis=1, concat_axis=0, tiled=True)
    silu_terms = right_trans(modulation_cols, modulation_weight)
    silu_sums = lax.psum_scatter(silu_terms, "zl", scatter_dimension=0, tiled=True)
    condition_grad = silu_sums * sigmoid * (1.0 + cond_full * (1.0 - sigmoid))
    factors = gather_dp(jnp.concatenate([silu_pair, modulation_cols], axis=1))
    silu_all = factors[:, :width]
    mod_all = factors[:, width:]
    dp_index = lax.axis_index(DP)
    dp_count = factors.shape[0] // silu_pair.shape[0]
    row_block = width // dp_count
    silu_rows = lax.dynamic_slice_in_dim(silu_all, dp_index * row_block, row_block, axis=1)
    modulation_weight_grad = left_trans(silu_rows, mod_all)
    bias_all = jnp.sum(mod_all.astype(jnp.float32), axis=0).reshape(-1, width)
    modulation_bias_grad = lax.dynamic_slice_in_dim(bias_all, dp_index * row_block, row_block, axis=1)
    chain_a = reduce_rest(chain_a, STAGES[2:])
    chain_b = reduce_rest(chain_b, STAGES_B[2:])
    three = input_weight.shape[1]
    fw = expand_weight.shape[1]
    input_weight_grad = chain_b[:, :three]
    output_weight_grad = chain_b[:, three : three + width]
    qb_grad = chain_b[:, three + width]
    vb_grad = chain_b[:, three + width + 1]
    ob_grad = chain_b[:, three + width + 2]
    expand_weight_grad = chain_a[:, :fw]
    contract_weight_grad = chain_a[:, fw : fw + split * width].reshape(-1, split, width)
    contract_weight_grad = contract_weight_grad.transpose(1, 0, 2).reshape(-1, width)
    cb_grad = chain_a[:, fw + split * width]
    eb_grad = chain_a[:, fw + split * width + 1 : fw + split * width + 1 + split].T.reshape(-1)
    summed = (
        input_weight_grad,
        qb_grad,
        vb_grad,
        output_weight_grad,
        ob_grad,
        expand_weight_grad,
        eb_grad,
        contract_weight_grad,
        cb_grad,
    )
    return (
        layer_out,
        tokens_grad,
        condition_grad,
        modulation_weight_grad,
        modulation_bias_grad,
        *summed,
    )


def solution(mesh):
    dp_size, mod_size = mesh.devices.shape
    rest = dp_size // 4
    side = int(round(rest ** 0.5))
    shape = (side, 2, rest // side, 2, mod_size)
    sizes = dict(zip(AXES, shape))
    physical = Mesh(np.asarray(mesh.devices).reshape(shape), AXES)
    ALL = AXES
    placed = (
        P(ALL, None, None),
        P(ALL, None),
        P(ALL),
        P(None, "zl"),
        P("zl", None),
        P(),
        P(),
        P(),
        P(),
        P(),
        P(),
        P(),
        P(),
        P(),
        P(ALL, None, None),
    )
    import functools

    return jax.shard_map(
        functools.partial(per_device, sizes),
        mesh=physical,
        in_specs=placed,
        out_specs=(
            P(ALL, None, None),
            P(ALL, None, None),
            P(ALL, None),
            P(DP, "zl"),
            P("zl", DP),
            P(ALL, None),
            P(ALL),
            P(ALL),
            P(ALL, None),
            P(ALL),
            P(ALL, None),
            P(ALL),
            P(ALL, None),
            P(ALL),
        ),
        check_vma=False,
    )
```

```python
import functools

import jax
import jax.numpy as jnp
import numpy as np
from jax import lax
from jax.experimental import pallas as pl
from jax.experimental.pallas import tpu as pltpu
from jax.sharding import Mesh
from jax.sharding import PartitionSpec as P

HEAD_DIM = 64
LANES = 128


def _nt(a, b):
    return lax.dot_general(a, b, (((1,), (1,)), ((), ())), preferred_element_type=jnp.float32)


def _tn(a, b):
    return lax.dot_general(a, b, (((0,), (0,)), ((), ())), preferred_element_type=jnp.float32)


def _probs(q, k, head, factor):
    lane = lax.broadcasted_iota(jnp.int32, (1, LANES), 1)
    mine = (lane // HEAD_DIM) == head
    qh = jnp.where(mine, q, jnp.zeros_like(q))
    scores = _nt(qh, k) * factor
    weights = jnp.exp(scores - jnp.max(scores, axis=-1, keepdims=True))
    return mine, qh, weights / jnp.sum(weights, axis=-1, keepdims=True)


def _fwd_kernel(factor, q_ref, k_ref, v_ref, o_ref):
    q = q_ref[...]
    k = k_ref[...]
    v = v_ref[...]
    out = jnp.zeros(o_ref.shape, jnp.float32)
    for head in range(LANES // HEAD_DIM):
        mine, _, probs = _probs(q, k, head, factor)
        vh = jnp.where(mine, v, jnp.zeros_like(v))
        out = out + jnp.dot(probs.astype(v.dtype), vh, preferred_element_type=jnp.float32)
    o_ref[...] = out.astype(o_ref.dtype)


def _bwd_kernel(factor, q_ref, k_ref, v_ref, d_ref, dq_ref, dk_ref, dv_ref):
    q = q_ref[...]
    k = k_ref[...]
    v = v_ref[...]
    d = d_ref[...]
    dq = jnp.zeros(dq_ref.shape, jnp.float32)
    dk = jnp.zeros(dk_ref.shape, jnp.float32)
    dv = jnp.zeros(dv_ref.shape, jnp.float32)
    for head in range(LANES // HEAD_DIM):
        mine, qh, probs = _probs(q, k, head, factor)
        dh = jnp.where(mine, d, jnp.zeros_like(d))
        kh = jnp.where(mine, k, jnp.zeros_like(k))
        dprobs = _nt(dh, v)
        dv = dv + _tn(probs.astype(d.dtype), dh)
        inner = jnp.sum(dprobs * probs, axis=-1, keepdims=True)
        dscores = (probs * (dprobs - inner)).astype(q.dtype)
        dq = dq + jnp.dot(dscores, kh, preferred_element_type=jnp.float32)
        dk = dk + _tn(dscores, qh)
    dq_ref[...] = (dq * factor).astype(dq_ref.dtype)
    dk_ref[...] = (dk * factor).astype(dk_ref.dtype)
    dv_ref[...] = dv.astype(dv_ref.dtype)


def attention_forward(projected, images):
    tokens, three = projected.shape
    rows, width = tokens // images, three // 3
    pairs = width // LANES
    factor = HEAD_DIM ** (-0.5)

    def part(offset):
        return pl.BlockSpec((rows, LANES), lambda b, j: (b, offset + j))

    flops = 2 * 2 * images * (width // HEAD_DIM) * rows * rows * LANES
    return pl.pallas_call(
        functools.partial(_fwd_kernel, factor),
        out_shape=jax.ShapeDtypeStruct((tokens, width), projected.dtype),
        grid=(images, pairs),
        in_specs=[part(0), part(pairs), part(2 * pairs)],
        out_specs=pl.BlockSpec((rows, LANES), lambda b, j: (b, j)),
        compiler_params=pltpu.CompilerParams(dimension_semantics=("parallel", "parallel")),
        cost_estimate=pl.CostEstimate(
            flops=flops, transcendentals=images * (width // HEAD_DIM) * rows * rows,
            bytes_accessed=2 * tokens * (three + width),
        ),
    )(projected, projected, projected)


def attention_backward(projected, grad_attended, images):
    tokens, three = projected.shape
    rows, width = tokens // images, three // 3
    pairs = width // LANES
    factor = HEAD_DIM ** (-0.5)

    def part(offset):
        return pl.BlockSpec((rows, LANES), lambda b, j: (b, offset + j))

    out = jax.ShapeDtypeStruct((tokens, width), projected.dtype)
    flops = 5 * 2 * 2 * images * (width // HEAD_DIM) * rows * rows * LANES
    dq, dk, dv = pl.pallas_call(
        functools.partial(_bwd_kernel, factor),
        out_shape=(out, out, out),
        grid=(images, pairs),
        in_specs=[part(0), part(pairs), part(2 * pairs), part(0)],
        out_specs=[part(0)] * 3,
        compiler_params=pltpu.CompilerParams(dimension_semantics=("parallel", "parallel")),
        cost_estimate=pl.CostEstimate(
            flops=flops, transcendentals=images * (width // HEAD_DIM) * rows * rows,
            bytes_accessed=2 * tokens * (three + 4 * width),
        ),
    )(projected, projected, projected, grad_attended)
    return jnp.concatenate([dq, dk, dv], axis=1)


EPS = 1e-06
GELU_C = 0.7978845608028654

AXES = ("y", "zh", "x", "c", "zl")
DP = ("y", "zh", "x", "c")
STAGES = ("c", "x", "y", "zh", "zl")
STAGES_B = ("c", "y", "x", "zh", "zl")


def matmul(left, right):
    return jnp.dot(left, right, preferred_element_type=jnp.float32)


def left_trans(left, right):
    return lax.dot_general(
        left, right, (((0,), (0,)), ((), ())), preferred_element_type=jnp.float32
    )


def right_trans(left, right):
    return lax.dot_general(
        left, right, (((1,), (1,)), ((), ())), preferred_element_type=jnp.float32
    )


def normalize(values):
    centre = values - jnp.mean(values, axis=-1, keepdims=True)
    inverse = lax.rsqrt(jnp.mean(centre * centre, axis=-1, keepdims=True) + EPS)
    return (centre * inverse, inverse)


def norm_back(grad, normed, inverse):
    return inverse * (
        grad
        - jnp.mean(grad, axis=-1, keepdims=True)
        - normed * jnp.mean(grad * normed, axis=-1, keepdims=True)
    )


def stage_order(values, sizes, inner, stages=STAGES):
    lead = values.shape[:-1]
    shape = [sizes[a] for a in AXES]
    values = values.reshape(*lead, *shape, inner)
    n = len(lead)
    order = list(range(n)) + [n + AXES.index(a) for a in stages] + [n + len(AXES)]
    return jnp.transpose(values, order).reshape(*lead, -1)


def reduce_stages(packed, stages):
    for a in stages:
        packed = lax.psum_scatter(packed, a, scatter_dimension=0, tiled=True)
    return packed


def reduce_rest(packed, axes):
    count = 1
    for a in axes:
        count *= lax.axis_size(a)
    chunks = packed.reshape(count, packed.shape[0] // count, packed.shape[1])
    chunks = lax.all_to_all(chunks, axes, 0, 0, tiled=False)
    return jnp.sum(chunks.astype(jnp.float32), axis=0)


def bias_columns(columns, rows):
    block = jnp.stack(columns, axis=1)
    return jnp.pad(block, ((0, 0), (0, 128 - block.shape[1]))).astype(jnp.bfloat16)


def gather_dp(values):
    count = 1
    for a in DP:
        count *= lax.axis_size(a)
    copies = jnp.broadcast_to(values[None], (count,) + values.shape)
    return lax.all_to_all(copies, DP, 0, 0, tiled=False).reshape(-1, values.shape[1])


def per_device(
    sizes,
    tokens,
    condition,
    occupied,
    modulation_weight,
    modulation_bias,
    input_weight,
    query_bias,
    value_bias,
    output_weight,
    output_bias,
    expand_weight,
    expand_bias,
    contract_weight,
    contract_bias,
    cotangent,
):
    images, rows, width = tokens.shape
    heads = width // HEAD_DIM
    flat = images * rows
    factor = HEAD_DIM ** (-0.5)
    cond_full = condition.astype(jnp.float32)
    sigmoid = jax.nn.sigmoid(cond_full)
    silu_b = (cond_full * sigmoid).astype(jnp.bfloat16)
    silu_pair = lax.all_gather(silu_b, "zl", axis=0, tiled=True)
    mod_cols = matmul(silu_pair, modulation_weight) + modulation_bias.reshape(1, -1)
    modulation = lax.all_to_all(mod_cols, "zl", split_axis=0, concat_axis=1, tiled=True).reshape(
        images, 6, 1, width
    )
    shift_a = modulation[:, 0]
    scale_a = modulation[:, 1]
    gate_a = modulation[:, 2]
    shift_b = modulation[:, 3]
    scale_b = modulation[:, 4]
    gate_b = modulation[:, 5]
    inputs = tokens.astype(jnp.float32)
    normed_a, inverse_a = normalize(inputs)
    mod_a = (normed_a * (1.0 + scale_a) + shift_a).astype(jnp.bfloat16).reshape(flat, width)
    qkv_bias = jnp.concatenate([query_bias, jnp.zeros_like(query_bias), value_bias])
    projected = (matmul(mod_a, input_weight) + qkv_bias).astype(jnp.bfloat16)
    attended_b = attention_forward(projected, images)
    branch_a = (matmul(attended_b, output_weight) + output_bias).reshape(images, rows, width)
    middle = inputs + gate_a * branch_a
    normed_b, inverse_b = normalize(middle)
    mod_b = (normed_b * (1.0 + scale_b) + shift_b).astype(jnp.bfloat16).reshape(flat, width)
    expanded = matmul(mod_b, expand_weight) + expand_bias
    tanh_part = jnp.tanh(GELU_C * (expanded + 0.044715 * expanded * expanded * expanded))
    activated_b = (0.5 * expanded * (1.0 + tanh_part)).astype(jnp.bfloat16)
    branch_b = (matmul(activated_b, contract_weight) + contract_bias).reshape(images, rows, width)
    alive = occupied.astype(jnp.float32)[:, None, None]
    layer_out = (middle + gate_b * branch_b) * alive
    grad_out = cotangent.astype(jnp.float32) * alive
    grad_gate_b = jnp.sum(grad_out * branch_b, axis=1)
    grad_branch_b = (grad_out * gate_b).astype(jnp.bfloat16).reshape(flat, width)
    blocks = 1
    for a in AXES:
        blocks *= sizes[a]
    ff = activated_b.shape[1]
    split = ff // width
    act_perm = stage_order(
        activated_b.reshape(flat, blocks, split, width // blocks)
        .transpose(0, 2, 1, 3)
        .reshape(flat, split, width),
        sizes,
        width // blocks,
    )
    contract_parts = [
        left_trans(act_perm[:, q], grad_branch_b).astype(jnp.bfloat16) for q in range(split)
    ]
    contract_bias_grad = stage_order(
        jnp.sum(grad_branch_b.astype(jnp.float32), axis=0), sizes, width // blocks
    )
    grad_act = right_trans(grad_branch_b, contract_weight)
    slope = 0.5 * (1.0 + tanh_part) + 0.5 * expanded * (1.0 - tanh_part * tanh_part) * GELU_C * (
        1.0 + 3.0 * 0.044715 * expanded * expanded
    )
    grad_exp_b = (grad_act * slope).astype(jnp.bfloat16)
    expand_grad = left_trans(stage_order(mod_b, sizes, width // blocks), grad_exp_b).astype(jnp.bfloat16)
    expand_bias_grad = stage_order(
        jnp.sum(grad_exp_b.astype(jnp.float32), axis=0)
        .reshape(blocks, split, width // blocks)
        .transpose(1, 0, 2)
        .reshape(split, width),
        sizes,
        width // blocks,
    )
    packed_a = jnp.concatenate(
        [expand_grad]
        + contract_parts
        + [bias_columns([contract_bias_grad] + [expand_bias_grad[q] for q in range(split)], width)],
        axis=1,
    )
    packed_a, grad_exp_b = lax.optimization_barrier((packed_a, grad_exp_b))
    chain_a = reduce_stages(packed_a, STAGES[:2])
    grad_mod_b = right_trans(grad_exp_b, expand_weight).reshape(images, rows, width)
    grad_shift_b = jnp.sum(grad_mod_b, axis=1)
    grad_scale_b = jnp.sum(grad_mod_b * normed_b, axis=1)
    grad_middle = grad_out + norm_back(grad_mod_b * (1.0 + scale_b), normed_b, inverse_b)
    grad_gate_a = jnp.sum(grad_middle * branch_a, axis=1)
    grad_branch_a = (grad_middle * gate_a).astype(jnp.bfloat16).reshape(flat, width)
    output_grad = left_trans(stage_order(attended_b, sizes, width // blocks, STAGES_B), grad_branch_a).astype(
        jnp.bfloat16
    )
    output_bias_grad = stage_order(
        jnp.sum(grad_branch_a.astype(jnp.float32), axis=0), sizes, width // blocks, STAGES_B
    )
    grad_att_b = right_trans(grad_branch_a, output_weight).astype(jnp.bfloat16)
    grad_proj_b = attention_backward(projected, grad_att_b, images)
    input_grad = left_trans(stage_order(mod_a, sizes, width // blocks, STAGES_B), grad_proj_b).astype(
        jnp.bfloat16
    )
    bias_sums = jnp.sum(grad_proj_b.astype(jnp.float32), axis=0)
    query_bias_grad = stage_order(bias_sums[:width], sizes, width // blocks, STAGES_B)
    value_bias_grad = stage_order(bias_sums[2 * width :], sizes, width // blocks, STAGES_B)
    chain_b = reduce_stages(
        jnp.concatenate(
            [
                input_grad,
                output_grad,
                bias_columns([query_bias_grad, value_bias_grad, output_bias_grad], width),
            ],
            axis=1,
        ),
        STAGES_B[:1],
    )
    chain_b = reduce_rest(chain_b, STAGES_B[1:2]).astype(jnp.bfloat16)
    grad_mod_a = right_trans(grad_proj_b, input_weight).reshape(images, rows, width)
    grad_shift_a = jnp.sum(grad_mod_a, axis=1)
    grad_scale_a = jnp.sum(grad_mod_a * normed_a, axis=1)
    tokens_grad = grad_middle + norm_back(grad_mod_a * (1.0 + scale_a), normed_a, inverse_a)
    modulation_terms = jnp.stack(
        [grad_shift_a, grad_scale_a, grad_gate_a, grad_shift_b, grad_scale_b, grad_gate_b], axis=1
    ).reshape(images, 6 * width)
    modulation_own = modulation_terms.astype(jnp.bfloat16)
    modulation_cols = lax.all_to_all(modulation_own, "zl", split_axis=1, concat_axis=0, tiled=True)
    silu_terms = right_trans(modulation_cols, modulation_weight)
    silu_sums = lax.psum_scatter(silu_terms, "zl", scatter_dimension=0, tiled=True)
    condition_grad = silu_sums * sigmoid * (1.0 + cond_full * (1.0 - sigmoid))
    factors = gather_dp(jnp.concatenate([silu_pair, modulation_cols], axis=1))
    silu_all = factors[:, :width]
    mod_all = factors[:, width:]
    dp_index = lax.axis_index(DP)
    dp_count = factors.shape[0] // silu_pair.shape[0]
    row_block = width // dp_count
    silu_rows = lax.dynamic_slice_in_dim(silu_all, dp_index * row_block, row_block, axis=1)
    modulation_weight_grad = left_trans(silu_rows, mod_all)
    bias_all = jnp.sum(mod_all.astype(jnp.float32), axis=0).reshape(-1, width)
    modulation_bias_grad = lax.dynamic_slice_in_dim(bias_all, dp_index * row_block, row_block, axis=1)
    chain_a = reduce_rest(chain_a, STAGES[2:])
    chain_b = reduce_rest(chain_b, STAGES_B[2:])
    three = input_weight.shape[1]
    fw = expand_weight.shape[1]
    input_weight_grad = chain_b[:, :three]
    output_weight_grad = chain_b[:, three : three + width]
    qb_grad = chain_b[:, three + width]
    vb_grad = chain_b[:, three + width + 1]
    ob_grad = chain_b[:, three + width + 2]
    expand_weight_grad = chain_a[:, :fw]
    contract_weight_grad = chain_a[:, fw : fw + split * width].reshape(-1, split, width)
    contract_weight_grad = contract_weight_grad.transpose(1, 0, 2).reshape(-1, width)
    cb_grad = chain_a[:, fw + split * width]
    eb_grad = chain_a[:, fw + split * width + 1 : fw + split * width + 1 + split].T.reshape(-1)
    summed = (
        input_weight_grad,
        qb_grad,
        vb_grad,
        output_weight_grad,
        ob_grad,
        expand_weight_grad,
        eb_grad,
        contract_weight_grad,
        cb_grad,
    )
    return (
        layer_out,
        tokens_grad,
        condition_grad,
        modulation_weight_grad,
        modulation_bias_grad,
        *summed,
    )


def solution(mesh):
    dp_size, mod_size = mesh.devices.shape
    rest = dp_size // 4
    side = int(round(rest ** 0.5))
    shape = (side, 2, rest // side, 2, mod_size)
    sizes = dict(zip(AXES, shape))
    physical = Mesh(np.asarray(mesh.devices).reshape(shape), AXES)
    ALL = AXES
    placed = (
        P(ALL, None, None),
        P(ALL, None),
        P(ALL),
        P(None, "zl"),
        P("zl", None),
        P(),
        P(),
        P(),
        P(),
        P(),
        P(),
        P(),
        P(),
        P(),
        P(ALL, None, None),
    )
    return jax.shard_map(
        functools.partial(per_device, sizes),
        mesh=physical,
        in_specs=placed,
        out_specs=(
            P(ALL, None, None),
            P(ALL, None, None),
            P(ALL, None),
            P(DP, "zl"),
            P("zl", DP),
            P(ALL, None),
            P(ALL),
            P(ALL),
            P(ALL, None),
            P(ALL),
            P(ALL, None),
            P(ALL),
            P(ALL, None),
            P(ALL),
        ),
        check_vma=False,
    )
```

```python
import functools

import jax
import jax.numpy as jnp
import numpy as np
from jax import lax
from jax.experimental import pallas as pl
from jax.experimental.pallas import tpu as pltpu
from jax.sharding import Mesh
from jax.sharding import PartitionSpec as P

HEAD_DIM = 64
LANES = 128


def _nt(a, b):
    return lax.dot_general(a, b, (((1,), (1,)), ((), ())), preferred_element_type=jnp.float32)


def _tn(a, b):
    return lax.dot_general(a, b, (((0,), (0,)), ((), ())), preferred_element_type=jnp.float32)


def _probs(q, k, head, factor):
    lane = lax.broadcasted_iota(jnp.int32, (1, LANES), 1)
    mine = (lane // HEAD_DIM) == head
    qh = jnp.where(mine, q, jnp.zeros_like(q))
    scores = _nt(qh, k) * factor
    weights = jnp.exp(scores - jnp.max(scores, axis=-1, keepdims=True))
    return mine, qh, weights / jnp.sum(weights, axis=-1, keepdims=True)


def _fwd_kernel(factor, q_ref, k_ref, v_ref, o_ref):
    q = q_ref[...]
    k = k_ref[...]
    v = v_ref[...]
    out = jnp.zeros(o_ref.shape, jnp.float32)
    for head in range(LANES // HEAD_DIM):
        mine, _, probs = _probs(q, k, head, factor)
        vh = jnp.where(mine, v, jnp.zeros_like(v))
        out = out + jnp.dot(probs.astype(v.dtype), vh, preferred_element_type=jnp.float32)
    o_ref[...] = out.astype(o_ref.dtype)


def _bwd_kernel(factor, q_ref, k_ref, v_ref, d_ref, dq_ref, dk_ref, dv_ref):
    q = q_ref[...]
    k = k_ref[...]
    v = v_ref[...]
    d = d_ref[...]
    dq = jnp.zeros(dq_ref.shape, jnp.float32)
    dk = jnp.zeros(dk_ref.shape, jnp.float32)
    dv = jnp.zeros(dv_ref.shape, jnp.float32)
    for head in range(LANES // HEAD_DIM):
        mine, qh, probs = _probs(q, k, head, factor)
        dh = jnp.where(mine, d, jnp.zeros_like(d))
        kh = jnp.where(mine, k, jnp.zeros_like(k))
        dprobs = _nt(dh, v)
        dv = dv + _tn(probs.astype(d.dtype), dh)
        inner = jnp.sum(dprobs * probs, axis=-1, keepdims=True)
        dscores = (probs * (dprobs - inner)).astype(q.dtype)
        dq = dq + jnp.dot(dscores, kh, preferred_element_type=jnp.float32)
        dk = dk + _tn(dscores, qh)
    dq_ref[...] = (dq * factor).astype(dq_ref.dtype)
    dk_ref[...] = (dk * factor).astype(dk_ref.dtype)
    dv_ref[...] = dv.astype(dv_ref.dtype)


def attention_forward(projected, images):
    tokens, three = projected.shape
    rows, width = tokens // images, three // 3
    pairs = width // LANES
    factor = HEAD_DIM ** (-0.5)

    def part(offset):
        return pl.BlockSpec((rows, LANES), lambda b, j: (b, offset + j))

    flops = 2 * 2 * images * (width // HEAD_DIM) * rows * rows * LANES
    return pl.pallas_call(
        functools.partial(_fwd_kernel, factor),
        out_shape=jax.ShapeDtypeStruct((tokens, width), projected.dtype),
        grid=(images, pairs),
        in_specs=[part(0), part(pairs), part(2 * pairs)],
        out_specs=pl.BlockSpec((rows, LANES), lambda b, j: (b, j)),
        compiler_params=pltpu.CompilerParams(dimension_semantics=("parallel", "parallel")),
        cost_estimate=pl.CostEstimate(
            flops=flops, transcendentals=images * (width // HEAD_DIM) * rows * rows,
            bytes_accessed=2 * tokens * (three + width),
        ),
    )(projected, projected, projected)


def attention_backward(projected, grad_attended, images):
    tokens, three = projected.shape
    rows, width = tokens // images, three // 3
    pairs = width // LANES
    factor = HEAD_DIM ** (-0.5)

    def part(offset):
        return pl.BlockSpec((rows, LANES), lambda b, j: (b, offset + j))

    out = jax.ShapeDtypeStruct((tokens, width), projected.dtype)
    flops = 5 * 2 * 2 * images * (width // HEAD_DIM) * rows * rows * LANES
    dq, dk, dv = pl.pallas_call(
        functools.partial(_bwd_kernel, factor),
        out_shape=(out, out, out),
        grid=(images, pairs),
        in_specs=[part(0), part(pairs), part(2 * pairs), part(0)],
        out_specs=[part(0)] * 3,
        compiler_params=pltpu.CompilerParams(dimension_semantics=("parallel", "parallel")),
        cost_estimate=pl.CostEstimate(
            flops=flops, transcendentals=images * (width // HEAD_DIM) * rows * rows,
            bytes_accessed=2 * tokens * (three + 4 * width),
        ),
    )(projected, projected, projected, grad_attended)
    return jnp.concatenate([dq, dk, dv], axis=1)


EPS = 1e-06
GELU_C = 0.7978845608028654

AXES = ("y", "zh", "x", "c", "zl")
DP = ("y", "zh", "x", "c")
STAGES = ("c", "x", "y", "zh", "zl")
STAGES_B = ("c", "y", "x", "zh", "zl")


def matmul(left, right):
    return jnp.dot(left, right, preferred_element_type=jnp.float32)


def left_trans(left, right):
    return lax.dot_general(
        left, right, (((0,), (0,)), ((), ())), preferred_element_type=jnp.float32
    )


def right_trans(left, right):
    return lax.dot_general(
        left, right, (((1,), (1,)), ((), ())), preferred_element_type=jnp.float32
    )


def normalize(values):
    centre = values - jnp.mean(values, axis=-1, keepdims=True)
    inverse = lax.rsqrt(jnp.mean(centre * centre, axis=-1, keepdims=True) + EPS)
    return (centre * inverse, inverse)


def norm_back(grad, normed, inverse):
    return inverse * (
        grad
        - jnp.mean(grad, axis=-1, keepdims=True)
        - normed * jnp.mean(grad * normed, axis=-1, keepdims=True)
    )


def stage_order(values, sizes, inner, stages=STAGES):
    lead = values.shape[:-1]
    shape = [sizes[a] for a in AXES]
    values = values.reshape(*lead, *shape, inner)
    n = len(lead)
    order = list(range(n)) + [n + AXES.index(a) for a in stages] + [n + len(AXES)]
    return jnp.transpose(values, order).reshape(*lead, -1)


def reduce_stages(packed, stages):
    for a in stages:
        packed = lax.psum_scatter(packed, a, scatter_dimension=0, tiled=True)
    return packed


def reduce_rest(packed, axes):
    count = 1
    for a in axes:
        count *= lax.axis_size(a)
    chunks = packed.reshape(count, packed.shape[0] // count, packed.shape[1])
    chunks = lax.all_to_all(chunks, axes, 0, 0, tiled=False)
    return jnp.sum(chunks.astype(jnp.float32), axis=0)


def bias_columns(columns, rows):
    block = jnp.stack(columns, axis=1)
    return jnp.pad(block, ((0, 0), (0, 128 - block.shape[1]))).astype(jnp.bfloat16)


def gather_dp(values):
    count = 1
    for a in DP:
        count *= lax.axis_size(a)
    copies = jnp.broadcast_to(values[None], (count,) + values.shape)
    return lax.all_to_all(copies, DP, 0, 0, tiled=False).reshape(-1, values.shape[1])


def per_device(
    sizes,
    tokens,
    condition,
    occupied,
    modulation_weight,
    modulation_bias,
    input_weight,
    query_bias,
    value_bias,
    output_weight,
    output_bias,
    expand_weight,
    expand_bias,
    contract_weight,
    contract_bias,
    cotangent,
):
    images, rows, width = tokens.shape
    heads = width // HEAD_DIM
    flat = images * rows
    factor = HEAD_DIM ** (-0.5)
    cond_full = condition.astype(jnp.float32)
    sigmoid = jax.nn.sigmoid(cond_full)
    silu_b = (cond_full * sigmoid).astype(jnp.bfloat16)
    silu_pair = lax.all_gather(silu_b, "zl", axis=0, tiled=True)
    mod_cols = matmul(silu_pair, modulation_weight) + modulation_bias.reshape(1, -1)
    modulation = lax.all_to_all(mod_cols, "zl", split_axis=0, concat_axis=1, tiled=True).reshape(
        images, 6, 1, width
    )
    shift_a = modulation[:, 0]
    scale_a = modulation[:, 1]
    gate_a = modulation[:, 2]
    shift_b = modulation[:, 3]
    scale_b = modulation[:, 4]
    gate_b = modulation[:, 5]
    inputs = tokens.astype(jnp.float32)
    normed_a, inverse_a = normalize(inputs)
    mod_a = (normed_a * (1.0 + scale_a) + shift_a).astype(jnp.bfloat16).reshape(flat, width)
    qkv_bias = jnp.concatenate([query_bias, jnp.zeros_like(query_bias), value_bias])
    projected = (matmul(mod_a, input_weight) + qkv_bias).astype(jnp.bfloat16)
    attended_b = attention_forward(projected, images)
    branch_a = (matmul(attended_b, output_weight) + output_bias).reshape(images, rows, width)
    middle = inputs + gate_a * branch_a
    normed_b, inverse_b = normalize(middle)
    mod_b = (normed_b * (1.0 + scale_b) + shift_b).astype(jnp.bfloat16).reshape(flat, width)
    expanded = matmul(mod_b, expand_weight) + expand_bias
    tanh_part = jnp.tanh(GELU_C * (expanded + 0.044715 * expanded * expanded * expanded))
    activated_b = (0.5 * expanded * (1.0 + tanh_part)).astype(jnp.bfloat16)
    branch_b = (matmul(activated_b, contract_weight) + contract_bias).reshape(images, rows, width)
    alive = occupied.astype(jnp.float32)[:, None, None]
    layer_out = (middle + gate_b * branch_b) * alive
    grad_out = cotangent.astype(jnp.float32) * alive
    grad_gate_b = jnp.sum(grad_out * branch_b, axis=1)
    grad_branch_b = (grad_out * gate_b).astype(jnp.bfloat16).reshape(flat, width)
    blocks = 1
    for a in AXES:
        blocks *= sizes[a]
    ff = activated_b.shape[1]
    split = ff // width
    act_perm = stage_order(
        activated_b.reshape(flat, blocks, split, width // blocks)
        .transpose(0, 2, 1, 3)
        .reshape(flat, split, width),
        sizes,
        width // blocks,
    )
    contract_parts = [
        left_trans(act_perm[:, q], grad_branch_b).astype(jnp.bfloat16) for q in range(split)
    ]
    contract_bias_grad = stage_order(
        jnp.sum(grad_branch_b.astype(jnp.float32), axis=0), sizes, width // blocks
    )
    grad_act = right_trans(grad_branch_b, contract_weight)
    slope = 0.5 * (1.0 + tanh_part) + 0.5 * expanded * (1.0 - tanh_part * tanh_part) * GELU_C * (
        1.0 + 3.0 * 0.044715 * expanded * expanded
    )
    grad_exp_b = (grad_act * slope).astype(jnp.bfloat16)
    expand_grad = left_trans(stage_order(mod_b, sizes, width // blocks), grad_exp_b).astype(jnp.bfloat16)
    expand_bias_grad = stage_order(
        jnp.sum(grad_exp_b.astype(jnp.float32), axis=0)
        .reshape(blocks, split, width // blocks)
        .transpose(1, 0, 2)
        .reshape(split, width),
        sizes,
        width // blocks,
    )
    packed_a = jnp.concatenate(
        [expand_grad]
        + contract_parts
        + [bias_columns([contract_bias_grad] + [expand_bias_grad[q] for q in range(split)], width)],
        axis=1,
    )
    packed_a, grad_exp_b = lax.optimization_barrier((packed_a, grad_exp_b))
    chain_a = reduce_stages(packed_a, STAGES[:1])
    grad_mod_b = right_trans(grad_exp_b, expand_weight).reshape(images, rows, width)
    grad_shift_b = jnp.sum(grad_mod_b, axis=1)
    grad_scale_b = jnp.sum(grad_mod_b * normed_b, axis=1)
    grad_middle = grad_out + norm_back(grad_mod_b * (1.0 + scale_b), normed_b, inverse_b)
    grad_gate_a = jnp.sum(grad_middle * branch_a, axis=1)
    grad_branch_a = (grad_middle * gate_a).astype(jnp.bfloat16).reshape(flat, width)
    output_grad = left_trans(stage_order(attended_b, sizes, width // blocks, STAGES_B), grad_branch_a).astype(
        jnp.bfloat16
    )
    output_bias_grad = stage_order(
        jnp.sum(grad_branch_a.astype(jnp.float32), axis=0), sizes, width // blocks, STAGES_B
    )
    grad_att_b = right_trans(grad_branch_a, output_weight).astype(jnp.bfloat16)
    chain_a, grad_att_b = lax.optimization_barrier((chain_a, grad_att_b))
    chain_a = reduce_stages(chain_a, STAGES[1:2])
    grad_proj_b = attention_backward(projected, grad_att_b, images)
    input_grad = left_trans(stage_order(mod_a, sizes, width // blocks, STAGES_B), grad_proj_b).astype(
        jnp.bfloat16
    )
    bias_sums = jnp.sum(grad_proj_b.astype(jnp.float32), axis=0)
    query_bias_grad = stage_order(bias_sums[:width], sizes, width // blocks, STAGES_B)
    value_bias_grad = stage_order(bias_sums[2 * width :], sizes, width // blocks, STAGES_B)
    chain_b = reduce_stages(
        jnp.concatenate(
            [
                input_grad,
                output_grad,
                bias_columns([query_bias_grad, value_bias_grad, output_bias_grad], width),
            ],
            axis=1,
        ),
        STAGES_B[:1],
    )
    chain_b = reduce_rest(chain_b, STAGES_B[1:2]).astype(jnp.bfloat16)
    grad_mod_a = right_trans(grad_proj_b, input_weight).reshape(images, rows, width)
    grad_shift_a = jnp.sum(grad_mod_a, axis=1)
    grad_scale_a = jnp.sum(grad_mod_a * normed_a, axis=1)
    tokens_grad = grad_middle + norm_back(grad_mod_a * (1.0 + scale_a), normed_a, inverse_a)
    modulation_terms = jnp.stack(
        [grad_shift_a, grad_scale_a, grad_gate_a, grad_shift_b, grad_scale_b, grad_gate_b], axis=1
    ).reshape(images, 6 * width)
    modulation_own = modulation_terms.astype(jnp.bfloat16)
    chain_a, modulation_own = lax.optimization_barrier((chain_a, modulation_own))
    modulation_cols = lax.all_to_all(modulation_own, "zl", split_axis=1, concat_axis=0, tiled=True)
    silu_terms = right_trans(modulation_cols, modulation_weight)
    silu_sums = lax.psum_scatter(silu_terms, "zl", scatter_dimension=0, tiled=True)
    condition_grad = silu_sums * sigmoid * (1.0 + cond_full * (1.0 - sigmoid))
    factors = gather_dp(jnp.concatenate([silu_pair, modulation_cols], axis=1))
    silu_all = factors[:, :width]
    mod_all = factors[:, width:]
    dp_index = lax.axis_index(DP)
    dp_count = factors.shape[0] // silu_pair.shape[0]
    row_block = width // dp_count
    silu_rows = lax.dynamic_slice_in_dim(silu_all, dp_index * row_block, row_block, axis=1)
    modulation_weight_grad = left_trans(silu_rows, mod_all)
    bias_all = jnp.sum(mod_all.astype(jnp.float32), axis=0).reshape(-1, width)
    modulation_bias_grad = lax.dynamic_slice_in_dim(bias_all, dp_index * row_block, row_block, axis=1)
    chain_a = reduce_rest(chain_a, STAGES[2:])
    chain_b = reduce_rest(chain_b, STAGES_B[2:])
    three = input_weight.shape[1]
    fw = expand_weight.shape[1]
    input_weight_grad = chain_b[:, :three]
    output_weight_grad = chain_b[:, three : three + width]
    qb_grad = chain_b[:, three + width]
    vb_grad = chain_b[:, three + width + 1]
    ob_grad = chain_b[:, three + width + 2]
    expand_weight_grad = chain_a[:, :fw]
    contract_weight_grad = chain_a[:, fw : fw + split * width].reshape(-1, split, width)
    contract_weight_grad = contract_weight_grad.transpose(1, 0, 2).reshape(-1, width)
    cb_grad = chain_a[:, fw + split * width]
    eb_grad = chain_a[:, fw + split * width + 1 : fw + split * width + 1 + split].T.reshape(-1)
    summed = (
        input_weight_grad,
        qb_grad,
        vb_grad,
        output_weight_grad,
        ob_grad,
        expand_weight_grad,
        eb_grad,
        contract_weight_grad,
        cb_grad,
    )
    return (
        layer_out,
        tokens_grad,
        condition_grad,
        modulation_weight_grad,
        modulation_bias_grad,
        *summed,
    )


def solution(mesh):
    dp_size, mod_size = mesh.devices.shape
    rest = dp_size // 4
    side = int(round(rest ** 0.5))
    shape = (side, 2, rest // side, 2, mod_size)
    sizes = dict(zip(AXES, shape))
    physical = Mesh(np.asarray(mesh.devices).reshape(shape), AXES)
    ALL = AXES
    placed = (
        P(ALL, None, None),
        P(ALL, None),
        P(ALL),
        P(None, "zl"),
        P("zl", None),
        P(),
        P(),
        P(),
        P(),
        P(),
        P(),
        P(),
        P(),
        P(),
        P(ALL, None, None),
    )
    return jax.shard_map(
        functools.partial(per_device, sizes),
        mesh=physical,
        in_specs=placed,
        out_specs=(
            P(ALL, None, None),
            P(ALL, None, None),
            P(ALL, None),
            P(DP, "zl"),
            P("zl", DP),
            P(ALL, None),
            P(ALL),
            P(ALL),
            P(ALL, None),
            P(ALL),
            P(ALL, None),
            P(ALL),
            P(ALL, None),
            P(ALL),
        ),
        check_vma=False,
    )
```

```python
import functools

import jax
import jax.numpy as jnp
import numpy as np
from jax import lax
from jax.experimental import pallas as pl
from jax.experimental.pallas import tpu as pltpu
from jax.sharding import Mesh
from jax.sharding import PartitionSpec as P

HEAD_DIM = 64
LANES = 128


def _nt(a, b):
    return lax.dot_general(a, b, (((1,), (1,)), ((), ())), preferred_element_type=jnp.float32)


def _tn(a, b):
    return lax.dot_general(a, b, (((0,), (0,)), ((), ())), preferred_element_type=jnp.float32)


def _probs(q, k, head, factor):
    lane = lax.broadcasted_iota(jnp.int32, (1, LANES), 1)
    mine = (lane // HEAD_DIM) == head
    qh = jnp.where(mine, q, jnp.zeros_like(q))
    scores = _nt(qh, k) * factor
    weights = jnp.exp(scores - jnp.max(scores, axis=-1, keepdims=True))
    return mine, qh, weights / jnp.sum(weights, axis=-1, keepdims=True)


def _fwd_kernel(factor, q_ref, k_ref, v_ref, o_ref):
    q = q_ref[...]
    k = k_ref[...]
    v = v_ref[...]
    out = jnp.zeros(o_ref.shape, jnp.float32)
    for head in range(LANES // HEAD_DIM):
        mine, _, probs = _probs(q, k, head, factor)
        vh = jnp.where(mine, v, jnp.zeros_like(v))
        out = out + jnp.dot(probs.astype(v.dtype), vh, preferred_element_type=jnp.float32)
    o_ref[...] = out.astype(o_ref.dtype)


def _bwd_kernel(factor, q_ref, k_ref, v_ref, d_ref, dq_ref, dk_ref, dv_ref):
    q = q_ref[...]
    k = k_ref[...]
    v = v_ref[...]
    d = d_ref[...]
    dq = jnp.zeros(dq_ref.shape, jnp.float32)
    dk = jnp.zeros(dk_ref.shape, jnp.float32)
    dv = jnp.zeros(dv_ref.shape, jnp.float32)
    for head in range(LANES // HEAD_DIM):
        mine, qh, probs = _probs(q, k, head, factor)
        dh = jnp.where(mine, d, jnp.zeros_like(d))
        kh = jnp.where(mine, k, jnp.zeros_like(k))
        dprobs = _nt(dh, v)
        dv = dv + _tn(probs.astype(d.dtype), dh)
        inner = jnp.sum(dprobs * probs, axis=-1, keepdims=True)
        dscores = (probs * (dprobs - inner)).astype(q.dtype)
        dq = dq + jnp.dot(dscores, kh, preferred_element_type=jnp.float32)
        dk = dk + _tn(dscores, qh)
    dq_ref[...] = (dq * factor).astype(dq_ref.dtype)
    dk_ref[...] = (dk * factor).astype(dk_ref.dtype)
    dv_ref[...] = dv.astype(dv_ref.dtype)


def attention_forward(projected, images):
    tokens, three = projected.shape
    rows, width = tokens // images, three // 3
    pairs = width // LANES
    factor = HEAD_DIM ** (-0.5)

    def part(offset):
        return pl.BlockSpec((rows, LANES), lambda b, j: (b, offset + j))

    flops = 2 * 2 * images * (width // HEAD_DIM) * rows * rows * LANES
    return pl.pallas_call(
        functools.partial(_fwd_kernel, factor),
        out_shape=jax.ShapeDtypeStruct((tokens, width), projected.dtype),
        grid=(images, pairs),
        in_specs=[part(0), part(pairs), part(2 * pairs)],
        out_specs=pl.BlockSpec((rows, LANES), lambda b, j: (b, j)),
        compiler_params=pltpu.CompilerParams(dimension_semantics=("parallel", "parallel")),
        cost_estimate=pl.CostEstimate(
            flops=flops, transcendentals=images * (width // HEAD_DIM) * rows * rows,
            bytes_accessed=2 * tokens * (three + width),
        ),
    )(projected, projected, projected)


def attention_backward(projected, grad_attended, images):
    tokens, three = projected.shape
    rows, width = tokens // images, three // 3
    pairs = width // LANES
    factor = HEAD_DIM ** (-0.5)

    def part(offset):
        return pl.BlockSpec((rows, LANES), lambda b, j: (b, offset + j))

    out = jax.ShapeDtypeStruct((tokens, width), projected.dtype)
    flops = 5 * 2 * 2 * images * (width // HEAD_DIM) * rows * rows * LANES
    dq, dk, dv = pl.pallas_call(
        functools.partial(_bwd_kernel, factor),
        out_shape=(out, out, out),
        grid=(images, pairs),
        in_specs=[part(0), part(pairs), part(2 * pairs), part(0)],
        out_specs=[part(0)] * 3,
        compiler_params=pltpu.CompilerParams(dimension_semantics=("parallel", "parallel")),
        cost_estimate=pl.CostEstimate(
            flops=flops, transcendentals=images * (width // HEAD_DIM) * rows * rows,
            bytes_accessed=2 * tokens * (three + 4 * width),
        ),
    )(projected, projected, projected, grad_attended)
    return jnp.concatenate([dq, dk, dv], axis=1)


EPS = 1e-06
GELU_C = 0.7978845608028654

AXES = ("y", "zh", "x", "c", "zl")
DP = ("y", "zh", "x", "c")
STAGES = ("c", "x", "y", "zh", "zl")
STAGES_B = ("c", "y", "x", "zh", "zl")


def matmul(left, right):
    return jnp.dot(left, right, preferred_element_type=jnp.float32)


def left_trans(left, right):
    return lax.dot_general(
        left, right, (((0,), (0,)), ((), ())), preferred_element_type=jnp.float32
    )


def right_trans(left, right):
    return lax.dot_general(
        left, right, (((1,), (1,)), ((), ())), preferred_element_type=jnp.float32
    )


def normalize(values):
    centre = values - jnp.mean(values, axis=-1, keepdims=True)
    inverse = lax.rsqrt(jnp.mean(centre * centre, axis=-1, keepdims=True) + EPS)
    return (centre * inverse, inverse)


def norm_back(grad, normed, inverse):
    return inverse * (
        grad
        - jnp.mean(grad, axis=-1, keepdims=True)
        - normed * jnp.mean(grad * normed, axis=-1, keepdims=True)
    )


def stage_order(values, sizes, inner, stages=STAGES):
    lead = values.shape[:-1]
    shape = [sizes[a] for a in AXES]
    values = values.reshape(*lead, *shape, inner)
    n = len(lead)
    order = list(range(n)) + [n + AXES.index(a) for a in stages] + [n + len(AXES)]
    return jnp.transpose(values, order).reshape(*lead, -1)


def reduce_stages(packed, stages):
    for a in stages:
        packed = lax.psum_scatter(packed, a, scatter_dimension=0, tiled=True)
    return packed


def reduce_rest(packed, axes):
    count = 1
    for a in axes:
        count *= lax.axis_size(a)
    chunks = packed.reshape(count, packed.shape[0] // count, packed.shape[1])
    chunks = lax.all_to_all(chunks, axes, 0, 0, tiled=False)
    return jnp.sum(chunks.astype(jnp.float32), axis=0)


def bias_columns(columns, rows):
    block = jnp.stack(columns, axis=1)
    return jnp.pad(block, ((0, 0), (0, 128 - block.shape[1]))).astype(jnp.bfloat16)


def gather_dp(values):
    count = 1
    for a in DP:
        count *= lax.axis_size(a)
    copies = jnp.broadcast_to(values[None], (count,) + values.shape)
    return lax.all_to_all(copies, DP, 0, 0, tiled=False).reshape(-1, values.shape[1])


def per_device(
    sizes,
    tokens,
    condition,
    occupied,
    modulation_weight,
    modulation_bias,
    input_weight,
    query_bias,
    value_bias,
    output_weight,
    output_bias,
    expand_weight,
    expand_bias,
    contract_weight,
    contract_bias,
    cotangent,
):
    images, rows, width = tokens.shape
    heads = width // HEAD_DIM
    flat = images * rows
    factor = HEAD_DIM ** (-0.5)
    cond_full = condition.astype(jnp.float32)
    sigmoid = jax.nn.sigmoid(cond_full)
    silu_b = (cond_full * sigmoid).astype(jnp.bfloat16)
    silu_pair = lax.all_gather(silu_b, "zl", axis=0, tiled=True)
    silu_all = gather_dp(silu_pair)
    mod_cols = matmul(silu_pair, modulation_weight) + modulation_bias.reshape(1, -1)
    modulation = lax.all_to_all(mod_cols, "zl", split_axis=0, concat_axis=1, tiled=True).reshape(
        images, 6, 1, width
    )
    shift_a = modulation[:, 0]
    scale_a = modulation[:, 1]
    gate_a = modulation[:, 2]
    shift_b = modulation[:, 3]
    scale_b = modulation[:, 4]
    gate_b = modulation[:, 5]
    inputs = tokens.astype(jnp.float32)
    normed_a, inverse_a = normalize(inputs)
    mod_a = (normed_a * (1.0 + scale_a) + shift_a).astype(jnp.bfloat16).reshape(flat, width)
    qkv_bias = jnp.concatenate([query_bias, jnp.zeros_like(query_bias), value_bias])
    projected = (matmul(mod_a, input_weight) + qkv_bias).astype(jnp.bfloat16)
    attended_b = attention_forward(projected, images)
    branch_a = (matmul(attended_b, output_weight) + output_bias).reshape(images, rows, width)
    middle = inputs + gate_a * branch_a
    normed_b, inverse_b = normalize(middle)
    mod_b = (normed_b * (1.0 + scale_b) + shift_b).astype(jnp.bfloat16).reshape(flat, width)
    expanded = matmul(mod_b, expand_weight) + expand_bias
    tanh_part = jnp.tanh(GELU_C * (expanded + 0.044715 * expanded * expanded * expanded))
    activated_b = (0.5 * expanded * (1.0 + tanh_part)).astype(jnp.bfloat16)
    branch_b = (matmul(activated_b, contract_weight) + contract_bias).reshape(images, rows, width)
    alive = occupied.astype(jnp.float32)[:, None, None]
    layer_out = (middle + gate_b * branch_b) * alive
    grad_out = cotangent.astype(jnp.float32) * alive
    grad_gate_b = jnp.sum(grad_out * branch_b, axis=1)
    grad_branch_b = (grad_out * gate_b).astype(jnp.bfloat16).reshape(flat, width)
    blocks = 1
    for a in AXES:
        blocks *= sizes[a]
    ff = activated_b.shape[1]
    split = ff // width
    act_perm = stage_order(
        activated_b.reshape(flat, blocks, split, width // blocks)
        .transpose(0, 2, 1, 3)
        .reshape(flat, split, width),
        sizes,
        width // blocks,
    )
    contract_parts = [
        left_trans(act_perm[:, q], grad_branch_b).astype(jnp.bfloat16) for q in range(split)
    ]
    contract_bias_grad = stage_order(
        jnp.sum(grad_branch_b.astype(jnp.float32), axis=0), sizes, width // blocks
    )
    grad_act = right_trans(grad_branch_b, contract_weight)
    slope = 0.5 * (1.0 + tanh_part) + 0.5 * expanded * (1.0 - tanh_part * tanh_part) * GELU_C * (
        1.0 + 3.0 * 0.044715 * expanded * expanded
    )
    grad_exp_b = (grad_act * slope).astype(jnp.bfloat16)
    expand_grad = left_trans(stage_order(mod_b, sizes, width // blocks), grad_exp_b).astype(jnp.bfloat16)
    expand_bias_grad = stage_order(
        jnp.sum(grad_exp_b.astype(jnp.float32), axis=0)
        .reshape(blocks, split, width // blocks)
        .transpose(1, 0, 2)
        .reshape(split, width),
        sizes,
        width // blocks,
    )
    packed_a = jnp.concatenate(
        [expand_grad]
        + contract_parts
        + [bias_columns([contract_bias_grad] + [expand_bias_grad[q] for q in range(split)], width)],
        axis=1,
    )
    packed_a, grad_exp_b = lax.optimization_barrier((packed_a, grad_exp_b))
    chain_a = reduce_stages(packed_a, STAGES[:1])
    grad_mod_b = right_trans(grad_exp_b, expand_weight).reshape(images, rows, width)
    grad_shift_b = jnp.sum(grad_mod_b, axis=1)
    grad_scale_b = jnp.sum(grad_mod_b * normed_b, axis=1)
    grad_middle = grad_out + norm_back(grad_mod_b * (1.0 + scale_b), normed_b, inverse_b)
    grad_gate_a = jnp.sum(grad_middle * branch_a, axis=1)
    grad_branch_a = (grad_middle * gate_a).astype(jnp.bfloat16).reshape(flat, width)
    output_grad = left_trans(stage_order(attended_b, sizes, width // blocks, STAGES_B), grad_branch_a).astype(
        jnp.bfloat16
    )
    output_bias_grad = stage_order(
        jnp.sum(grad_branch_a.astype(jnp.float32), axis=0), sizes, width // blocks, STAGES_B
    )
    grad_att_b = right_trans(grad_branch_a, output_weight).astype(jnp.bfloat16)
    chain_a, grad_att_b = lax.optimization_barrier((chain_a, grad_att_b))
    chain_a = reduce_stages(chain_a, STAGES[1:2])
    grad_proj_b = attention_backward(projected, grad_att_b, images)
    input_grad = left_trans(stage_order(mod_a, sizes, width // blocks, STAGES_B), grad_proj_b).astype(
        jnp.bfloat16
    )
    bias_sums = jnp.sum(grad_proj_b.astype(jnp.float32), axis=0)
    query_bias_grad = stage_order(bias_sums[:width], sizes, width // blocks, STAGES_B)
    value_bias_grad = stage_order(bias_sums[2 * width :], sizes, width // blocks, STAGES_B)
    packed_b = jnp.concatenate(
        [
            input_grad,
            output_grad,
            bias_columns([query_bias_grad, value_bias_grad, output_bias_grad], width),
        ],
        axis=1,
    )
    chain_a, packed_b = lax.optimization_barrier((chain_a, packed_b))
    chain_b = reduce_stages(packed_b, STAGES_B[:2])
    grad_mod_a = right_trans(grad_proj_b, input_weight).reshape(images, rows, width)
    grad_shift_a = jnp.sum(grad_mod_a, axis=1)
    grad_scale_a = jnp.sum(grad_mod_a * normed_a, axis=1)
    tokens_grad = grad_middle + norm_back(grad_mod_a * (1.0 + scale_a), normed_a, inverse_a)
    modulation_terms = jnp.stack(
        [grad_shift_a, grad_scale_a, grad_gate_a, grad_shift_b, grad_scale_b, grad_gate_b], axis=1
    ).reshape(images, 6 * width)
    modulation_own = modulation_terms.astype(jnp.bfloat16)
    modulation_cols = lax.all_to_all(modulation_own, "zl", split_axis=1, concat_axis=0, tiled=True)
    silu_terms = right_trans(modulation_cols, modulation_weight)
    pair_index = lax.axis_index("zl")
    own_rows = lax.dynamic_slice_in_dim(silu_terms, pair_index * images, images, axis=0)
    other_rows = lax.dynamic_slice_in_dim(silu_terms, (1 - pair_index) * images, images, axis=0)
    silu_sums = own_rows + lax.ppermute(other_rows, "zl", [(0, 1), (1, 0)])
    condition_grad = silu_sums * sigmoid * (1.0 + cond_full * (1.0 - sigmoid))
    mod_all = gather_dp(modulation_cols)
    dp_index = lax.axis_index(DP)
    dp_count = silu_all.shape[0] // silu_pair.shape[0]
    row_block = width // dp_count
    silu_rows = lax.dynamic_slice_in_dim(silu_all, dp_index * row_block, row_block, axis=1)
    modulation_weight_grad = left_trans(silu_rows, mod_all)
    bias_all = jnp.sum(mod_all.astype(jnp.float32), axis=0).reshape(-1, width)
    modulation_bias_grad = lax.dynamic_slice_in_dim(bias_all, dp_index * row_block, row_block, axis=1)
    chain_a = reduce_rest(chain_a, STAGES[2:])
    chain_b = reduce_rest(chain_b, STAGES_B[2:])
    three = input_weight.shape[1]
    fw = expand_weight.shape[1]
    input_weight_grad = chain_b[:, :three]
    output_weight_grad = chain_b[:, three : three + width]
    qb_grad = chain_b[:, three + width]
    vb_grad = chain_b[:, three + width + 1]
    ob_grad = chain_b[:, three + width + 2]
    expand_weight_grad = chain_a[:, :fw]
    contract_weight_grad = chain_a[:, fw : fw + split * width].reshape(-1, split, width)
    contract_weight_grad = contract_weight_grad.transpose(1, 0, 2).reshape(-1, width)
    cb_grad = chain_a[:, fw + split * width]
    eb_grad = chain_a[:, fw + split * width + 1 : fw + split * width + 1 + split].T.reshape(-1)
    summed = (
        input_weight_grad,
        qb_grad,
        vb_grad,
        output_weight_grad,
        ob_grad,
        expand_weight_grad,
        eb_grad,
        contract_weight_grad,
        cb_grad,
    )
    return (
        layer_out,
        tokens_grad,
        condition_grad,
        modulation_weight_grad,
        modulation_bias_grad,
        *summed,
    )


def solution(mesh):
    dp_size, mod_size = mesh.devices.shape
    rest = dp_size // 4
    side = int(round(rest ** 0.5))
    shape = (side, 2, rest // side, 2, mod_size)
    sizes = dict(zip(AXES, shape))
    physical = Mesh(np.asarray(mesh.devices).reshape(shape), AXES)
    ALL = AXES
    placed = (
        P(ALL, None, None),
        P(ALL, None),
        P(ALL),
        P(None, "zl"),
        P("zl", None),
        P(),
        P(),
        P(),
        P(),
        P(),
        P(),
        P(),
        P(),
        P(),
        P(ALL, None, None),
    )
    return jax.shard_map(
        functools.partial(per_device, sizes),
        mesh=physical,
        in_specs=placed,
        out_specs=(
            P(ALL, None, None),
            P(ALL, None, None),
            P(ALL, None),
            P(DP, "zl"),
            P("zl", DP),
            P(ALL, None),
            P(ALL),
            P(ALL),
            P(ALL, None),
            P(ALL),
            P(ALL, None),
            P(ALL),
            P(ALL, None),
            P(ALL),
        ),
        check_vma=False,
    )
```

```python
import functools

import jax
import jax.numpy as jnp
import numpy as np
from jax import lax
from jax.experimental import pallas as pl
from jax.experimental.pallas import tpu as pltpu
from jax.sharding import Mesh
from jax.sharding import PartitionSpec as P

HEAD_DIM = 64
LANES = 128


def _nt(a, b):
    return lax.dot_general(a, b, (((1,), (1,)), ((), ())), preferred_element_type=jnp.float32)


def _tn(a, b):
    return lax.dot_general(a, b, (((0,), (0,)), ((), ())), preferred_element_type=jnp.float32)


def _probs(q, k, head, factor):
    lane = lax.broadcasted_iota(jnp.int32, (1, LANES), 1)
    mine = (lane // HEAD_DIM) == head
    qh = jnp.where(mine, q, jnp.zeros_like(q))
    scores = _nt(qh, k) * factor
    weights = jnp.exp(scores - jnp.max(scores, axis=-1, keepdims=True))
    return mine, qh, weights / jnp.sum(weights, axis=-1, keepdims=True)


def _fwd_kernel(factor, q_ref, k_ref, v_ref, o_ref):
    q = q_ref[...]
    k = k_ref[...]
    v = v_ref[...]
    out = jnp.zeros(o_ref.shape, jnp.float32)
    for head in range(LANES // HEAD_DIM):
        mine, _, probs = _probs(q, k, head, factor)
        vh = jnp.where(mine, v, jnp.zeros_like(v))
        out = out + jnp.dot(probs.astype(v.dtype), vh, preferred_element_type=jnp.float32)
    o_ref[...] = out.astype(o_ref.dtype)


def _bwd_kernel(factor, q_ref, k_ref, v_ref, d_ref, dq_ref, dk_ref, dv_ref):
    q = q_ref[...]
    k = k_ref[...]
    v = v_ref[...]
    d = d_ref[...]
    dq = jnp.zeros(dq_ref.shape, jnp.float32)
    dk = jnp.zeros(dk_ref.shape, jnp.float32)
    dv = jnp.zeros(dv_ref.shape, jnp.float32)
    for head in range(LANES // HEAD_DIM):
        mine, qh, probs = _probs(q, k, head, factor)
        dh = jnp.where(mine, d, jnp.zeros_like(d))
        kh = jnp.where(mine, k, jnp.zeros_like(k))
        dprobs = _nt(dh, v)
        dv = dv + _tn(probs.astype(d.dtype), dh)
        inner = jnp.sum(dprobs * probs, axis=-1, keepdims=True)
        dscores = (probs * (dprobs - inner)).astype(q.dtype)
        dq = dq + jnp.dot(dscores, kh, preferred_element_type=jnp.float32)
        dk = dk + _tn(dscores, qh)
    dq_ref[...] = (dq * factor).astype(dq_ref.dtype)
    dk_ref[...] = (dk * factor).astype(dk_ref.dtype)
    dv_ref[...] = dv.astype(dv_ref.dtype)


def attention_forward(projected, images):
    tokens, three = projected.shape
    rows, width = tokens // images, three // 3
    pairs = width // LANES
    factor = HEAD_DIM ** (-0.5)

    def part(offset):
        return pl.BlockSpec((rows, LANES), lambda b, j: (b, offset + j))

    flops = 2 * 2 * images * (width // HEAD_DIM) * rows * rows * LANES
    return pl.pallas_call(
        functools.partial(_fwd_kernel, factor),
        out_shape=jax.ShapeDtypeStruct((tokens, width), projected.dtype),
        grid=(images, pairs),
        in_specs=[part(0), part(pairs), part(2 * pairs)],
        out_specs=pl.BlockSpec((rows, LANES), lambda b, j: (b, j)),
        compiler_params=pltpu.CompilerParams(dimension_semantics=("parallel", "parallel")),
        cost_estimate=pl.CostEstimate(
            flops=flops, transcendentals=images * (width // HEAD_DIM) * rows * rows,
            bytes_accessed=2 * tokens * (three + width),
        ),
    )(projected, projected, projected)


def attention_backward(projected, grad_attended, images):
    tokens, three = projected.shape
    rows, width = tokens // images, three // 3
    pairs = width // LANES
    factor = HEAD_DIM ** (-0.5)

    def part(offset):
        return pl.BlockSpec((rows, LANES), lambda b, j: (b, offset + j))

    out = jax.ShapeDtypeStruct((tokens, width), projected.dtype)
    flops = 5 * 2 * 2 * images * (width // HEAD_DIM) * rows * rows * LANES
    dq, dk, dv = pl.pallas_call(
        functools.partial(_bwd_kernel, factor),
        out_shape=(out, out, out),
        grid=(images, pairs),
        in_specs=[part(0), part(pairs), part(2 * pairs), part(0)],
        out_specs=[part(0)] * 3,
        compiler_params=pltpu.CompilerParams(dimension_semantics=("parallel", "parallel")),
        cost_estimate=pl.CostEstimate(
            flops=flops, transcendentals=images * (width // HEAD_DIM) * rows * rows,
            bytes_accessed=2 * tokens * (three + 4 * width),
        ),
    )(projected, projected, projected, grad_attended)
    return jnp.concatenate([dq, dk, dv], axis=1)


EPS = 1e-06
GELU_C = 0.7978845608028654

AXES = ("y", "zh", "x", "c", "zl")
DP = ("y", "zh", "x", "c")
STAGES = ("c", "x", "y", "zh", "zl")
STAGES_B = STAGES


def matmul(left, right):
    return jnp.dot(left, right, preferred_element_type=jnp.float32)


def left_trans(left, right):
    return lax.dot_general(
        left, right, (((0,), (0,)), ((), ())), preferred_element_type=jnp.float32
    )


def right_trans(left, right):
    return lax.dot_general(
        left, right, (((1,), (1,)), ((), ())), preferred_element_type=jnp.float32
    )


def normalize(values):
    centre = values - jnp.mean(values, axis=-1, keepdims=True)
    inverse = lax.rsqrt(jnp.mean(centre * centre, axis=-1, keepdims=True) + EPS)
    return (centre * inverse, inverse)


def norm_back(grad, normed, inverse):
    return inverse * (
        grad
        - jnp.mean(grad, axis=-1, keepdims=True)
        - normed * jnp.mean(grad * normed, axis=-1, keepdims=True)
    )


def stage_order(values, sizes, inner, stages=STAGES):
    lead = values.shape[:-1]
    shape = [sizes[a] for a in AXES]
    values = values.reshape(*lead, *shape, inner)
    n = len(lead)
    order = list(range(n)) + [n + AXES.index(a) for a in stages] + [n + len(AXES)]
    return jnp.transpose(values, order).reshape(*lead, -1)


def reduce_stages(packed, stages):
    for a in stages:
        packed = lax.psum_scatter(packed, a, scatter_dimension=0, tiled=True)
    return packed


def reduce_rest(packed, axes):
    count = 1
    for a in axes:
        count *= lax.axis_size(a)
    chunks = packed.reshape(count, packed.shape[0] // count, packed.shape[1])
    chunks = lax.all_to_all(chunks, axes, 0, 0, tiled=False)
    return jnp.sum(chunks.astype(jnp.float32), axis=0)


def bias_columns(columns, rows):
    block = jnp.stack(columns, axis=1)
    return jnp.pad(block, ((0, 0), (0, 128 - block.shape[1]))).astype(jnp.bfloat16)


def gather_dp(values):
    count = 1
    for a in DP:
        count *= lax.axis_size(a)
    copies = jnp.broadcast_to(values[None], (count,) + values.shape)
    return lax.all_to_all(copies, DP, 0, 0, tiled=False).reshape(-1, values.shape[1])


def per_device(
    sizes,
    tokens,
    condition,
    occupied,
    modulation_weight,
    modulation_bias,
    input_weight,
    query_bias,
    value_bias,
    output_weight,
    output_bias,
    expand_weight,
    expand_bias,
    contract_weight,
    contract_bias,
    cotangent,
):
    images, rows, width = tokens.shape
    heads = width // HEAD_DIM
    flat = images * rows
    factor = HEAD_DIM ** (-0.5)
    cond_full = condition.astype(jnp.float32)
    sigmoid = jax.nn.sigmoid(cond_full)
    silu_b = (cond_full * sigmoid).astype(jnp.bfloat16)
    silu_pair = lax.all_gather(silu_b, "zl", axis=0, tiled=True)
    silu_all = gather_dp(silu_pair)
    mod_cols = matmul(silu_pair, modulation_weight) + modulation_bias.reshape(1, -1)
    modulation = lax.all_to_all(mod_cols, "zl", split_axis=0, concat_axis=1, tiled=True).reshape(
        images, 6, 1, width
    )
    shift_a = modulation[:, 0]
    scale_a = modulation[:, 1]
    gate_a = modulation[:, 2]
    shift_b = modulation[:, 3]
    scale_b = modulation[:, 4]
    gate_b = modulation[:, 5]
    inputs = tokens.astype(jnp.float32)
    normed_a, inverse_a = normalize(inputs)
    mod_a = (normed_a * (1.0 + scale_a) + shift_a).astype(jnp.bfloat16).reshape(flat, width)
    qkv_bias = jnp.concatenate([query_bias, jnp.zeros_like(query_bias), value_bias])
    projected = (matmul(mod_a, input_weight) + qkv_bias).astype(jnp.bfloat16)
    attended_b = attention_forward(projected, images)
    branch_a = (matmul(attended_b, output_weight) + output_bias).reshape(images, rows, width)
    middle = inputs + gate_a * branch_a
    normed_b, inverse_b = normalize(middle)
    mod_b = (normed_b * (1.0 + scale_b) + shift_b).astype(jnp.bfloat16).reshape(flat, width)
    expanded = matmul(mod_b, expand_weight) + expand_bias
    tanh_part = jnp.tanh(GELU_C * (expanded + 0.044715 * expanded * expanded * expanded))
    activated_b = (0.5 * expanded * (1.0 + tanh_part)).astype(jnp.bfloat16)
    branch_b = (matmul(activated_b, contract_weight) + contract_bias).reshape(images, rows, width)
    alive = occupied.astype(jnp.float32)[:, None, None]
    layer_out = (middle + gate_b * branch_b) * alive
    grad_out = cotangent.astype(jnp.float32) * alive
    grad_gate_b = jnp.sum(grad_out * branch_b, axis=1)
    grad_branch_b = (grad_out * gate_b).astype(jnp.bfloat16).reshape(flat, width)
    blocks = 1
    for a in AXES:
        blocks *= sizes[a]
    ff = activated_b.shape[1]
    split = ff // width
    act_perm = stage_order(
        activated_b.reshape(flat, blocks, split, width // blocks)
        .transpose(0, 2, 1, 3)
        .reshape(flat, split, width),
        sizes,
        width // blocks,
    )
    contract_parts = [
        left_trans(act_perm[:, q], grad_branch_b).astype(jnp.bfloat16) for q in range(split)
    ]
    contract_bias_grad = stage_order(
        jnp.sum(grad_branch_b.astype(jnp.float32), axis=0), sizes, width // blocks
    )
    grad_act = right_trans(grad_branch_b, contract_weight)
    slope = 0.5 * (1.0 + tanh_part) + 0.5 * expanded * (1.0 - tanh_part * tanh_part) * GELU_C * (
        1.0 + 3.0 * 0.044715 * expanded * expanded
    )
    grad_exp_b = (grad_act * slope).astype(jnp.bfloat16)
    expand_grad = left_trans(stage_order(mod_b, sizes, width // blocks), grad_exp_b).astype(jnp.bfloat16)
    expand_bias_grad = stage_order(
        jnp.sum(grad_exp_b.astype(jnp.float32), axis=0)
        .reshape(blocks, split, width // blocks)
        .transpose(1, 0, 2)
        .reshape(split, width),
        sizes,
        width // blocks,
    )
    packed_a = jnp.concatenate(
        [expand_grad]
        + contract_parts
        + [bias_columns([contract_bias_grad] + [expand_bias_grad[q] for q in range(split)], width)],
        axis=1,
    )
    packed_a, grad_exp_b = lax.optimization_barrier((packed_a, grad_exp_b))
    chain_a = reduce_stages(packed_a, STAGES[:1])
    grad_mod_b = right_trans(grad_exp_b, expand_weight).reshape(images, rows, width)
    grad_shift_b = jnp.sum(grad_mod_b, axis=1)
    grad_scale_b = jnp.sum(grad_mod_b * normed_b, axis=1)
    grad_middle = grad_out + norm_back(grad_mod_b * (1.0 + scale_b), normed_b, inverse_b)
    grad_gate_a = jnp.sum(grad_middle * branch_a, axis=1)
    grad_branch_a = (grad_middle * gate_a).astype(jnp.bfloat16).reshape(flat, width)
    output_grad = left_trans(stage_order(attended_b, sizes, width // blocks, STAGES_B), grad_branch_a).astype(
        jnp.bfloat16
    )
    output_bias_grad = stage_order(
        jnp.sum(grad_branch_a.astype(jnp.float32), axis=0), sizes, width // blocks, STAGES_B
    )
    grad_att_b = right_trans(grad_branch_a, output_weight).astype(jnp.bfloat16)
    chain_a, grad_att_b = lax.optimization_barrier((chain_a, grad_att_b))
    chain_a = reduce_stages(chain_a, STAGES[1:2])
    grad_proj_b = attention_backward(projected, grad_att_b, images)
    input_grad = left_trans(stage_order(mod_a, sizes, width // blocks, STAGES_B), grad_proj_b).astype(
        jnp.bfloat16
    )
    bias_sums = jnp.sum(grad_proj_b.astype(jnp.float32), axis=0)
    query_bias_grad = stage_order(bias_sums[:width], sizes, width // blocks, STAGES_B)
    value_bias_grad = stage_order(bias_sums[2 * width :], sizes, width // blocks, STAGES_B)
    packed_b = jnp.concatenate(
        [
            input_grad,
            output_grad,
            bias_columns([query_bias_grad, value_bias_grad, output_bias_grad], width),
        ],
        axis=1,
    )
    chain_b = reduce_stages(packed_b, STAGES_B[:2])
    grad_mod_a = right_trans(grad_proj_b, input_weight).reshape(images, rows, width)
    grad_shift_a = jnp.sum(grad_mod_a, axis=1)
    grad_scale_a = jnp.sum(grad_mod_a * normed_a, axis=1)
    tokens_grad = grad_middle + norm_back(grad_mod_a * (1.0 + scale_a), normed_a, inverse_a)
    modulation_terms = jnp.stack(
        [grad_shift_a, grad_scale_a, grad_gate_a, grad_shift_b, grad_scale_b, grad_gate_b], axis=1
    ).reshape(images, 6 * width)
    modulation_own = modulation_terms.astype(jnp.bfloat16)
    chain_a, modulation_own = lax.optimization_barrier((chain_a, modulation_own))
    modulation_cols = lax.all_to_all(modulation_own, "zl", split_axis=1, concat_axis=0, tiled=True)
    silu_terms = right_trans(modulation_cols, modulation_weight)
    pair_index = lax.axis_index("zl")
    own_rows = lax.dynamic_slice_in_dim(silu_terms, pair_index * images, images, axis=0)
    other_rows = lax.dynamic_slice_in_dim(silu_terms, (1 - pair_index) * images, images, axis=0)
    silu_sums = own_rows + lax.ppermute(other_rows, "zl", [(0, 1), (1, 0)])
    condition_grad = silu_sums * sigmoid * (1.0 + cond_full * (1.0 - sigmoid))
    mod_all = gather_dp(modulation_cols)
    dp_index = lax.axis_index(DP)
    dp_count = silu_all.shape[0] // silu_pair.shape[0]
    row_block = width // dp_count
    silu_rows = lax.dynamic_slice_in_dim(silu_all, dp_index * row_block, row_block, axis=1)
    modulation_weight_grad = left_trans(silu_rows, mod_all)
    bias_all = jnp.sum(mod_all.astype(jnp.float32), axis=0).reshape(-1, width)
    modulation_bias_grad = lax.dynamic_slice_in_dim(bias_all, dp_index * row_block, row_block, axis=1)
    rest = reduce_rest(jnp.concatenate([chain_a, chain_b], axis=1), STAGES[2:])
    chain_a = rest[:, : chain_a.shape[1]]
    chain_b = rest[:, chain_a.shape[1] :]
    three = input_weight.shape[1]
    fw = expand_weight.shape[1]
    input_weight_grad = chain_b[:, :three]
    output_weight_grad = chain_b[:, three : three + width]
    qb_grad = chain_b[:, three + width]
    vb_grad = chain_b[:, three + width + 1]
    ob_grad = chain_b[:, three + width + 2]
    expand_weight_grad = chain_a[:, :fw]
    contract_weight_grad = chain_a[:, fw : fw + split * width].reshape(-1, split, width)
    contract_weight_grad = contract_weight_grad.transpose(1, 0, 2).reshape(-1, width)
    cb_grad = chain_a[:, fw + split * width]
    eb_grad = chain_a[:, fw + split * width + 1 : fw + split * width + 1 + split].T.reshape(-1)
    summed = (
        input_weight_grad,
        qb_grad,
        vb_grad,
        output_weight_grad,
        ob_grad,
        expand_weight_grad,
        eb_grad,
        contract_weight_grad,
        cb_grad,
    )
    return (
        layer_out,
        tokens_grad,
        condition_grad,
        modulation_weight_grad,
        modulation_bias_grad,
        *summed,
    )


def solution(mesh):
    dp_size, mod_size = mesh.devices.shape
    rest = dp_size // 4
    side = int(round(rest ** 0.5))
    shape = (side, 2, rest // side, 2, mod_size)
    sizes = dict(zip(AXES, shape))
    physical = Mesh(np.asarray(mesh.devices).reshape(shape), AXES)
    ALL = AXES
    placed = (
        P(ALL, None, None),
        P(ALL, None),
        P(ALL),
        P(None, "zl"),
        P("zl", None),
        P(),
        P(),
        P(),
        P(),
        P(),
        P(),
        P(),
        P(),
        P(),
        P(ALL, None, None),
    )
    return jax.shard_map(
        functools.partial(per_device, sizes),
        mesh=physical,
        in_specs=placed,
        out_specs=(
            P(ALL, None, None),
            P(ALL, None, None),
            P(ALL, None),
            P(DP, "zl"),
            P("zl", DP),
            P(ALL, None),
            P(ALL),
            P(ALL),
            P(ALL, None),
            P(ALL),
            P(ALL, None),
            P(ALL),
            P(ALL, None),
            P(ALL),
        ),
        check_vma=False,
    )
```

```python
import functools

import jax
import jax.numpy as jnp
import numpy as np
from jax import lax
from jax.experimental import pallas as pl
from jax.experimental.pallas import tpu as pltpu
from jax.sharding import Mesh
from jax.sharding import PartitionSpec as P

HEAD_DIM = 64
LANES = 128


def _nt(a, b):
    return lax.dot_general(a, b, (((1,), (1,)), ((), ())), preferred_element_type=jnp.float32)


def _tn(a, b):
    return lax.dot_general(a, b, (((0,), (0,)), ((), ())), preferred_element_type=jnp.float32)


def _probs(q, k, head, factor):
    lane = lax.broadcasted_iota(jnp.int32, (1, LANES), 1)
    mine = (lane // HEAD_DIM) == head
    qh = jnp.where(mine, q, jnp.zeros_like(q))
    scores = _nt(qh, k) * factor
    weights = jnp.exp(scores - jnp.max(scores, axis=-1, keepdims=True))
    return mine, qh, weights / jnp.sum(weights, axis=-1, keepdims=True)


def _fwd_kernel(factor, q_ref, k_ref, v_ref, o_ref):
    q = q_ref[...]
    k = k_ref[...]
    v = v_ref[...]
    out = jnp.zeros(o_ref.shape, jnp.float32)
    for head in range(LANES // HEAD_DIM):
        mine, _, probs = _probs(q, k, head, factor)
        vh = jnp.where(mine, v, jnp.zeros_like(v))
        out = out + jnp.dot(probs.astype(v.dtype), vh, preferred_element_type=jnp.float32)
    o_ref[...] = out.astype(o_ref.dtype)


def _bwd_kernel(factor, q_ref, k_ref, v_ref, d_ref, dq_ref, dk_ref, dv_ref):
    q = q_ref[...]
    k = k_ref[...]
    v = v_ref[...]
    d = d_ref[...]
    dq = jnp.zeros(dq_ref.shape, jnp.float32)
    dk = jnp.zeros(dk_ref.shape, jnp.float32)
    dv = jnp.zeros(dv_ref.shape, jnp.float32)
    for head in range(LANES // HEAD_DIM):
        mine, qh, probs = _probs(q, k, head, factor)
        dh = jnp.where(mine, d, jnp.zeros_like(d))
        kh = jnp.where(mine, k, jnp.zeros_like(k))
        dprobs = _nt(dh, v)
        dv = dv + _tn(probs.astype(d.dtype), dh)
        inner = jnp.sum(dprobs * probs, axis=-1, keepdims=True)
        dscores = (probs * (dprobs - inner)).astype(q.dtype)
        dq = dq + jnp.dot(dscores, kh, preferred_element_type=jnp.float32)
        dk = dk + _tn(dscores, qh)
    dq_ref[...] = (dq * factor).astype(dq_ref.dtype)
    dk_ref[...] = (dk * factor).astype(dk_ref.dtype)
    dv_ref[...] = dv.astype(dv_ref.dtype)


def attention_forward(projected, images):
    tokens, three = projected.shape
    rows, width = tokens // images, three // 3
    pairs = width // LANES
    factor = HEAD_DIM ** (-0.5)

    def part(offset):
        return pl.BlockSpec((rows, LANES), lambda b, j: (b, offset + j))

    flops = 2 * 2 * images * (width // HEAD_DIM) * rows * rows * LANES
    return pl.pallas_call(
        functools.partial(_fwd_kernel, factor),
        out_shape=jax.ShapeDtypeStruct((tokens, width), projected.dtype),
        grid=(images, pairs),
        in_specs=[part(0), part(pairs), part(2 * pairs)],
        out_specs=pl.BlockSpec((rows, LANES), lambda b, j: (b, j)),
        compiler_params=pltpu.CompilerParams(dimension_semantics=("parallel", "parallel")),
        cost_estimate=pl.CostEstimate(
            flops=flops, transcendentals=images * (width // HEAD_DIM) * rows * rows,
            bytes_accessed=2 * tokens * (three + width),
        ),
    )(projected, projected, projected)


def attention_backward(projected, grad_attended, images):
    tokens, three = projected.shape
    rows, width = tokens // images, three // 3
    pairs = width // LANES
    factor = HEAD_DIM ** (-0.5)

    def part(offset):
        return pl.BlockSpec((rows, LANES), lambda b, j: (b, offset + j))

    out = jax.ShapeDtypeStruct((tokens, width), projected.dtype)
    flops = 5 * 2 * 2 * images * (width // HEAD_DIM) * rows * rows * LANES
    dq, dk, dv = pl.pallas_call(
        functools.partial(_bwd_kernel, factor),
        out_shape=(out, out, out),
        grid=(images, pairs),
        in_specs=[part(0), part(pairs), part(2 * pairs), part(0)],
        out_specs=[part(0)] * 3,
        compiler_params=pltpu.CompilerParams(dimension_semantics=("parallel", "parallel")),
        cost_estimate=pl.CostEstimate(
            flops=flops, transcendentals=images * (width // HEAD_DIM) * rows * rows,
            bytes_accessed=2 * tokens * (three + 4 * width),
        ),
    )(projected, projected, projected, grad_attended)
    return jnp.concatenate([dq, dk, dv], axis=1)


EPS = 1e-06
GELU_C = 0.7978845608028654

AXES = ("y", "zh", "x", "c", "zl")
DP = ("y", "zh", "x", "c")
STAGES = ("c", "x", "y", "zh", "zl")
STAGES_B = ("c", "y", "x", "zh", "zl")


def matmul(left, right):
    return jnp.dot(left, right, preferred_element_type=jnp.float32)


def left_trans(left, right):
    return lax.dot_general(
        left, right, (((0,), (0,)), ((), ())), preferred_element_type=jnp.float32
    )


def right_trans(left, right):
    return lax.dot_general(
        left, right, (((1,), (1,)), ((), ())), preferred_element_type=jnp.float32
    )


def normalize(values):
    centre = values - jnp.mean(values, axis=-1, keepdims=True)
    inverse = lax.rsqrt(jnp.mean(centre * centre, axis=-1, keepdims=True) + EPS)
    return (centre * inverse, inverse)


def norm_back(grad, normed, inverse):
    return inverse * (
        grad
        - jnp.mean(grad, axis=-1, keepdims=True)
        - normed * jnp.mean(grad * normed, axis=-1, keepdims=True)
    )


def stage_order(values, sizes, inner, stages=STAGES):
    lead = values.shape[:-1]
    shape = [sizes[a] for a in AXES]
    values = values.reshape(*lead, *shape, inner)
    n = len(lead)
    order = list(range(n)) + [n + AXES.index(a) for a in stages] + [n + len(AXES)]
    return jnp.transpose(values, order).reshape(*lead, -1)


def reduce_stages(packed, stages):
    for a in stages:
        packed = lax.psum_scatter(packed, a, scatter_dimension=0, tiled=True)
    return packed


def reduce_pair(packed, axis):
    half = packed.shape[0] // 2
    index = lax.axis_index(axis)
    keep = lax.dynamic_slice_in_dim(packed, index * half, half, axis=0)
    send = lax.dynamic_slice_in_dim(packed, (1 - index) * half, half, axis=0)
    got = lax.ppermute(send, axis, [(0, 1), (1, 0)])
    return (keep.astype(jnp.float32) + got.astype(jnp.float32)).astype(packed.dtype)


def reduce_rest(packed, axes):
    count = 1
    for a in axes:
        count *= lax.axis_size(a)
    chunks = packed.reshape(count, packed.shape[0] // count, packed.shape[1])
    chunks = lax.all_to_all(chunks, axes, 0, 0, tiled=False)
    return jnp.sum(chunks.astype(jnp.float32), axis=0)


def bias_columns(columns, rows):
    block = jnp.stack(columns, axis=1)
    return jnp.pad(block, ((0, 0), (0, 128 - block.shape[1]))).astype(jnp.bfloat16)


def gather_dp(values):
    count = 1
    for a in DP:
        count *= lax.axis_size(a)
    copies = jnp.broadcast_to(values[None], (count,) + values.shape)
    return lax.all_to_all(copies, DP, 0, 0, tiled=False).reshape(-1, values.shape[1])


def per_device(
    sizes,
    tokens,
    condition,
    occupied,
    modulation_weight,
    modulation_bias,
    input_weight,
    query_bias,
    value_bias,
    output_weight,
    output_bias,
    expand_weight,
    expand_bias,
    contract_weight,
    contract_bias,
    cotangent,
):
    images, rows, width = tokens.shape
    heads = width // HEAD_DIM
    flat = images * rows
    factor = HEAD_DIM ** (-0.5)
    cond_full = condition.astype(jnp.float32)
    sigmoid = jax.nn.sigmoid(cond_full)
    silu_b = (cond_full * sigmoid).astype(jnp.bfloat16)
    silu_pair = lax.all_gather(silu_b, "zl", axis=0, tiled=True)
    mod_cols = matmul(silu_pair, modulation_weight) + modulation_bias.reshape(1, -1)
    modulation = lax.all_to_all(mod_cols, "zl", split_axis=0, concat_axis=1, tiled=True).reshape(
        images, 6, 1, width
    )
    shift_a = modulation[:, 0]
    scale_a = modulation[:, 1]
    gate_a = modulation[:, 2]
    shift_b = modulation[:, 3]
    scale_b = modulation[:, 4]
    gate_b = modulation[:, 5]
    inputs = tokens.astype(jnp.float32)
    normed_a, inverse_a = normalize(inputs)
    mod_a = (normed_a * (1.0 + scale_a) + shift_a).astype(jnp.bfloat16).reshape(flat, width)
    qkv_bias = jnp.concatenate([query_bias, jnp.zeros_like(query_bias), value_bias])
    projected = (matmul(mod_a, input_weight) + qkv_bias).astype(jnp.bfloat16)
    attended_b = attention_forward(projected, images)
    branch_a = (matmul(attended_b, output_weight) + output_bias).reshape(images, rows, width)
    middle = inputs + gate_a * branch_a
    normed_b, inverse_b = normalize(middle)
    mod_b = (normed_b * (1.0 + scale_b) + shift_b).astype(jnp.bfloat16).reshape(flat, width)
    expanded = matmul(mod_b, expand_weight) + expand_bias
    tanh_part = jnp.tanh(GELU_C * (expanded + 0.044715 * expanded * expanded * expanded))
    activated_b = (0.5 * expanded * (1.0 + tanh_part)).astype(jnp.bfloat16)
    branch_b = (matmul(activated_b, contract_weight) + contract_bias).reshape(images, rows, width)
    alive = occupied.astype(jnp.float32)[:, None, None]
    layer_out = (middle + gate_b * branch_b) * alive
    grad_out = cotangent.astype(jnp.float32) * alive
    grad_gate_b = jnp.sum(grad_out * branch_b, axis=1)
    grad_branch_b = (grad_out * gate_b).astype(jnp.bfloat16).reshape(flat, width)
    blocks = 1
    for a in AXES:
        blocks *= sizes[a]
    ff = activated_b.shape[1]
    split = ff // width
    act_perm = stage_order(
        activated_b.reshape(flat, blocks, split, width // blocks)
        .transpose(0, 2, 1, 3)
        .reshape(flat, split, width),
        sizes,
        width // blocks,
    )
    contract_parts = [
        left_trans(act_perm[:, q], grad_branch_b).astype(jnp.bfloat16) for q in range(split)
    ]
    contract_bias_grad = stage_order(
        jnp.sum(grad_branch_b.astype(jnp.float32), axis=0), sizes, width // blocks
    )
    grad_act = right_trans(grad_branch_b, contract_weight)
    slope = 0.5 * (1.0 + tanh_part) + 0.5 * expanded * (1.0 - tanh_part * tanh_part) * GELU_C * (
        1.0 + 3.0 * 0.044715 * expanded * expanded
    )
    grad_exp_b = (grad_act * slope).astype(jnp.bfloat16)
    expand_grad = left_trans(stage_order(mod_b, sizes, width // blocks), grad_exp_b).astype(jnp.bfloat16)
    expand_bias_grad = stage_order(
        jnp.sum(grad_exp_b.astype(jnp.float32), axis=0)
        .reshape(blocks, split, width // blocks)
        .transpose(1, 0, 2)
        .reshape(split, width),
        sizes,
        width // blocks,
    )
    packed_a = jnp.concatenate(
        [expand_grad]
        + contract_parts
        + [bias_columns([contract_bias_grad] + [expand_bias_grad[q] for q in range(split)], width)],
        axis=1,
    )
    packed_a, grad_exp_b = lax.optimization_barrier((packed_a, grad_exp_b))
    chain_a = reduce_stages(packed_a, STAGES[:1])
    grad_mod_b = right_trans(grad_exp_b, expand_weight).reshape(images, rows, width)
    grad_shift_b = jnp.sum(grad_mod_b, axis=1)
    grad_scale_b = jnp.sum(grad_mod_b * normed_b, axis=1)
    grad_middle = grad_out + norm_back(grad_mod_b * (1.0 + scale_b), normed_b, inverse_b)
    grad_gate_a = jnp.sum(grad_middle * branch_a, axis=1)
    grad_branch_a = (grad_middle * gate_a).astype(jnp.bfloat16).reshape(flat, width)
    output_grad = left_trans(stage_order(attended_b, sizes, width // blocks, STAGES_B), grad_branch_a).astype(
        jnp.bfloat16
    )
    output_bias_grad = stage_order(
        jnp.sum(grad_branch_a.astype(jnp.float32), axis=0), sizes, width // blocks, STAGES_B
    )
    grad_att_b = right_trans(grad_branch_a, output_weight).astype(jnp.bfloat16)
    chain_a, grad_att_b = lax.optimization_barrier((chain_a, grad_att_b))
    chain_a = reduce_stages(chain_a, STAGES[1:2])
    grad_proj_b = attention_backward(projected, grad_att_b, images)
    input_grad = left_trans(stage_order(mod_a, sizes, width // blocks, STAGES_B), grad_proj_b).astype(
        jnp.bfloat16
    )
    bias_sums = jnp.sum(grad_proj_b.astype(jnp.float32), axis=0)
    query_bias_grad = stage_order(bias_sums[:width], sizes, width // blocks, STAGES_B)
    value_bias_grad = stage_order(bias_sums[2 * width :], sizes, width // blocks, STAGES_B)
    chain_b = reduce_pair(
        jnp.concatenate(
            [
                input_grad,
                output_grad,
                bias_columns([query_bias_grad, value_bias_grad, output_bias_grad], width),
            ],
            axis=1,
        ),
        STAGES_B[0],
    )
    chain_b = reduce_rest(chain_b, STAGES_B[1:2]).astype(jnp.bfloat16)
    grad_mod_a = right_trans(grad_proj_b, input_weight).reshape(images, rows, width)
    grad_shift_a = jnp.sum(grad_mod_a, axis=1)
    grad_scale_a = jnp.sum(grad_mod_a * normed_a, axis=1)
    tokens_grad = grad_middle + norm_back(grad_mod_a * (1.0 + scale_a), normed_a, inverse_a)
    modulation_terms = jnp.stack(
        [grad_shift_a, grad_scale_a, grad_gate_a, grad_shift_b, grad_scale_b, grad_gate_b], axis=1
    ).reshape(images, 6 * width)
    modulation_own = modulation_terms.astype(jnp.bfloat16)
    chain_a, modulation_own = lax.optimization_barrier((chain_a, modulation_own))
    modulation_cols = lax.all_to_all(modulation_own, "zl", split_axis=1, concat_axis=0, tiled=True)
    silu_terms = right_trans(modulation_cols, modulation_weight)
    silu_sums = lax.psum_scatter(silu_terms, "zl", scatter_dimension=0, tiled=True)
    condition_grad = silu_sums * sigmoid * (1.0 + cond_full * (1.0 - sigmoid))
    factors = gather_dp(jnp.concatenate([silu_pair, modulation_cols], axis=1))
    silu_all = factors[:, :width]
    mod_all = factors[:, width:]
    dp_index = lax.axis_index(DP)
    dp_count = factors.shape[0] // silu_pair.shape[0]
    row_block = width // dp_count
    silu_rows = lax.dynamic_slice_in_dim(silu_all, dp_index * row_block, row_block, axis=1)
    modulation_weight_grad = left_trans(silu_rows, mod_all)
    bias_all = jnp.sum(mod_all.astype(jnp.float32), axis=0).reshape(-1, width)
    modulation_bias_grad = lax.dynamic_slice_in_dim(bias_all, dp_index * row_block, row_block, axis=1)
    chain_a = reduce_rest(chain_a, STAGES[2:])
    chain_b = reduce_rest(chain_b, STAGES_B[2:])
    three = input_weight.shape[1]
    fw = expand_weight.shape[1]
    input_weight_grad = chain_b[:, :three]
    output_weight_grad = chain_b[:, three : three + width]
    qb_grad = chain_b[:, three + width]
    vb_grad = chain_b[:, three + width + 1]
    ob_grad = chain_b[:, three + width + 2]
    expand_weight_grad = chain_a[:, :fw]
    contract_weight_grad = chain_a[:, fw : fw + split * width].reshape(-1, split, width)
    contract_weight_grad = contract_weight_grad.transpose(1, 0, 2).reshape(-1, width)
    cb_grad = chain_a[:, fw + split * width]
    eb_grad = chain_a[:, fw + split * width + 1 : fw + split * width + 1 + split].T.reshape(-1)
    summed = (
        input_weight_grad,
        qb_grad,
        vb_grad,
        output_weight_grad,
        ob_grad,
        expand_weight_grad,
        eb_grad,
        contract_weight_grad,
        cb_grad,
    )
    return (
        layer_out,
        tokens_grad,
        condition_grad,
        modulation_weight_grad,
        modulation_bias_grad,
        *summed,
    )


def solution(mesh):
    dp_size, mod_size = mesh.devices.shape
    rest = dp_size // 4
    side = int(round(rest ** 0.5))
    shape = (side, 2, rest // side, 2, mod_size)
    sizes = dict(zip(AXES, shape))
    physical = Mesh(np.asarray(mesh.devices).reshape(shape), AXES)
    ALL = AXES
    placed = (
        P(ALL, None, None),
        P(ALL, None),
        P(ALL),
        P(None, "zl"),
        P("zl", None),
        P(),
        P(),
        P(),
        P(),
        P(),
        P(),
        P(),
        P(),
        P(),
        P(ALL, None, None),
    )
    return jax.shard_map(
        functools.partial(per_device, sizes),
        mesh=physical,
        in_specs=placed,
        out_specs=(
            P(ALL, None, None),
            P(ALL, None, None),
            P(ALL, None),
            P(DP, "zl"),
            P("zl", DP),
            P(ALL, None),
            P(ALL),
            P(ALL),
            P(ALL, None),
            P(ALL),
            P(ALL, None),
            P(ALL),
            P(ALL, None),
            P(ALL),
        ),
        check_vma=False,
    )
```

```python
import functools

import jax
import jax.numpy as jnp
import numpy as np
from jax import lax
from jax.experimental import pallas as pl
from jax.experimental.pallas import tpu as pltpu
from jax.sharding import Mesh
from jax.sharding import PartitionSpec as P

HEAD_DIM = 64
LANES = 128


def _nt(a, b):
    return lax.dot_general(a, b, (((1,), (1,)), ((), ())), preferred_element_type=jnp.float32)


def _tn(a, b):
    return lax.dot_general(a, b, (((0,), (0,)), ((), ())), preferred_element_type=jnp.float32)


def _probs(q, k, head, factor):
    lane = lax.broadcasted_iota(jnp.int32, (1, LANES), 1)
    mine = (lane // HEAD_DIM) == head
    qh = jnp.where(mine, q, jnp.zeros_like(q))
    scores = _nt(qh, k) * factor
    weights = jnp.exp(scores - jnp.max(scores, axis=-1, keepdims=True))
    return mine, qh, weights / jnp.sum(weights, axis=-1, keepdims=True)


def _fwd_kernel(factor, q_ref, k_ref, v_ref, o_ref):
    q = q_ref[...]
    k = k_ref[...]
    v = v_ref[...]
    out = jnp.zeros(o_ref.shape, jnp.float32)
    for head in range(LANES // HEAD_DIM):
        mine, _, probs = _probs(q, k, head, factor)
        vh = jnp.where(mine, v, jnp.zeros_like(v))
        out = out + jnp.dot(probs.astype(v.dtype), vh, preferred_element_type=jnp.float32)
    o_ref[...] = out.astype(o_ref.dtype)


def _bwd_kernel(factor, q_ref, k_ref, v_ref, d_ref, dq_ref, dk_ref, dv_ref):
    q = q_ref[...]
    k = k_ref[...]
    v = v_ref[...]
    d = d_ref[...]
    dq = jnp.zeros(dq_ref.shape, jnp.float32)
    dk = jnp.zeros(dk_ref.shape, jnp.float32)
    dv = jnp.zeros(dv_ref.shape, jnp.float32)
    for head in range(LANES // HEAD_DIM):
        mine, qh, probs = _probs(q, k, head, factor)
        dh = jnp.where(mine, d, jnp.zeros_like(d))
        kh = jnp.where(mine, k, jnp.zeros_like(k))
        dprobs = _nt(dh, v)
        dv = dv + _tn(probs.astype(d.dtype), dh)
        inner = jnp.sum(dprobs * probs, axis=-1, keepdims=True)
        dscores = (probs * (dprobs - inner)).astype(q.dtype)
        dq = dq + jnp.dot(dscores, kh, preferred_element_type=jnp.float32)
        dk = dk + _tn(dscores, qh)
    dq_ref[...] = (dq * factor).astype(dq_ref.dtype)
    dk_ref[...] = (dk * factor).astype(dk_ref.dtype)
    dv_ref[...] = dv.astype(dv_ref.dtype)


def attention_forward(projected, images):
    tokens, three = projected.shape
    rows, width = tokens // images, three // 3
    pairs = width // LANES
    factor = HEAD_DIM ** (-0.5)

    def part(offset):
        return pl.BlockSpec((rows, LANES), lambda b, j: (b, offset + j))

    flops = 2 * 2 * images * (width // HEAD_DIM) * rows * rows * LANES
    return pl.pallas_call(
        functools.partial(_fwd_kernel, factor),
        out_shape=jax.ShapeDtypeStruct((tokens, width), projected.dtype),
        grid=(images, pairs),
        in_specs=[part(0), part(pairs), part(2 * pairs)],
        out_specs=pl.BlockSpec((rows, LANES), lambda b, j: (b, j)),
        compiler_params=pltpu.CompilerParams(dimension_semantics=("parallel", "parallel")),
        cost_estimate=pl.CostEstimate(
            flops=flops, transcendentals=images * (width // HEAD_DIM) * rows * rows,
            bytes_accessed=2 * tokens * (three + width),
        ),
    )(projected, projected, projected)


def attention_backward(projected, grad_attended, images):
    tokens, three = projected.shape
    rows, width = tokens // images, three // 3
    pairs = width // LANES
    factor = HEAD_DIM ** (-0.5)

    def part(offset):
        return pl.BlockSpec((rows, LANES), lambda b, j: (b, offset + j))

    out = jax.ShapeDtypeStruct((tokens, width), projected.dtype)
    flops = 5 * 2 * 2 * images * (width // HEAD_DIM) * rows * rows * LANES
    dq, dk, dv = pl.pallas_call(
        functools.partial(_bwd_kernel, factor),
        out_shape=(out, out, out),
        grid=(images, pairs),
        in_specs=[part(0), part(pairs), part(2 * pairs), part(0)],
        out_specs=[part(0)] * 3,
        compiler_params=pltpu.CompilerParams(dimension_semantics=("parallel", "parallel")),
        cost_estimate=pl.CostEstimate(
            flops=flops, transcendentals=images * (width // HEAD_DIM) * rows * rows,
            bytes_accessed=2 * tokens * (three + 4 * width),
        ),
    )(projected, projected, projected, grad_attended)
    return jnp.concatenate([dq, dk, dv], axis=1)


EPS = 1e-06
GELU_C = 0.7978845608028654

AXES = ("y", "zh", "x", "c", "zl")
DP = ("y", "zh", "x", "c")
STAGES = ("c", "x", "y", "zh", "zl")
STAGES_B = ("c", "y", "x", "zh", "zl")


def matmul(left, right):
    return jnp.dot(left, right, preferred_element_type=jnp.float32)


def left_trans(left, right):
    return lax.dot_general(
        left, right, (((0,), (0,)), ((), ())), preferred_element_type=jnp.float32
    )


def right_trans(left, right):
    return lax.dot_general(
        left, right, (((1,), (1,)), ((), ())), preferred_element_type=jnp.float32
    )


def normalize(values):
    centre = values - jnp.mean(values, axis=-1, keepdims=True)
    inverse = lax.rsqrt(jnp.mean(centre * centre, axis=-1, keepdims=True) + EPS)
    return (centre * inverse, inverse)


def norm_back(grad, normed, inverse):
    return inverse * (
        grad
        - jnp.mean(grad, axis=-1, keepdims=True)
        - normed * jnp.mean(grad * normed, axis=-1, keepdims=True)
    )


def stage_order(values, sizes, inner, stages=STAGES):
    lead = values.shape[:-1]
    shape = [sizes[a] for a in AXES]
    values = values.reshape(*lead, *shape, inner)
    n = len(lead)
    order = list(range(n)) + [n + AXES.index(a) for a in stages] + [n + len(AXES)]
    return jnp.transpose(values, order).reshape(*lead, -1)


def reduce_stages(packed, stages):
    for a in stages:
        packed = lax.psum_scatter(packed, a, scatter_dimension=0, tiled=True)
    return packed


def reduce_pair(packed, axis):
    half = packed.shape[0] // 2
    index = lax.axis_index(axis)
    keep = lax.dynamic_slice_in_dim(packed, index * half, half, axis=0)
    send = lax.dynamic_slice_in_dim(packed, (1 - index) * half, half, axis=0)
    got = lax.ppermute(send, axis, [(0, 1), (1, 0)])
    return (keep.astype(jnp.float32) + got.astype(jnp.float32)).astype(packed.dtype)


def reduce_rest(packed, axes):
    count = 1
    for a in axes:
        count *= lax.axis_size(a)
    chunks = packed.reshape(count, packed.shape[0] // count, packed.shape[1])
    chunks = lax.all_to_all(chunks, axes, 0, 0, tiled=False)
    return jnp.sum(chunks.astype(jnp.float32), axis=0)


def bias_columns(columns, rows):
    block = jnp.stack(columns, axis=1)
    return jnp.pad(block, ((0, 0), (0, 128 - block.shape[1]))).astype(jnp.bfloat16)


def gather_dp(values):
    count = 1
    for a in DP:
        count *= lax.axis_size(a)
    copies = jnp.broadcast_to(values[None], (count,) + values.shape)
    return lax.all_to_all(copies, DP, 0, 0, tiled=False).reshape(-1, values.shape[1])


def per_device(
    sizes,
    tokens,
    condition,
    occupied,
    modulation_weight,
    modulation_bias,
    input_weight,
    query_bias,
    value_bias,
    output_weight,
    output_bias,
    expand_weight,
    expand_bias,
    contract_weight,
    contract_bias,
    cotangent,
):
    images, rows, width = tokens.shape
    heads = width // HEAD_DIM
    flat = images * rows
    factor = HEAD_DIM ** (-0.5)
    cond_full = condition.astype(jnp.float32)
    sigmoid = jax.nn.sigmoid(cond_full)
    silu_b = (cond_full * sigmoid).astype(jnp.bfloat16)
    silu_pair = lax.all_gather(silu_b, "zl", axis=0, tiled=True)
    silu_all = gather_dp(silu_pair)
    mod_cols = matmul(silu_pair, modulation_weight) + modulation_bias.reshape(1, -1)
    modulation = lax.all_to_all(mod_cols, "zl", split_axis=0, concat_axis=1, tiled=True).reshape(
        images, 6, 1, width
    )
    shift_a = modulation[:, 0]
    scale_a = modulation[:, 1]
    gate_a = modulation[:, 2]
    shift_b = modulation[:, 3]
    scale_b = modulation[:, 4]
    gate_b = modulation[:, 5]
    inputs = tokens.astype(jnp.float32)
    normed_a, inverse_a = normalize(inputs)
    mod_a = (normed_a * (1.0 + scale_a) + shift_a).astype(jnp.bfloat16).reshape(flat, width)
    qkv_bias = jnp.concatenate([query_bias, jnp.zeros_like(query_bias), value_bias])
    projected = (matmul(mod_a, input_weight) + qkv_bias).astype(jnp.bfloat16)
    attended_b = attention_forward(projected, images)
    branch_a = (matmul(attended_b, output_weight) + output_bias).reshape(images, rows, width)
    middle = inputs + gate_a * branch_a
    normed_b, inverse_b = normalize(middle)
    mod_b = (normed_b * (1.0 + scale_b) + shift_b).astype(jnp.bfloat16).reshape(flat, width)
    expanded = matmul(mod_b, expand_weight) + expand_bias
    tanh_part = jnp.tanh(GELU_C * (expanded + 0.044715 * expanded * expanded * expanded))
    activated_b = (0.5 * expanded * (1.0 + tanh_part)).astype(jnp.bfloat16)
    branch_b = (matmul(activated_b, contract_weight) + contract_bias).reshape(images, rows, width)
    alive = occupied.astype(jnp.float32)[:, None, None]
    layer_out = (middle + gate_b * branch_b) * alive
    grad_out = cotangent.astype(jnp.float32) * alive
    grad_gate_b = jnp.sum(grad_out * branch_b, axis=1)
    grad_branch_b = (grad_out * gate_b).astype(jnp.bfloat16).reshape(flat, width)
    blocks = 1
    for a in AXES:
        blocks *= sizes[a]
    ff = activated_b.shape[1]
    split = ff // width
    act_perm = stage_order(
        activated_b.reshape(flat, blocks, split, width // blocks)
        .transpose(0, 2, 1, 3)
        .reshape(flat, split, width),
        sizes,
        width // blocks,
    )
    contract_parts = [
        left_trans(act_perm[:, q], grad_branch_b).astype(jnp.bfloat16) for q in range(split)
    ]
    contract_bias_grad = stage_order(
        jnp.sum(grad_branch_b.astype(jnp.float32), axis=0), sizes, width // blocks
    )
    grad_act = right_trans(grad_branch_b, contract_weight)
    slope = 0.5 * (1.0 + tanh_part) + 0.5 * expanded * (1.0 - tanh_part * tanh_part) * GELU_C * (
        1.0 + 3.0 * 0.044715 * expanded * expanded
    )
    grad_exp_b = (grad_act * slope).astype(jnp.bfloat16)
    expand_grad = left_trans(stage_order(mod_b, sizes, width // blocks), grad_exp_b).astype(jnp.bfloat16)
    expand_bias_grad = stage_order(
        jnp.sum(grad_exp_b.astype(jnp.float32), axis=0)
        .reshape(blocks, split, width // blocks)
        .transpose(1, 0, 2)
        .reshape(split, width),
        sizes,
        width // blocks,
    )
    packed_a = jnp.concatenate(
        [expand_grad]
        + contract_parts
        + [bias_columns([contract_bias_grad] + [expand_bias_grad[q] for q in range(split)], width)],
        axis=1,
    )
    packed_a, grad_exp_b = lax.optimization_barrier((packed_a, grad_exp_b))
    chain_a = reduce_stages(packed_a, STAGES[:1])
    grad_mod_b = right_trans(grad_exp_b, expand_weight).reshape(images, rows, width)
    grad_shift_b = jnp.sum(grad_mod_b, axis=1)
    grad_scale_b = jnp.sum(grad_mod_b * normed_b, axis=1)
    grad_middle = grad_out + norm_back(grad_mod_b * (1.0 + scale_b), normed_b, inverse_b)
    grad_gate_a = jnp.sum(grad_middle * branch_a, axis=1)
    grad_branch_a = (grad_middle * gate_a).astype(jnp.bfloat16).reshape(flat, width)
    output_grad = left_trans(stage_order(attended_b, sizes, width // blocks, STAGES_B), grad_branch_a).astype(
        jnp.bfloat16
    )
    output_bias_grad = stage_order(
        jnp.sum(grad_branch_a.astype(jnp.float32), axis=0), sizes, width // blocks, STAGES_B
    )
    grad_att_b = right_trans(grad_branch_a, output_weight).astype(jnp.bfloat16)
    chain_a, grad_att_b = lax.optimization_barrier((chain_a, grad_att_b))
    chain_a = reduce_stages(chain_a, STAGES[1:2])
    grad_proj_b = attention_backward(projected, grad_att_b, images)
    input_grad = left_trans(stage_order(mod_a, sizes, width // blocks, STAGES_B), grad_proj_b).astype(
        jnp.bfloat16
    )
    bias_sums = jnp.sum(grad_proj_b.astype(jnp.float32), axis=0)
    query_bias_grad = stage_order(bias_sums[:width], sizes, width // blocks, STAGES_B)
    value_bias_grad = stage_order(bias_sums[2 * width :], sizes, width // blocks, STAGES_B)
    chain_b = reduce_pair(
        jnp.concatenate(
            [
                input_grad,
                output_grad,
                bias_columns([query_bias_grad, value_bias_grad, output_bias_grad], width),
            ],
            axis=1,
        ),
        STAGES_B[0],
    )
    chain_b = reduce_stages(chain_b, STAGES_B[1:2])
    grad_mod_a = right_trans(grad_proj_b, input_weight).reshape(images, rows, width)
    grad_shift_a = jnp.sum(grad_mod_a, axis=1)
    grad_scale_a = jnp.sum(grad_mod_a * normed_a, axis=1)
    tokens_grad = grad_middle + norm_back(grad_mod_a * (1.0 + scale_a), normed_a, inverse_a)
    modulation_terms = jnp.stack(
        [grad_shift_a, grad_scale_a, grad_gate_a, grad_shift_b, grad_scale_b, grad_gate_b], axis=1
    ).reshape(images, 6 * width)
    modulation_own = modulation_terms.astype(jnp.bfloat16)
    chain_a, modulation_own = lax.optimization_barrier((chain_a, modulation_own))
    modulation_cols = lax.all_to_all(modulation_own, "zl", split_axis=1, concat_axis=0, tiled=True)
    silu_terms = right_trans(modulation_cols, modulation_weight)
    pair_index = lax.axis_index("zl")
    own_rows = lax.dynamic_slice_in_dim(silu_terms, pair_index * images, images, axis=0)
    other_rows = lax.dynamic_slice_in_dim(silu_terms, (1 - pair_index) * images, images, axis=0)
    silu_sums = own_rows + lax.ppermute(other_rows, "zl", [(0, 1), (1, 0)])
    condition_grad = silu_sums * sigmoid * (1.0 + cond_full * (1.0 - sigmoid))
    mod_all = gather_dp(modulation_cols)
    dp_index = lax.axis_index(DP)
    dp_count = silu_all.shape[0] // silu_pair.shape[0]
    row_block = width // dp_count
    silu_rows = lax.dynamic_slice_in_dim(silu_all, dp_index * row_block, row_block, axis=1)
    modulation_weight_grad = left_trans(silu_rows, mod_all)
    bias_all = jnp.sum(mod_all.astype(jnp.float32), axis=0).reshape(-1, width)
    modulation_bias_grad = lax.dynamic_slice_in_dim(bias_all, dp_index * row_block, row_block, axis=1)
    chain_a = reduce_rest(chain_a, STAGES[2:])
    chain_b = reduce_rest(chain_b, STAGES_B[2:])
    three = input_weight.shape[1]
    fw = expand_weight.shape[1]
    input_weight_grad = chain_b[:, :three]
    output_weight_grad = chain_b[:, three : three + width]
    qb_grad = chain_b[:, three + width]
    vb_grad = chain_b[:, three + width + 1]
    ob_grad = chain_b[:, three + width + 2]
    expand_weight_grad = chain_a[:, :fw]
    contract_weight_grad = chain_a[:, fw : fw + split * width].reshape(-1, split, width)
    contract_weight_grad = contract_weight_grad.transpose(1, 0, 2).reshape(-1, width)
    cb_grad = chain_a[:, fw + split * width]
    eb_grad = chain_a[:, fw + split * width + 1 : fw + split * width + 1 + split].T.reshape(-1)
    summed = (
        input_weight_grad,
        qb_grad,
        vb_grad,
        output_weight_grad,
        ob_grad,
        expand_weight_grad,
        eb_grad,
        contract_weight_grad,
        cb_grad,
    )
    return (
        layer_out,
        tokens_grad,
        condition_grad,
        modulation_weight_grad,
        modulation_bias_grad,
        *summed,
    )


def solution(mesh):
    dp_size, mod_size = mesh.devices.shape
    rest = dp_size // 4
    side = int(round(rest ** 0.5))
    shape = (side, 2, rest // side, 2, mod_size)
    sizes = dict(zip(AXES, shape))
    physical = Mesh(np.asarray(mesh.devices).reshape(shape), AXES)
    ALL = AXES
    placed = (
        P(ALL, None, None),
        P(ALL, None),
        P(ALL),
        P(None, "zl"),
        P("zl", None),
        P(),
        P(),
        P(),
        P(),
        P(),
        P(),
        P(),
        P(),
        P(),
        P(ALL, None, None),
    )
    return jax.shard_map(
        functools.partial(per_device, sizes),
        mesh=physical,
        in_specs=placed,
        out_specs=(
            P(ALL, None, None),
            P(ALL, None, None),
            P(ALL, None),
            P(DP, "zl"),
            P("zl", DP),
            P(ALL, None),
            P(ALL),
            P(ALL),
            P(ALL, None),
            P(ALL),
            P(ALL, None),
            P(ALL),
            P(ALL, None),
            P(ALL),
        ),
        check_vma=False,
    )
```

```python
import functools

import jax
import jax.numpy as jnp
import numpy as np
from jax import lax
from jax.experimental import pallas as pl
from jax.experimental.pallas import tpu as pltpu
from jax.sharding import Mesh
from jax.sharding import PartitionSpec as P

HEAD_DIM = 64
LANES = 128


def _nt(a, b):
    return lax.dot_general(a, b, (((1,), (1,)), ((), ())), preferred_element_type=jnp.float32)


def _tn(a, b):
    return lax.dot_general(a, b, (((0,), (0,)), ((), ())), preferred_element_type=jnp.float32)


def _probs(q, k, head, factor):
    lane = lax.broadcasted_iota(jnp.int32, (1, LANES), 1)
    mine = (lane // HEAD_DIM) == head
    qh = jnp.where(mine, q, jnp.zeros_like(q))
    scores = _nt(qh, k) * factor
    weights = jnp.exp(scores - jnp.max(scores, axis=-1, keepdims=True))
    return mine, qh, weights / jnp.sum(weights, axis=-1, keepdims=True)


def _fwd_kernel(factor, q_ref, k_ref, v_ref, o_ref):
    q = q_ref[...]
    k = k_ref[...]
    v = v_ref[...]
    out = jnp.zeros(o_ref.shape, jnp.float32)
    for head in range(LANES // HEAD_DIM):
        mine, _, probs = _probs(q, k, head, factor)
        vh = jnp.where(mine, v, jnp.zeros_like(v))
        out = out + jnp.dot(probs.astype(v.dtype), vh, preferred_element_type=jnp.float32)
    o_ref[...] = out.astype(o_ref.dtype)


def _bwd_kernel(factor, q_ref, k_ref, v_ref, d_ref, dq_ref, dk_ref, dv_ref):
    q = q_ref[...]
    k = k_ref[...]
    v = v_ref[...]
    d = d_ref[...]
    dq = jnp.zeros(dq_ref.shape, jnp.float32)
    dk = jnp.zeros(dk_ref.shape, jnp.float32)
    dv = jnp.zeros(dv_ref.shape, jnp.float32)
    for head in range(LANES // HEAD_DIM):
        mine, qh, probs = _probs(q, k, head, factor)
        dh = jnp.where(mine, d, jnp.zeros_like(d))
        kh = jnp.where(mine, k, jnp.zeros_like(k))
        dprobs = _nt(dh, v)
        dv = dv + _tn(probs.astype(d.dtype), dh)
        inner = jnp.sum(dprobs * probs, axis=-1, keepdims=True)
        dscores = (probs * (dprobs - inner)).astype(q.dtype)
        dq = dq + jnp.dot(dscores, kh, preferred_element_type=jnp.float32)
        dk = dk + _tn(dscores, qh)
    dq_ref[...] = (dq * factor).astype(dq_ref.dtype)
    dk_ref[...] = (dk * factor).astype(dk_ref.dtype)
    dv_ref[...] = dv.astype(dv_ref.dtype)


def attention_forward(projected, images):
    tokens, three = projected.shape
    rows, width = tokens // images, three // 3
    pairs = width // LANES
    factor = HEAD_DIM ** (-0.5)

    def part(offset):
        return pl.BlockSpec((rows, LANES), lambda b, j: (b, offset + j))

    flops = 2 * 2 * images * (width // HEAD_DIM) * rows * rows * LANES
    return pl.pallas_call(
        functools.partial(_fwd_kernel, factor),
        out_shape=jax.ShapeDtypeStruct((tokens, width), projected.dtype),
        grid=(images, pairs),
        in_specs=[part(0), part(pairs), part(2 * pairs)],
        out_specs=pl.BlockSpec((rows, LANES), lambda b, j: (b, j)),
        compiler_params=pltpu.CompilerParams(dimension_semantics=("parallel", "parallel")),
        cost_estimate=pl.CostEstimate(
            flops=flops, transcendentals=images * (width // HEAD_DIM) * rows * rows,
            bytes_accessed=2 * tokens * (three + width),
        ),
    )(projected, projected, projected)


def attention_backward(projected, grad_attended, images):
    tokens, three = projected.shape
    rows, width = tokens // images, three // 3
    pairs = width // LANES
    factor = HEAD_DIM ** (-0.5)

    def part(offset):
        return pl.BlockSpec((rows, LANES), lambda b, j: (b, offset + j))

    out = jax.ShapeDtypeStruct((tokens, width), projected.dtype)
    flops = 5 * 2 * 2 * images * (width // HEAD_DIM) * rows * rows * LANES
    dq, dk, dv = pl.pallas_call(
        functools.partial(_bwd_kernel, factor),
        out_shape=(out, out, out),
        grid=(images, pairs),
        in_specs=[part(0), part(pairs), part(2 * pairs), part(0)],
        out_specs=[part(0)] * 3,
        compiler_params=pltpu.CompilerParams(dimension_semantics=("parallel", "parallel")),
        cost_estimate=pl.CostEstimate(
            flops=flops, transcendentals=images * (width // HEAD_DIM) * rows * rows,
            bytes_accessed=2 * tokens * (three + 4 * width),
        ),
    )(projected, projected, projected, grad_attended)
    return jnp.concatenate([dq, dk, dv], axis=1)


EPS = 1e-06
GELU_C = 0.7978845608028654

AXES = ("y", "zh", "x", "c", "zl")
DP = ("y", "zh", "x", "c")
STAGES = ("c", "x", "y", "zh", "zl")
STAGES_B = ("c", "y", "x", "zh", "zl")


def matmul(left, right):
    return jnp.dot(left, right, preferred_element_type=jnp.float32)


def left_trans(left, right):
    return lax.dot_general(
        left, right, (((0,), (0,)), ((), ())), preferred_element_type=jnp.float32
    )


def right_trans(left, right):
    return lax.dot_general(
        left, right, (((1,), (1,)), ((), ())), preferred_element_type=jnp.float32
    )


def normalize(values):
    centre = values - jnp.mean(values, axis=-1, keepdims=True)
    inverse = lax.rsqrt(jnp.mean(centre * centre, axis=-1, keepdims=True) + EPS)
    return (centre * inverse, inverse)


def norm_back(grad, normed, inverse):
    return inverse * (
        grad
        - jnp.mean(grad, axis=-1, keepdims=True)
        - normed * jnp.mean(grad * normed, axis=-1, keepdims=True)
    )


def stage_order(values, sizes, inner, stages=STAGES):
    lead = values.shape[:-1]
    shape = [sizes[a] for a in AXES]
    values = values.reshape(*lead, *shape, inner)
    n = len(lead)
    order = list(range(n)) + [n + AXES.index(a) for a in stages] + [n + len(AXES)]
    return jnp.transpose(values, order).reshape(*lead, -1)


def reduce_stages(packed, stages):
    for a in stages:
        packed = lax.psum_scatter(packed, a, scatter_dimension=0, tiled=True)
    return packed


def reduce_pair(packed, axis):
    half = packed.shape[0] // 2
    index = lax.axis_index(axis)
    keep = lax.dynamic_slice_in_dim(packed, index * half, half, axis=0)
    send = lax.dynamic_slice_in_dim(packed, (1 - index) * half, half, axis=0)
    got = lax.ppermute(send, axis, [(0, 1), (1, 0)])
    return (keep.astype(jnp.float32) + got.astype(jnp.float32)).astype(packed.dtype)


def reduce_rest(packed, axes):
    count = 1
    for a in axes:
        count *= lax.axis_size(a)
    chunks = packed.reshape(count, packed.shape[0] // count, packed.shape[1])
    chunks = lax.all_to_all(chunks, axes, 0, 0, tiled=False)
    return jnp.sum(chunks.astype(jnp.float32), axis=0)


def bias_columns(columns, rows):
    block = jnp.stack(columns, axis=1)
    return jnp.pad(block, ((0, 0), (0, 128 - block.shape[1]))).astype(jnp.bfloat16)


def gather_dp(values):
    count = 1
    for a in DP:
        count *= lax.axis_size(a)
    copies = jnp.broadcast_to(values[None], (count,) + values.shape)
    return lax.all_to_all(copies, DP, 0, 0, tiled=False).reshape(-1, values.shape[1])


def per_device(
    sizes,
    tokens,
    condition,
    occupied,
    modulation_weight,
    modulation_bias,
    input_weight,
    query_bias,
    value_bias,
    output_weight,
    output_bias,
    expand_weight,
    expand_bias,
    contract_weight,
    contract_bias,
    cotangent,
):
    images, rows, width = tokens.shape
    heads = width // HEAD_DIM
    flat = images * rows
    factor = HEAD_DIM ** (-0.5)
    cond_full = condition.astype(jnp.float32)
    sigmoid = jax.nn.sigmoid(cond_full)
    silu_b = (cond_full * sigmoid).astype(jnp.bfloat16)
    silu_pair = lax.all_gather(silu_b, "zl", axis=0, tiled=True)
    mod_cols = matmul(silu_pair, modulation_weight) + modulation_bias.reshape(1, -1)
    modulation = lax.all_to_all(mod_cols, "zl", split_axis=0, concat_axis=1, tiled=True).reshape(
        images, 6, 1, width
    )
    shift_a = modulation[:, 0]
    scale_a = modulation[:, 1]
    gate_a = modulation[:, 2]
    shift_b = modulation[:, 3]
    scale_b = modulation[:, 4]
    gate_b = modulation[:, 5]
    inputs = tokens.astype(jnp.float32)
    normed_a, inverse_a = normalize(inputs)
    mod_a = (normed_a * (1.0 + scale_a) + shift_a).astype(jnp.bfloat16).reshape(flat, width)
    qkv_bias = jnp.concatenate([query_bias, jnp.zeros_like(query_bias), value_bias])
    projected = (matmul(mod_a, input_weight) + qkv_bias).astype(jnp.bfloat16)
    attended_b = attention_forward(projected, images)
    branch_a = (matmul(attended_b, output_weight) + output_bias).reshape(images, rows, width)
    middle = inputs + gate_a * branch_a
    normed_b, inverse_b = normalize(middle)
    mod_b = (normed_b * (1.0 + scale_b) + shift_b).astype(jnp.bfloat16).reshape(flat, width)
    expanded = matmul(mod_b, expand_weight) + expand_bias
    tanh_part = jnp.tanh(GELU_C * (expanded + 0.044715 * expanded * expanded * expanded))
    activated_b = (0.5 * expanded * (1.0 + tanh_part)).astype(jnp.bfloat16)
    branch_b = (matmul(activated_b, contract_weight) + contract_bias).reshape(images, rows, width)
    alive = occupied.astype(jnp.float32)[:, None, None]
    layer_out = (middle + gate_b * branch_b) * alive
    grad_out = cotangent.astype(jnp.float32) * alive
    grad_gate_b = jnp.sum(grad_out * branch_b, axis=1)
    grad_branch_b = (grad_out * gate_b).astype(jnp.bfloat16).reshape(flat, width)
    blocks = 1
    for a in AXES:
        blocks *= sizes[a]
    ff = activated_b.shape[1]
    split = ff // width
    act_perm = stage_order(
        activated_b.reshape(flat, blocks, split, width // blocks)
        .transpose(0, 2, 1, 3)
        .reshape(flat, split, width),
        sizes,
        width // blocks,
    )
    contract_parts = [
        left_trans(act_perm[:, q], grad_branch_b).astype(jnp.bfloat16) for q in range(split)
    ]
    contract_bias_grad = stage_order(
        jnp.sum(grad_branch_b.astype(jnp.float32), axis=0), sizes, width // blocks
    )
    grad_act = right_trans(grad_branch_b, contract_weight)
    slope = 0.5 * (1.0 + tanh_part) + 0.5 * expanded * (1.0 - tanh_part * tanh_part) * GELU_C * (
        1.0 + 3.0 * 0.044715 * expanded * expanded
    )
    grad_exp_b = (grad_act * slope).astype(jnp.bfloat16)
    expand_grad = left_trans(stage_order(mod_b, sizes, width // blocks), grad_exp_b).astype(jnp.bfloat16)
    expand_bias_grad = stage_order(
        jnp.sum(grad_exp_b.astype(jnp.float32), axis=0)
        .reshape(blocks, split, width // blocks)
        .transpose(1, 0, 2)
        .reshape(split, width),
        sizes,
        width // blocks,
    )
    packed_a = jnp.concatenate(
        [expand_grad]
        + contract_parts
        + [bias_columns([contract_bias_grad] + [expand_bias_grad[q] for q in range(split)], width)],
        axis=1,
    )
    packed_a, grad_exp_b = lax.optimization_barrier((packed_a, grad_exp_b))
    chain_a = reduce_stages(packed_a, STAGES[:1])
    grad_mod_b = right_trans(grad_exp_b, expand_weight).reshape(images, rows, width)
    grad_shift_b = jnp.sum(grad_mod_b, axis=1)
    grad_scale_b = jnp.sum(grad_mod_b * normed_b, axis=1)
    grad_middle = grad_out + norm_back(grad_mod_b * (1.0 + scale_b), normed_b, inverse_b)
    grad_gate_a = jnp.sum(grad_middle * branch_a, axis=1)
    grad_branch_a = (grad_middle * gate_a).astype(jnp.bfloat16).reshape(flat, width)
    output_grad = left_trans(stage_order(attended_b, sizes, width // blocks, STAGES_B), grad_branch_a).astype(
        jnp.bfloat16
    )
    output_bias_grad = stage_order(
        jnp.sum(grad_branch_a.astype(jnp.float32), axis=0), sizes, width // blocks, STAGES_B
    )
    grad_att_b = right_trans(grad_branch_a, output_weight).astype(jnp.bfloat16)
    chain_a, grad_att_b = lax.optimization_barrier((chain_a, grad_att_b))
    chain_a = reduce_stages(chain_a, STAGES[1:2])
    grad_proj_b = attention_backward(projected, grad_att_b, images)
    input_grad = left_trans(stage_order(mod_a, sizes, width // blocks, STAGES_B), grad_proj_b).astype(
        jnp.bfloat16
    )
    bias_sums = jnp.sum(grad_proj_b.astype(jnp.float32), axis=0)
    query_bias_grad = stage_order(bias_sums[:width], sizes, width // blocks, STAGES_B)
    value_bias_grad = stage_order(bias_sums[2 * width :], sizes, width // blocks, STAGES_B)
    chain_b = reduce_pair(
        jnp.concatenate(
            [
                input_grad,
                output_grad,
                bias_columns([query_bias_grad, value_bias_grad, output_bias_grad], width),
            ],
            axis=1,
        ),
        STAGES_B[0],
    )
    chain_a, chain_b = lax.optimization_barrier((chain_a, chain_b))
    chain_b = reduce_stages(chain_b, STAGES_B[1:2])
    grad_mod_a = right_trans(grad_proj_b, input_weight).reshape(images, rows, width)
    grad_shift_a = jnp.sum(grad_mod_a, axis=1)
    grad_scale_a = jnp.sum(grad_mod_a * normed_a, axis=1)
    tokens_grad = grad_middle + norm_back(grad_mod_a * (1.0 + scale_a), normed_a, inverse_a)
    modulation_terms = jnp.stack(
        [grad_shift_a, grad_scale_a, grad_gate_a, grad_shift_b, grad_scale_b, grad_gate_b], axis=1
    ).reshape(images, 6 * width)
    modulation_own = modulation_terms.astype(jnp.bfloat16)
    modulation_cols = lax.all_to_all(modulation_own, "zl", split_axis=1, concat_axis=0, tiled=True)
    silu_terms = right_trans(modulation_cols, modulation_weight)
    pair_index = lax.axis_index("zl")
    own_rows = lax.dynamic_slice_in_dim(silu_terms, pair_index * images, images, axis=0)
    other_rows = lax.dynamic_slice_in_dim(silu_terms, (1 - pair_index) * images, images, axis=0)
    silu_sums = own_rows + lax.ppermute(other_rows, "zl", [(0, 1), (1, 0)])
    condition_grad = silu_sums * sigmoid * (1.0 + cond_full * (1.0 - sigmoid))
    factors = gather_dp(jnp.concatenate([silu_pair, modulation_cols], axis=1))
    silu_all = factors[:, :width]
    mod_all = factors[:, width:]
    dp_index = lax.axis_index(DP)
    dp_count = silu_all.shape[0] // silu_pair.shape[0]
    row_block = width // dp_count
    silu_rows = lax.dynamic_slice_in_dim(silu_all, dp_index * row_block, row_block, axis=1)
    modulation_weight_grad = left_trans(silu_rows, mod_all)
    bias_all = jnp.sum(mod_all.astype(jnp.float32), axis=0).reshape(-1, width)
    modulation_bias_grad = lax.dynamic_slice_in_dim(bias_all, dp_index * row_block, row_block, axis=1)
    chain_a = reduce_rest(chain_a, STAGES[2:])
    chain_b, mod_all = lax.optimization_barrier((chain_b, mod_all))
    chain_b = reduce_rest(chain_b, STAGES_B[2:])
    three = input_weight.shape[1]
    fw = expand_weight.shape[1]
    input_weight_grad = chain_b[:, :three]
    output_weight_grad = chain_b[:, three : three + width]
    qb_grad = chain_b[:, three + width]
    vb_grad = chain_b[:, three + width + 1]
    ob_grad = chain_b[:, three + width + 2]
    expand_weight_grad = chain_a[:, :fw]
    contract_weight_grad = chain_a[:, fw : fw + split * width].reshape(-1, split, width)
    contract_weight_grad = contract_weight_grad.transpose(1, 0, 2).reshape(-1, width)
    cb_grad = chain_a[:, fw + split * width]
    eb_grad = chain_a[:, fw + split * width + 1 : fw + split * width + 1 + split].T.reshape(-1)
    summed = (
        input_weight_grad,
        qb_grad,
        vb_grad,
        output_weight_grad,
        ob_grad,
        expand_weight_grad,
        eb_grad,
        contract_weight_grad,
        cb_grad,
    )
    return (
        layer_out,
        tokens_grad,
        condition_grad,
        modulation_weight_grad,
        modulation_bias_grad,
        *summed,
    )


def solution(mesh):
    dp_size, mod_size = mesh.devices.shape
    rest = dp_size // 4
    side = int(round(rest ** 0.5))
    shape = (side, 2, rest // side, 2, mod_size)
    sizes = dict(zip(AXES, shape))
    physical = Mesh(np.asarray(mesh.devices).reshape(shape), AXES)
    ALL = AXES
    placed = (
        P(ALL, None, None),
        P(ALL, None),
        P(ALL),
        P(None, "zl"),
        P("zl", None),
        P(),
        P(),
        P(),
        P(),
        P(),
        P(),
        P(),
        P(),
        P(),
        P(ALL, None, None),
    )
    return jax.shard_map(
        functools.partial(per_device, sizes),
        mesh=physical,
        in_specs=placed,
        out_specs=(
            P(ALL, None, None),
            P(ALL, None, None),
            P(ALL, None),
            P(DP, "zl"),
            P("zl", DP),
            P(ALL, None),
            P(ALL),
            P(ALL),
            P(ALL, None),
            P(ALL),
            P(ALL, None),
            P(ALL),
            P(ALL, None),
            P(ALL),
        ),
        check_vma=False,
    )
```

```python
import functools

import jax
import jax.numpy as jnp
import numpy as np
from jax import lax
from jax.experimental import pallas as pl
from jax.experimental.pallas import tpu as pltpu
from jax.sharding import Mesh
from jax.sharding import PartitionSpec as P

HEAD_DIM = 64
LANES = 128


def _nt(a, b):
    return lax.dot_general(a, b, (((1,), (1,)), ((), ())), preferred_element_type=jnp.float32)


def _tn(a, b):
    return lax.dot_general(a, b, (((0,), (0,)), ((), ())), preferred_element_type=jnp.float32)


def _probs(q, k, head, factor):
    lane = lax.broadcasted_iota(jnp.int32, (1, LANES), 1)
    mine = (lane // HEAD_DIM) == head
    qh = jnp.where(mine, q, jnp.zeros_like(q))
    scores = _nt(qh, k) * factor
    weights = jnp.exp(scores - jnp.max(scores, axis=-1, keepdims=True))
    return mine, qh, weights / jnp.sum(weights, axis=-1, keepdims=True)


def _fwd_kernel(factor, q_ref, k_ref, v_ref, o_ref):
    q = q_ref[...]
    k = k_ref[...]
    v = v_ref[...]
    out = jnp.zeros(o_ref.shape, jnp.float32)
    for head in range(LANES // HEAD_DIM):
        mine, _, probs = _probs(q, k, head, factor)
        vh = jnp.where(mine, v, jnp.zeros_like(v))
        out = out + jnp.dot(probs.astype(v.dtype), vh, preferred_element_type=jnp.float32)
    o_ref[...] = out.astype(o_ref.dtype)


def _bwd_kernel(factor, q_ref, k_ref, v_ref, d_ref, dq_ref, dk_ref, dv_ref):
    q = q_ref[...]
    k = k_ref[...]
    v = v_ref[...]
    d = d_ref[...]
    dq = jnp.zeros(dq_ref.shape, jnp.float32)
    dk = jnp.zeros(dk_ref.shape, jnp.float32)
    dv = jnp.zeros(dv_ref.shape, jnp.float32)
    for head in range(LANES // HEAD_DIM):
        mine, qh, probs = _probs(q, k, head, factor)
        dh = jnp.where(mine, d, jnp.zeros_like(d))
        kh = jnp.where(mine, k, jnp.zeros_like(k))
        dprobs = _nt(dh, v)
        dv = dv + _tn(probs.astype(d.dtype), dh)
        inner = jnp.sum(dprobs * probs, axis=-1, keepdims=True)
        dscores = (probs * (dprobs - inner)).astype(q.dtype)
        dq = dq + jnp.dot(dscores, kh, preferred_element_type=jnp.float32)
        dk = dk + _tn(dscores, qh)
    dq_ref[...] = (dq * factor).astype(dq_ref.dtype)
    dk_ref[...] = (dk * factor).astype(dk_ref.dtype)
    dv_ref[...] = dv.astype(dv_ref.dtype)


def _wgrad_kernel(expand_tiles, modb_ref, du_ref, act_ref, dz_ref, out_ref):
    j = pl.program_id(0)

    @pl.when(j < expand_tiles)
    def _():
        out_ref[...] = _tn(modb_ref[...], du_ref[...]).astype(out_ref.dtype)

    @pl.when(j >= expand_tiles)
    def _():
        out_ref[...] = _tn(act_ref[...], dz_ref[...]).astype(out_ref.dtype)


def ffn_weight_grads(mod_perm, grad_exp, act_perm, grad_branch, tile=512):
    tokens, width = mod_perm.shape
    ff = grad_exp.shape[1]
    expand_tiles = ff // tile
    per_part = width // tile
    tiles = expand_tiles + (ff // width) * per_part

    def act_index(j):
        return (0, jnp.maximum(j - expand_tiles, 0) // per_part)

    def dz_index(j):
        return (0, jnp.maximum(j - expand_tiles, 0) % per_part)

    return pl.pallas_call(
        functools.partial(_wgrad_kernel, expand_tiles),
        out_shape=jax.ShapeDtypeStruct((width, tiles * tile), jnp.bfloat16),
        grid=(tiles,),
        in_specs=[
            pl.BlockSpec((tokens, width), lambda j: (0, 0)),
            pl.BlockSpec((tokens, tile), lambda j: (0, jnp.minimum(j, expand_tiles - 1))),
            pl.BlockSpec((tokens, width), act_index),
            pl.BlockSpec((tokens, tile), dz_index),
        ],
        out_specs=pl.BlockSpec((width, tile), lambda j: (0, j)),
        compiler_params=pltpu.CompilerParams(dimension_semantics=("arbitrary",)),
        cost_estimate=pl.CostEstimate(
            flops=2 * tokens * width * tiles * tile,
            transcendentals=0,
            bytes_accessed=2 * (tokens * (width + 2 * ff + width) + width * tiles * tile),
        ),
    )(mod_perm, grad_exp, act_perm, grad_branch)


def attention_forward(projected, images):
    tokens, three = projected.shape
    rows, width = tokens // images, three // 3
    pairs = width // LANES
    factor = HEAD_DIM ** (-0.5)

    def part(offset):
        return pl.BlockSpec((rows, LANES), lambda b, j: (b, offset + j))

    flops = 2 * 2 * images * (width // HEAD_DIM) * rows * rows * LANES
    return pl.pallas_call(
        functools.partial(_fwd_kernel, factor),
        out_shape=jax.ShapeDtypeStruct((tokens, width), projected.dtype),
        grid=(images, pairs),
        in_specs=[part(0), part(pairs), part(2 * pairs)],
        out_specs=pl.BlockSpec((rows, LANES), lambda b, j: (b, j)),
        compiler_params=pltpu.CompilerParams(dimension_semantics=("parallel", "parallel")),
        cost_estimate=pl.CostEstimate(
            flops=flops, transcendentals=images * (width // HEAD_DIM) * rows * rows,
            bytes_accessed=2 * tokens * (three + width),
        ),
    )(projected, projected, projected)


def attention_backward(projected, grad_attended, images):
    tokens, three = projected.shape
    rows, width = tokens // images, three // 3
    pairs = width // LANES
    factor = HEAD_DIM ** (-0.5)

    def part(offset):
        return pl.BlockSpec((rows, LANES), lambda b, j: (b, offset + j))

    out = jax.ShapeDtypeStruct((tokens, width), projected.dtype)
    flops = 5 * 2 * 2 * images * (width // HEAD_DIM) * rows * rows * LANES
    dq, dk, dv = pl.pallas_call(
        functools.partial(_bwd_kernel, factor),
        out_shape=(out, out, out),
        grid=(images, pairs),
        in_specs=[part(0), part(pairs), part(2 * pairs), part(0)],
        out_specs=[part(0)] * 3,
        compiler_params=pltpu.CompilerParams(dimension_semantics=("parallel", "parallel")),
        cost_estimate=pl.CostEstimate(
            flops=flops, transcendentals=images * (width // HEAD_DIM) * rows * rows,
            bytes_accessed=2 * tokens * (three + 4 * width),
        ),
    )(projected, projected, projected, grad_attended)
    return jnp.concatenate([dq, dk, dv], axis=1)


EPS = 1e-06
GELU_C = 0.7978845608028654

AXES = ("y", "zh", "x", "c", "zl")
DP = ("y", "zh", "x", "c")
STAGES = ("c", "x", "y", "zh", "zl")
STAGES_B = ("c", "y", "x", "zh", "zl")


def matmul(left, right):
    return jnp.dot(left, right, preferred_element_type=jnp.float32)


def left_trans(left, right):
    return lax.dot_general(
        left, right, (((0,), (0,)), ((), ())), preferred_element_type=jnp.float32
    )


def right_trans(left, right):
    return lax.dot_general(
        left, right, (((1,), (1,)), ((), ())), preferred_element_type=jnp.float32
    )


def normalize(values):
    centre = values - jnp.mean(values, axis=-1, keepdims=True)
    inverse = lax.rsqrt(jnp.mean(centre * centre, axis=-1, keepdims=True) + EPS)
    return (centre * inverse, inverse)


def norm_back(grad, normed, inverse):
    return inverse * (
        grad
        - jnp.mean(grad, axis=-1, keepdims=True)
        - normed * jnp.mean(grad * normed, axis=-1, keepdims=True)
    )


def stage_order(values, sizes, inner, stages=STAGES):
    lead = values.shape[:-1]
    shape = [sizes[a] for a in AXES]
    values = values.reshape(*lead, *shape, inner)
    n = len(lead)
    order = list(range(n)) + [n + AXES.index(a) for a in stages] + [n + len(AXES)]
    return jnp.transpose(values, order).reshape(*lead, -1)


def reduce_stages(packed, stages):
    for a in stages:
        packed = lax.psum_scatter(packed, a, scatter_dimension=0, tiled=True)
    return packed


def reduce_pair(packed, axis):
    half = packed.shape[0] // 2
    index = lax.axis_index(axis)
    keep = lax.dynamic_slice_in_dim(packed, index * half, half, axis=0)
    send = lax.dynamic_slice_in_dim(packed, (1 - index) * half, half, axis=0)
    got = lax.ppermute(send, axis, [(0, 1), (1, 0)])
    return (keep.astype(jnp.float32) + got.astype(jnp.float32)).astype(packed.dtype)


def reduce_rest(packed, axes):
    count = 1
    for a in axes:
        count *= lax.axis_size(a)
    chunks = packed.reshape(count, packed.shape[0] // count, packed.shape[1])
    chunks = lax.all_to_all(chunks, axes, 0, 0, tiled=False)
    return jnp.sum(chunks.astype(jnp.float32), axis=0)


def bias_columns(columns, rows):
    block = jnp.stack(columns, axis=1)
    return jnp.pad(block, ((0, 0), (0, 128 - block.shape[1]))).astype(jnp.bfloat16)


def gather_dp(values):
    count = 1
    for a in DP:
        count *= lax.axis_size(a)
    copies = jnp.broadcast_to(values[None], (count,) + values.shape)
    return lax.all_to_all(copies, DP, 0, 0, tiled=False).reshape(-1, values.shape[1])


def per_device(
    sizes,
    tokens,
    condition,
    occupied,
    modulation_weight,
    modulation_bias,
    input_weight,
    query_bias,
    value_bias,
    output_weight,
    output_bias,
    expand_weight,
    expand_bias,
    contract_weight,
    contract_bias,
    cotangent,
):
    images, rows, width = tokens.shape
    heads = width // HEAD_DIM
    flat = images * rows
    factor = HEAD_DIM ** (-0.5)
    cond_full = condition.astype(jnp.float32)
    sigmoid = jax.nn.sigmoid(cond_full)
    silu_b = (cond_full * sigmoid).astype(jnp.bfloat16)
    silu_pair = lax.all_gather(silu_b, "zl", axis=0, tiled=True)
    mod_cols = matmul(silu_pair, modulation_weight) + modulation_bias.reshape(1, -1)
    modulation = lax.all_to_all(mod_cols, "zl", split_axis=0, concat_axis=1, tiled=True).reshape(
        images, 6, 1, width
    )
    shift_a = modulation[:, 0]
    scale_a = modulation[:, 1]
    gate_a = modulation[:, 2]
    shift_b = modulation[:, 3]
    scale_b = modulation[:, 4]
    gate_b = modulation[:, 5]
    inputs = tokens.astype(jnp.float32)
    normed_a, inverse_a = normalize(inputs)
    mod_a = (normed_a * (1.0 + scale_a) + shift_a).astype(jnp.bfloat16).reshape(flat, width)
    qkv_bias = jnp.concatenate([query_bias, jnp.zeros_like(query_bias), value_bias])
    projected = (matmul(mod_a, input_weight) + qkv_bias).astype(jnp.bfloat16)
    attended_b = attention_forward(projected, images)
    branch_a = (matmul(attended_b, output_weight) + output_bias).reshape(images, rows, width)
    middle = inputs + gate_a * branch_a
    normed_b, inverse_b = normalize(middle)
    mod_b = (normed_b * (1.0 + scale_b) + shift_b).astype(jnp.bfloat16).reshape(flat, width)
    expanded = matmul(mod_b, expand_weight) + expand_bias
    tanh_part = jnp.tanh(GELU_C * (expanded + 0.044715 * expanded * expanded * expanded))
    activated_b = (0.5 * expanded * (1.0 + tanh_part)).astype(jnp.bfloat16)
    branch_b = (matmul(activated_b, contract_weight) + contract_bias).reshape(images, rows, width)
    alive = occupied.astype(jnp.float32)[:, None, None]
    layer_out = (middle + gate_b * branch_b) * alive
    grad_out = cotangent.astype(jnp.float32) * alive
    grad_gate_b = jnp.sum(grad_out * branch_b, axis=1)
    grad_branch_b = (grad_out * gate_b).astype(jnp.bfloat16).reshape(flat, width)
    blocks = 1
    for a in AXES:
        blocks *= sizes[a]
    ff = activated_b.shape[1]
    split = ff // width
    act_perm = stage_order(
        activated_b.reshape(flat, blocks, split, width // blocks)
        .transpose(0, 2, 1, 3)
        .reshape(flat, split, width),
        sizes,
        width // blocks,
    )
    contract_bias_grad = stage_order(
        jnp.sum(grad_branch_b.astype(jnp.float32), axis=0), sizes, width // blocks, STAGES_B
    )
    grad_act = right_trans(grad_branch_b, contract_weight)
    slope = 0.5 * (1.0 + tanh_part) + 0.5 * expanded * (1.0 - tanh_part * tanh_part) * GELU_C * (
        1.0 + 3.0 * 0.044715 * expanded * expanded
    )
    grad_exp_b = (grad_act * slope).astype(jnp.bfloat16)
    expand_bias_grad = stage_order(
        jnp.sum(grad_exp_b.astype(jnp.float32), axis=0)
        .reshape(blocks, split, width // blocks)
        .transpose(1, 0, 2)
        .reshape(split, width),
        sizes,
        width // blocks,
        STAGES_B,
    )
    packed_a = ffn_weight_grads(
        stage_order(mod_b, sizes, width // blocks), grad_exp_b, act_perm.reshape(flat, -1), grad_branch_b
    )
    packed_a, grad_exp_b = lax.optimization_barrier((packed_a, grad_exp_b))
    chain_a = reduce_stages(packed_a, STAGES[:1])
    grad_mod_b = right_trans(grad_exp_b, expand_weight).reshape(images, rows, width)
    grad_shift_b = jnp.sum(grad_mod_b, axis=1)
    grad_scale_b = jnp.sum(grad_mod_b * normed_b, axis=1)
    grad_middle = grad_out + norm_back(grad_mod_b * (1.0 + scale_b), normed_b, inverse_b)
    grad_gate_a = jnp.sum(grad_middle * branch_a, axis=1)
    grad_branch_a = (grad_middle * gate_a).astype(jnp.bfloat16).reshape(flat, width)
    output_grad = left_trans(stage_order(attended_b, sizes, width // blocks, STAGES_B), grad_branch_a).astype(
        jnp.bfloat16
    )
    output_bias_grad = stage_order(
        jnp.sum(grad_branch_a.astype(jnp.float32), axis=0), sizes, width // blocks, STAGES_B
    )
    grad_att_b = right_trans(grad_branch_a, output_weight).astype(jnp.bfloat16)
    chain_a, grad_att_b = lax.optimization_barrier((chain_a, grad_att_b))
    chain_a = reduce_stages(chain_a, STAGES[1:2])
    grad_proj_b = attention_backward(projected, grad_att_b, images)
    input_grad = left_trans(stage_order(mod_a, sizes, width // blocks, STAGES_B), grad_proj_b).astype(
        jnp.bfloat16
    )
    bias_sums = jnp.sum(grad_proj_b.astype(jnp.float32), axis=0)
    query_bias_grad = stage_order(bias_sums[:width], sizes, width // blocks, STAGES_B)
    value_bias_grad = stage_order(bias_sums[2 * width :], sizes, width // blocks, STAGES_B)
    chain_b = reduce_pair(
        jnp.concatenate(
            [
                input_grad,
                output_grad,
                bias_columns(
                [query_bias_grad, value_bias_grad, output_bias_grad, contract_bias_grad]
                + [expand_bias_grad[q] for q in range(split)],
                width,
            ),
            ],
            axis=1,
        ),
        STAGES_B[0],
    )
    chain_a, chain_b = lax.optimization_barrier((chain_a, chain_b))
    chain_b = reduce_stages(chain_b, STAGES_B[1:2])
    grad_mod_a = right_trans(grad_proj_b, input_weight).reshape(images, rows, width)
    grad_shift_a = jnp.sum(grad_mod_a, axis=1)
    grad_scale_a = jnp.sum(grad_mod_a * normed_a, axis=1)
    tokens_grad = grad_middle + norm_back(grad_mod_a * (1.0 + scale_a), normed_a, inverse_a)
    modulation_terms = jnp.stack(
        [grad_shift_a, grad_scale_a, grad_gate_a, grad_shift_b, grad_scale_b, grad_gate_b], axis=1
    ).reshape(images, 6 * width)
    modulation_own = modulation_terms.astype(jnp.bfloat16)
    modulation_cols = lax.all_to_all(modulation_own, "zl", split_axis=1, concat_axis=0, tiled=True)
    silu_terms = right_trans(modulation_cols, modulation_weight)
    pair_index = lax.axis_index("zl")
    own_rows = lax.dynamic_slice_in_dim(silu_terms, pair_index * images, images, axis=0)
    other_rows = lax.dynamic_slice_in_dim(silu_terms, (1 - pair_index) * images, images, axis=0)
    silu_sums = own_rows + lax.ppermute(other_rows, "zl", [(0, 1), (1, 0)])
    condition_grad = silu_sums * sigmoid * (1.0 + cond_full * (1.0 - sigmoid))
    factors = gather_dp(jnp.concatenate([silu_pair, modulation_cols], axis=1))
    silu_all = factors[:, :width]
    mod_all = factors[:, width:]
    dp_index = lax.axis_index(DP)
    dp_count = silu_all.shape[0] // silu_pair.shape[0]
    row_block = width // dp_count
    silu_rows = lax.dynamic_slice_in_dim(silu_all, dp_index * row_block, row_block, axis=1)
    modulation_weight_grad = left_trans(silu_rows, mod_all)
    bias_all = jnp.sum(mod_all.astype(jnp.float32), axis=0).reshape(-1, width)
    modulation_bias_grad = lax.dynamic_slice_in_dim(bias_all, dp_index * row_block, row_block, axis=1)
    chain_a = reduce_rest(chain_a, STAGES[2:])
    chain_b, mod_all = lax.optimization_barrier((chain_b, mod_all))
    chain_b = reduce_rest(chain_b, STAGES_B[2:])
    three = input_weight.shape[1]
    fw = expand_weight.shape[1]
    input_weight_grad = chain_b[:, :three]
    output_weight_grad = chain_b[:, three : three + width]
    qb_grad = chain_b[:, three + width]
    vb_grad = chain_b[:, three + width + 1]
    ob_grad = chain_b[:, three + width + 2]
    expand_weight_grad = chain_a[:, :fw]
    contract_weight_grad = chain_a[:, fw : fw + split * width].reshape(-1, split, width)
    contract_weight_grad = contract_weight_grad.transpose(1, 0, 2).reshape(-1, width)
    cb_grad = chain_b[:, three + width + 3]
    eb_grad = chain_b[:, three + width + 4 : three + width + 4 + split].T.reshape(-1)
    summed = (
        input_weight_grad,
        qb_grad,
        vb_grad,
        output_weight_grad,
        ob_grad,
        expand_weight_grad,
        eb_grad,
        contract_weight_grad,
        cb_grad,
    )
    return (
        layer_out,
        tokens_grad,
        condition_grad,
        modulation_weight_grad,
        modulation_bias_grad,
        *summed,
    )


def solution(mesh):
    dp_size, mod_size = mesh.devices.shape
    rest = dp_size // 4
    side = int(round(rest ** 0.5))
    shape = (side, 2, rest // side, 2, mod_size)
    sizes = dict(zip(AXES, shape))
    physical = Mesh(np.asarray(mesh.devices).reshape(shape), AXES)
    ALL = AXES
    placed = (
        P(ALL, None, None),
        P(ALL, None),
        P(ALL),
        P(None, "zl"),
        P("zl", None),
        P(),
        P(),
        P(),
        P(),
        P(),
        P(),
        P(),
        P(),
        P(),
        P(ALL, None, None),
    )
    return jax.shard_map(
        functools.partial(per_device, sizes),
        mesh=physical,
        in_specs=placed,
        out_specs=(
            P(ALL, None, None),
            P(ALL, None, None),
            P(ALL, None),
            P(DP, "zl"),
            P("zl", DP),
            P(ALL, None),
            P(ALL),
            P(ALL),
            P(ALL, None),
            P(ALL),
            P(ALL, None),
            P(ALL),
            P(ALL, None),
            P(ALL),
        ),
        check_vma=False,
    )
```

```python
import functools

import jax
import jax.numpy as jnp
import numpy as np
from jax import lax
from jax.experimental import pallas as pl
from jax.experimental.pallas import tpu as pltpu
from jax.sharding import Mesh
from jax.sharding import PartitionSpec as P

HEAD_DIM = 64
LANES = 128


def _nt(a, b):
    return lax.dot_general(a, b, (((1,), (1,)), ((), ())), preferred_element_type=jnp.float32)


def _tn(a, b):
    return lax.dot_general(a, b, (((0,), (0,)), ((), ())), preferred_element_type=jnp.float32)


def _probs(q, k, head, factor):
    lane = lax.broadcasted_iota(jnp.int32, (1, LANES), 1)
    mine = (lane // HEAD_DIM) == head
    qh = jnp.where(mine, q, jnp.zeros_like(q))
    scores = _nt(qh, k) * factor
    weights = jnp.exp(scores - jnp.max(scores, axis=-1, keepdims=True))
    return mine, qh, weights / jnp.sum(weights, axis=-1, keepdims=True)


def _fwd_kernel(factor, q_ref, k_ref, v_ref, o_ref):
    q = q_ref[...]
    k = k_ref[...]
    v = v_ref[...]
    out = jnp.zeros(o_ref.shape, jnp.float32)
    for head in range(LANES // HEAD_DIM):
        mine, _, probs = _probs(q, k, head, factor)
        vh = jnp.where(mine, v, jnp.zeros_like(v))
        out = out + jnp.dot(probs.astype(v.dtype), vh, preferred_element_type=jnp.float32)
    o_ref[...] = out.astype(o_ref.dtype)


def _bwd_kernel(factor, q_ref, k_ref, v_ref, d_ref, dq_ref, dk_ref, dv_ref):
    q = q_ref[...]
    k = k_ref[...]
    v = v_ref[...]
    d = d_ref[...]
    dq = jnp.zeros(dq_ref.shape, jnp.float32)
    dk = jnp.zeros(dk_ref.shape, jnp.float32)
    dv = jnp.zeros(dv_ref.shape, jnp.float32)
    for head in range(LANES // HEAD_DIM):
        mine, qh, probs = _probs(q, k, head, factor)
        dh = jnp.where(mine, d, jnp.zeros_like(d))
        kh = jnp.where(mine, k, jnp.zeros_like(k))
        dprobs = _nt(dh, v)
        dv = dv + _tn(probs.astype(d.dtype), dh)
        inner = jnp.sum(dprobs * probs, axis=-1, keepdims=True)
        dscores = (probs * (dprobs - inner)).astype(q.dtype)
        dq = dq + jnp.dot(dscores, kh, preferred_element_type=jnp.float32)
        dk = dk + _tn(dscores, qh)
    dq_ref[...] = (dq * factor).astype(dq_ref.dtype)
    dk_ref[...] = (dk * factor).astype(dk_ref.dtype)
    dv_ref[...] = dv.astype(dv_ref.dtype)


def _wgrad_kernel(expand_tiles, modb_ref, du_ref, act_ref, dz_ref, out_ref):
    j = pl.program_id(0)

    @pl.when(j < expand_tiles)
    def _():
        out_ref[...] = jnp.dot(
            modb_ref[...], du_ref[...], preferred_element_type=jnp.float32
        ).astype(out_ref.dtype)

    @pl.when(j >= expand_tiles)
    def _():
        out_ref[...] = jnp.dot(
            act_ref[...], dz_ref[...], preferred_element_type=jnp.float32
        ).astype(out_ref.dtype)


def ffn_weight_grads(mod_t, grad_exp, act_t, grad_branch, tile=512):
    width, tokens = mod_t.shape
    ff = grad_exp.shape[1]
    expand_tiles = ff // tile
    per_part = width // tile
    tiles = expand_tiles + (ff // width) * per_part

    def act_index(j):
        return (jnp.maximum(j - expand_tiles, 0) // per_part, 0)

    def dz_index(j):
        return (0, jnp.maximum(j - expand_tiles, 0) % per_part)

    return pl.pallas_call(
        functools.partial(_wgrad_kernel, expand_tiles),
        out_shape=jax.ShapeDtypeStruct((width, tiles * tile), jnp.bfloat16),
        grid=(tiles,),
        in_specs=[
            pl.BlockSpec((width, tokens), lambda j: (0, 0)),
            pl.BlockSpec((tokens, tile), lambda j: (0, jnp.minimum(j, expand_tiles - 1))),
            pl.BlockSpec((width, tokens), act_index),
            pl.BlockSpec((tokens, tile), dz_index),
        ],
        out_specs=pl.BlockSpec((width, tile), lambda j: (0, j)),
        compiler_params=pltpu.CompilerParams(dimension_semantics=("arbitrary",)),
        cost_estimate=pl.CostEstimate(
            flops=2 * tokens * width * tiles * tile,
            transcendentals=0,
            bytes_accessed=2 * (tokens * (width + 2 * ff + width) + width * tiles * tile),
        ),
    )(mod_t, grad_exp, act_t, grad_branch)

def attention_forward(projected, images):
    tokens, three = projected.shape
    rows, width = tokens // images, three // 3
    pairs = width // LANES
    factor = HEAD_DIM ** (-0.5)

    def part(offset):
        return pl.BlockSpec((rows, LANES), lambda b, j: (b, offset + j))

    flops = 2 * 2 * images * (width // HEAD_DIM) * rows * rows * LANES
    return pl.pallas_call(
        functools.partial(_fwd_kernel, factor),
        out_shape=jax.ShapeDtypeStruct((tokens, width), projected.dtype),
        grid=(images, pairs),
        in_specs=[part(0), part(pairs), part(2 * pairs)],
        out_specs=pl.BlockSpec((rows, LANES), lambda b, j: (b, j)),
        compiler_params=pltpu.CompilerParams(dimension_semantics=("parallel", "parallel")),
        cost_estimate=pl.CostEstimate(
            flops=flops, transcendentals=images * (width // HEAD_DIM) * rows * rows,
            bytes_accessed=2 * tokens * (three + width),
        ),
    )(projected, projected, projected)


def attention_backward(projected, grad_attended, images):
    tokens, three = projected.shape
    rows, width = tokens // images, three // 3
    pairs = width // LANES
    factor = HEAD_DIM ** (-0.5)

    def part(offset):
        return pl.BlockSpec((rows, LANES), lambda b, j: (b, offset + j))

    out = jax.ShapeDtypeStruct((tokens, width), projected.dtype)
    flops = 5 * 2 * 2 * images * (width // HEAD_DIM) * rows * rows * LANES
    dq, dk, dv = pl.pallas_call(
        functools.partial(_bwd_kernel, factor),
        out_shape=(out, out, out),
        grid=(images, pairs),
        in_specs=[part(0), part(pairs), part(2 * pairs), part(0)],
        out_specs=[part(0)] * 3,
        compiler_params=pltpu.CompilerParams(dimension_semantics=("parallel", "parallel")),
        cost_estimate=pl.CostEstimate(
            flops=flops, transcendentals=images * (width // HEAD_DIM) * rows * rows,
            bytes_accessed=2 * tokens * (three + 4 * width),
        ),
    )(projected, projected, projected, grad_attended)
    return jnp.concatenate([dq, dk, dv], axis=1)


EPS = 1e-06
GELU_C = 0.7978845608028654

AXES = ("y", "zh", "x", "c", "zl")
DP = ("y", "zh", "x", "c")
STAGES = ("c", "x", "y", "zh", "zl")
STAGES_B = ("c", "y", "x", "zh", "zl")


def matmul(left, right):
    return jnp.dot(left, right, preferred_element_type=jnp.float32)


def left_trans(left, right):
    return lax.dot_general(
        left, right, (((0,), (0,)), ((), ())), preferred_element_type=jnp.float32
    )


def right_trans(left, right):
    return lax.dot_general(
        left, right, (((1,), (1,)), ((), ())), preferred_element_type=jnp.float32
    )


def normalize(values):
    centre = values - jnp.mean(values, axis=-1, keepdims=True)
    inverse = lax.rsqrt(jnp.mean(centre * centre, axis=-1, keepdims=True) + EPS)
    return (centre * inverse, inverse)


def norm_back(grad, normed, inverse):
    return inverse * (
        grad
        - jnp.mean(grad, axis=-1, keepdims=True)
        - normed * jnp.mean(grad * normed, axis=-1, keepdims=True)
    )


def stage_order(values, sizes, inner, stages=STAGES):
    lead = values.shape[:-1]
    shape = [sizes[a] for a in AXES]
    values = values.reshape(*lead, *shape, inner)
    n = len(lead)
    order = list(range(n)) + [n + AXES.index(a) for a in stages] + [n + len(AXES)]
    return jnp.transpose(values, order).reshape(*lead, -1)


def reduce_stages(packed, stages):
    for a in stages:
        packed = lax.psum_scatter(packed, a, scatter_dimension=0, tiled=True)
    return packed


def reduce_pair(packed, axis):
    half = packed.shape[0] // 2
    index = lax.axis_index(axis)
    keep = lax.dynamic_slice_in_dim(packed, index * half, half, axis=0)
    send = lax.dynamic_slice_in_dim(packed, (1 - index) * half, half, axis=0)
    got = lax.ppermute(send, axis, [(0, 1), (1, 0)])
    return (keep.astype(jnp.float32) + got.astype(jnp.float32)).astype(packed.dtype)


def reduce_rest(packed, axes):
    count = 1
    for a in axes:
        count *= lax.axis_size(a)
    chunks = packed.reshape(count, packed.shape[0] // count, packed.shape[1])
    chunks = lax.all_to_all(chunks, axes, 0, 0, tiled=False)
    return jnp.sum(chunks.astype(jnp.float32), axis=0)


def bias_columns(columns, rows):
    block = jnp.stack(columns, axis=1)
    return jnp.pad(block, ((0, 0), (0, 128 - block.shape[1]))).astype(jnp.bfloat16)


def gather_dp(values):
    count = 1
    for a in DP:
        count *= lax.axis_size(a)
    copies = jnp.broadcast_to(values[None], (count,) + values.shape)
    return lax.all_to_all(copies, DP, 0, 0, tiled=False).reshape(-1, values.shape[1])


def per_device(
    sizes,
    tokens,
    condition,
    occupied,
    modulation_weight,
    modulation_bias,
    input_weight,
    query_bias,
    value_bias,
    output_weight,
    output_bias,
    expand_weight,
    expand_bias,
    contract_weight,
    contract_bias,
    cotangent,
):
    images, rows, width = tokens.shape
    heads = width // HEAD_DIM
    flat = images * rows
    factor = HEAD_DIM ** (-0.5)
    cond_full = condition.astype(jnp.float32)
    sigmoid = jax.nn.sigmoid(cond_full)
    silu_b = (cond_full * sigmoid).astype(jnp.bfloat16)
    silu_pair = lax.all_gather(silu_b, "zl", axis=0, tiled=True)
    mod_cols = matmul(silu_pair, modulation_weight) + modulation_bias.reshape(1, -1)
    modulation = lax.all_to_all(mod_cols, "zl", split_axis=0, concat_axis=1, tiled=True).reshape(
        images, 6, 1, width
    )
    shift_a = modulation[:, 0]
    scale_a = modulation[:, 1]
    gate_a = modulation[:, 2]
    shift_b = modulation[:, 3]
    scale_b = modulation[:, 4]
    gate_b = modulation[:, 5]
    inputs = tokens.astype(jnp.float32)
    normed_a, inverse_a = normalize(inputs)
    mod_a = (normed_a * (1.0 + scale_a) + shift_a).astype(jnp.bfloat16).reshape(flat, width)
    qkv_bias = jnp.concatenate([query_bias, jnp.zeros_like(query_bias), value_bias])
    projected = (matmul(mod_a, input_weight) + qkv_bias).astype(jnp.bfloat16)
    attended_b = attention_forward(projected, images)
    branch_a = (matmul(attended_b, output_weight) + output_bias).reshape(images, rows, width)
    middle = inputs + gate_a * branch_a
    normed_b, inverse_b = normalize(middle)
    mod_b = (normed_b * (1.0 + scale_b) + shift_b).astype(jnp.bfloat16).reshape(flat, width)
    expanded = matmul(mod_b, expand_weight) + expand_bias
    tanh_part = jnp.tanh(GELU_C * (expanded + 0.044715 * expanded * expanded * expanded))
    activated_b = (0.5 * expanded * (1.0 + tanh_part)).astype(jnp.bfloat16)
    branch_b = (matmul(activated_b, contract_weight) + contract_bias).reshape(images, rows, width)
    alive = occupied.astype(jnp.float32)[:, None, None]
    layer_out = (middle + gate_b * branch_b) * alive
    grad_out = cotangent.astype(jnp.float32) * alive
    grad_gate_b = jnp.sum(grad_out * branch_b, axis=1)
    grad_branch_b = (grad_out * gate_b).astype(jnp.bfloat16).reshape(flat, width)
    blocks = 1
    for a in AXES:
        blocks *= sizes[a]
    ff = activated_b.shape[1]
    split = ff // width
    act_perm = stage_order(
        activated_b.reshape(flat, blocks, split, width // blocks)
        .transpose(0, 2, 1, 3)
        .reshape(flat, split, width),
        sizes,
        width // blocks,
    )
    contract_bias_grad = stage_order(
        jnp.sum(grad_branch_b.astype(jnp.float32), axis=0), sizes, width // blocks, STAGES_B
    )
    grad_act = right_trans(grad_branch_b, contract_weight)
    slope = 0.5 * (1.0 + tanh_part) + 0.5 * expanded * (1.0 - tanh_part * tanh_part) * GELU_C * (
        1.0 + 3.0 * 0.044715 * expanded * expanded
    )
    grad_exp_b = (grad_act * slope).astype(jnp.bfloat16)
    expand_bias_grad = stage_order(
        jnp.sum(grad_exp_b.astype(jnp.float32), axis=0)
        .reshape(blocks, split, width // blocks)
        .transpose(1, 0, 2)
        .reshape(split, width),
        sizes,
        width // blocks,
        STAGES_B,
    )
    packed_a = ffn_weight_grads(
        stage_order(mod_b, sizes, width // blocks).T, grad_exp_b, act_perm.reshape(flat, -1).T, grad_branch_b
    )
    packed_a, grad_exp_b = lax.optimization_barrier((packed_a, grad_exp_b))
    chain_a = reduce_stages(packed_a, STAGES[:1])
    grad_mod_b = right_trans(grad_exp_b, expand_weight).reshape(images, rows, width)
    grad_shift_b = jnp.sum(grad_mod_b, axis=1)
    grad_scale_b = jnp.sum(grad_mod_b * normed_b, axis=1)
    grad_middle = grad_out + norm_back(grad_mod_b * (1.0 + scale_b), normed_b, inverse_b)
    grad_gate_a = jnp.sum(grad_middle * branch_a, axis=1)
    grad_branch_a = (grad_middle * gate_a).astype(jnp.bfloat16).reshape(flat, width)
    output_grad = left_trans(stage_order(attended_b, sizes, width // blocks, STAGES_B), grad_branch_a).astype(
        jnp.bfloat16
    )
    output_bias_grad = stage_order(
        jnp.sum(grad_branch_a.astype(jnp.float32), axis=0), sizes, width // blocks, STAGES_B
    )
    grad_att_b = right_trans(grad_branch_a, output_weight).astype(jnp.bfloat16)
    chain_a, grad_att_b = lax.optimization_barrier((chain_a, grad_att_b))
    chain_a = reduce_stages(chain_a, STAGES[1:2])
    grad_proj_b = attention_backward(projected, grad_att_b, images)
    input_grad = left_trans(stage_order(mod_a, sizes, width // blocks, STAGES_B), grad_proj_b).astype(
        jnp.bfloat16
    )
    bias_sums = jnp.sum(grad_proj_b.astype(jnp.float32), axis=0)
    query_bias_grad = stage_order(bias_sums[:width], sizes, width // blocks, STAGES_B)
    value_bias_grad = stage_order(bias_sums[2 * width :], sizes, width // blocks, STAGES_B)
    chain_b = reduce_pair(
        jnp.concatenate(
            [
                input_grad,
                output_grad,
                bias_columns(
                [query_bias_grad, value_bias_grad, output_bias_grad, contract_bias_grad]
                + [expand_bias_grad[q] for q in range(split)],
                width,
            ),
            ],
            axis=1,
        ),
        STAGES_B[0],
    )
    chain_a, chain_b = lax.optimization_barrier((chain_a, chain_b))
    chain_b = reduce_stages(chain_b, STAGES_B[1:2])
    grad_mod_a = right_trans(grad_proj_b, input_weight).reshape(images, rows, width)
    grad_shift_a = jnp.sum(grad_mod_a, axis=1)
    grad_scale_a = jnp.sum(grad_mod_a * normed_a, axis=1)
    tokens_grad = grad_middle + norm_back(grad_mod_a * (1.0 + scale_a), normed_a, inverse_a)
    modulation_terms = jnp.stack(
        [grad_shift_a, grad_scale_a, grad_gate_a, grad_shift_b, grad_scale_b, grad_gate_b], axis=1
    ).reshape(images, 6 * width)
    modulation_own = modulation_terms.astype(jnp.bfloat16)
    modulation_cols = lax.all_to_all(modulation_own, "zl", split_axis=1, concat_axis=0, tiled=True)
    silu_terms = right_trans(modulation_cols, modulation_weight)
    pair_index = lax.axis_index("zl")
    own_rows = lax.dynamic_slice_in_dim(silu_terms, pair_index * images, images, axis=0)
    other_rows = lax.dynamic_slice_in_dim(silu_terms, (1 - pair_index) * images, images, axis=0)
    silu_sums = own_rows + lax.ppermute(other_rows, "zl", [(0, 1), (1, 0)])
    condition_grad = silu_sums * sigmoid * (1.0 + cond_full * (1.0 - sigmoid))
    factors = gather_dp(jnp.concatenate([silu_pair, modulation_cols], axis=1))
    silu_all = factors[:, :width]
    mod_all = factors[:, width:]
    dp_index = lax.axis_index(DP)
    dp_count = silu_all.shape[0] // silu_pair.shape[0]
    row_block = width // dp_count
    silu_rows = lax.dynamic_slice_in_dim(silu_all, dp_index * row_block, row_block, axis=1)
    modulation_weight_grad = left_trans(silu_rows, mod_all)
    bias_all = jnp.sum(mod_all.astype(jnp.float32), axis=0).reshape(-1, width)
    modulation_bias_grad = lax.dynamic_slice_in_dim(bias_all, dp_index * row_block, row_block, axis=1)
    chain_a = reduce_rest(chain_a, STAGES[2:])
    chain_b, mod_all = lax.optimization_barrier((chain_b, mod_all))
    chain_b = reduce_rest(chain_b, STAGES_B[2:])
    three = input_weight.shape[1]
    fw = expand_weight.shape[1]
    input_weight_grad = chain_b[:, :three]
    output_weight_grad = chain_b[:, three : three + width]
    qb_grad = chain_b[:, three + width]
    vb_grad = chain_b[:, three + width + 1]
    ob_grad = chain_b[:, three + width + 2]
    expand_weight_grad = chain_a[:, :fw]
    contract_weight_grad = chain_a[:, fw : fw + split * width].reshape(-1, split, width)
    contract_weight_grad = contract_weight_grad.transpose(1, 0, 2).reshape(-1, width)
    cb_grad = chain_b[:, three + width + 3]
    eb_grad = chain_b[:, three + width + 4 : three + width + 4 + split].T.reshape(-1)
    summed = (
        input_weight_grad,
        qb_grad,
        vb_grad,
        output_weight_grad,
        ob_grad,
        expand_weight_grad,
        eb_grad,
        contract_weight_grad,
        cb_grad,
    )
    return (
        layer_out,
        tokens_grad,
        condition_grad,
        modulation_weight_grad,
        modulation_bias_grad,
        *summed,
    )


def solution(mesh):
    dp_size, mod_size = mesh.devices.shape
    rest = dp_size // 4
    side = int(round(rest ** 0.5))
    shape = (side, 2, rest // side, 2, mod_size)
    sizes = dict(zip(AXES, shape))
    physical = Mesh(np.asarray(mesh.devices).reshape(shape), AXES)
    ALL = AXES
    placed = (
        P(ALL, None, None),
        P(ALL, None),
        P(ALL),
        P(None, "zl"),
        P("zl", None),
        P(),
        P(),
        P(),
        P(),
        P(),
        P(),
        P(),
        P(),
        P(),
        P(ALL, None, None),
    )
    return jax.shard_map(
        functools.partial(per_device, sizes),
        mesh=physical,
        in_specs=placed,
        out_specs=(
            P(ALL, None, None),
            P(ALL, None, None),
            P(ALL, None),
            P(DP, "zl"),
            P("zl", DP),
            P(ALL, None),
            P(ALL),
            P(ALL),
            P(ALL, None),
            P(ALL),
            P(ALL, None),
            P(ALL),
            P(ALL, None),
            P(ALL),
        ),
        check_vma=False,
    )
```

```python
import functools

import jax
import jax.numpy as jnp
import numpy as np
from jax import lax
from jax.experimental import pallas as pl
from jax.experimental.pallas import tpu as pltpu
from jax.sharding import Mesh
from jax.sharding import PartitionSpec as P

HEAD_DIM = 64
LANES = 128


def _nt(a, b):
    return lax.dot_general(a, b, (((1,), (1,)), ((), ())), preferred_element_type=jnp.float32)


def _tn(a, b):
    return lax.dot_general(a, b, (((0,), (0,)), ((), ())), preferred_element_type=jnp.float32)


def _probs(q, k, head, factor):
    lane = lax.broadcasted_iota(jnp.int32, (1, LANES), 1)
    mine = (lane // HEAD_DIM) == head
    qh = jnp.where(mine, q, jnp.zeros_like(q))
    scores = _nt(qh, k) * factor
    weights = jnp.exp(scores - jnp.max(scores, axis=-1, keepdims=True))
    return mine, qh, weights / jnp.sum(weights, axis=-1, keepdims=True)


def _fwd_kernel(factor, q_ref, k_ref, v_ref, o_ref):
    q = q_ref[...]
    k = k_ref[...]
    v = v_ref[...]
    out = jnp.zeros(o_ref.shape, jnp.float32)
    for head in range(LANES // HEAD_DIM):
        mine, _, probs = _probs(q, k, head, factor)
        vh = jnp.where(mine, v, jnp.zeros_like(v))
        out = out + jnp.dot(probs.astype(v.dtype), vh, preferred_element_type=jnp.float32)
    o_ref[...] = out.astype(o_ref.dtype)


def _bwd_kernel(factor, q_ref, k_ref, v_ref, d_ref, dq_ref, dk_ref, dv_ref):
    q = q_ref[...]
    k = k_ref[...]
    v = v_ref[...]
    d = d_ref[...]
    dq = jnp.zeros(dq_ref.shape, jnp.float32)
    dk = jnp.zeros(dk_ref.shape, jnp.float32)
    dv = jnp.zeros(dv_ref.shape, jnp.float32)
    for head in range(LANES // HEAD_DIM):
        mine, qh, probs = _probs(q, k, head, factor)
        dh = jnp.where(mine, d, jnp.zeros_like(d))
        kh = jnp.where(mine, k, jnp.zeros_like(k))
        dprobs = _nt(dh, v)
        dv = dv + _tn(probs.astype(d.dtype), dh)
        inner = jnp.sum(dprobs * probs, axis=-1, keepdims=True)
        dscores = (probs * (dprobs - inner)).astype(q.dtype)
        dq = dq + jnp.dot(dscores, kh, preferred_element_type=jnp.float32)
        dk = dk + _tn(dscores, qh)
    dq_ref[...] = (dq * factor).astype(dq_ref.dtype)
    dk_ref[...] = (dk * factor).astype(dk_ref.dtype)
    dv_ref[...] = dv.astype(dv_ref.dtype)


def _wgrad_kernel(expand_tiles, modb_ref, du_ref, act_ref, dz_ref, out_ref):
    j = pl.program_id(0)

    @pl.when(j < expand_tiles)
    def _():
        out_ref[...] = jnp.dot(
            modb_ref[...], du_ref[...], preferred_element_type=jnp.float32
        ).astype(out_ref.dtype)

    @pl.when(j >= expand_tiles)
    def _():
        out_ref[...] = jnp.dot(
            act_ref[...], dz_ref[...], preferred_element_type=jnp.float32
        ).astype(out_ref.dtype)


def ffn_weight_grads(mod_t, grad_exp, act_t, grad_branch, tile=1024):
    width, tokens = mod_t.shape
    ff = grad_exp.shape[1]
    expand_tiles = ff // tile
    per_part = width // tile
    tiles = expand_tiles + (ff // width) * per_part

    def act_index(j):
        return (jnp.maximum(j - expand_tiles, 0) // per_part, 0)

    def dz_index(j):
        return (0, jnp.maximum(j - expand_tiles, 0) % per_part)

    return pl.pallas_call(
        functools.partial(_wgrad_kernel, expand_tiles),
        out_shape=jax.ShapeDtypeStruct((width, tiles * tile), jnp.bfloat16),
        grid=(tiles,),
        in_specs=[
            pl.BlockSpec((width, tokens), lambda j: (0, 0)),
            pl.BlockSpec((tokens, tile), lambda j: (0, jnp.minimum(j, expand_tiles - 1))),
            pl.BlockSpec((width, tokens), act_index),
            pl.BlockSpec((tokens, tile), dz_index),
        ],
        out_specs=pl.BlockSpec((width, tile), lambda j: (0, j)),
        compiler_params=pltpu.CompilerParams(dimension_semantics=("arbitrary",)),
        cost_estimate=pl.CostEstimate(
            flops=2 * tokens * width * tiles * tile,
            transcendentals=0,
            bytes_accessed=2 * (tokens * (width + 2 * ff + width) + width * tiles * tile),
        ),
    )(mod_t, grad_exp, act_t, grad_branch)

def attention_forward(projected, images):
    tokens, three = projected.shape
    rows, width = tokens // images, three // 3
    pairs = width // LANES
    factor = HEAD_DIM ** (-0.5)

    def part(offset):
        return pl.BlockSpec((rows, LANES), lambda b, j: (b, offset + j))

    flops = 2 * 2 * images * (width // HEAD_DIM) * rows * rows * LANES
    return pl.pallas_call(
        functools.partial(_fwd_kernel, factor),
        out_shape=jax.ShapeDtypeStruct((tokens, width), projected.dtype),
        grid=(images, pairs),
        in_specs=[part(0), part(pairs), part(2 * pairs)],
        out_specs=pl.BlockSpec((rows, LANES), lambda b, j: (b, j)),
        compiler_params=pltpu.CompilerParams(dimension_semantics=("parallel", "parallel")),
        cost_estimate=pl.CostEstimate(
            flops=flops, transcendentals=images * (width // HEAD_DIM) * rows * rows,
            bytes_accessed=2 * tokens * (three + width),
        ),
    )(projected, projected, projected)


def attention_backward(projected, grad_attended, images):
    tokens, three = projected.shape
    rows, width = tokens // images, three // 3
    pairs = width // LANES
    factor = HEAD_DIM ** (-0.5)

    def part(offset):
        return pl.BlockSpec((rows, LANES), lambda b, j: (b, offset + j))

    out = jax.ShapeDtypeStruct((tokens, width), projected.dtype)
    flops = 5 * 2 * 2 * images * (width // HEAD_DIM) * rows * rows * LANES
    dq, dk, dv = pl.pallas_call(
        functools.partial(_bwd_kernel, factor),
        out_shape=(out, out, out),
        grid=(images, pairs),
        in_specs=[part(0), part(pairs), part(2 * pairs), part(0)],
        out_specs=[part(0)] * 3,
        compiler_params=pltpu.CompilerParams(dimension_semantics=("parallel", "parallel")),
        cost_estimate=pl.CostEstimate(
            flops=flops, transcendentals=images * (width // HEAD_DIM) * rows * rows,
            bytes_accessed=2 * tokens * (three + 4 * width),
        ),
    )(projected, projected, projected, grad_attended)
    return jnp.concatenate([dq, dk, dv], axis=1)


EPS = 1e-06
GELU_C = 0.7978845608028654

AXES = ("y", "zh", "x", "c", "zl")
DP = ("y", "zh", "x", "c")
STAGES = ("c", "x", "y", "zh", "zl")
STAGES_B = ("c", "y", "x", "zh", "zl")


def matmul(left, right):
    return jnp.dot(left, right, preferred_element_type=jnp.float32)


def left_trans(left, right):
    return lax.dot_general(
        left, right, (((0,), (0,)), ((), ())), preferred_element_type=jnp.float32
    )


def right_trans(left, right):
    return lax.dot_general(
        left, right, (((1,), (1,)), ((), ())), preferred_element_type=jnp.float32
    )


def normalize(values):
    centre = values - jnp.mean(values, axis=-1, keepdims=True)
    inverse = lax.rsqrt(jnp.mean(centre * centre, axis=-1, keepdims=True) + EPS)
    return (centre * inverse, inverse)


def norm_back(grad, normed, inverse):
    return inverse * (
        grad
        - jnp.mean(grad, axis=-1, keepdims=True)
        - normed * jnp.mean(grad * normed, axis=-1, keepdims=True)
    )


def stage_order(values, sizes, inner, stages=STAGES):
    lead = values.shape[:-1]
    shape = [sizes[a] for a in AXES]
    values = values.reshape(*lead, *shape, inner)
    n = len(lead)
    order = list(range(n)) + [n + AXES.index(a) for a in stages] + [n + len(AXES)]
    return jnp.transpose(values, order).reshape(*lead, -1)


def reduce_stages(packed, stages):
    for a in stages:
        packed = lax.psum_scatter(packed, a, scatter_dimension=0, tiled=True)
    return packed


def reduce_pair(packed, axis):
    half = packed.shape[0] // 2
    index = lax.axis_index(axis)
    keep = lax.dynamic_slice_in_dim(packed, index * half, half, axis=0)
    send = lax.dynamic_slice_in_dim(packed, (1 - index) * half, half, axis=0)
    got = lax.ppermute(send, axis, [(0, 1), (1, 0)])
    return (keep.astype(jnp.float32) + got.astype(jnp.float32)).astype(packed.dtype)


def reduce_rest(packed, axes):
    count = 1
    for a in axes:
        count *= lax.axis_size(a)
    chunks = packed.reshape(count, packed.shape[0] // count, packed.shape[1])
    chunks = lax.all_to_all(chunks, axes, 0, 0, tiled=False)
    return jnp.sum(chunks.astype(jnp.float32), axis=0)


def bias_columns(columns, rows):
    block = jnp.stack(columns, axis=1)
    return jnp.pad(block, ((0, 0), (0, 128 - block.shape[1]))).astype(jnp.bfloat16)


def gather_dp(values):
    count = 1
    for a in DP:
        count *= lax.axis_size(a)
    copies = jnp.broadcast_to(values[None], (count,) + values.shape)
    return lax.all_to_all(copies, DP, 0, 0, tiled=False).reshape(-1, values.shape[1])


def per_device(
    sizes,
    tokens,
    condition,
    occupied,
    modulation_weight,
    modulation_bias,
    input_weight,
    query_bias,
    value_bias,
    output_weight,
    output_bias,
    expand_weight,
    expand_bias,
    contract_weight,
    contract_bias,
    cotangent,
):
    images, rows, width = tokens.shape
    heads = width // HEAD_DIM
    flat = images * rows
    factor = HEAD_DIM ** (-0.5)
    cond_full = condition.astype(jnp.float32)
    sigmoid = jax.nn.sigmoid(cond_full)
    silu_b = (cond_full * sigmoid).astype(jnp.bfloat16)
    silu_pair = lax.all_gather(silu_b, "zl", axis=0, tiled=True)
    mod_cols = matmul(silu_pair, modulation_weight) + modulation_bias.reshape(1, -1)
    modulation = lax.all_to_all(mod_cols, "zl", split_axis=0, concat_axis=1, tiled=True).reshape(
        images, 6, 1, width
    )
    shift_a = modulation[:, 0]
    scale_a = modulation[:, 1]
    gate_a = modulation[:, 2]
    shift_b = modulation[:, 3]
    scale_b = modulation[:, 4]
    gate_b = modulation[:, 5]
    inputs = tokens.astype(jnp.float32)
    normed_a, inverse_a = normalize(inputs)
    mod_a = (normed_a * (1.0 + scale_a) + shift_a).astype(jnp.bfloat16).reshape(flat, width)
    qkv_bias = jnp.concatenate([query_bias, jnp.zeros_like(query_bias), value_bias])
    projected = (matmul(mod_a, input_weight) + qkv_bias).astype(jnp.bfloat16)
    attended_b = attention_forward(projected, images)
    branch_a = (matmul(attended_b, output_weight) + output_bias).reshape(images, rows, width)
    middle = inputs + gate_a * branch_a
    normed_b, inverse_b = normalize(middle)
    mod_b = (normed_b * (1.0 + scale_b) + shift_b).astype(jnp.bfloat16).reshape(flat, width)
    expanded = matmul(mod_b, expand_weight) + expand_bias
    tanh_part = jnp.tanh(GELU_C * (expanded + 0.044715 * expanded * expanded * expanded))
    activated_b = (0.5 * expanded * (1.0 + tanh_part)).astype(jnp.bfloat16)
    branch_b = (matmul(activated_b, contract_weight) + contract_bias).reshape(images, rows, width)
    alive = occupied.astype(jnp.float32)[:, None, None]
    layer_out = (middle + gate_b * branch_b) * alive
    grad_out = cotangent.astype(jnp.float32) * alive
    grad_gate_b = jnp.sum(grad_out * branch_b, axis=1)
    grad_branch_b = (grad_out * gate_b).astype(jnp.bfloat16).reshape(flat, width)
    blocks = 1
    for a in AXES:
        blocks *= sizes[a]
    ff = activated_b.shape[1]
    split = ff // width
    act_perm = stage_order(
        activated_b.reshape(flat, blocks, split, width // blocks)
        .transpose(0, 2, 1, 3)
        .reshape(flat, split, width),
        sizes,
        width // blocks,
    )
    contract_bias_grad = stage_order(
        jnp.sum(grad_branch_b.astype(jnp.float32), axis=0), sizes, width // blocks, STAGES_B
    )
    grad_act = right_trans(grad_branch_b, contract_weight)
    slope = 0.5 * (1.0 + tanh_part) + 0.5 * expanded * (1.0 - tanh_part * tanh_part) * GELU_C * (
        1.0 + 3.0 * 0.044715 * expanded * expanded
    )
    grad_exp_b = (grad_act * slope).astype(jnp.bfloat16)
    expand_bias_grad = stage_order(
        jnp.sum(grad_exp_b.astype(jnp.float32), axis=0)
        .reshape(blocks, split, width // blocks)
        .transpose(1, 0, 2)
        .reshape(split, width),
        sizes,
        width // blocks,
        STAGES_B,
    )
    packed_a = ffn_weight_grads(
        stage_order(mod_b, sizes, width // blocks).T, grad_exp_b, act_perm.reshape(flat, -1).T, grad_branch_b
    )
    packed_a, grad_exp_b = lax.optimization_barrier((packed_a, grad_exp_b))
    chain_a = reduce_stages(packed_a, STAGES[:1])
    grad_mod_b = right_trans(grad_exp_b, expand_weight).reshape(images, rows, width)
    grad_shift_b = jnp.sum(grad_mod_b, axis=1)
    grad_scale_b = jnp.sum(grad_mod_b * normed_b, axis=1)
    grad_middle = grad_out + norm_back(grad_mod_b * (1.0 + scale_b), normed_b, inverse_b)
    grad_gate_a = jnp.sum(grad_middle * branch_a, axis=1)
    grad_branch_a = (grad_middle * gate_a).astype(jnp.bfloat16).reshape(flat, width)
    output_grad = left_trans(stage_order(attended_b, sizes, width // blocks, STAGES_B), grad_branch_a).astype(
        jnp.bfloat16
    )
    output_bias_grad = stage_order(
        jnp.sum(grad_branch_a.astype(jnp.float32), axis=0), sizes, width // blocks, STAGES_B
    )
    grad_att_b = right_trans(grad_branch_a, output_weight).astype(jnp.bfloat16)
    chain_a, grad_att_b = lax.optimization_barrier((chain_a, grad_att_b))
    chain_a = reduce_stages(chain_a, STAGES[1:2])
    grad_proj_b = attention_backward(projected, grad_att_b, images)
    input_grad = left_trans(stage_order(mod_a, sizes, width // blocks, STAGES_B), grad_proj_b).astype(
        jnp.bfloat16
    )
    bias_sums = jnp.sum(grad_proj_b.astype(jnp.float32), axis=0)
    query_bias_grad = stage_order(bias_sums[:width], sizes, width // blocks, STAGES_B)
    value_bias_grad = stage_order(bias_sums[2 * width :], sizes, width // blocks, STAGES_B)
    chain_b = reduce_pair(
        jnp.concatenate(
            [
                input_grad,
                output_grad,
                bias_columns(
                [query_bias_grad, value_bias_grad, output_bias_grad, contract_bias_grad]
                + [expand_bias_grad[q] for q in range(split)],
                width,
            ),
            ],
            axis=1,
        ),
        STAGES_B[0],
    )
    chain_a, chain_b = lax.optimization_barrier((chain_a, chain_b))
    chain_b = reduce_stages(chain_b, STAGES_B[1:2])
    grad_mod_a = right_trans(grad_proj_b, input_weight).reshape(images, rows, width)
    grad_shift_a = jnp.sum(grad_mod_a, axis=1)
    grad_scale_a = jnp.sum(grad_mod_a * normed_a, axis=1)
    tokens_grad = grad_middle + norm_back(grad_mod_a * (1.0 + scale_a), normed_a, inverse_a)
    modulation_terms = jnp.stack(
        [grad_shift_a, grad_scale_a, grad_gate_a, grad_shift_b, grad_scale_b, grad_gate_b], axis=1
    ).reshape(images, 6 * width)
    modulation_own = modulation_terms.astype(jnp.bfloat16)
    modulation_cols = lax.all_to_all(modulation_own, "zl", split_axis=1, concat_axis=0, tiled=True)
    silu_terms = right_trans(modulation_cols, modulation_weight)
    pair_index = lax.axis_index("zl")
    own_rows = lax.dynamic_slice_in_dim(silu_terms, pair_index * images, images, axis=0)
    other_rows = lax.dynamic_slice_in_dim(silu_terms, (1 - pair_index) * images, images, axis=0)
    silu_sums = own_rows + lax.ppermute(other_rows, "zl", [(0, 1), (1, 0)])
    condition_grad = silu_sums * sigmoid * (1.0 + cond_full * (1.0 - sigmoid))
    dp_count = lax.axis_size(DP)
    row_block = width // dp_count
    silu_parts = silu_pair.reshape(-1, dp_count, row_block).transpose(1, 0, 2)
    silu_parts = jnp.pad(silu_parts, ((0, 0), (0, 0), (0, 128 - row_block)))
    payload = jnp.concatenate(
        [jnp.broadcast_to(modulation_cols[None], (dp_count,) + modulation_cols.shape), silu_parts], axis=2
    )
    factors = lax.all_to_all(payload, DP, 0, 0, tiled=False)
    mod_all = factors[:, :, : modulation_cols.shape[1]].reshape(-1, modulation_cols.shape[1])
    silu_rows = factors[:, :, modulation_cols.shape[1] : modulation_cols.shape[1] + row_block]
    silu_rows = silu_rows.reshape(-1, row_block)
    dp_index = lax.axis_index(DP)
    modulation_weight_grad = left_trans(silu_rows, mod_all)
    bias_all = jnp.sum(mod_all.astype(jnp.float32), axis=0).reshape(-1, width)
    modulation_bias_grad = lax.dynamic_slice_in_dim(bias_all, dp_index * row_block, row_block, axis=1)
    chain_a = reduce_rest(chain_a, STAGES[2:])
    chain_b, mod_all = lax.optimization_barrier((chain_b, mod_all))
    chain_b = reduce_rest(chain_b, STAGES_B[2:])
    three = input_weight.shape[1]
    fw = expand_weight.shape[1]
    input_weight_grad = chain_b[:, :three]
    output_weight_grad = chain_b[:, three : three + width]
    qb_grad = chain_b[:, three + width]
    vb_grad = chain_b[:, three + width + 1]
    ob_grad = chain_b[:, three + width + 2]
    expand_weight_grad = chain_a[:, :fw]
    contract_weight_grad = chain_a[:, fw : fw + split * width].reshape(-1, split, width)
    contract_weight_grad = contract_weight_grad.transpose(1, 0, 2).reshape(-1, width)
    cb_grad = chain_b[:, three + width + 3]
    eb_grad = chain_b[:, three + width + 4 : three + width + 4 + split].T.reshape(-1)
    summed = (
        input_weight_grad,
        qb_grad,
        vb_grad,
        output_weight_grad,
        ob_grad,
        expand_weight_grad,
        eb_grad,
        contract_weight_grad,
        cb_grad,
    )
    return (
        layer_out,
        tokens_grad,
        condition_grad,
        modulation_weight_grad,
        modulation_bias_grad,
        *summed,
    )


def solution(mesh):
    dp_size, mod_size = mesh.devices.shape
    rest = dp_size // 4
    side = int(round(rest ** 0.5))
    shape = (side, 2, rest // side, 2, mod_size)
    sizes = dict(zip(AXES, shape))
    physical = Mesh(np.asarray(mesh.devices).reshape(shape), AXES)
    ALL = AXES
    placed = (
        P(ALL, None, None),
        P(ALL, None),
        P(ALL),
        P(None, "zl"),
        P("zl", None),
        P(),
        P(),
        P(),
        P(),
        P(),
        P(),
        P(),
        P(),
        P(),
        P(ALL, None, None),
    )
    return jax.shard_map(
        functools.partial(per_device, sizes),
        mesh=physical,
        in_specs=placed,
        out_specs=(
            P(ALL, None, None),
            P(ALL, None, None),
            P(ALL, None),
            P(DP, "zl"),
            P("zl", DP),
            P(ALL, None),
            P(ALL),
            P(ALL),
            P(ALL, None),
            P(ALL),
            P(ALL, None),
            P(ALL),
            P(ALL, None),
            P(ALL),
        ),
        check_vma=False,
    )
```

```python
import functools

import jax
import jax.numpy as jnp
import numpy as np
from jax import lax
from jax.experimental import pallas as pl
from jax.experimental.pallas import tpu as pltpu
from jax.sharding import Mesh
from jax.sharding import PartitionSpec as P

HEAD_DIM = 64
LANES = 128


def _nt(a, b):
    return lax.dot_general(a, b, (((1,), (1,)), ((), ())), preferred_element_type=jnp.float32)


def _tn(a, b):
    return lax.dot_general(a, b, (((0,), (0,)), ((), ())), preferred_element_type=jnp.float32)


def _probs(q, k, head, factor):
    lane = lax.broadcasted_iota(jnp.int32, (1, LANES), 1)
    mine = (lane // HEAD_DIM) == head
    qh = jnp.where(mine, q, jnp.zeros_like(q))
    scores = _nt(qh, k) * factor
    weights = jnp.exp(scores - jnp.max(scores, axis=-1, keepdims=True))
    return mine, qh, weights / jnp.sum(weights, axis=-1, keepdims=True)


def _fwd_kernel(factor, q_ref, k_ref, v_ref, o_ref):
    q = q_ref[...]
    k = k_ref[...]
    v = v_ref[...]
    out = jnp.zeros(o_ref.shape, jnp.float32)
    for head in range(LANES // HEAD_DIM):
        mine, _, probs = _probs(q, k, head, factor)
        vh = jnp.where(mine, v, jnp.zeros_like(v))
        out = out + jnp.dot(probs.astype(v.dtype), vh, preferred_element_type=jnp.float32)
    o_ref[...] = out.astype(o_ref.dtype)


def _bwd_kernel(factor, q_ref, k_ref, v_ref, d_ref, dq_ref, dk_ref, dv_ref):
    q = q_ref[...]
    k = k_ref[...]
    v = v_ref[...]
    d = d_ref[...]
    dq = jnp.zeros(dq_ref.shape, jnp.float32)
    dk = jnp.zeros(dk_ref.shape, jnp.float32)
    dv = jnp.zeros(dv_ref.shape, jnp.float32)
    for head in range(LANES // HEAD_DIM):
        mine, qh, probs = _probs(q, k, head, factor)
        dh = jnp.where(mine, d, jnp.zeros_like(d))
        kh = jnp.where(mine, k, jnp.zeros_like(k))
        dprobs = _nt(dh, v)
        dv = dv + _tn(probs.astype(d.dtype), dh)
        inner = jnp.sum(dprobs * probs, axis=-1, keepdims=True)
        dscores = (probs * (dprobs - inner)).astype(q.dtype)
        dq = dq + jnp.dot(dscores, kh, preferred_element_type=jnp.float32)
        dk = dk + _tn(dscores, qh)
    dq_ref[...] = (dq * factor).astype(dq_ref.dtype)
    dk_ref[...] = (dk * factor).astype(dk_ref.dtype)
    dv_ref[...] = dv.astype(dv_ref.dtype)


def _wgrad_kernel(expand_tiles, modb_ref, du_ref, act_ref, dz_ref, out_ref):
    j = pl.program_id(0)

    @pl.when(j < expand_tiles)
    def _():
        out_ref[...] = jnp.dot(
            modb_ref[...], du_ref[...], preferred_element_type=jnp.float32
        ).astype(out_ref.dtype)

    @pl.when(j >= expand_tiles)
    def _():
        out_ref[...] = jnp.dot(
            act_ref[...], dz_ref[...], preferred_element_type=jnp.float32
        ).astype(out_ref.dtype)


def ffn_weight_grads(mod_t, grad_exp, act_t, grad_branch, tile=1024):
    width, tokens = mod_t.shape
    ff = grad_exp.shape[1]
    expand_tiles = ff // tile
    per_part = width // tile
    tiles = expand_tiles + (ff // width) * per_part

    def act_index(j):
        return (jnp.maximum(j - expand_tiles, 0) // per_part, 0)

    def dz_index(j):
        return (0, jnp.maximum(j - expand_tiles, 0) % per_part)

    return pl.pallas_call(
        functools.partial(_wgrad_kernel, expand_tiles),
        out_shape=jax.ShapeDtypeStruct((width, tiles * tile), jnp.bfloat16),
        grid=(tiles,),
        in_specs=[
            pl.BlockSpec((width, tokens), lambda j: (0, 0)),
            pl.BlockSpec((tokens, tile), lambda j: (0, jnp.minimum(j, expand_tiles - 1))),
            pl.BlockSpec((width, tokens), act_index),
            pl.BlockSpec((tokens, tile), dz_index),
        ],
        out_specs=pl.BlockSpec((width, tile), lambda j: (0, j)),
        compiler_params=pltpu.CompilerParams(dimension_semantics=("arbitrary",)),
        cost_estimate=pl.CostEstimate(
            flops=2 * tokens * width * tiles * tile,
            transcendentals=0,
            bytes_accessed=2 * (tokens * (width + 2 * ff + width) + width * tiles * tile),
        ),
    )(mod_t, grad_exp, act_t, grad_branch)

def attention_forward(projected, images):
    tokens, three = projected.shape
    rows, width = tokens // images, three // 3
    pairs = width // LANES
    factor = HEAD_DIM ** (-0.5)

    def part(offset):
        return pl.BlockSpec((rows, LANES), lambda b, j: (b, offset + j))

    flops = 2 * 2 * images * (width // HEAD_DIM) * rows * rows * LANES
    return pl.pallas_call(
        functools.partial(_fwd_kernel, factor),
        out_shape=jax.ShapeDtypeStruct((tokens, width), projected.dtype),
        grid=(images, pairs),
        in_specs=[part(0), part(pairs), part(2 * pairs)],
        out_specs=pl.BlockSpec((rows, LANES), lambda b, j: (b, j)),
        compiler_params=pltpu.CompilerParams(dimension_semantics=("parallel", "parallel")),
        cost_estimate=pl.CostEstimate(
            flops=flops, transcendentals=images * (width // HEAD_DIM) * rows * rows,
            bytes_accessed=2 * tokens * (three + width),
        ),
    )(projected, projected, projected)


def attention_backward(projected, grad_attended, images):
    tokens, three = projected.shape
    rows, width = tokens // images, three // 3
    pairs = width // LANES
    factor = HEAD_DIM ** (-0.5)

    def part(offset):
        return pl.BlockSpec((rows, LANES), lambda b, j: (b, offset + j))

    out = jax.ShapeDtypeStruct((tokens, width), projected.dtype)
    flops = 5 * 2 * 2 * images * (width // HEAD_DIM) * rows * rows * LANES
    dq, dk, dv = pl.pallas_call(
        functools.partial(_bwd_kernel, factor),
        out_shape=(out, out, out),
        grid=(images, pairs),
        in_specs=[part(0), part(pairs), part(2 * pairs), part(0)],
        out_specs=[part(0)] * 3,
        compiler_params=pltpu.CompilerParams(dimension_semantics=("parallel", "parallel")),
        cost_estimate=pl.CostEstimate(
            flops=flops, transcendentals=images * (width // HEAD_DIM) * rows * rows,
            bytes_accessed=2 * tokens * (three + 4 * width),
        ),
    )(projected, projected, projected, grad_attended)
    return jnp.concatenate([dq, dk, dv], axis=1)


EPS = 1e-06
GELU_C = 0.7978845608028654

AXES = ("y", "zh", "x", "c", "zl")
DP = ("y", "zh", "x", "c")
STAGES = ("c", "x", "y", "zh", "zl")
STAGES_B = ("c", "y", "x", "zh", "zl")


def matmul(left, right):
    return jnp.dot(left, right, preferred_element_type=jnp.float32)


def left_trans(left, right):
    return lax.dot_general(
        left, right, (((0,), (0,)), ((), ())), preferred_element_type=jnp.float32
    )


def right_trans(left, right):
    return lax.dot_general(
        left, right, (((1,), (1,)), ((), ())), preferred_element_type=jnp.float32
    )


def normalize(values):
    centre = values - jnp.mean(values, axis=-1, keepdims=True)
    inverse = lax.rsqrt(jnp.mean(centre * centre, axis=-1, keepdims=True) + EPS)
    return (centre * inverse, inverse)


def norm_back(grad, normed, inverse):
    return inverse * (
        grad
        - jnp.mean(grad, axis=-1, keepdims=True)
        - normed * jnp.mean(grad * normed, axis=-1, keepdims=True)
    )


def stage_order(values, sizes, inner, stages=STAGES):
    lead = values.shape[:-1]
    shape = [sizes[a] for a in AXES]
    values = values.reshape(*lead, *shape, inner)
    n = len(lead)
    order = list(range(n)) + [n + AXES.index(a) for a in stages] + [n + len(AXES)]
    return jnp.transpose(values, order).reshape(*lead, -1)


def reduce_stages(packed, stages):
    for a in stages:
        packed = lax.psum_scatter(packed, a, scatter_dimension=0, tiled=True)
    return packed


def reduce_pair(packed, axis):
    half = packed.shape[0] // 2
    index = lax.axis_index(axis)
    keep = lax.dynamic_slice_in_dim(packed, index * half, half, axis=0)
    send = lax.dynamic_slice_in_dim(packed, (1 - index) * half, half, axis=0)
    got = lax.ppermute(send, axis, [(0, 1), (1, 0)])
    return (keep.astype(jnp.float32) + got.astype(jnp.float32)).astype(packed.dtype)


def reduce_rest(packed, axes):
    count = 1
    for a in axes:
        count *= lax.axis_size(a)
    chunks = packed.reshape(count, packed.shape[0] // count, packed.shape[1])
    chunks = lax.all_to_all(chunks, axes, 0, 0, tiled=False)
    return jnp.sum(chunks.astype(jnp.float32), axis=0)


def bias_columns(columns, rows):
    block = jnp.stack(columns, axis=1)
    return jnp.pad(block, ((0, 0), (0, 128 - block.shape[1]))).astype(jnp.bfloat16)


def gather_dp(values):
    count = 1
    for a in DP:
        count *= lax.axis_size(a)
    copies = jnp.broadcast_to(values[None], (count,) + values.shape)
    return lax.all_to_all(copies, DP, 0, 0, tiled=False).reshape(-1, values.shape[1])


def per_device(
    sizes,
    tokens,
    condition,
    occupied,
    modulation_weight,
    modulation_bias,
    input_weight,
    query_bias,
    value_bias,
    output_weight,
    output_bias,
    expand_weight,
    expand_bias,
    contract_weight,
    contract_bias,
    cotangent,
):
    images, rows, width = tokens.shape
    heads = width // HEAD_DIM
    flat = images * rows
    factor = HEAD_DIM ** (-0.5)
    cond_full = condition.astype(jnp.float32)
    sigmoid = jax.nn.sigmoid(cond_full)
    silu_b = (cond_full * sigmoid).astype(jnp.bfloat16)
    silu_pair = lax.all_gather(silu_b, "zl", axis=0, tiled=True)
    mod_cols = matmul(silu_pair, modulation_weight) + modulation_bias.reshape(1, -1)
    modulation = lax.all_to_all(mod_cols, "zl", split_axis=0, concat_axis=1, tiled=True).reshape(
        images, 6, 1, width
    )
    shift_a = modulation[:, 0]
    scale_a = modulation[:, 1]
    gate_a = modulation[:, 2]
    shift_b = modulation[:, 3]
    scale_b = modulation[:, 4]
    gate_b = modulation[:, 5]
    inputs = tokens.astype(jnp.float32)
    normed_a, inverse_a = normalize(inputs)
    mod_a = (normed_a * (1.0 + scale_a) + shift_a).astype(jnp.bfloat16).reshape(flat, width)
    qkv_bias = jnp.concatenate([query_bias, jnp.zeros_like(query_bias), value_bias])
    projected = (matmul(mod_a, input_weight) + qkv_bias).astype(jnp.bfloat16)
    attended_b = attention_forward(projected, images)
    branch_a = (matmul(attended_b, output_weight) + output_bias).reshape(images, rows, width)
    middle = inputs + gate_a * branch_a
    normed_b, inverse_b = normalize(middle)
    mod_b = (normed_b * (1.0 + scale_b) + shift_b).astype(jnp.bfloat16).reshape(flat, width)
    expanded = matmul(mod_b, expand_weight) + expand_bias
    tanh_part = jnp.tanh(GELU_C * (expanded + 0.044715 * expanded * expanded * expanded))
    activated_b = (0.5 * expanded * (1.0 + tanh_part)).astype(jnp.bfloat16)
    branch_b = (matmul(activated_b, contract_weight) + contract_bias).reshape(images, rows, width)
    alive = occupied.astype(jnp.float32)[:, None, None]
    layer_out = (middle + gate_b * branch_b) * alive
    grad_out = cotangent.astype(jnp.float32) * alive
    grad_gate_b = jnp.sum(grad_out * branch_b, axis=1)
    grad_branch_b = (grad_out * gate_b).astype(jnp.bfloat16).reshape(flat, width)
    blocks = 1
    for a in AXES:
        blocks *= sizes[a]
    ff = activated_b.shape[1]
    split = ff // width
    act_perm = stage_order(
        activated_b.reshape(flat, blocks, split, width // blocks)
        .transpose(0, 2, 1, 3)
        .reshape(flat, split, width),
        sizes,
        width // blocks,
    )
    contract_bias_grad = stage_order(
        jnp.sum(grad_branch_b.astype(jnp.float32), axis=0), sizes, width // blocks, STAGES_B
    )
    grad_act = right_trans(grad_branch_b, contract_weight)
    slope = 0.5 * (1.0 + tanh_part) + 0.5 * expanded * (1.0 - tanh_part * tanh_part) * GELU_C * (
        1.0 + 3.0 * 0.044715 * expanded * expanded
    )
    grad_exp_b = (grad_act * slope).astype(jnp.bfloat16)
    expand_bias_grad = stage_order(
        jnp.sum(grad_exp_b.astype(jnp.float32), axis=0)
        .reshape(blocks, split, width // blocks)
        .transpose(1, 0, 2)
        .reshape(split, width),
        sizes,
        width // blocks,
        STAGES_B,
    )
    packed_a = ffn_weight_grads(
        stage_order(mod_b, sizes, width // blocks).T, grad_exp_b, act_perm.reshape(flat, -1).T, grad_branch_b
    )
    packed_a, grad_exp_b = lax.optimization_barrier((packed_a, grad_exp_b))
    chain_a = reduce_stages(packed_a, STAGES[:1])
    grad_mod_b = right_trans(grad_exp_b, expand_weight).reshape(images, rows, width)
    grad_shift_b = jnp.sum(grad_mod_b, axis=1)
    grad_scale_b = jnp.sum(grad_mod_b * normed_b, axis=1)
    grad_middle = grad_out + norm_back(grad_mod_b * (1.0 + scale_b), normed_b, inverse_b)
    grad_gate_a = jnp.sum(grad_middle * branch_a, axis=1)
    grad_branch_a = (grad_middle * gate_a).astype(jnp.bfloat16).reshape(flat, width)
    output_grad = left_trans(stage_order(attended_b, sizes, width // blocks, STAGES_B), grad_branch_a).astype(
        jnp.bfloat16
    )
    output_bias_grad = stage_order(
        jnp.sum(grad_branch_a.astype(jnp.float32), axis=0), sizes, width // blocks, STAGES_B
    )
    grad_att_b = right_trans(grad_branch_a, output_weight).astype(jnp.bfloat16)
    chain_a, grad_att_b = lax.optimization_barrier((chain_a, grad_att_b))
    chain_a = reduce_stages(chain_a, STAGES[1:2])
    grad_proj_b = attention_backward(projected, grad_att_b, images)
    input_grad = left_trans(stage_order(mod_a, sizes, width // blocks, STAGES_B), grad_proj_b).astype(
        jnp.bfloat16
    )
    bias_sums = jnp.sum(grad_proj_b.astype(jnp.float32), axis=0)
    query_bias_grad = stage_order(bias_sums[:width], sizes, width // blocks, STAGES_B)
    value_bias_grad = stage_order(bias_sums[2 * width :], sizes, width // blocks, STAGES_B)
    chain_b = reduce_pair(
        jnp.concatenate(
            [
                input_grad,
                output_grad,
                bias_columns(
                [query_bias_grad, value_bias_grad, output_bias_grad, contract_bias_grad]
                + [expand_bias_grad[q] for q in range(split)],
                width,
            ),
            ],
            axis=1,
        ),
        STAGES_B[0],
    )
    chain_a, chain_b = lax.optimization_barrier((chain_a, chain_b))
    chain_b = reduce_stages(chain_b, STAGES_B[1:2])
    chain_a = reduce_rest(chain_a, STAGES[2:])
    grad_mod_a = right_trans(grad_proj_b, input_weight).reshape(images, rows, width)
    grad_shift_a = jnp.sum(grad_mod_a, axis=1)
    grad_scale_a = jnp.sum(grad_mod_a * normed_a, axis=1)
    tokens_grad = grad_middle + norm_back(grad_mod_a * (1.0 + scale_a), normed_a, inverse_a)
    modulation_terms = jnp.stack(
        [grad_shift_a, grad_scale_a, grad_gate_a, grad_shift_b, grad_scale_b, grad_gate_b], axis=1
    ).reshape(images, 6 * width)
    modulation_own = modulation_terms.astype(jnp.bfloat16)
    chain_a, modulation_own = lax.optimization_barrier((chain_a, modulation_own))
    modulation_cols = lax.all_to_all(modulation_own, "zl", split_axis=1, concat_axis=0, tiled=True)
    silu_terms = right_trans(modulation_cols, modulation_weight)
    pair_index = lax.axis_index("zl")
    own_rows = lax.dynamic_slice_in_dim(silu_terms, pair_index * images, images, axis=0)
    other_rows = lax.dynamic_slice_in_dim(silu_terms, (1 - pair_index) * images, images, axis=0)
    silu_sums = own_rows + lax.ppermute(other_rows, "zl", [(0, 1), (1, 0)])
    condition_grad = silu_sums * sigmoid * (1.0 + cond_full * (1.0 - sigmoid))
    dp_count = lax.axis_size(DP)
    row_block = width // dp_count
    silu_parts = silu_pair.reshape(-1, dp_count, row_block).transpose(1, 0, 2)
    silu_parts = jnp.pad(silu_parts, ((0, 0), (0, 0), (0, 128 - row_block)))
    payload = jnp.concatenate(
        [jnp.broadcast_to(modulation_cols[None], (dp_count,) + modulation_cols.shape), silu_parts], axis=2
    )
    factors = lax.all_to_all(payload, DP, 0, 0, tiled=False)
    mod_all = factors[:, :, : modulation_cols.shape[1]].reshape(-1, modulation_cols.shape[1])
    silu_rows = factors[:, :, modulation_cols.shape[1] : modulation_cols.shape[1] + row_block]
    silu_rows = silu_rows.reshape(-1, row_block)
    dp_index = lax.axis_index(DP)
    modulation_weight_grad = left_trans(silu_rows, mod_all)
    bias_all = jnp.sum(mod_all.astype(jnp.float32), axis=0).reshape(-1, width)
    modulation_bias_grad = lax.dynamic_slice_in_dim(bias_all, dp_index * row_block, row_block, axis=1)
    chain_b, mod_all = lax.optimization_barrier((chain_b, mod_all))
    chain_b = reduce_rest(chain_b, STAGES_B[2:])
    three = input_weight.shape[1]
    fw = expand_weight.shape[1]
    input_weight_grad = chain_b[:, :three]
    output_weight_grad = chain_b[:, three : three + width]
    qb_grad = chain_b[:, three + width]
    vb_grad = chain_b[:, three + width + 1]
    ob_grad = chain_b[:, three + width + 2]
    expand_weight_grad = chain_a[:, :fw]
    contract_weight_grad = chain_a[:, fw : fw + split * width].reshape(-1, split, width)
    contract_weight_grad = contract_weight_grad.transpose(1, 0, 2).reshape(-1, width)
    cb_grad = chain_b[:, three + width + 3]
    eb_grad = chain_b[:, three + width + 4 : three + width + 4 + split].T.reshape(-1)
    summed = (
        input_weight_grad,
        qb_grad,
        vb_grad,
        output_weight_grad,
        ob_grad,
        expand_weight_grad,
        eb_grad,
        contract_weight_grad,
        cb_grad,
    )
    return (
        layer_out,
        tokens_grad,
        condition_grad,
        modulation_weight_grad,
        modulation_bias_grad,
        *summed,
    )


def solution(mesh):
    dp_size, mod_size = mesh.devices.shape
    rest = dp_size // 4
    side = int(round(rest ** 0.5))
    shape = (side, 2, rest // side, 2, mod_size)
    sizes = dict(zip(AXES, shape))
    physical = Mesh(np.asarray(mesh.devices).reshape(shape), AXES)
    ALL = AXES
    placed = (
        P(ALL, None, None),
        P(ALL, None),
        P(ALL),
        P(None, "zl"),
        P("zl", None),
        P(),
        P(),
        P(),
        P(),
        P(),
        P(),
        P(),
        P(),
        P(),
        P(ALL, None, None),
    )
    return jax.shard_map(
        functools.partial(per_device, sizes),
        mesh=physical,
        in_specs=placed,
        out_specs=(
            P(ALL, None, None),
            P(ALL, None, None),
            P(ALL, None),
            P(DP, "zl"),
            P("zl", DP),
            P(ALL, None),
            P(ALL),
            P(ALL),
            P(ALL, None),
            P(ALL),
            P(ALL, None),
            P(ALL),
            P(ALL, None),
            P(ALL),
        ),
        check_vma=False,
    )
```

```python
import functools

import jax
import jax.numpy as jnp
import numpy as np
from jax import lax
from jax.experimental import pallas as pl
from jax.experimental.pallas import tpu as pltpu
from jax.sharding import Mesh
from jax.sharding import PartitionSpec as P

HEAD_DIM = 64
LANES = 128


def _nt(a, b):
    return lax.dot_general(a, b, (((1,), (1,)), ((), ())), preferred_element_type=jnp.float32)


def _tn(a, b):
    return lax.dot_general(a, b, (((0,), (0,)), ((), ())), preferred_element_type=jnp.float32)


def _probs(q, k, head, factor):
    lane = lax.broadcasted_iota(jnp.int32, (1, LANES), 1)
    mine = (lane // HEAD_DIM) == head
    qh = jnp.where(mine, q, jnp.zeros_like(q))
    scores = _nt(qh, k) * factor
    weights = jnp.exp(scores - jnp.max(scores, axis=-1, keepdims=True))
    return mine, qh, weights / jnp.sum(weights, axis=-1, keepdims=True)


def _fwd_kernel(factor, q_ref, k_ref, v_ref, o_ref):
    q = q_ref[...]
    k = k_ref[...]
    v = v_ref[...]
    out = jnp.zeros(o_ref.shape, jnp.float32)
    for head in range(LANES // HEAD_DIM):
        mine, _, probs = _probs(q, k, head, factor)
        vh = jnp.where(mine, v, jnp.zeros_like(v))
        out = out + jnp.dot(probs.astype(v.dtype), vh, preferred_element_type=jnp.float32)
    o_ref[...] = out.astype(o_ref.dtype)


def _bwd_kernel(factor, q_ref, k_ref, v_ref, d_ref, dq_ref, dk_ref, dv_ref):
    q = q_ref[...]
    k = k_ref[...]
    v = v_ref[...]
    d = d_ref[...]
    dq = jnp.zeros(dq_ref.shape, jnp.float32)
    dk = jnp.zeros(dk_ref.shape, jnp.float32)
    dv = jnp.zeros(dv_ref.shape, jnp.float32)
    for head in range(LANES // HEAD_DIM):
        mine, qh, probs = _probs(q, k, head, factor)
        dh = jnp.where(mine, d, jnp.zeros_like(d))
        kh = jnp.where(mine, k, jnp.zeros_like(k))
        dprobs = _nt(dh, v)
        dv = dv + _tn(probs.astype(d.dtype), dh)
        inner = jnp.sum(dprobs * probs, axis=-1, keepdims=True)
        dscores = (probs * (dprobs - inner)).astype(q.dtype)
        dq = dq + jnp.dot(dscores, kh, preferred_element_type=jnp.float32)
        dk = dk + _tn(dscores, qh)
    dq_ref[...] = (dq * factor).astype(dq_ref.dtype)
    dk_ref[...] = (dk * factor).astype(dk_ref.dtype)
    dv_ref[...] = dv.astype(dv_ref.dtype)


def _wgrad_kernel(expand_tiles, modb_ref, du_ref, act_ref, dz_ref, out_ref):
    j = pl.program_id(0)

    @pl.when(j < expand_tiles)
    def _():
        out_ref[...] = jnp.dot(
            modb_ref[...], du_ref[...], preferred_element_type=jnp.float32
        ).astype(out_ref.dtype)

    @pl.when(j >= expand_tiles)
    def _():
        out_ref[...] = jnp.dot(
            act_ref[...], dz_ref[...], preferred_element_type=jnp.float32
        ).astype(out_ref.dtype)


def ffn_weight_grads(mod_t, grad_exp, act_t, grad_branch, tile=1024):
    width, tokens = mod_t.shape
    ff = grad_exp.shape[1]
    expand_tiles = ff // tile
    per_part = width // tile
    tiles = expand_tiles + (ff // width) * per_part

    def act_index(j):
        return (jnp.maximum(j - expand_tiles, 0) // per_part, 0)

    def dz_index(j):
        return (0, jnp.maximum(j - expand_tiles, 0) % per_part)

    return pl.pallas_call(
        functools.partial(_wgrad_kernel, expand_tiles),
        out_shape=jax.ShapeDtypeStruct((width, tiles * tile), jnp.bfloat16),
        grid=(tiles,),
        in_specs=[
            pl.BlockSpec((width, tokens), lambda j: (0, 0)),
            pl.BlockSpec((tokens, tile), lambda j: (0, jnp.minimum(j, expand_tiles - 1))),
            pl.BlockSpec((width, tokens), act_index),
            pl.BlockSpec((tokens, tile), dz_index),
        ],
        out_specs=pl.BlockSpec((width, tile), lambda j: (0, j)),
        compiler_params=pltpu.CompilerParams(dimension_semantics=("arbitrary",)),
        cost_estimate=pl.CostEstimate(
            flops=2 * tokens * width * tiles * tile,
            transcendentals=0,
            bytes_accessed=2 * (tokens * (width + 2 * ff + width) + width * tiles * tile),
        ),
    )(mod_t, grad_exp, act_t, grad_branch)

def attention_forward(projected, images):
    tokens, three = projected.shape
    rows, width = tokens // images, three // 3
    pairs = width // LANES
    factor = HEAD_DIM ** (-0.5)

    def part(offset):
        return pl.BlockSpec((rows, LANES), lambda b, j: (b, offset + j))

    flops = 2 * 2 * images * (width // HEAD_DIM) * rows * rows * LANES
    return pl.pallas_call(
        functools.partial(_fwd_kernel, factor),
        out_shape=jax.ShapeDtypeStruct((tokens, width), projected.dtype),
        grid=(images, pairs),
        in_specs=[part(0), part(pairs), part(2 * pairs)],
        out_specs=pl.BlockSpec((rows, LANES), lambda b, j: (b, j)),
        compiler_params=pltpu.CompilerParams(dimension_semantics=("parallel", "parallel")),
        cost_estimate=pl.CostEstimate(
            flops=flops, transcendentals=images * (width // HEAD_DIM) * rows * rows,
            bytes_accessed=2 * tokens * (three + width),
        ),
    )(projected, projected, projected)


def attention_backward(projected, grad_attended, images):
    tokens, three = projected.shape
    rows, width = tokens // images, three // 3
    pairs = width // LANES
    factor = HEAD_DIM ** (-0.5)

    def part(offset):
        return pl.BlockSpec((rows, LANES), lambda b, j: (b, offset + j))

    out = jax.ShapeDtypeStruct((tokens, width), projected.dtype)
    flops = 5 * 2 * 2 * images * (width // HEAD_DIM) * rows * rows * LANES
    dq, dk, dv = pl.pallas_call(
        functools.partial(_bwd_kernel, factor),
        out_shape=(out, out, out),
        grid=(images, pairs),
        in_specs=[part(0), part(pairs), part(2 * pairs), part(0)],
        out_specs=[part(0)] * 3,
        compiler_params=pltpu.CompilerParams(dimension_semantics=("parallel", "parallel")),
        cost_estimate=pl.CostEstimate(
            flops=flops, transcendentals=images * (width // HEAD_DIM) * rows * rows,
            bytes_accessed=2 * tokens * (three + 4 * width),
        ),
    )(projected, projected, projected, grad_attended)
    return jnp.concatenate([dq, dk, dv], axis=1)


EPS = 1e-06
GELU_C = 0.7978845608028654

AXES = ("y", "zh", "x", "c", "zl")
DP = ("y", "zh", "x", "c")
STAGES = ("c", "x", "y", "zh", "zl")
STAGES_B = STAGES


def matmul(left, right):
    return jnp.dot(left, right, preferred_element_type=jnp.float32)


def left_trans(left, right):
    return lax.dot_general(
        left, right, (((0,), (0,)), ((), ())), preferred_element_type=jnp.float32
    )


def right_trans(left, right):
    return lax.dot_general(
        left, right, (((1,), (1,)), ((), ())), preferred_element_type=jnp.float32
    )


def normalize(values):
    centre = values - jnp.mean(values, axis=-1, keepdims=True)
    inverse = lax.rsqrt(jnp.mean(centre * centre, axis=-1, keepdims=True) + EPS)
    return (centre * inverse, inverse)


def norm_back(grad, normed, inverse):
    return inverse * (
        grad
        - jnp.mean(grad, axis=-1, keepdims=True)
        - normed * jnp.mean(grad * normed, axis=-1, keepdims=True)
    )


def stage_order(values, sizes, inner, stages=STAGES):
    lead = values.shape[:-1]
    shape = [sizes[a] for a in AXES]
    values = values.reshape(*lead, *shape, inner)
    n = len(lead)
    order = list(range(n)) + [n + AXES.index(a) for a in stages] + [n + len(AXES)]
    return jnp.transpose(values, order).reshape(*lead, -1)


def reduce_stages(packed, stages):
    for a in stages:
        packed = lax.psum_scatter(packed, a, scatter_dimension=0, tiled=True)
    return packed


def reduce_pair(packed, axis):
    half = packed.shape[0] // 2
    index = lax.axis_index(axis)
    keep = lax.dynamic_slice_in_dim(packed, index * half, half, axis=0)
    send = lax.dynamic_slice_in_dim(packed, (1 - index) * half, half, axis=0)
    got = lax.ppermute(send, axis, [(0, 1), (1, 0)])
    return (keep.astype(jnp.float32) + got.astype(jnp.float32)).astype(packed.dtype)


def reduce_rest(packed, axes):
    count = 1
    for a in axes:
        count *= lax.axis_size(a)
    chunks = packed.reshape(count, packed.shape[0] // count, packed.shape[1])
    chunks = lax.all_to_all(chunks, axes, 0, 0, tiled=False)
    return jnp.sum(chunks.astype(jnp.float32), axis=0)


def bias_columns(columns, rows):
    block = jnp.stack(columns, axis=1)
    return jnp.pad(block, ((0, 0), (0, 128 - block.shape[1]))).astype(jnp.bfloat16)


def gather_dp(values):
    count = 1
    for a in DP:
        count *= lax.axis_size(a)
    copies = jnp.broadcast_to(values[None], (count,) + values.shape)
    return lax.all_to_all(copies, DP, 0, 0, tiled=False).reshape(-1, values.shape[1])


def per_device(
    sizes,
    tokens,
    condition,
    occupied,
    modulation_weight,
    modulation_bias,
    input_weight,
    query_bias,
    value_bias,
    output_weight,
    output_bias,
    expand_weight,
    expand_bias,
    contract_weight,
    contract_bias,
    cotangent,
):
    images, rows, width = tokens.shape
    heads = width // HEAD_DIM
    flat = images * rows
    factor = HEAD_DIM ** (-0.5)
    cond_full = condition.astype(jnp.float32)
    sigmoid = jax.nn.sigmoid(cond_full)
    silu_b = (cond_full * sigmoid).astype(jnp.bfloat16)
    silu_pair = lax.all_gather(silu_b, "zl", axis=0, tiled=True)
    mod_cols = matmul(silu_pair, modulation_weight) + modulation_bias.reshape(1, -1)
    modulation = lax.all_to_all(mod_cols, "zl", split_axis=0, concat_axis=1, tiled=True).reshape(
        images, 6, 1, width
    )
    shift_a = modulation[:, 0]
    scale_a = modulation[:, 1]
    gate_a = modulation[:, 2]
    shift_b = modulation[:, 3]
    scale_b = modulation[:, 4]
    gate_b = modulation[:, 5]
    inputs = tokens.astype(jnp.float32)
    normed_a, inverse_a = normalize(inputs)
    mod_a = (normed_a * (1.0 + scale_a) + shift_a).astype(jnp.bfloat16).reshape(flat, width)
    qkv_bias = jnp.concatenate([query_bias, jnp.zeros_like(query_bias), value_bias])
    projected = (matmul(mod_a, input_weight) + qkv_bias).astype(jnp.bfloat16)
    attended_b = attention_forward(projected, images)
    branch_a = (matmul(attended_b, output_weight) + output_bias).reshape(images, rows, width)
    middle = inputs + gate_a * branch_a
    normed_b, inverse_b = normalize(middle)
    mod_b = (normed_b * (1.0 + scale_b) + shift_b).astype(jnp.bfloat16).reshape(flat, width)
    expanded = matmul(mod_b, expand_weight) + expand_bias
    tanh_part = jnp.tanh(GELU_C * (expanded + 0.044715 * expanded * expanded * expanded))
    activated_b = (0.5 * expanded * (1.0 + tanh_part)).astype(jnp.bfloat16)
    branch_b = (matmul(activated_b, contract_weight) + contract_bias).reshape(images, rows, width)
    alive = occupied.astype(jnp.float32)[:, None, None]
    layer_out = (middle + gate_b * branch_b) * alive
    grad_out = cotangent.astype(jnp.float32) * alive
    grad_gate_b = jnp.sum(grad_out * branch_b, axis=1)
    grad_branch_b = (grad_out * gate_b).astype(jnp.bfloat16).reshape(flat, width)
    blocks = 1
    for a in AXES:
        blocks *= sizes[a]
    ff = activated_b.shape[1]
    split = ff // width
    act_perm = stage_order(
        activated_b.reshape(flat, blocks, split, width // blocks)
        .transpose(0, 2, 1, 3)
        .reshape(flat, split, width),
        sizes,
        width // blocks,
    )
    contract_bias_grad = stage_order(
        jnp.sum(grad_branch_b.astype(jnp.float32), axis=0), sizes, width // blocks, STAGES_B
    )
    grad_act = right_trans(grad_branch_b, contract_weight)
    slope = 0.5 * (1.0 + tanh_part) + 0.5 * expanded * (1.0 - tanh_part * tanh_part) * GELU_C * (
        1.0 + 3.0 * 0.044715 * expanded * expanded
    )
    grad_exp_b = (grad_act * slope).astype(jnp.bfloat16)
    expand_bias_grad = stage_order(
        jnp.sum(grad_exp_b.astype(jnp.float32), axis=0)
        .reshape(blocks, split, width // blocks)
        .transpose(1, 0, 2)
        .reshape(split, width),
        sizes,
        width // blocks,
        STAGES_B,
    )
    packed_a = ffn_weight_grads(
        stage_order(mod_b, sizes, width // blocks).T, grad_exp_b, act_perm.reshape(flat, -1).T, grad_branch_b
    )
    packed_a, grad_exp_b = lax.optimization_barrier((packed_a, grad_exp_b))
    chain_a = reduce_stages(packed_a, STAGES[:1])
    grad_mod_b = right_trans(grad_exp_b, expand_weight).reshape(images, rows, width)
    grad_shift_b = jnp.sum(grad_mod_b, axis=1)
    grad_scale_b = jnp.sum(grad_mod_b * normed_b, axis=1)
    grad_middle = grad_out + norm_back(grad_mod_b * (1.0 + scale_b), normed_b, inverse_b)
    grad_gate_a = jnp.sum(grad_middle * branch_a, axis=1)
    grad_branch_a = (grad_middle * gate_a).astype(jnp.bfloat16).reshape(flat, width)
    output_grad = left_trans(stage_order(attended_b, sizes, width // blocks, STAGES_B), grad_branch_a).astype(
        jnp.bfloat16
    )
    output_bias_grad = stage_order(
        jnp.sum(grad_branch_a.astype(jnp.float32), axis=0), sizes, width // blocks, STAGES_B
    )
    grad_att_b = right_trans(grad_branch_a, output_weight).astype(jnp.bfloat16)
    chain_a, grad_att_b = lax.optimization_barrier((chain_a, grad_att_b))
    chain_a = reduce_stages(chain_a, STAGES[1:2])
    grad_proj_b = attention_backward(projected, grad_att_b, images)
    input_grad = left_trans(stage_order(mod_a, sizes, width // blocks, STAGES_B), grad_proj_b).astype(
        jnp.bfloat16
    )
    bias_sums = jnp.sum(grad_proj_b.astype(jnp.float32), axis=0)
    query_bias_grad = stage_order(bias_sums[:width], sizes, width // blocks, STAGES_B)
    value_bias_grad = stage_order(bias_sums[2 * width :], sizes, width // blocks, STAGES_B)
    chain_b = reduce_pair(
        jnp.concatenate(
            [
                input_grad,
                output_grad,
                bias_columns(
                [query_bias_grad, value_bias_grad, output_bias_grad, contract_bias_grad]
                + [expand_bias_grad[q] for q in range(split)],
                width,
            ),
            ],
            axis=1,
        ),
        STAGES_B[0],
    )
    chain_a, chain_b = lax.optimization_barrier((chain_a, chain_b))
    chain_b = reduce_stages(chain_b, STAGES_B[1:2])
    grad_mod_a = right_trans(grad_proj_b, input_weight).reshape(images, rows, width)
    grad_shift_a = jnp.sum(grad_mod_a, axis=1)
    grad_scale_a = jnp.sum(grad_mod_a * normed_a, axis=1)
    tokens_grad = grad_middle + norm_back(grad_mod_a * (1.0 + scale_a), normed_a, inverse_a)
    modulation_terms = jnp.stack(
        [grad_shift_a, grad_scale_a, grad_gate_a, grad_shift_b, grad_scale_b, grad_gate_b], axis=1
    ).reshape(images, 6 * width)
    modulation_own = modulation_terms.astype(jnp.bfloat16)
    modulation_cols = lax.all_to_all(modulation_own, "zl", split_axis=1, concat_axis=0, tiled=True)
    silu_terms = right_trans(modulation_cols, modulation_weight)
    pair_index = lax.axis_index("zl")
    own_rows = lax.dynamic_slice_in_dim(silu_terms, pair_index * images, images, axis=0)
    other_rows = lax.dynamic_slice_in_dim(silu_terms, (1 - pair_index) * images, images, axis=0)
    silu_sums = own_rows + lax.ppermute(other_rows, "zl", [(0, 1), (1, 0)])
    condition_grad = silu_sums * sigmoid * (1.0 + cond_full * (1.0 - sigmoid))
    dp_count = lax.axis_size(DP)
    row_block = width // dp_count
    silu_parts = silu_pair.reshape(-1, dp_count, row_block).transpose(1, 0, 2)
    silu_parts = jnp.pad(silu_parts, ((0, 0), (0, 0), (0, 128 - row_block)))
    payload = jnp.concatenate(
        [jnp.broadcast_to(modulation_cols[None], (dp_count,) + modulation_cols.shape), silu_parts], axis=2
    )
    factors = lax.all_to_all(payload, DP, 0, 0, tiled=False)
    mod_all = factors[:, :, : modulation_cols.shape[1]].reshape(-1, modulation_cols.shape[1])
    silu_rows = factors[:, :, modulation_cols.shape[1] : modulation_cols.shape[1] + row_block]
    silu_rows = silu_rows.reshape(-1, row_block)
    dp_index = lax.axis_index(DP)
    modulation_weight_grad = left_trans(silu_rows, mod_all)
    bias_all = jnp.sum(mod_all.astype(jnp.float32), axis=0).reshape(-1, width)
    modulation_bias_grad = lax.dynamic_slice_in_dim(bias_all, dp_index * row_block, row_block, axis=1)
    chain_b, mod_all = lax.optimization_barrier((chain_b, mod_all))
    rest = reduce_rest(jnp.concatenate([chain_a, chain_b], axis=1), STAGES[2:])
    chain_a = rest[:, : chain_a.shape[1]]
    chain_b = rest[:, chain_a.shape[1] :]
    three = input_weight.shape[1]
    fw = expand_weight.shape[1]
    input_weight_grad = chain_b[:, :three]
    output_weight_grad = chain_b[:, three : three + width]
    qb_grad = chain_b[:, three + width]
    vb_grad = chain_b[:, three + width + 1]
    ob_grad = chain_b[:, three + width + 2]
    expand_weight_grad = chain_a[:, :fw]
    contract_weight_grad = chain_a[:, fw : fw + split * width].reshape(-1, split, width)
    contract_weight_grad = contract_weight_grad.transpose(1, 0, 2).reshape(-1, width)
    cb_grad = chain_b[:, three + width + 3]
    eb_grad = chain_b[:, three + width + 4 : three + width + 4 + split].T.reshape(-1)
    summed = (
        input_weight_grad,
        qb_grad,
        vb_grad,
        output_weight_grad,
        ob_grad,
        expand_weight_grad,
        eb_grad,
        contract_weight_grad,
        cb_grad,
    )
    return (
        layer_out,
        tokens_grad,
        condition_grad,
        modulation_weight_grad,
        modulation_bias_grad,
        *summed,
    )


def solution(mesh):
    dp_size, mod_size = mesh.devices.shape
    rest = dp_size // 4
    side = int(round(rest ** 0.5))
    shape = (side, 2, rest // side, 2, mod_size)
    sizes = dict(zip(AXES, shape))
    physical = Mesh(np.asarray(mesh.devices).reshape(shape), AXES)
    ALL = AXES
    placed = (
        P(ALL, None, None),
        P(ALL, None),
        P(ALL),
        P(None, "zl"),
        P("zl", None),
        P(),
        P(),
        P(),
        P(),
        P(),
        P(),
        P(),
        P(),
        P(),
        P(ALL, None, None),
    )
    return jax.shard_map(
        functools.partial(per_device, sizes),
        mesh=physical,
        in_specs=placed,
        out_specs=(
            P(ALL, None, None),
            P(ALL, None, None),
            P(ALL, None),
            P(DP, "zl"),
            P("zl", DP),
            P(ALL, None),
            P(ALL),
            P(ALL),
            P(ALL, None),
            P(ALL),
            P(ALL, None),
            P(ALL),
            P(ALL, None),
            P(ALL),
        ),
        check_vma=False,
    )
```

```python
import functools

import jax
import jax.numpy as jnp
import numpy as np
from jax import lax
from jax.experimental import pallas as pl
from jax.experimental.pallas import tpu as pltpu
from jax.sharding import Mesh
from jax.sharding import PartitionSpec as P

HEAD_DIM = 64
LANES = 128


def _nt(a, b):
    return lax.dot_general(a, b, (((1,), (1,)), ((), ())), preferred_element_type=jnp.float32)


def _tn(a, b):
    return lax.dot_general(a, b, (((0,), (0,)), ((), ())), preferred_element_type=jnp.float32)


def _probs(q, k, head, factor):
    lane = lax.broadcasted_iota(jnp.int32, (1, LANES), 1)
    mine = (lane // HEAD_DIM) == head
    qh = jnp.where(mine, q, jnp.zeros_like(q))
    scores = _nt(qh, k) * factor
    weights = jnp.exp(scores - jnp.max(scores, axis=-1, keepdims=True))
    return mine, qh, weights / jnp.sum(weights, axis=-1, keepdims=True)


def _fwd_kernel(factor, q_ref, k_ref, v_ref, o_ref):
    q = q_ref[...]
    k = k_ref[...]
    v = v_ref[...]
    out = jnp.zeros(o_ref.shape, jnp.float32)
    for head in range(LANES // HEAD_DIM):
        mine, _, probs = _probs(q, k, head, factor)
        vh = jnp.where(mine, v, jnp.zeros_like(v))
        out = out + jnp.dot(probs.astype(v.dtype), vh, preferred_element_type=jnp.float32)
    o_ref[...] = out.astype(o_ref.dtype)


def _bwd_kernel(factor, q_ref, k_ref, v_ref, d_ref, dq_ref, dk_ref, dv_ref):
    q = q_ref[...]
    k = k_ref[...]
    v = v_ref[...]
    d = d_ref[...]
    dq = jnp.zeros(dq_ref.shape, jnp.float32)
    dk = jnp.zeros(dk_ref.shape, jnp.float32)
    dv = jnp.zeros(dv_ref.shape, jnp.float32)
    for head in range(LANES // HEAD_DIM):
        mine, qh, probs = _probs(q, k, head, factor)
        dh = jnp.where(mine, d, jnp.zeros_like(d))
        kh = jnp.where(mine, k, jnp.zeros_like(k))
        dprobs = _nt(dh, v)
        dv = dv + _tn(probs.astype(d.dtype), dh)
        inner = jnp.sum(dprobs * probs, axis=-1, keepdims=True)
        dscores = (probs * (dprobs - inner)).astype(q.dtype)
        dq = dq + jnp.dot(dscores, kh, preferred_element_type=jnp.float32)
        dk = dk + _tn(dscores, qh)
    dq_ref[...] = (dq * factor).astype(dq_ref.dtype)
    dk_ref[...] = (dk * factor).astype(dk_ref.dtype)
    dv_ref[...] = dv.astype(dv_ref.dtype)


def _wgrad_kernel(expand_tiles, modb_ref, du_ref, act_ref, dz_ref, out_ref):
    j = pl.program_id(0)

    @pl.when(j < expand_tiles)
    def _():
        out_ref[...] = jnp.dot(
            modb_ref[...], du_ref[...], preferred_element_type=jnp.float32
        ).astype(out_ref.dtype)

    @pl.when(j >= expand_tiles)
    def _():
        out_ref[...] = jnp.dot(
            act_ref[...], dz_ref[...], preferred_element_type=jnp.float32
        ).astype(out_ref.dtype)


def ffn_weight_grads(mod_t, grad_exp, act_t, grad_branch, tile=1024):
    width, tokens = mod_t.shape
    ff = grad_exp.shape[1]
    expand_tiles = ff // tile
    per_part = width // tile
    tiles = expand_tiles + (ff // width) * per_part

    def act_index(j):
        return (jnp.maximum(j - expand_tiles, 0) // per_part, 0)

    def dz_index(j):
        return (0, jnp.maximum(j - expand_tiles, 0) % per_part)

    return pl.pallas_call(
        functools.partial(_wgrad_kernel, expand_tiles),
        out_shape=jax.ShapeDtypeStruct((width, tiles * tile), jnp.bfloat16),
        grid=(tiles,),
        in_specs=[
            pl.BlockSpec((width, tokens), lambda j: (0, 0)),
            pl.BlockSpec((tokens, tile), lambda j: (0, jnp.minimum(j, expand_tiles - 1))),
            pl.BlockSpec((width, tokens), act_index),
            pl.BlockSpec((tokens, tile), dz_index),
        ],
        out_specs=pl.BlockSpec((width, tile), lambda j: (0, j)),
        compiler_params=pltpu.CompilerParams(dimension_semantics=("arbitrary",)),
        cost_estimate=pl.CostEstimate(
            flops=2 * tokens * width * tiles * tile,
            transcendentals=0,
            bytes_accessed=2 * (tokens * (width + 2 * ff + width) + width * tiles * tile),
        ),
    )(mod_t, grad_exp, act_t, grad_branch)

def attention_forward(projected, images):
    tokens, three = projected.shape
    rows, width = tokens // images, three // 3
    pairs = width // LANES
    factor = HEAD_DIM ** (-0.5)

    def part(offset):
        return pl.BlockSpec((rows, LANES), lambda b, j: (b, offset + j))

    flops = 2 * 2 * images * (width // HEAD_DIM) * rows * rows * LANES
    return pl.pallas_call(
        functools.partial(_fwd_kernel, factor),
        out_shape=jax.ShapeDtypeStruct((tokens, width), projected.dtype),
        grid=(images, pairs),
        in_specs=[part(0), part(pairs), part(2 * pairs)],
        out_specs=pl.BlockSpec((rows, LANES), lambda b, j: (b, j)),
        compiler_params=pltpu.CompilerParams(dimension_semantics=("parallel", "parallel")),
        cost_estimate=pl.CostEstimate(
            flops=flops, transcendentals=images * (width // HEAD_DIM) * rows * rows,
            bytes_accessed=2 * tokens * (three + width),
        ),
    )(projected, projected, projected)


def attention_backward(projected, grad_attended, images):
    tokens, three = projected.shape
    rows, width = tokens // images, three // 3
    pairs = width // LANES
    factor = HEAD_DIM ** (-0.5)

    def part(offset):
        return pl.BlockSpec((rows, LANES), lambda b, j: (b, offset + j))

    out = jax.ShapeDtypeStruct((tokens, width), projected.dtype)
    flops = 5 * 2 * 2 * images * (width // HEAD_DIM) * rows * rows * LANES
    dq, dk, dv = pl.pallas_call(
        functools.partial(_bwd_kernel, factor),
        out_shape=(out, out, out),
        grid=(images, pairs),
        in_specs=[part(0), part(pairs), part(2 * pairs), part(0)],
        out_specs=[part(0)] * 3,
        compiler_params=pltpu.CompilerParams(dimension_semantics=("parallel", "parallel")),
        cost_estimate=pl.CostEstimate(
            flops=flops, transcendentals=images * (width // HEAD_DIM) * rows * rows,
            bytes_accessed=2 * tokens * (three + 4 * width),
        ),
    )(projected, projected, projected, grad_attended)
    return jnp.concatenate([dq, dk, dv], axis=1)


EPS = 1e-06
GELU_C = 0.7978845608028654

AXES = ("y", "zh", "x", "c", "zl")
DP = ("y", "zh", "x", "c")
STAGES = ("c", "x", "y", "zh", "zl")
STAGES_B = ("c", "y", "x", "zh", "zl")


def matmul(left, right):
    return jnp.dot(left, right, preferred_element_type=jnp.float32)


def left_trans(left, right):
    return lax.dot_general(
        left, right, (((0,), (0,)), ((), ())), preferred_element_type=jnp.float32
    )


def right_trans(left, right):
    return lax.dot_general(
        left, right, (((1,), (1,)), ((), ())), preferred_element_type=jnp.float32
    )


def normalize(values):
    centre = values - jnp.mean(values, axis=-1, keepdims=True)
    inverse = lax.rsqrt(jnp.mean(centre * centre, axis=-1, keepdims=True) + EPS)
    return (centre * inverse, inverse)


def norm_back(grad, normed, inverse):
    return inverse * (
        grad
        - jnp.mean(grad, axis=-1, keepdims=True)
        - normed * jnp.mean(grad * normed, axis=-1, keepdims=True)
    )


def stage_order(values, sizes, inner, stages=STAGES):
    lead = values.shape[:-1]
    shape = [sizes[a] for a in AXES]
    values = values.reshape(*lead, *shape, inner)
    n = len(lead)
    order = list(range(n)) + [n + AXES.index(a) for a in stages] + [n + len(AXES)]
    return jnp.transpose(values, order).reshape(*lead, -1)


def reduce_stages(packed, stages):
    for a in stages:
        packed = lax.psum_scatter(packed, a, scatter_dimension=0, tiled=True)
    return packed


def reduce_pair(packed, axis):
    half = packed.shape[0] // 2
    index = lax.axis_index(axis)
    keep = lax.dynamic_slice_in_dim(packed, index * half, half, axis=0)
    send = lax.dynamic_slice_in_dim(packed, (1 - index) * half, half, axis=0)
    got = lax.ppermute(send, axis, [(0, 1), (1, 0)])
    return (keep.astype(jnp.float32) + got.astype(jnp.float32)).astype(packed.dtype)


def reduce_rest(packed, axes):
    count = 1
    for a in axes:
        count *= lax.axis_size(a)
    chunks = packed.reshape(count, packed.shape[0] // count, packed.shape[1])
    chunks = lax.all_to_all(chunks, axes, 0, 0, tiled=False)
    return jnp.sum(chunks.astype(jnp.float32), axis=0)


def bias_columns(columns, rows):
    block = jnp.stack(columns, axis=1)
    return jnp.pad(block, ((0, 0), (0, 128 - block.shape[1]))).astype(jnp.bfloat16)


def gather_dp(values):
    count = 1
    for a in DP:
        count *= lax.axis_size(a)
    copies = jnp.broadcast_to(values[None], (count,) + values.shape)
    return lax.all_to_all(copies, DP, 0, 0, tiled=False).reshape(-1, values.shape[1])


def per_device(
    sizes,
    tokens,
    condition,
    occupied,
    modulation_weight,
    modulation_bias,
    input_weight,
    query_bias,
    value_bias,
    output_weight,
    output_bias,
    expand_weight,
    expand_bias,
    contract_weight,
    contract_bias,
    cotangent,
):
    images, rows, width = tokens.shape
    heads = width // HEAD_DIM
    flat = images * rows
    factor = HEAD_DIM ** (-0.5)
    cond_full = condition.astype(jnp.float32)
    sigmoid = jax.nn.sigmoid(cond_full)
    silu_b = (cond_full * sigmoid).astype(jnp.bfloat16)
    silu_pair = lax.all_gather(silu_b, "zl", axis=0, tiled=True)
    mod_cols = matmul(silu_pair, modulation_weight) + modulation_bias.reshape(1, -1)
    modulation = lax.all_to_all(mod_cols, "zl", split_axis=0, concat_axis=1, tiled=True).reshape(
        images, 6, 1, width
    )
    shift_a = modulation[:, 0]
    scale_a = modulation[:, 1]
    gate_a = modulation[:, 2]
    shift_b = modulation[:, 3]
    scale_b = modulation[:, 4]
    gate_b = modulation[:, 5]
    inputs = tokens.astype(jnp.float32)
    normed_a, inverse_a = normalize(inputs)
    mod_a = (normed_a * (1.0 + scale_a) + shift_a).astype(jnp.bfloat16).reshape(flat, width)
    qkv_bias = jnp.concatenate([query_bias, jnp.zeros_like(query_bias), value_bias])
    projected = (matmul(mod_a, input_weight) + qkv_bias).astype(jnp.bfloat16)
    attended_b = attention_forward(projected, images)
    branch_a = (matmul(attended_b, output_weight) + output_bias).reshape(images, rows, width)
    middle = inputs + gate_a * branch_a
    normed_b, inverse_b = normalize(middle)
    mod_b = (normed_b * (1.0 + scale_b) + shift_b).astype(jnp.bfloat16).reshape(flat, width)
    expanded = matmul(mod_b, expand_weight) + expand_bias
    tanh_part = jnp.tanh(GELU_C * (expanded + 0.044715 * expanded * expanded * expanded))
    activated_b = (0.5 * expanded * (1.0 + tanh_part)).astype(jnp.bfloat16)
    branch_b = (matmul(activated_b, contract_weight) + contract_bias).reshape(images, rows, width)
    alive = occupied.astype(jnp.float32)[:, None, None]
    layer_out = (middle + gate_b * branch_b) * alive
    grad_out = cotangent.astype(jnp.float32) * alive
    grad_gate_b = jnp.sum(grad_out * branch_b, axis=1)
    grad_branch_b = (grad_out * gate_b).astype(jnp.bfloat16).reshape(flat, width)
    blocks = 1
    for a in AXES:
        blocks *= sizes[a]
    ff = activated_b.shape[1]
    split = ff // width
    act_perm = stage_order(
        activated_b.reshape(flat, blocks, split, width // blocks)
        .transpose(0, 2, 1, 3)
        .reshape(flat, split, width),
        sizes,
        width // blocks,
        STAGES_B,
    )
    contract_bias_grad = stage_order(
        jnp.sum(grad_branch_b.astype(jnp.float32), axis=0), sizes, width // blocks, STAGES_B
    )
    grad_act = right_trans(grad_branch_b, contract_weight)
    slope = 0.5 * (1.0 + tanh_part) + 0.5 * expanded * (1.0 - tanh_part * tanh_part) * GELU_C * (
        1.0 + 3.0 * 0.044715 * expanded * expanded
    )
    grad_exp_b = (grad_act * slope).astype(jnp.bfloat16)
    expand_bias_grad = stage_order(
        jnp.sum(grad_exp_b.astype(jnp.float32), axis=0)
        .reshape(blocks, split, width // blocks)
        .transpose(1, 0, 2)
        .reshape(split, width),
        sizes,
        width // blocks,
        STAGES_B,
    )
    packed_a = ffn_weight_grads(
        stage_order(mod_b, sizes, width // blocks).T, grad_exp_b, act_perm.reshape(flat, -1).T, grad_branch_b
    )
    packed_a, grad_exp_b = lax.optimization_barrier((packed_a, grad_exp_b))
    chain_a = reduce_stages(packed_a, STAGES[:1])
    grad_mod_b = right_trans(grad_exp_b, expand_weight).reshape(images, rows, width)
    grad_shift_b = jnp.sum(grad_mod_b, axis=1)
    grad_scale_b = jnp.sum(grad_mod_b * normed_b, axis=1)
    grad_middle = grad_out + norm_back(grad_mod_b * (1.0 + scale_b), normed_b, inverse_b)
    grad_gate_a = jnp.sum(grad_middle * branch_a, axis=1)
    grad_branch_a = (grad_middle * gate_a).astype(jnp.bfloat16).reshape(flat, width)
    chain_a, grad_branch_a = lax.optimization_barrier((chain_a, grad_branch_a))
    output_grad = left_trans(stage_order(attended_b, sizes, width // blocks, STAGES_B), grad_branch_a).astype(
        jnp.bfloat16
    )
    output_bias_grad = stage_order(
        jnp.sum(grad_branch_a.astype(jnp.float32), axis=0), sizes, width // blocks, STAGES_B
    )
    grad_att_b = right_trans(grad_branch_a, output_weight).astype(jnp.bfloat16)
    chain_c = reduce_rest(chain_a[:, ff:], STAGES_B[1:2]).astype(jnp.bfloat16)
    chain_a = reduce_stages(chain_a[:, :ff], STAGES[1:2])
    grad_proj_b = attention_backward(projected, grad_att_b, images)
    chain_c, grad_proj_b = lax.optimization_barrier((chain_c, grad_proj_b))
    input_grad = left_trans(stage_order(mod_a, sizes, width // blocks, STAGES_B), grad_proj_b).astype(
        jnp.bfloat16
    )
    bias_sums = jnp.sum(grad_proj_b.astype(jnp.float32), axis=0)
    query_bias_grad = stage_order(bias_sums[:width], sizes, width // blocks, STAGES_B)
    value_bias_grad = stage_order(bias_sums[2 * width :], sizes, width // blocks, STAGES_B)
    chain_b = reduce_pair(
        jnp.concatenate(
            [
                input_grad,
                output_grad,
                bias_columns(
                [query_bias_grad, value_bias_grad, output_bias_grad, contract_bias_grad]
                + [expand_bias_grad[q] for q in range(split)],
                width,
            ),
            ],
            axis=1,
        ),
        STAGES_B[0],
    )
    chain_a, chain_c, chain_b = lax.optimization_barrier((chain_a, chain_c, chain_b))
    chain_b = reduce_stages(chain_b, STAGES_B[1:2])
    grad_mod_a = right_trans(grad_proj_b, input_weight).reshape(images, rows, width)
    grad_shift_a = jnp.sum(grad_mod_a, axis=1)
    grad_scale_a = jnp.sum(grad_mod_a * normed_a, axis=1)
    tokens_grad = grad_middle + norm_back(grad_mod_a * (1.0 + scale_a), normed_a, inverse_a)
    modulation_terms = jnp.stack(
        [grad_shift_a, grad_scale_a, grad_gate_a, grad_shift_b, grad_scale_b, grad_gate_b], axis=1
    ).reshape(images, 6 * width)
    modulation_own = modulation_terms.astype(jnp.bfloat16)
    modulation_cols = lax.all_to_all(modulation_own, "zl", split_axis=1, concat_axis=0, tiled=True)
    silu_terms = right_trans(modulation_cols, modulation_weight)
    pair_index = lax.axis_index("zl")
    own_rows = lax.dynamic_slice_in_dim(silu_terms, pair_index * images, images, axis=0)
    other_rows = lax.dynamic_slice_in_dim(silu_terms, (1 - pair_index) * images, images, axis=0)
    silu_sums = own_rows + lax.ppermute(other_rows, "zl", [(0, 1), (1, 0)])
    condition_grad = silu_sums * sigmoid * (1.0 + cond_full * (1.0 - sigmoid))
    dp_count = lax.axis_size(DP)
    row_block = width // dp_count
    silu_parts = silu_pair.reshape(-1, dp_count, row_block).transpose(1, 0, 2)
    silu_parts = jnp.pad(silu_parts, ((0, 0), (0, 0), (0, 128 - row_block)))
    payload = jnp.concatenate(
        [jnp.broadcast_to(modulation_cols[None], (dp_count,) + modulation_cols.shape), silu_parts], axis=2
    )
    factors = lax.all_to_all(payload, DP, 0, 0, tiled=False)
    mod_all = factors[:, :, : modulation_cols.shape[1]].reshape(-1, modulation_cols.shape[1])
    silu_rows = factors[:, :, modulation_cols.shape[1] : modulation_cols.shape[1] + row_block]
    silu_rows = silu_rows.reshape(-1, row_block)
    dp_index = lax.axis_index(DP)
    modulation_weight_grad = left_trans(silu_rows, mod_all)
    bias_all = jnp.sum(mod_all.astype(jnp.float32), axis=0).reshape(-1, width)
    modulation_bias_grad = lax.dynamic_slice_in_dim(bias_all, dp_index * row_block, row_block, axis=1)
    chain_a = reduce_rest(chain_a, STAGES[2:])
    chain_b, mod_all = lax.optimization_barrier((chain_b, mod_all))
    rest = reduce_rest(jnp.concatenate([chain_c, chain_b], axis=1), STAGES_B[2:])
    chain_c = rest[:, : chain_c.shape[1]]
    chain_b = rest[:, chain_c.shape[1] :]
    three = input_weight.shape[1]
    fw = expand_weight.shape[1]
    input_weight_grad = chain_b[:, :three]
    output_weight_grad = chain_b[:, three : three + width]
    qb_grad = chain_b[:, three + width]
    vb_grad = chain_b[:, three + width + 1]
    ob_grad = chain_b[:, three + width + 2]
    expand_weight_grad = chain_a[:, :fw]
    contract_weight_grad = chain_c.reshape(-1, split, width)
    contract_weight_grad = contract_weight_grad.transpose(1, 0, 2).reshape(-1, width)
    cb_grad = chain_b[:, three + width + 3]
    eb_grad = chain_b[:, three + width + 4 : three + width + 4 + split].T.reshape(-1)
    summed = (
        input_weight_grad,
        qb_grad,
        vb_grad,
        output_weight_grad,
        ob_grad,
        expand_weight_grad,
        eb_grad,
        contract_weight_grad,
        cb_grad,
    )
    return (
        layer_out,
        tokens_grad,
        condition_grad,
        modulation_weight_grad,
        modulation_bias_grad,
        *summed,
    )


def solution(mesh):
    dp_size, mod_size = mesh.devices.shape
    rest = dp_size // 4
    side = int(round(rest ** 0.5))
    shape = (side, 2, rest // side, 2, mod_size)
    sizes = dict(zip(AXES, shape))
    physical = Mesh(np.asarray(mesh.devices).reshape(shape), AXES)
    ALL = AXES
    placed = (
        P(ALL, None, None),
        P(ALL, None),
        P(ALL),
        P(None, "zl"),
        P("zl", None),
        P(),
        P(),
        P(),
        P(),
        P(),
        P(),
        P(),
        P(),
        P(),
        P(ALL, None, None),
    )
    return jax.shard_map(
        functools.partial(per_device, sizes),
        mesh=physical,
        in_specs=placed,
        out_specs=(
            P(ALL, None, None),
            P(ALL, None, None),
            P(ALL, None),
            P(DP, "zl"),
            P("zl", DP),
            P(ALL, None),
            P(ALL),
            P(ALL),
            P(ALL, None),
            P(ALL),
            P(ALL, None),
            P(ALL),
            P(ALL, None),
            P(ALL),
        ),
        check_vma=False,
    )
```

```python
import functools

import jax
import jax.numpy as jnp
import numpy as np
from jax import lax
from jax.experimental import pallas as pl
from jax.experimental.pallas import tpu as pltpu
from jax.sharding import Mesh
from jax.sharding import PartitionSpec as P

HEAD_DIM = 64
LANES = 128


def _nt(a, b):
    return lax.dot_general(a, b, (((1,), (1,)), ((), ())), preferred_element_type=jnp.float32)


def _tn(a, b):
    return lax.dot_general(a, b, (((0,), (0,)), ((), ())), preferred_element_type=jnp.float32)


def _probs(q, k, head, factor):
    lane = lax.broadcasted_iota(jnp.int32, (1, LANES), 1)
    mine = (lane // HEAD_DIM) == head
    qh = jnp.where(mine, q, jnp.zeros_like(q))
    scores = _nt(qh, k) * factor
    weights = jnp.exp(scores - jnp.max(scores, axis=-1, keepdims=True))
    return mine, qh, weights / jnp.sum(weights, axis=-1, keepdims=True)


def _fwd_kernel(factor, q_ref, k_ref, v_ref, o_ref):
    def pair(j, carry):
        cols = pl.ds(pl.multiple_of(j * LANES, LANES), LANES)
        q = q_ref[:, cols]
        k = k_ref[:, cols]
        v = v_ref[:, cols]
        out = jnp.zeros((q.shape[0], LANES), jnp.float32)
        for head in range(LANES // HEAD_DIM):
            mine, _, probs = _probs(q, k, head, factor)
            vh = jnp.where(mine, v, jnp.zeros_like(v))
            out = out + jnp.dot(probs.astype(v.dtype), vh, preferred_element_type=jnp.float32)
        o_ref[:, cols] = out.astype(o_ref.dtype)
        return carry

    lax.fori_loop(0, o_ref.shape[1] // LANES, pair, 0)


def _bwd_kernel(factor, q_ref, k_ref, v_ref, d_ref, dq_ref, dk_ref, dv_ref):
    def pair(j, carry):
        cols = pl.ds(pl.multiple_of(j * LANES, LANES), LANES)
        q = q_ref[:, cols]
        k = k_ref[:, cols]
        v = v_ref[:, cols]
        d = d_ref[:, cols]
        dq = jnp.zeros((q.shape[0], LANES), jnp.float32)
        dk = jnp.zeros((q.shape[0], LANES), jnp.float32)
        dv = jnp.zeros((q.shape[0], LANES), jnp.float32)
        for head in range(LANES // HEAD_DIM):
            mine, qh, probs = _probs(q, k, head, factor)
            dh = jnp.where(mine, d, jnp.zeros_like(d))
            kh = jnp.where(mine, k, jnp.zeros_like(k))
            dprobs = _nt(dh, v)
            dv = dv + _tn(probs.astype(d.dtype), dh)
            inner = jnp.sum(dprobs * probs, axis=-1, keepdims=True)
            dscores = (probs * (dprobs - inner)).astype(q.dtype)
            dq = dq + jnp.dot(dscores, kh, preferred_element_type=jnp.float32)
            dk = dk + _tn(dscores, qh)
        dq_ref[:, cols] = (dq * factor).astype(dq_ref.dtype)
        dk_ref[:, cols] = (dk * factor).astype(dk_ref.dtype)
        dv_ref[:, cols] = dv.astype(dv_ref.dtype)
        return carry

    lax.fori_loop(0, dq_ref.shape[1] // LANES, pair, 0)


def _wgrad_kernel(expand_tiles, modb_ref, du_ref, act_ref, dz_ref, out_ref):
    j = pl.program_id(0)

    @pl.when(j < expand_tiles)
    def _():
        out_ref[...] = jnp.dot(
            modb_ref[...], du_ref[...], preferred_element_type=jnp.float32
        ).astype(out_ref.dtype)

    @pl.when(j >= expand_tiles)
    def _():
        out_ref[...] = jnp.dot(
            act_ref[...], dz_ref[...], preferred_element_type=jnp.float32
        ).astype(out_ref.dtype)


def ffn_weight_grads(mod_t, grad_exp, act_t, grad_branch, tile=1024):
    width, tokens = mod_t.shape
    ff = grad_exp.shape[1]
    expand_tiles = ff // tile
    per_part = width // tile
    tiles = expand_tiles + (ff // width) * per_part

    def act_index(j):
        return (jnp.maximum(j - expand_tiles, 0) // per_part, 0)

    def dz_index(j):
        return (0, jnp.maximum(j - expand_tiles, 0) % per_part)

    return pl.pallas_call(
        functools.partial(_wgrad_kernel, expand_tiles),
        out_shape=jax.ShapeDtypeStruct((width, tiles * tile), jnp.bfloat16),
        grid=(tiles,),
        in_specs=[
            pl.BlockSpec((width, tokens), lambda j: (0, 0)),
            pl.BlockSpec((tokens, tile), lambda j: (0, jnp.minimum(j, expand_tiles - 1))),
            pl.BlockSpec((width, tokens), act_index),
            pl.BlockSpec((tokens, tile), dz_index),
        ],
        out_specs=pl.BlockSpec((width, tile), lambda j: (0, j)),
        compiler_params=pltpu.CompilerParams(dimension_semantics=("arbitrary",)),
        cost_estimate=pl.CostEstimate(
            flops=2 * tokens * width * tiles * tile,
            transcendentals=0,
            bytes_accessed=2 * (tokens * (width + 2 * ff + width) + width * tiles * tile),
        ),
    )(mod_t, grad_exp, act_t, grad_branch)

def attention_forward(projected, images):
    tokens, three = projected.shape
    rows, width = tokens // images, three // 3
    pairs = width // LANES
    factor = HEAD_DIM ** (-0.5)

    def part(offset):
        return pl.BlockSpec((rows, width), lambda b: (b, offset))

    flops = 2 * 2 * images * (width // HEAD_DIM) * rows * rows * LANES
    return pl.pallas_call(
        functools.partial(_fwd_kernel, factor),
        out_shape=jax.ShapeDtypeStruct((tokens, width), projected.dtype),
        grid=(images,),
        in_specs=[part(0), part(1), part(2)],
        out_specs=part(0),
        compiler_params=pltpu.CompilerParams(dimension_semantics=("parallel",)),
        cost_estimate=pl.CostEstimate(
            flops=flops, transcendentals=images * (width // HEAD_DIM) * rows * rows,
            bytes_accessed=2 * tokens * (three + width),
        ),
    )(projected, projected, projected)


def attention_backward(projected, grad_attended, images):
    tokens, three = projected.shape
    rows, width = tokens // images, three // 3
    pairs = width // LANES
    factor = HEAD_DIM ** (-0.5)

    def part(offset):
        return pl.BlockSpec((rows, width), lambda b: (b, offset))

    out = jax.ShapeDtypeStruct((tokens, width), projected.dtype)
    flops = 5 * 2 * 2 * images * (width // HEAD_DIM) * rows * rows * LANES
    dq, dk, dv = pl.pallas_call(
        functools.partial(_bwd_kernel, factor),
        out_shape=(out, out, out),
        grid=(images,),
        in_specs=[part(0), part(1), part(2), part(0)],
        out_specs=[part(0)] * 3,
        compiler_params=pltpu.CompilerParams(dimension_semantics=("parallel",)),
        cost_estimate=pl.CostEstimate(
            flops=flops, transcendentals=images * (width // HEAD_DIM) * rows * rows,
            bytes_accessed=2 * tokens * (three + 4 * width),
        ),
    )(projected, projected, projected, grad_attended)
    return jnp.concatenate([dq, dk, dv], axis=1)


EPS = 1e-06
GELU_C = 0.7978845608028654

AXES = ("y", "zh", "x", "c", "zl")
DP = ("y", "zh", "x", "c")
STAGES = ("c", "x", "y", "zh", "zl")
STAGES_B = ("c", "y", "x", "zh", "zl")


def matmul(left, right):
    return jnp.dot(left, right, preferred_element_type=jnp.float32)


def left_trans(left, right):
    return lax.dot_general(
        left, right, (((0,), (0,)), ((), ())), preferred_element_type=jnp.float32
    )


def right_trans(left, right):
    return lax.dot_general(
        left, right, (((1,), (1,)), ((), ())), preferred_element_type=jnp.float32
    )


def normalize(values):
    centre = values - jnp.mean(values, axis=-1, keepdims=True)
    inverse = lax.rsqrt(jnp.mean(centre * centre, axis=-1, keepdims=True) + EPS)
    return (centre * inverse, inverse)


def norm_back(grad, normed, inverse):
    return inverse * (
        grad
        - jnp.mean(grad, axis=-1, keepdims=True)
        - normed * jnp.mean(grad * normed, axis=-1, keepdims=True)
    )


def stage_order(values, sizes, inner, stages=STAGES):
    lead = values.shape[:-1]
    shape = [sizes[a] for a in AXES]
    values = values.reshape(*lead, *shape, inner)
    n = len(lead)
    order = list(range(n)) + [n + AXES.index(a) for a in stages] + [n + len(AXES)]
    return jnp.transpose(values, order).reshape(*lead, -1)


def reduce_stages(packed, stages):
    for a in stages:
        packed = lax.psum_scatter(packed, a, scatter_dimension=0, tiled=True)
    return packed


def reduce_pair(packed, axis):
    half = packed.shape[0] // 2
    index = lax.axis_index(axis)
    keep = lax.dynamic_slice_in_dim(packed, index * half, half, axis=0)
    send = lax.dynamic_slice_in_dim(packed, (1 - index) * half, half, axis=0)
    got = lax.ppermute(send, axis, [(0, 1), (1, 0)])
    return (keep.astype(jnp.float32) + got.astype(jnp.float32)).astype(packed.dtype)


def reduce_rest(packed, axes):
    count = 1
    for a in axes:
        count *= lax.axis_size(a)
    chunks = packed.reshape(count, packed.shape[0] // count, packed.shape[1])
    chunks = lax.all_to_all(chunks, axes, 0, 0, tiled=False)
    return jnp.sum(chunks.astype(jnp.float32), axis=0)


def bias_columns(columns, rows):
    block = jnp.stack(columns, axis=1)
    return jnp.pad(block, ((0, 0), (0, 128 - block.shape[1]))).astype(jnp.bfloat16)


def gather_dp(values):
    count = 1
    for a in DP:
        count *= lax.axis_size(a)
    copies = jnp.broadcast_to(values[None], (count,) + values.shape)
    return lax.all_to_all(copies, DP, 0, 0, tiled=False).reshape(-1, values.shape[1])


def per_device(
    sizes,
    tokens,
    condition,
    occupied,
    modulation_weight,
    modulation_bias,
    input_weight,
    query_bias,
    value_bias,
    output_weight,
    output_bias,
    expand_weight,
    expand_bias,
    contract_weight,
    contract_bias,
    cotangent,
):
    images, rows, width = tokens.shape
    heads = width // HEAD_DIM
    flat = images * rows
    factor = HEAD_DIM ** (-0.5)
    cond_full = condition.astype(jnp.float32)
    sigmoid = jax.nn.sigmoid(cond_full)
    silu_b = (cond_full * sigmoid).astype(jnp.bfloat16)
    silu_pair = lax.all_gather(silu_b, "zl", axis=0, tiled=True)
    mod_cols = matmul(silu_pair, modulation_weight) + modulation_bias.reshape(1, -1)
    modulation = lax.all_to_all(mod_cols, "zl", split_axis=0, concat_axis=1, tiled=True).reshape(
        images, 6, 1, width
    )
    shift_a = modulation[:, 0]
    scale_a = modulation[:, 1]
    gate_a = modulation[:, 2]
    shift_b = modulation[:, 3]
    scale_b = modulation[:, 4]
    gate_b = modulation[:, 5]
    inputs = tokens.astype(jnp.float32)
    normed_a, inverse_a = normalize(inputs)
    mod_a = (normed_a * (1.0 + scale_a) + shift_a).astype(jnp.bfloat16).reshape(flat, width)
    qkv_bias = jnp.concatenate([query_bias, jnp.zeros_like(query_bias), value_bias])
    projected = (matmul(mod_a, input_weight) + qkv_bias).astype(jnp.bfloat16)
    attended_b = attention_forward(projected, images)
    branch_a = (matmul(attended_b, output_weight) + output_bias).reshape(images, rows, width)
    middle = inputs + gate_a * branch_a
    normed_b, inverse_b = normalize(middle)
    mod_b = (normed_b * (1.0 + scale_b) + shift_b).astype(jnp.bfloat16).reshape(flat, width)
    expanded = matmul(mod_b, expand_weight) + expand_bias
    tanh_part = jnp.tanh(GELU_C * (expanded + 0.044715 * expanded * expanded * expanded))
    activated_b = (0.5 * expanded * (1.0 + tanh_part)).astype(jnp.bfloat16)
    branch_b = (matmul(activated_b, contract_weight) + contract_bias).reshape(images, rows, width)
    alive = occupied.astype(jnp.float32)[:, None, None]
    layer_out = (middle + gate_b * branch_b) * alive
    grad_out = cotangent.astype(jnp.float32) * alive
    grad_gate_b = jnp.sum(grad_out * branch_b, axis=1)
    grad_branch_b = (grad_out * gate_b).astype(jnp.bfloat16).reshape(flat, width)
    blocks = 1
    for a in AXES:
        blocks *= sizes[a]
    ff = activated_b.shape[1]
    split = ff // width
    act_perm = stage_order(
        activated_b.reshape(flat, blocks, split, width // blocks)
        .transpose(0, 2, 1, 3)
        .reshape(flat, split, width),
        sizes,
        width // blocks,
    )
    contract_bias_grad = stage_order(
        jnp.sum(grad_branch_b.astype(jnp.float32), axis=0), sizes, width // blocks, STAGES_B
    )
    grad_act = right_trans(grad_branch_b, contract_weight)
    slope = 0.5 * (1.0 + tanh_part) + 0.5 * expanded * (1.0 - tanh_part * tanh_part) * GELU_C * (
        1.0 + 3.0 * 0.044715 * expanded * expanded
    )
    grad_exp_b = (grad_act * slope).astype(jnp.bfloat16)
    expand_bias_grad = stage_order(
        jnp.sum(grad_exp_b.astype(jnp.float32), axis=0)
        .reshape(blocks, split, width // blocks)
        .transpose(1, 0, 2)
        .reshape(split, width),
        sizes,
        width // blocks,
        STAGES_B,
    )
    packed_a = ffn_weight_grads(
        stage_order(mod_b, sizes, width // blocks).T, grad_exp_b, act_perm.reshape(flat, -1).T, grad_branch_b
    )
    packed_a, grad_exp_b = lax.optimization_barrier((packed_a, grad_exp_b))
    chain_a = reduce_stages(packed_a, STAGES[:1])
    grad_mod_b = right_trans(grad_exp_b, expand_weight).reshape(images, rows, width)
    grad_shift_b = jnp.sum(grad_mod_b, axis=1)
    grad_scale_b = jnp.sum(grad_mod_b * normed_b, axis=1)
    grad_middle = grad_out + norm_back(grad_mod_b * (1.0 + scale_b), normed_b, inverse_b)
    grad_gate_a = jnp.sum(grad_middle * branch_a, axis=1)
    grad_branch_a = (grad_middle * gate_a).astype(jnp.bfloat16).reshape(flat, width)
    output_grad = left_trans(stage_order(attended_b, sizes, width // blocks, STAGES_B), grad_branch_a).astype(
        jnp.bfloat16
    )
    output_bias_grad = stage_order(
        jnp.sum(grad_branch_a.astype(jnp.float32), axis=0), sizes, width // blocks, STAGES_B
    )
    grad_att_b = right_trans(grad_branch_a, output_weight).astype(jnp.bfloat16)
    chain_a, grad_att_b = lax.optimization_barrier((chain_a, grad_att_b))
    chain_a = reduce_stages(chain_a, STAGES[1:2])
    grad_proj_b = attention_backward(projected, grad_att_b, images)
    input_grad = left_trans(stage_order(mod_a, sizes, width // blocks, STAGES_B), grad_proj_b).astype(
        jnp.bfloat16
    )
    bias_sums = jnp.sum(grad_proj_b.astype(jnp.float32), axis=0)
    query_bias_grad = stage_order(bias_sums[:width], sizes, width // blocks, STAGES_B)
    value_bias_grad = stage_order(bias_sums[2 * width :], sizes, width // blocks, STAGES_B)
    chain_b = reduce_pair(
        jnp.concatenate(
            [
                input_grad,
                output_grad,
                bias_columns(
                [query_bias_grad, value_bias_grad, output_bias_grad, contract_bias_grad]
                + [expand_bias_grad[q] for q in range(split)],
                width,
            ),
            ],
            axis=1,
        ),
        STAGES_B[0],
    )
    chain_a, chain_b = lax.optimization_barrier((chain_a, chain_b))
    chain_b = reduce_stages(chain_b, STAGES_B[1:2])
    grad_mod_a = right_trans(grad_proj_b, input_weight).reshape(images, rows, width)
    grad_shift_a = jnp.sum(grad_mod_a, axis=1)
    grad_scale_a = jnp.sum(grad_mod_a * normed_a, axis=1)
    tokens_grad = grad_middle + norm_back(grad_mod_a * (1.0 + scale_a), normed_a, inverse_a)
    modulation_terms = jnp.stack(
        [grad_shift_a, grad_scale_a, grad_gate_a, grad_shift_b, grad_scale_b, grad_gate_b], axis=1
    ).reshape(images, 6 * width)
    modulation_own = modulation_terms.astype(jnp.bfloat16)
    modulation_cols = lax.all_to_all(modulation_own, "zl", split_axis=1, concat_axis=0, tiled=True)
    silu_terms = right_trans(modulation_cols, modulation_weight)
    pair_index = lax.axis_index("zl")
    own_rows = lax.dynamic_slice_in_dim(silu_terms, pair_index * images, images, axis=0)
    other_rows = lax.dynamic_slice_in_dim(silu_terms, (1 - pair_index) * images, images, axis=0)
    silu_sums = own_rows + lax.ppermute(other_rows, "zl", [(0, 1), (1, 0)])
    condition_grad = silu_sums * sigmoid * (1.0 + cond_full * (1.0 - sigmoid))
    dp_count = lax.axis_size(DP)
    row_block = width // dp_count
    silu_parts = silu_pair.reshape(-1, dp_count, row_block).transpose(1, 0, 2)
    silu_parts = jnp.pad(silu_parts, ((0, 0), (0, 0), (0, 128 - row_block)))
    payload = jnp.concatenate(
        [jnp.broadcast_to(modulation_cols[None], (dp_count,) + modulation_cols.shape), silu_parts], axis=2
    )
    factors = lax.all_to_all(payload, DP, 0, 0, tiled=False)
    mod_all = factors[:, :, : modulation_cols.shape[1]].reshape(-1, modulation_cols.shape[1])
    silu_rows = factors[:, :, modulation_cols.shape[1] : modulation_cols.shape[1] + row_block]
    silu_rows = silu_rows.reshape(-1, row_block)
    dp_index = lax.axis_index(DP)
    modulation_weight_grad = left_trans(silu_rows, mod_all)
    bias_all = jnp.sum(mod_all.astype(jnp.float32), axis=0).reshape(-1, width)
    modulation_bias_grad = lax.dynamic_slice_in_dim(bias_all, dp_index * row_block, row_block, axis=1)
    chain_a = reduce_rest(chain_a, STAGES[2:])
    chain_b, mod_all = lax.optimization_barrier((chain_b, mod_all))
    chain_b = reduce_rest(chain_b, STAGES_B[2:])
    three = input_weight.shape[1]
    fw = expand_weight.shape[1]
    input_weight_grad = chain_b[:, :three]
    output_weight_grad = chain_b[:, three : three + width]
    qb_grad = chain_b[:, three + width]
    vb_grad = chain_b[:, three + width + 1]
    ob_grad = chain_b[:, three + width + 2]
    expand_weight_grad = chain_a[:, :fw]
    contract_weight_grad = chain_a[:, fw : fw + split * width].reshape(-1, split, width)
    contract_weight_grad = contract_weight_grad.transpose(1, 0, 2).reshape(-1, width)
    cb_grad = chain_b[:, three + width + 3]
    eb_grad = chain_b[:, three + width + 4 : three + width + 4 + split].T.reshape(-1)
    summed = (
        input_weight_grad,
        qb_grad,
        vb_grad,
        output_weight_grad,
        ob_grad,
        expand_weight_grad,
        eb_grad,
        contract_weight_grad,
        cb_grad,
    )
    return (
        layer_out,
        tokens_grad,
        condition_grad,
        modulation_weight_grad,
        modulation_bias_grad,
        *summed,
    )


def solution(mesh):
    dp_size, mod_size = mesh.devices.shape
    rest = dp_size // 4
    side = int(round(rest ** 0.5))
    shape = (side, 2, rest // side, 2, mod_size)
    sizes = dict(zip(AXES, shape))
    physical = Mesh(np.asarray(mesh.devices).reshape(shape), AXES)
    ALL = AXES
    placed = (
        P(ALL, None, None),
        P(ALL, None),
        P(ALL),
        P(None, "zl"),
        P("zl", None),
        P(),
        P(),
        P(),
        P(),
        P(),
        P(),
        P(),
        P(),
        P(),
        P(ALL, None, None),
    )
    return jax.shard_map(
        functools.partial(per_device, sizes),
        mesh=physical,
        in_specs=placed,
        out_specs=(
            P(ALL, None, None),
            P(ALL, None, None),
            P(ALL, None),
            P(DP, "zl"),
            P("zl", DP),
            P(ALL, None),
            P(ALL),
            P(ALL),
            P(ALL, None),
            P(ALL),
            P(ALL, None),
            P(ALL),
            P(ALL, None),
            P(ALL),
        ),
        check_vma=False,
    )
```

```python
import functools

import jax
import jax.numpy as jnp
import numpy as np
from jax import lax
from jax.experimental import pallas as pl
from jax.experimental.pallas import tpu as pltpu
from jax.sharding import Mesh
from jax.sharding import PartitionSpec as P

HEAD_DIM = 64
LANES = 128


def _nt(a, b):
    return lax.dot_general(a, b, (((1,), (1,)), ((), ())), preferred_element_type=jnp.float32)


def _tn(a, b):
    return lax.dot_general(a, b, (((0,), (0,)), ((), ())), preferred_element_type=jnp.float32)


def _probs(q, k, head, factor):
    lane = lax.broadcasted_iota(jnp.int32, (1, LANES), 1)
    mine = (lane // HEAD_DIM) == head
    qh = jnp.where(mine, q, jnp.zeros_like(q))
    scores = _nt(qh, k) * factor
    weights = jnp.exp(scores - jnp.max(scores, axis=-1, keepdims=True))
    return mine, qh, weights / jnp.sum(weights, axis=-1, keepdims=True)


def _fwd_kernel(factor, q_ref, k_ref, v_ref, o_ref):
    def pair(j, carry):
        cols = pl.ds(pl.multiple_of(j * LANES, LANES), LANES)
        q = q_ref[:, cols]
        k = k_ref[:, cols]
        v = v_ref[:, cols]
        out = jnp.zeros((q.shape[0], LANES), jnp.float32)
        for head in range(LANES // HEAD_DIM):
            mine, _, probs = _probs(q, k, head, factor)
            vh = jnp.where(mine, v, jnp.zeros_like(v))
            out = out + jnp.dot(probs.astype(v.dtype), vh, preferred_element_type=jnp.float32)
        o_ref[:, cols] = out.astype(o_ref.dtype)
        return carry

    lax.fori_loop(0, o_ref.shape[1] // LANES, pair, 0, unroll=2)


def _bwd_kernel(factor, q_ref, k_ref, v_ref, d_ref, dq_ref, dk_ref, dv_ref):
    def pair(j, carry):
        cols = pl.ds(pl.multiple_of(j * LANES, LANES), LANES)
        q = q_ref[:, cols]
        k = k_ref[:, cols]
        v = v_ref[:, cols]
        d = d_ref[:, cols]
        dq = jnp.zeros((q.shape[0], LANES), jnp.float32)
        dk = jnp.zeros((q.shape[0], LANES), jnp.float32)
        dv = jnp.zeros((q.shape[0], LANES), jnp.float32)
        for head in range(LANES // HEAD_DIM):
            mine, qh, probs = _probs(q, k, head, factor)
            dh = jnp.where(mine, d, jnp.zeros_like(d))
            kh = jnp.where(mine, k, jnp.zeros_like(k))
            dprobs = _nt(dh, v)
            dv = dv + _tn(probs.astype(d.dtype), dh)
            inner = jnp.sum(dprobs * probs, axis=-1, keepdims=True)
            dscores = (probs * (dprobs - inner)).astype(q.dtype)
            dq = dq + jnp.dot(dscores, kh, preferred_element_type=jnp.float32)
            dk = dk + _tn(dscores, qh)
        dq_ref[:, cols] = (dq * factor).astype(dq_ref.dtype)
        dk_ref[:, cols] = (dk * factor).astype(dk_ref.dtype)
        dv_ref[:, cols] = dv.astype(dv_ref.dtype)
        return carry

    lax.fori_loop(0, dq_ref.shape[1] // LANES, pair, 0, unroll=2)


def _wgrad_kernel(expand_tiles, modb_ref, du_ref, act_ref, dz_ref, out_ref):
    j = pl.program_id(0)

    @pl.when(j < expand_tiles)
    def _():
        out_ref[...] = jnp.dot(
            modb_ref[...], du_ref[...], preferred_element_type=jnp.float32
        ).astype(out_ref.dtype)

    @pl.when(j >= expand_tiles)
    def _():
        out_ref[...] = jnp.dot(
            act_ref[...], dz_ref[...], preferred_element_type=jnp.float32
        ).astype(out_ref.dtype)


def ffn_weight_grads(mod_t, grad_exp, act_t, grad_branch, tile=1024):
    width, tokens = mod_t.shape
    ff = grad_exp.shape[1]
    expand_tiles = ff // tile
    per_part = width // tile
    tiles = expand_tiles + (ff // width) * per_part

    def act_index(j):
        return (jnp.maximum(j - expand_tiles, 0) // per_part, 0)

    def dz_index(j):
        return (0, jnp.maximum(j - expand_tiles, 0) % per_part)

    return pl.pallas_call(
        functools.partial(_wgrad_kernel, expand_tiles),
        out_shape=jax.ShapeDtypeStruct((width, tiles * tile), jnp.bfloat16),
        grid=(tiles,),
        in_specs=[
            pl.BlockSpec((width, tokens), lambda j: (0, 0)),
            pl.BlockSpec((tokens, tile), lambda j: (0, jnp.minimum(j, expand_tiles - 1))),
            pl.BlockSpec((width, tokens), act_index),
            pl.BlockSpec((tokens, tile), dz_index),
        ],
        out_specs=pl.BlockSpec((width, tile), lambda j: (0, j)),
        compiler_params=pltpu.CompilerParams(dimension_semantics=("arbitrary",)),
        cost_estimate=pl.CostEstimate(
            flops=2 * tokens * width * tiles * tile,
            transcendentals=0,
            bytes_accessed=2 * (tokens * (width + 2 * ff + width) + width * tiles * tile),
        ),
    )(mod_t, grad_exp, act_t, grad_branch)

def attention_forward(projected, images):
    tokens, three = projected.shape
    rows, width = tokens // images, three // 3
    pairs = width // LANES
    factor = HEAD_DIM ** (-0.5)

    def part(offset):
        return pl.BlockSpec((rows, width), lambda b: (b, offset))

    flops = 2 * 2 * images * (width // HEAD_DIM) * rows * rows * LANES
    return pl.pallas_call(
        functools.partial(_fwd_kernel, factor),
        out_shape=jax.ShapeDtypeStruct((tokens, width), projected.dtype),
        grid=(images,),
        in_specs=[part(0), part(1), part(2)],
        out_specs=part(0),
        compiler_params=pltpu.CompilerParams(dimension_semantics=("parallel",)),
        cost_estimate=pl.CostEstimate(
            flops=flops, transcendentals=images * (width // HEAD_DIM) * rows * rows,
            bytes_accessed=2 * tokens * (three + width),
        ),
    )(projected, projected, projected)


def attention_backward(projected, grad_attended, images):
    tokens, three = projected.shape
    rows, width = tokens // images, three // 3
    pairs = width // LANES
    factor = HEAD_DIM ** (-0.5)

    def part(offset):
        return pl.BlockSpec((rows, width), lambda b: (b, offset))

    out = jax.ShapeDtypeStruct((tokens, width), projected.dtype)
    flops = 5 * 2 * 2 * images * (width // HEAD_DIM) * rows * rows * LANES
    dq, dk, dv = pl.pallas_call(
        functools.partial(_bwd_kernel, factor),
        out_shape=(out, out, out),
        grid=(images,),
        in_specs=[part(0), part(1), part(2), part(0)],
        out_specs=[part(0)] * 3,
        compiler_params=pltpu.CompilerParams(dimension_semantics=("parallel",)),
        cost_estimate=pl.CostEstimate(
            flops=flops, transcendentals=images * (width // HEAD_DIM) * rows * rows,
            bytes_accessed=2 * tokens * (three + 4 * width),
        ),
    )(projected, projected, projected, grad_attended)
    return jnp.concatenate([dq, dk, dv], axis=1)


EPS = 1e-06
GELU_C = 0.7978845608028654

AXES = ("y", "zh", "x", "c", "zl")
DP = ("y", "zh", "x", "c")
STAGES = ("c", "x", "y", "zh", "zl")
STAGES_B = ("c", "y", "x", "zh", "zl")


def matmul(left, right):
    return jnp.dot(left, right, preferred_element_type=jnp.float32)


def left_trans(left, right):
    return lax.dot_general(
        left, right, (((0,), (0,)), ((), ())), preferred_element_type=jnp.float32
    )


def right_trans(left, right):
    return lax.dot_general(
        left, right, (((1,), (1,)), ((), ())), preferred_element_type=jnp.float32
    )


def normalize(values):
    centre = values - jnp.mean(values, axis=-1, keepdims=True)
    inverse = lax.rsqrt(jnp.mean(centre * centre, axis=-1, keepdims=True) + EPS)
    return (centre * inverse, inverse)


def norm_back(grad, normed, inverse):
    return inverse * (
        grad
        - jnp.mean(grad, axis=-1, keepdims=True)
        - normed * jnp.mean(grad * normed, axis=-1, keepdims=True)
    )


def stage_order(values, sizes, inner, stages=STAGES):
    lead = values.shape[:-1]
    shape = [sizes[a] for a in AXES]
    values = values.reshape(*lead, *shape, inner)
    n = len(lead)
    order = list(range(n)) + [n + AXES.index(a) for a in stages] + [n + len(AXES)]
    return jnp.transpose(values, order).reshape(*lead, -1)


def reduce_stages(packed, stages):
    for a in stages:
        packed = lax.psum_scatter(packed, a, scatter_dimension=0, tiled=True)
    return packed


def reduce_pair(packed, axis):
    half = packed.shape[0] // 2
    index = lax.axis_index(axis)
    keep = lax.dynamic_slice_in_dim(packed, index * half, half, axis=0)
    send = lax.dynamic_slice_in_dim(packed, (1 - index) * half, half, axis=0)
    got = lax.ppermute(send, axis, [(0, 1), (1, 0)])
    return (keep.astype(jnp.float32) + got.astype(jnp.float32)).astype(packed.dtype)


def reduce_rest(packed, axes):
    count = 1
    for a in axes:
        count *= lax.axis_size(a)
    chunks = packed.reshape(count, packed.shape[0] // count, packed.shape[1])
    chunks = lax.all_to_all(chunks, axes, 0, 0, tiled=False)
    return jnp.sum(chunks.astype(jnp.float32), axis=0)


def bias_columns(columns, rows):
    block = jnp.stack(columns, axis=1)
    return jnp.pad(block, ((0, 0), (0, 128 - block.shape[1]))).astype(jnp.bfloat16)


def gather_dp(values):
    count = 1
    for a in DP:
        count *= lax.axis_size(a)
    copies = jnp.broadcast_to(values[None], (count,) + values.shape)
    return lax.all_to_all(copies, DP, 0, 0, tiled=False).reshape(-1, values.shape[1])


def per_device(
    sizes,
    tokens,
    condition,
    occupied,
    modulation_weight,
    modulation_bias,
    input_weight,
    query_bias,
    value_bias,
    output_weight,
    output_bias,
    expand_weight,
    expand_bias,
    contract_weight,
    contract_bias,
    cotangent,
):
    images, rows, width = tokens.shape
    heads = width // HEAD_DIM
    flat = images * rows
    factor = HEAD_DIM ** (-0.5)
    cond_full = condition.astype(jnp.float32)
    sigmoid = jax.nn.sigmoid(cond_full)
    silu_b = (cond_full * sigmoid).astype(jnp.bfloat16)
    silu_pair = lax.all_gather(silu_b, "zl", axis=0, tiled=True)
    mod_cols = matmul(silu_pair, modulation_weight) + modulation_bias.reshape(1, -1)
    modulation = lax.all_to_all(mod_cols, "zl", split_axis=0, concat_axis=1, tiled=True).reshape(
        images, 6, 1, width
    )
    shift_a = modulation[:, 0]
    scale_a = modulation[:, 1]
    gate_a = modulation[:, 2]
    shift_b = modulation[:, 3]
    scale_b = modulation[:, 4]
    gate_b = modulation[:, 5]
    inputs = tokens.astype(jnp.float32)
    normed_a, inverse_a = normalize(inputs)
    mod_a = (normed_a * (1.0 + scale_a) + shift_a).astype(jnp.bfloat16).reshape(flat, width)
    qkv_bias = jnp.concatenate([query_bias, jnp.zeros_like(query_bias), value_bias])
    projected = (matmul(mod_a, input_weight) + qkv_bias).astype(jnp.bfloat16)
    attended_b = attention_forward(projected, images)
    branch_a = (matmul(attended_b, output_weight) + output_bias).reshape(images, rows, width)
    middle = inputs + gate_a * branch_a
    normed_b, inverse_b = normalize(middle)
    mod_b = (normed_b * (1.0 + scale_b) + shift_b).astype(jnp.bfloat16).reshape(flat, width)
    expanded = matmul(mod_b, expand_weight) + expand_bias
    tanh_part = jnp.tanh(GELU_C * (expanded + 0.044715 * expanded * expanded * expanded))
    activated_b = (0.5 * expanded * (1.0 + tanh_part)).astype(jnp.bfloat16)
    branch_b = (matmul(activated_b, contract_weight) + contract_bias).reshape(images, rows, width)
    alive = occupied.astype(jnp.float32)[:, None, None]
    layer_out = (middle + gate_b * branch_b) * alive
    grad_out = cotangent.astype(jnp.float32) * alive
    grad_gate_b = jnp.sum(grad_out * branch_b, axis=1)
    grad_branch_b = (grad_out * gate_b).astype(jnp.bfloat16).reshape(flat, width)
    blocks = 1
    for a in AXES:
        blocks *= sizes[a]
    ff = activated_b.shape[1]
    split = ff // width
    act_perm = stage_order(
        activated_b.reshape(flat, blocks, split, width // blocks)
        .transpose(0, 2, 1, 3)
        .reshape(flat, split, width),
        sizes,
        width // blocks,
    )
    contract_bias_grad = stage_order(
        jnp.sum(grad_branch_b.astype(jnp.float32), axis=0), sizes, width // blocks, STAGES_B
    )
    grad_act = right_trans(grad_branch_b, contract_weight)
    slope = 0.5 * (1.0 + tanh_part) + 0.5 * expanded * (1.0 - tanh_part * tanh_part) * GELU_C * (
        1.0 + 3.0 * 0.044715 * expanded * expanded
    )
    grad_exp_b = (grad_act * slope).astype(jnp.bfloat16)
    expand_bias_grad = stage_order(
        jnp.sum(grad_exp_b.astype(jnp.float32), axis=0)
        .reshape(blocks, split, width // blocks)
        .transpose(1, 0, 2)
        .reshape(split, width),
        sizes,
        width // blocks,
        STAGES_B,
    )
    packed_a = ffn_weight_grads(
        stage_order(mod_b, sizes, width // blocks).T, grad_exp_b, act_perm.reshape(flat, -1).T, grad_branch_b
    )
    packed_a, grad_exp_b = lax.optimization_barrier((packed_a, grad_exp_b))
    chain_a = reduce_stages(packed_a, STAGES[:1])
    grad_mod_b = right_trans(grad_exp_b, expand_weight).reshape(images, rows, width)
    grad_shift_b = jnp.sum(grad_mod_b, axis=1)
    grad_scale_b = jnp.sum(grad_mod_b * normed_b, axis=1)
    grad_middle = grad_out + norm_back(grad_mod_b * (1.0 + scale_b), normed_b, inverse_b)
    grad_gate_a = jnp.sum(grad_middle * branch_a, axis=1)
    grad_branch_a = (grad_middle * gate_a).astype(jnp.bfloat16).reshape(flat, width)
    output_grad = left_trans(stage_order(attended_b, sizes, width // blocks, STAGES_B), grad_branch_a).astype(
        jnp.bfloat16
    )
    output_bias_grad = stage_order(
        jnp.sum(grad_branch_a.astype(jnp.float32), axis=0), sizes, width // blocks, STAGES_B
    )
    grad_att_b = right_trans(grad_branch_a, output_weight).astype(jnp.bfloat16)
    chain_a, grad_att_b = lax.optimization_barrier((chain_a, grad_att_b))
    chain_a = reduce_stages(chain_a, STAGES[1:2])
    grad_proj_b = attention_backward(projected, grad_att_b, images)
    input_grad = left_trans(stage_order(mod_a, sizes, width // blocks, STAGES_B), grad_proj_b).astype(
        jnp.bfloat16
    )
    bias_sums = jnp.sum(grad_proj_b.astype(jnp.float32), axis=0)
    query_bias_grad = stage_order(bias_sums[:width], sizes, width // blocks, STAGES_B)
    value_bias_grad = stage_order(bias_sums[2 * width :], sizes, width // blocks, STAGES_B)
    chain_b = reduce_pair(
        jnp.concatenate(
            [
                input_grad,
                output_grad,
                bias_columns(
                [query_bias_grad, value_bias_grad, output_bias_grad, contract_bias_grad]
                + [expand_bias_grad[q] for q in range(split)],
                width,
            ),
            ],
            axis=1,
        ),
        STAGES_B[0],
    )
    chain_a, chain_b = lax.optimization_barrier((chain_a, chain_b))
    chain_b = reduce_stages(chain_b, STAGES_B[1:2])
    grad_mod_a = right_trans(grad_proj_b, input_weight).reshape(images, rows, width)
    grad_shift_a = jnp.sum(grad_mod_a, axis=1)
    grad_scale_a = jnp.sum(grad_mod_a * normed_a, axis=1)
    tokens_grad = grad_middle + norm_back(grad_mod_a * (1.0 + scale_a), normed_a, inverse_a)
    modulation_terms = jnp.stack(
        [grad_shift_a, grad_scale_a, grad_gate_a, grad_shift_b, grad_scale_b, grad_gate_b], axis=1
    ).reshape(images, 6 * width)
    modulation_own = modulation_terms.astype(jnp.bfloat16)
    modulation_cols = lax.all_to_all(modulation_own, "zl", split_axis=1, concat_axis=0, tiled=True)
    silu_terms = right_trans(modulation_cols, modulation_weight)
    pair_index = lax.axis_index("zl")
    own_rows = lax.dynamic_slice_in_dim(silu_terms, pair_index * images, images, axis=0)
    other_rows = lax.dynamic_slice_in_dim(silu_terms, (1 - pair_index) * images, images, axis=0)
    silu_sums = own_rows + lax.ppermute(other_rows, "zl", [(0, 1), (1, 0)])
    condition_grad = silu_sums * sigmoid * (1.0 + cond_full * (1.0 - sigmoid))
    dp_count = lax.axis_size(DP)
    row_block = width // dp_count
    silu_parts = silu_pair.reshape(-1, dp_count, row_block).transpose(1, 0, 2)
    silu_parts = jnp.pad(silu_parts, ((0, 0), (0, 0), (0, 128 - row_block)))
    payload = jnp.concatenate(
        [jnp.broadcast_to(modulation_cols[None], (dp_count,) + modulation_cols.shape), silu_parts], axis=2
    )
    factors = lax.all_to_all(payload, DP, 0, 0, tiled=False)
    mod_all = factors[:, :, : modulation_cols.shape[1]].reshape(-1, modulation_cols.shape[1])
    silu_rows = factors[:, :, modulation_cols.shape[1] : modulation_cols.shape[1] + row_block]
    silu_rows = silu_rows.reshape(-1, row_block)
    dp_index = lax.axis_index(DP)
    modulation_weight_grad = left_trans(silu_rows, mod_all)
    bias_all = jnp.sum(mod_all.astype(jnp.float32), axis=0).reshape(-1, width)
    modulation_bias_grad = lax.dynamic_slice_in_dim(bias_all, dp_index * row_block, row_block, axis=1)
    chain_a = reduce_rest(chain_a, STAGES[2:])
    chain_b, mod_all = lax.optimization_barrier((chain_b, mod_all))
    chain_b = reduce_rest(chain_b, STAGES_B[2:])
    three = input_weight.shape[1]
    fw = expand_weight.shape[1]
    input_weight_grad = chain_b[:, :three]
    output_weight_grad = chain_b[:, three : three + width]
    qb_grad = chain_b[:, three + width]
    vb_grad = chain_b[:, three + width + 1]
    ob_grad = chain_b[:, three + width + 2]
    expand_weight_grad = chain_a[:, :fw]
    contract_weight_grad = chain_a[:, fw : fw + split * width].reshape(-1, split, width)
    contract_weight_grad = contract_weight_grad.transpose(1, 0, 2).reshape(-1, width)
    cb_grad = chain_b[:, three + width + 3]
    eb_grad = chain_b[:, three + width + 4 : three + width + 4 + split].T.reshape(-1)
    summed = (
        input_weight_grad,
        qb_grad,
        vb_grad,
        output_weight_grad,
        ob_grad,
        expand_weight_grad,
        eb_grad,
        contract_weight_grad,
        cb_grad,
    )
    return (
        layer_out,
        tokens_grad,
        condition_grad,
        modulation_weight_grad,
        modulation_bias_grad,
        *summed,
    )


def solution(mesh):
    dp_size, mod_size = mesh.devices.shape
    rest = dp_size // 4
    side = int(round(rest ** 0.5))
    shape = (side, 2, rest // side, 2, mod_size)
    sizes = dict(zip(AXES, shape))
    physical = Mesh(np.asarray(mesh.devices).reshape(shape), AXES)
    ALL = AXES
    placed = (
        P(ALL, None, None),
        P(ALL, None),
        P(ALL),
        P(None, "zl"),
        P("zl", None),
        P(),
        P(),
        P(),
        P(),
        P(),
        P(),
        P(),
        P(),
        P(),
        P(ALL, None, None),
    )
    return jax.shard_map(
        functools.partial(per_device, sizes),
        mesh=physical,
        in_specs=placed,
        out_specs=(
            P(ALL, None, None),
            P(ALL, None, None),
            P(ALL, None),
            P(DP, "zl"),
            P("zl", DP),
            P(ALL, None),
            P(ALL),
            P(ALL),
            P(ALL, None),
            P(ALL),
            P(ALL, None),
            P(ALL),
            P(ALL, None),
            P(ALL),
        ),
        check_vma=False,
    )
```

```python
import functools

import jax
import jax.numpy as jnp
import numpy as np
from jax import lax
from jax.experimental import pallas as pl
from jax.experimental.pallas import tpu as pltpu
from jax.sharding import Mesh
from jax.sharding import PartitionSpec as P

HEAD_DIM = 64
LANES = 128


def _nt(a, b):
    return lax.dot_general(a, b, (((1,), (1,)), ((), ())), preferred_element_type=jnp.float32)


def _tn(a, b):
    return lax.dot_general(a, b, (((0,), (0,)), ((), ())), preferred_element_type=jnp.float32)


def _probs(q, k, head, factor):
    lane = lax.broadcasted_iota(jnp.int32, (1, LANES), 1)
    mine = (lane // HEAD_DIM) == head
    qh = jnp.where(mine, q, jnp.zeros_like(q))
    scores = _nt(qh, k) * factor
    weights = jnp.exp(scores - jnp.max(scores, axis=-1, keepdims=True))
    return mine, qh, weights / jnp.sum(weights, axis=-1, keepdims=True)


def _fwd_kernel(factor, q_ref, k_ref, v_ref, o_ref):
    def pair(j, carry):
        cols = pl.ds(pl.multiple_of(j * LANES, LANES), LANES)
        q = q_ref[:, cols]
        k = k_ref[:, cols]
        v = v_ref[:, cols]
        out = jnp.zeros((q.shape[0], LANES), jnp.float32)
        for head in range(LANES // HEAD_DIM):
            mine, _, probs = _probs(q, k, head, factor)
            vh = jnp.where(mine, v, jnp.zeros_like(v))
            out = out + jnp.dot(probs.astype(v.dtype), vh, preferred_element_type=jnp.float32)
        o_ref[:, cols] = out.astype(o_ref.dtype)
        return carry

    lax.fori_loop(0, o_ref.shape[1] // LANES, pair, 0, unroll=4)


def _bwd_kernel(factor, q_ref, k_ref, v_ref, d_ref, dq_ref, dk_ref, dv_ref):
    def pair(j, carry):
        cols = pl.ds(pl.multiple_of(j * LANES, LANES), LANES)
        q = q_ref[:, cols]
        k = k_ref[:, cols]
        v = v_ref[:, cols]
        d = d_ref[:, cols]
        dq = jnp.zeros((q.shape[0], LANES), jnp.float32)
        dk = jnp.zeros((q.shape[0], LANES), jnp.float32)
        dv = jnp.zeros((q.shape[0], LANES), jnp.float32)
        for head in range(LANES // HEAD_DIM):
            mine, qh, probs = _probs(q, k, head, factor)
            dh = jnp.where(mine, d, jnp.zeros_like(d))
            kh = jnp.where(mine, k, jnp.zeros_like(k))
            dprobs = _nt(dh, v)
            dv = dv + _tn(probs.astype(d.dtype), dh)
            inner = jnp.sum(dprobs * probs, axis=-1, keepdims=True)
            dscores = (probs * (dprobs - inner)).astype(q.dtype)
            dq = dq + jnp.dot(dscores, kh, preferred_element_type=jnp.float32)
            dk = dk + _tn(dscores, qh)
        dq_ref[:, cols] = (dq * factor).astype(dq_ref.dtype)
        dk_ref[:, cols] = (dk * factor).astype(dk_ref.dtype)
        dv_ref[:, cols] = dv.astype(dv_ref.dtype)
        return carry

    lax.fori_loop(0, dq_ref.shape[1] // LANES, pair, 0, unroll=4)


def _wgrad_kernel(expand_tiles, modb_ref, du_ref, act_ref, dz_ref, out_ref):
    j = pl.program_id(0)

    @pl.when(j < expand_tiles)
    def _():
        out_ref[...] = jnp.dot(
            modb_ref[...], du_ref[...], preferred_element_type=jnp.float32
        ).astype(out_ref.dtype)

    @pl.when(j >= expand_tiles)
    def _():
        out_ref[...] = jnp.dot(
            act_ref[...], dz_ref[...], preferred_element_type=jnp.float32
        ).astype(out_ref.dtype)


def ffn_weight_grads(mod_t, grad_exp, act_t, grad_branch, tile=1024):
    width, tokens = mod_t.shape
    ff = grad_exp.shape[1]
    expand_tiles = ff // tile
    per_part = width // tile
    tiles = expand_tiles + (ff // width) * per_part

    def act_index(j):
        return (jnp.maximum(j - expand_tiles, 0) // per_part, 0)

    def dz_index(j):
        return (0, jnp.maximum(j - expand_tiles, 0) % per_part)

    return pl.pallas_call(
        functools.partial(_wgrad_kernel, expand_tiles),
        out_shape=jax.ShapeDtypeStruct((width, tiles * tile), jnp.bfloat16),
        grid=(tiles,),
        in_specs=[
            pl.BlockSpec((width, tokens), lambda j: (0, 0)),
            pl.BlockSpec((tokens, tile), lambda j: (0, jnp.minimum(j, expand_tiles - 1))),
            pl.BlockSpec((width, tokens), act_index),
            pl.BlockSpec((tokens, tile), dz_index),
        ],
        out_specs=pl.BlockSpec((width, tile), lambda j: (0, j)),
        compiler_params=pltpu.CompilerParams(dimension_semantics=("arbitrary",)),
        cost_estimate=pl.CostEstimate(
            flops=2 * tokens * width * tiles * tile,
            transcendentals=0,
            bytes_accessed=2 * (tokens * (width + 2 * ff + width) + width * tiles * tile),
        ),
    )(mod_t, grad_exp, act_t, grad_branch)

def attention_forward(projected, images):
    tokens, three = projected.shape
    rows, width = tokens // images, three // 3
    pairs = width // LANES
    factor = HEAD_DIM ** (-0.5)

    def part(offset):
        return pl.BlockSpec((rows, width), lambda b: (b, offset))

    flops = 2 * 2 * images * (width // HEAD_DIM) * rows * rows * LANES
    return pl.pallas_call(
        functools.partial(_fwd_kernel, factor),
        out_shape=jax.ShapeDtypeStruct((tokens, width), projected.dtype),
        grid=(images,),
        in_specs=[part(0), part(1), part(2)],
        out_specs=part(0),
        compiler_params=pltpu.CompilerParams(dimension_semantics=("parallel",)),
        cost_estimate=pl.CostEstimate(
            flops=flops, transcendentals=images * (width // HEAD_DIM) * rows * rows,
            bytes_accessed=2 * tokens * (three + width),
        ),
    )(projected, projected, projected)


def attention_backward(projected, grad_attended, images):
    tokens, three = projected.shape
    rows, width = tokens // images, three // 3
    pairs = width // LANES
    factor = HEAD_DIM ** (-0.5)

    def part(offset):
        return pl.BlockSpec((rows, width), lambda b: (b, offset))

    out = jax.ShapeDtypeStruct((tokens, width), projected.dtype)
    flops = 5 * 2 * 2 * images * (width // HEAD_DIM) * rows * rows * LANES
    dq, dk, dv = pl.pallas_call(
        functools.partial(_bwd_kernel, factor),
        out_shape=(out, out, out),
        grid=(images,),
        in_specs=[part(0), part(1), part(2), part(0)],
        out_specs=[part(0)] * 3,
        compiler_params=pltpu.CompilerParams(dimension_semantics=("parallel",)),
        cost_estimate=pl.CostEstimate(
            flops=flops, transcendentals=images * (width // HEAD_DIM) * rows * rows,
            bytes_accessed=2 * tokens * (three + 4 * width),
        ),
    )(projected, projected, projected, grad_attended)
    return jnp.concatenate([dq, dk, dv], axis=1)


EPS = 1e-06
GELU_C = 0.7978845608028654

AXES = ("y", "zh", "x", "c", "zl")
DP = ("y", "zh", "x", "c")
STAGES = ("c", "x", "y", "zh", "zl")
STAGES_B = ("c", "y", "x", "zh", "zl")


def matmul(left, right):
    return jnp.dot(left, right, preferred_element_type=jnp.float32)


def left_trans(left, right):
    return lax.dot_general(
        left, right, (((0,), (0,)), ((), ())), preferred_element_type=jnp.float32
    )


def right_trans(left, right):
    return lax.dot_general(
        left, right, (((1,), (1,)), ((), ())), preferred_element_type=jnp.float32
    )


def normalize(values):
    centre = values - jnp.mean(values, axis=-1, keepdims=True)
    inverse = lax.rsqrt(jnp.mean(centre * centre, axis=-1, keepdims=True) + EPS)
    return (centre * inverse, inverse)


def norm_back(grad, normed, inverse):
    return inverse * (
        grad
        - jnp.mean(grad, axis=-1, keepdims=True)
        - normed * jnp.mean(grad * normed, axis=-1, keepdims=True)
    )


def stage_order(values, sizes, inner, stages=STAGES):
    lead = values.shape[:-1]
    shape = [sizes[a] for a in AXES]
    values = values.reshape(*lead, *shape, inner)
    n = len(lead)
    order = list(range(n)) + [n + AXES.index(a) for a in stages] + [n + len(AXES)]
    return jnp.transpose(values, order).reshape(*lead, -1)


def reduce_stages(packed, stages):
    for a in stages:
        packed = lax.psum_scatter(packed, a, scatter_dimension=0, tiled=True)
    return packed


def reduce_pair(packed, axis):
    half = packed.shape[0] // 2
    index = lax.axis_index(axis)
    keep = lax.dynamic_slice_in_dim(packed, index * half, half, axis=0)
    send = lax.dynamic_slice_in_dim(packed, (1 - index) * half, half, axis=0)
    got = lax.ppermute(send, axis, [(0, 1), (1, 0)])
    return (keep.astype(jnp.float32) + got.astype(jnp.float32)).astype(packed.dtype)


def reduce_rest(packed, axes):
    count = 1
    for a in axes:
        count *= lax.axis_size(a)
    chunks = packed.reshape(count, packed.shape[0] // count, packed.shape[1])
    chunks = lax.all_to_all(chunks, axes, 0, 0, tiled=False)
    return jnp.sum(chunks.astype(jnp.float32), axis=0)


def bias_columns(columns, rows):
    block = jnp.stack(columns, axis=1)
    return jnp.pad(block, ((0, 0), (0, 128 - block.shape[1]))).astype(jnp.bfloat16)


def gather_dp(values):
    count = 1
    for a in DP:
        count *= lax.axis_size(a)
    copies = jnp.broadcast_to(values[None], (count,) + values.shape)
    return lax.all_to_all(copies, DP, 0, 0, tiled=False).reshape(-1, values.shape[1])


def per_device(
    sizes,
    tokens,
    condition,
    occupied,
    modulation_weight,
    modulation_bias,
    input_weight,
    query_bias,
    value_bias,
    output_weight,
    output_bias,
    expand_weight,
    expand_bias,
    contract_weight,
    contract_bias,
    cotangent,
):
    images, rows, width = tokens.shape
    heads = width // HEAD_DIM
    flat = images * rows
    factor = HEAD_DIM ** (-0.5)
    cond_full = condition.astype(jnp.float32)
    sigmoid = jax.nn.sigmoid(cond_full)
    silu_b = (cond_full * sigmoid).astype(jnp.bfloat16)
    silu_pair = lax.all_gather(silu_b, "zl", axis=0, tiled=True)
    mod_cols = matmul(silu_pair, modulation_weight) + modulation_bias.reshape(1, -1)
    modulation = lax.all_to_all(mod_cols, "zl", split_axis=0, concat_axis=1, tiled=True).reshape(
        images, 6, 1, width
    )
    shift_a = modulation[:, 0]
    scale_a = modulation[:, 1]
    gate_a = modulation[:, 2]
    shift_b = modulation[:, 3]
    scale_b = modulation[:, 4]
    gate_b = modulation[:, 5]
    inputs = tokens.astype(jnp.float32)
    normed_a, inverse_a = normalize(inputs)
    mod_a = (normed_a * (1.0 + scale_a) + shift_a).astype(jnp.bfloat16).reshape(flat, width)
    qkv_bias = jnp.concatenate([query_bias, jnp.zeros_like(query_bias), value_bias])
    projected = (matmul(mod_a, input_weight) + qkv_bias).astype(jnp.bfloat16)
    attended_b = attention_forward(projected, images)
    branch_a = (matmul(attended_b, output_weight) + output_bias).reshape(images, rows, width)
    middle = inputs + gate_a * branch_a
    normed_b, inverse_b = normalize(middle)
    mod_b = (normed_b * (1.0 + scale_b) + shift_b).astype(jnp.bfloat16).reshape(flat, width)
    expanded = matmul(mod_b, expand_weight) + expand_bias
    tanh_part = jnp.tanh(GELU_C * (expanded + 0.044715 * expanded * expanded * expanded))
    activated_b = (0.5 * expanded * (1.0 + tanh_part)).astype(jnp.bfloat16)
    branch_b = (matmul(activated_b, contract_weight) + contract_bias).reshape(images, rows, width)
    alive = occupied.astype(jnp.float32)[:, None, None]
    layer_out = (middle + gate_b * branch_b) * alive
    grad_out = cotangent.astype(jnp.float32) * alive
    grad_gate_b = jnp.sum(grad_out * branch_b, axis=1)
    grad_branch_b = (grad_out * gate_b).astype(jnp.bfloat16).reshape(flat, width)
    blocks = 1
    for a in AXES:
        blocks *= sizes[a]
    ff = activated_b.shape[1]
    split = ff // width
    act_perm = stage_order(
        activated_b.reshape(flat, blocks, split, width // blocks)
        .transpose(0, 2, 1, 3)
        .reshape(flat, split, width),
        sizes,
        width // blocks,
    )
    contract_bias_grad = stage_order(
        jnp.sum(grad_branch_b.astype(jnp.float32), axis=0), sizes, width // blocks, STAGES_B
    )
    grad_act = right_trans(grad_branch_b, contract_weight)
    slope = 0.5 * (1.0 + tanh_part) + 0.5 * expanded * (1.0 - tanh_part * tanh_part) * GELU_C * (
        1.0 + 3.0 * 0.044715 * expanded * expanded
    )
    grad_exp_b = (grad_act * slope).astype(jnp.bfloat16)
    expand_bias_grad = stage_order(
        jnp.sum(grad_exp_b.astype(jnp.float32), axis=0)
        .reshape(blocks, split, width // blocks)
        .transpose(1, 0, 2)
        .reshape(split, width),
        sizes,
        width // blocks,
        STAGES_B,
    )
    packed_a = ffn_weight_grads(
        stage_order(mod_b, sizes, width // blocks).T, grad_exp_b, act_perm.reshape(flat, -1).T, grad_branch_b
    )
    packed_a, grad_exp_b = lax.optimization_barrier((packed_a, grad_exp_b))
    chain_a = reduce_stages(packed_a, STAGES[:1])
    grad_mod_b = right_trans(grad_exp_b, expand_weight).reshape(images, rows, width)
    grad_shift_b = jnp.sum(grad_mod_b, axis=1)
    grad_scale_b = jnp.sum(grad_mod_b * normed_b, axis=1)
    grad_middle = grad_out + norm_back(grad_mod_b * (1.0 + scale_b), normed_b, inverse_b)
    grad_gate_a = jnp.sum(grad_middle * branch_a, axis=1)
    grad_branch_a = (grad_middle * gate_a).astype(jnp.bfloat16).reshape(flat, width)
    output_grad = left_trans(stage_order(attended_b, sizes, width // blocks, STAGES_B), grad_branch_a).astype(
        jnp.bfloat16
    )
    output_bias_grad = stage_order(
        jnp.sum(grad_branch_a.astype(jnp.float32), axis=0), sizes, width // blocks, STAGES_B
    )
    grad_att_b = right_trans(grad_branch_a, output_weight).astype(jnp.bfloat16)
    chain_a, grad_att_b = lax.optimization_barrier((chain_a, grad_att_b))
    chain_a = reduce_stages(chain_a, STAGES[1:2])
    grad_proj_b = attention_backward(projected, grad_att_b, images)
    input_grad = left_trans(stage_order(mod_a, sizes, width // blocks, STAGES_B), grad_proj_b).astype(
        jnp.bfloat16
    )
    bias_sums = jnp.sum(grad_proj_b.astype(jnp.float32), axis=0)
    query_bias_grad = stage_order(bias_sums[:width], sizes, width // blocks, STAGES_B)
    value_bias_grad = stage_order(bias_sums[2 * width :], sizes, width // blocks, STAGES_B)
    chain_b = reduce_pair(
        jnp.concatenate(
            [
                input_grad,
                output_grad,
                bias_columns(
                [query_bias_grad, value_bias_grad, output_bias_grad, contract_bias_grad]
                + [expand_bias_grad[q] for q in range(split)],
                width,
            ),
            ],
            axis=1,
        ),
        STAGES_B[0],
    )
    chain_a, chain_b = lax.optimization_barrier((chain_a, chain_b))
    chain_b = reduce_stages(chain_b, STAGES_B[1:2])
    grad_mod_a = right_trans(grad_proj_b, input_weight).reshape(images, rows, width)
    grad_shift_a = jnp.sum(grad_mod_a, axis=1)
    grad_scale_a = jnp.sum(grad_mod_a * normed_a, axis=1)
    tokens_grad = grad_middle + norm_back(grad_mod_a * (1.0 + scale_a), normed_a, inverse_a)
    modulation_terms = jnp.stack(
        [grad_shift_a, grad_scale_a, grad_gate_a, grad_shift_b, grad_scale_b, grad_gate_b], axis=1
    ).reshape(images, 6 * width)
    modulation_own = modulation_terms.astype(jnp.bfloat16)
    modulation_cols = lax.all_to_all(modulation_own, "zl", split_axis=1, concat_axis=0, tiled=True)
    silu_terms = right_trans(modulation_cols, modulation_weight)
    pair_index = lax.axis_index("zl")
    own_rows = lax.dynamic_slice_in_dim(silu_terms, pair_index * images, images, axis=0)
    other_rows = lax.dynamic_slice_in_dim(silu_terms, (1 - pair_index) * images, images, axis=0)
    silu_sums = own_rows + lax.ppermute(other_rows, "zl", [(0, 1), (1, 0)])
    condition_grad = silu_sums * sigmoid * (1.0 + cond_full * (1.0 - sigmoid))
    dp_count = lax.axis_size(DP)
    row_block = width // dp_count
    silu_parts = silu_pair.reshape(-1, dp_count, row_block).transpose(1, 0, 2)
    silu_parts = jnp.pad(silu_parts, ((0, 0), (0, 0), (0, 128 - row_block)))
    payload = jnp.concatenate(
        [jnp.broadcast_to(modulation_cols[None], (dp_count,) + modulation_cols.shape), silu_parts], axis=2
    )
    factors = lax.all_to_all(payload, DP, 0, 0, tiled=False)
    mod_all = factors[:, :, : modulation_cols.shape[1]].reshape(-1, modulation_cols.shape[1])
    silu_rows = factors[:, :, modulation_cols.shape[1] : modulation_cols.shape[1] + row_block]
    silu_rows = silu_rows.reshape(-1, row_block)
    dp_index = lax.axis_index(DP)
    modulation_weight_grad = left_trans(silu_rows, mod_all)
    bias_all = jnp.sum(mod_all.astype(jnp.float32), axis=0).reshape(-1, width)
    modulation_bias_grad = lax.dynamic_slice_in_dim(bias_all, dp_index * row_block, row_block, axis=1)
    chain_a = reduce_rest(chain_a, STAGES[2:])
    chain_b, mod_all = lax.optimization_barrier((chain_b, mod_all))
    chain_b = reduce_rest(chain_b, STAGES_B[2:])
    three = input_weight.shape[1]
    fw = expand_weight.shape[1]
    input_weight_grad = chain_b[:, :three]
    output_weight_grad = chain_b[:, three : three + width]
    qb_grad = chain_b[:, three + width]
    vb_grad = chain_b[:, three + width + 1]
    ob_grad = chain_b[:, three + width + 2]
    expand_weight_grad = chain_a[:, :fw]
    contract_weight_grad = chain_a[:, fw : fw + split * width].reshape(-1, split, width)
    contract_weight_grad = contract_weight_grad.transpose(1, 0, 2).reshape(-1, width)
    cb_grad = chain_b[:, three + width + 3]
    eb_grad = chain_b[:, three + width + 4 : three + width + 4 + split].T.reshape(-1)
    summed = (
        input_weight_grad,
        qb_grad,
        vb_grad,
        output_weight_grad,
        ob_grad,
        expand_weight_grad,
        eb_grad,
        contract_weight_grad,
        cb_grad,
    )
    return (
        layer_out,
        tokens_grad,
        condition_grad,
        modulation_weight_grad,
        modulation_bias_grad,
        *summed,
    )


def solution(mesh):
    dp_size, mod_size = mesh.devices.shape
    rest = dp_size // 4
    side = int(round(rest ** 0.5))
    shape = (side, 2, rest // side, 2, mod_size)
    sizes = dict(zip(AXES, shape))
    physical = Mesh(np.asarray(mesh.devices).reshape(shape), AXES)
    ALL = AXES
    placed = (
        P(ALL, None, None),
        P(ALL, None),
        P(ALL),
        P(None, "zl"),
        P("zl", None),
        P(),
        P(),
        P(),
        P(),
        P(),
        P(),
        P(),
        P(),
        P(),
        P(ALL, None, None),
    )
    return jax.shard_map(
        functools.partial(per_device, sizes),
        mesh=physical,
        in_specs=placed,
        out_specs=(
            P(ALL, None, None),
            P(ALL, None, None),
            P(ALL, None),
            P(DP, "zl"),
            P("zl", DP),
            P(ALL, None),
            P(ALL),
            P(ALL),
            P(ALL, None),
            P(ALL),
            P(ALL, None),
            P(ALL),
            P(ALL, None),
            P(ALL),
        ),
        check_vma=False,
    )
```

```python
import functools

import jax
import jax.numpy as jnp
import numpy as np
from jax import lax
from jax.experimental import pallas as pl
from jax.experimental.pallas import tpu as pltpu
from jax.sharding import Mesh
from jax.sharding import PartitionSpec as P

HEAD_DIM = 64
LANES = 128


def _nt(a, b):
    return lax.dot_general(a, b, (((1,), (1,)), ((), ())), preferred_element_type=jnp.float32)


def _tn(a, b):
    return lax.dot_general(a, b, (((0,), (0,)), ((), ())), preferred_element_type=jnp.float32)


def _probs(q, k, head, factor):
    lane = lax.broadcasted_iota(jnp.int32, (1, LANES), 1)
    mine = (lane // HEAD_DIM) == head
    qh = jnp.where(mine, q, jnp.zeros_like(q))
    scores = _nt(qh, k) * factor
    weights = jnp.exp(scores - jnp.max(scores, axis=-1, keepdims=True))
    return mine, qh, weights / jnp.sum(weights, axis=-1, keepdims=True)


def _fwd_kernel(factor, q_ref, k_ref, v_ref, o_ref):
    def pair(j, carry):
        cols = pl.ds(pl.multiple_of(j * LANES, LANES), LANES)
        q = q_ref[:, cols]
        k = k_ref[:, cols]
        v = v_ref[:, cols]
        out = jnp.zeros((q.shape[0], LANES), jnp.float32)
        for head in range(LANES // HEAD_DIM):
            mine, _, probs = _probs(q, k, head, factor)
            vh = jnp.where(mine, v, jnp.zeros_like(v))
            out = out + jnp.dot(probs.astype(v.dtype), vh, preferred_element_type=jnp.float32)
        o_ref[:, cols] = out.astype(o_ref.dtype)
        return carry

    lax.fori_loop(0, o_ref.shape[1] // LANES, pair, 0, unroll=4)


def _bwd_kernel(factor, q_ref, k_ref, v_ref, d_ref, dq_ref, dk_ref, dv_ref):
    def pair(j, carry):
        cols = pl.ds(pl.multiple_of(j * LANES, LANES), LANES)
        q = q_ref[:, cols]
        k = k_ref[:, cols]
        v = v_ref[:, cols]
        d = d_ref[:, cols]
        dq = jnp.zeros((q.shape[0], LANES), jnp.float32)
        dk = jnp.zeros((q.shape[0], LANES), jnp.float32)
        dv = jnp.zeros((q.shape[0], LANES), jnp.float32)
        for head in range(LANES // HEAD_DIM):
            mine, qh, probs = _probs(q, k, head, factor)
            dh = jnp.where(mine, d, jnp.zeros_like(d))
            kh = jnp.where(mine, k, jnp.zeros_like(k))
            dprobs = _nt(dh, v)
            dv = dv + _tn(probs.astype(d.dtype), dh)
            inner = jnp.sum(dprobs * probs, axis=-1, keepdims=True)
            dscores = (probs * (dprobs - inner)).astype(q.dtype)
            dq = dq + jnp.dot(dscores, kh, preferred_element_type=jnp.float32)
            dk = dk + _tn(dscores, qh)
        dq_ref[:, cols] = (dq * factor).astype(dq_ref.dtype)
        dk_ref[:, cols] = (dk * factor).astype(dk_ref.dtype)
        dv_ref[:, cols] = dv.astype(dv_ref.dtype)
        return carry

    lax.fori_loop(0, dq_ref.shape[1] // LANES, pair, 0, unroll=4)


def _wgrad_kernel(expand_tiles, modb_ref, du_ref, act_ref, dz_ref, out_ref):
    j = pl.program_id(0)

    @pl.when(j < expand_tiles)
    def _():
        out_ref[...] = jnp.dot(
            modb_ref[...], du_ref[...], preferred_element_type=jnp.float32
        ).astype(out_ref.dtype)

    @pl.when(j >= expand_tiles)
    def _():
        out_ref[...] = jnp.dot(
            act_ref[...], dz_ref[...], preferred_element_type=jnp.float32
        ).astype(out_ref.dtype)


def ffn_weight_grads(mod_t, grad_exp, act_t, grad_branch, tile=1024):
    width, tokens = mod_t.shape
    ff = grad_exp.shape[1]
    expand_tiles = ff // tile
    per_part = width // tile
    tiles = expand_tiles + (ff // width) * per_part

    def act_index(j):
        return (jnp.maximum(j - expand_tiles, 0) // per_part, 0)

    def dz_index(j):
        return (0, jnp.maximum(j - expand_tiles, 0) % per_part)

    return pl.pallas_call(
        functools.partial(_wgrad_kernel, expand_tiles),
        out_shape=jax.ShapeDtypeStruct((width, tiles * tile), jnp.bfloat16),
        grid=(tiles,),
        in_specs=[
            pl.BlockSpec((width, tokens), lambda j: (0, 0)),
            pl.BlockSpec((tokens, tile), lambda j: (0, jnp.minimum(j, expand_tiles - 1))),
            pl.BlockSpec((width, tokens), act_index),
            pl.BlockSpec((tokens, tile), dz_index),
        ],
        out_specs=pl.BlockSpec((width, tile), lambda j: (0, j)),
        compiler_params=pltpu.CompilerParams(dimension_semantics=("arbitrary",)),
        cost_estimate=pl.CostEstimate(
            flops=2 * tokens * width * tiles * tile,
            transcendentals=0,
            bytes_accessed=2 * (tokens * (width + 2 * ff + width) + width * tiles * tile),
        ),
    )(mod_t, grad_exp, act_t, grad_branch)

def attention_forward(projected, images):
    tokens, three = projected.shape
    rows, width = tokens // images, three // 3
    pairs = width // LANES
    factor = HEAD_DIM ** (-0.5)

    def part(offset):
        return pl.BlockSpec((rows, width), lambda b: (b, offset))

    flops = 2 * 2 * images * (width // HEAD_DIM) * rows * rows * LANES
    return pl.pallas_call(
        functools.partial(_fwd_kernel, factor),
        out_shape=jax.ShapeDtypeStruct((tokens, width), projected.dtype),
        grid=(images,),
        in_specs=[part(0), part(1), part(2)],
        out_specs=part(0),
        compiler_params=pltpu.CompilerParams(dimension_semantics=("parallel",)),
        cost_estimate=pl.CostEstimate(
            flops=flops, transcendentals=images * (width // HEAD_DIM) * rows * rows,
            bytes_accessed=2 * tokens * (three + width),
        ),
    )(projected, projected, projected)


def attention_backward(projected, grad_attended, images):
    tokens, three = projected.shape
    rows, width = tokens // images, three // 3
    pairs = width // LANES
    factor = HEAD_DIM ** (-0.5)

    def part(offset):
        return pl.BlockSpec((rows, width), lambda b: (b, offset))

    out = jax.ShapeDtypeStruct((tokens, width), projected.dtype)
    flops = 5 * 2 * 2 * images * (width // HEAD_DIM) * rows * rows * LANES
    dq, dk, dv = pl.pallas_call(
        functools.partial(_bwd_kernel, factor),
        out_shape=(out, out, out),
        grid=(images,),
        in_specs=[part(0), part(1), part(2), part(0)],
        out_specs=[part(0)] * 3,
        compiler_params=pltpu.CompilerParams(dimension_semantics=("parallel",)),
        cost_estimate=pl.CostEstimate(
            flops=flops, transcendentals=images * (width // HEAD_DIM) * rows * rows,
            bytes_accessed=2 * tokens * (three + 4 * width),
        ),
    )(projected, projected, projected, grad_attended)
    return jnp.concatenate([dq, dk, dv], axis=1)


EPS = 1e-06
GELU_C = 0.7978845608028654

AXES = ("y", "zh", "x", "c", "zl")
DP = ("y", "zh", "x", "c")
STAGES = ("c", "x", "y", "zh", "zl")
STAGES_B = ("c", "y", "x", "zh", "zl")


def matmul(left, right):
    return jnp.dot(left, right, preferred_element_type=jnp.float32)


def left_trans(left, right):
    return lax.dot_general(
        left, right, (((0,), (0,)), ((), ())), preferred_element_type=jnp.float32
    )


def right_trans(left, right):
    return lax.dot_general(
        left, right, (((1,), (1,)), ((), ())), preferred_element_type=jnp.float32
    )


def normalize(values):
    centre = values - jnp.mean(values, axis=-1, keepdims=True)
    inverse = lax.rsqrt(jnp.mean(centre * centre, axis=-1, keepdims=True) + EPS)
    return (centre * inverse, inverse)


def norm_back(grad, normed, inverse):
    return inverse * (
        grad
        - jnp.mean(grad, axis=-1, keepdims=True)
        - normed * jnp.mean(grad * normed, axis=-1, keepdims=True)
    )


def stage_order(values, sizes, inner, stages=STAGES):
    lead = values.shape[:-1]
    shape = [sizes[a] for a in AXES]
    values = values.reshape(*lead, *shape, inner)
    n = len(lead)
    order = list(range(n)) + [n + AXES.index(a) for a in stages] + [n + len(AXES)]
    return jnp.transpose(values, order).reshape(*lead, -1)


def reduce_stages(packed, stages):
    for a in stages:
        packed = lax.psum_scatter(packed, a, scatter_dimension=0, tiled=True)
    return packed


def reduce_pair(packed, axis):
    half = packed.shape[0] // 2
    index = lax.axis_index(axis)
    keep = lax.dynamic_slice_in_dim(packed, index * half, half, axis=0)
    send = lax.dynamic_slice_in_dim(packed, (1 - index) * half, half, axis=0)
    got = lax.ppermute(send, axis, [(0, 1), (1, 0)])
    return (keep.astype(jnp.float32) + got.astype(jnp.float32)).astype(packed.dtype)


def reduce_rest(packed, axes):
    count = 1
    for a in axes:
        count *= lax.axis_size(a)
    chunks = packed.reshape(count, packed.shape[0] // count, packed.shape[1])
    chunks = lax.all_to_all(chunks, axes, 0, 0, tiled=False)
    return jnp.sum(chunks.astype(jnp.float32), axis=0)


def bias_columns(columns, rows):
    block = jnp.stack(columns, axis=1)
    return jnp.pad(block, ((0, 0), (0, 128 - block.shape[1]))).astype(jnp.bfloat16)


def gather_dp(values):
    count = 1
    for a in DP:
        count *= lax.axis_size(a)
    copies = jnp.broadcast_to(values[None], (count,) + values.shape)
    return lax.all_to_all(copies, DP, 0, 0, tiled=False).reshape(-1, values.shape[1])


def per_device(
    sizes,
    tokens,
    condition,
    occupied,
    modulation_weight,
    modulation_bias,
    input_weight,
    query_bias,
    value_bias,
    output_weight,
    output_bias,
    expand_weight,
    expand_bias,
    contract_weight,
    contract_bias,
    cotangent,
):
    images, rows, width = tokens.shape
    heads = width // HEAD_DIM
    flat = images * rows
    factor = HEAD_DIM ** (-0.5)
    cond_full = condition.astype(jnp.float32)
    sigmoid = jax.nn.sigmoid(cond_full)
    silu_b = (cond_full * sigmoid).astype(jnp.bfloat16)
    silu_pair = lax.all_gather(silu_b, "zl", axis=0, tiled=True)
    mod_cols = matmul(silu_pair, modulation_weight) + modulation_bias.reshape(1, -1)
    modulation = lax.all_to_all(mod_cols, "zl", split_axis=0, concat_axis=1, tiled=True).reshape(
        images, 6, 1, width
    )
    shift_a = modulation[:, 0]
    scale_a = modulation[:, 1]
    gate_a = modulation[:, 2]
    shift_b = modulation[:, 3]
    scale_b = modulation[:, 4]
    gate_b = modulation[:, 5]
    inputs = tokens.astype(jnp.float32)
    normed_a, inverse_a = normalize(inputs)
    mod_a = (normed_a * (1.0 + scale_a) + shift_a).astype(jnp.bfloat16).reshape(flat, width)
    qkv_bias = jnp.concatenate([query_bias, jnp.zeros_like(query_bias), value_bias])
    projected = (matmul(mod_a, input_weight) + qkv_bias).astype(jnp.bfloat16)
    attended_b = attention_forward(projected, images)
    branch_a = (matmul(attended_b, output_weight) + output_bias).reshape(images, rows, width)
    middle = inputs + gate_a * branch_a
    normed_b, inverse_b = normalize(middle)
    mod_b = (normed_b * (1.0 + scale_b) + shift_b).astype(jnp.bfloat16).reshape(flat, width)
    expanded = matmul(mod_b, expand_weight) + expand_bias
    tanh_part = jnp.tanh(GELU_C * (expanded + 0.044715 * expanded * expanded * expanded))
    activated_b = (0.5 * expanded * (1.0 + tanh_part)).astype(jnp.bfloat16)
    branch_b = (matmul(activated_b, contract_weight) + contract_bias).reshape(images, rows, width)
    alive = occupied.astype(jnp.float32)[:, None, None]
    layer_out = (middle + gate_b * branch_b) * alive
    grad_out = cotangent.astype(jnp.float32) * alive
    grad_gate_b = jnp.sum(grad_out * branch_b, axis=1)
    grad_branch_b = (grad_out * gate_b).astype(jnp.bfloat16).reshape(flat, width)
    blocks = 1
    for a in AXES:
        blocks *= sizes[a]
    ff = activated_b.shape[1]
    split = ff // width
    act_perm = stage_order(
        activated_b.reshape(flat, blocks, split, width // blocks)
        .transpose(0, 2, 1, 3)
        .reshape(flat, split, width),
        sizes,
        width // blocks,
    )
    contract_bias_grad = stage_order(
        jnp.sum(grad_branch_b.astype(jnp.float32), axis=0), sizes, width // blocks, STAGES_B
    )
    grad_act = right_trans(grad_branch_b, contract_weight)
    slope = 0.5 * (1.0 + tanh_part) + 0.5 * expanded * (1.0 - tanh_part * tanh_part) * GELU_C * (
        1.0 + 3.0 * 0.044715 * expanded * expanded
    )
    grad_exp_b = (grad_act * slope).astype(jnp.bfloat16)
    expand_bias_grad = stage_order(
        jnp.sum(grad_exp_b.astype(jnp.float32), axis=0)
        .reshape(blocks, split, width // blocks)
        .transpose(1, 0, 2)
        .reshape(split, width),
        sizes,
        width // blocks,
        STAGES_B,
    )
    packed_a = ffn_weight_grads(
        stage_order(mod_b, sizes, width // blocks).T, grad_exp_b, act_perm.reshape(flat, -1).T, grad_branch_b
    )
    packed_a, grad_exp_b = lax.optimization_barrier((packed_a, grad_exp_b))
    chain_a = reduce_stages(packed_a, STAGES[:1])
    grad_mod_b = right_trans(grad_exp_b, expand_weight).reshape(images, rows, width)
    grad_shift_b = jnp.sum(grad_mod_b, axis=1)
    grad_scale_b = jnp.sum(grad_mod_b * normed_b, axis=1)
    grad_middle = grad_out + norm_back(grad_mod_b * (1.0 + scale_b), normed_b, inverse_b)
    grad_gate_a = jnp.sum(grad_middle * branch_a, axis=1)
    grad_branch_a = (grad_middle * gate_a).astype(jnp.bfloat16).reshape(flat, width)
    output_grad = left_trans(stage_order(attended_b, sizes, width // blocks, STAGES_B), grad_branch_a).astype(
        jnp.bfloat16
    )
    output_bias_grad = stage_order(
        jnp.sum(grad_branch_a.astype(jnp.float32), axis=0), sizes, width // blocks, STAGES_B
    )
    grad_att_b = right_trans(grad_branch_a, output_weight).astype(jnp.bfloat16)
    chain_a, grad_att_b = lax.optimization_barrier((chain_a, grad_att_b))
    chain_a = reduce_stages(chain_a, STAGES[1:2])
    grad_proj_b = attention_backward(projected, grad_att_b, images)
    input_grad = left_trans(stage_order(mod_a, sizes, width // blocks, STAGES_B), grad_proj_b).astype(
        jnp.bfloat16
    )
    bias_sums = jnp.sum(grad_proj_b.astype(jnp.float32), axis=0)
    query_bias_grad = stage_order(bias_sums[:width], sizes, width // blocks, STAGES_B)
    value_bias_grad = stage_order(bias_sums[2 * width :], sizes, width // blocks, STAGES_B)
    chain_b = reduce_pair(
        jnp.concatenate(
            [
                input_grad,
                output_grad,
                bias_columns(
                [query_bias_grad, value_bias_grad, output_bias_grad, contract_bias_grad]
                + [expand_bias_grad[q] for q in range(split)],
                width,
            ),
            ],
            axis=1,
        ),
        STAGES_B[0],
    )
    grad_mod_a = right_trans(grad_proj_b, input_weight).reshape(images, rows, width)
    grad_shift_a = jnp.sum(grad_mod_a, axis=1)
    grad_scale_a = jnp.sum(grad_mod_a * normed_a, axis=1)
    tokens_grad = grad_middle + norm_back(grad_mod_a * (1.0 + scale_a), normed_a, inverse_a)
    modulation_terms = jnp.stack(
        [grad_shift_a, grad_scale_a, grad_gate_a, grad_shift_b, grad_scale_b, grad_gate_b], axis=1
    ).reshape(images, 6 * width)
    modulation_own = modulation_terms.astype(jnp.bfloat16)
    chain_a, chain_b, modulation_own = lax.optimization_barrier((chain_a, chain_b, modulation_own))
    chain_b = reduce_stages(chain_b, STAGES_B[1:2])
    modulation_cols = lax.all_to_all(modulation_own, "zl", split_axis=1, concat_axis=0, tiled=True)
    silu_terms = right_trans(modulation_cols, modulation_weight)
    pair_index = lax.axis_index("zl")
    own_rows = lax.dynamic_slice_in_dim(silu_terms, pair_index * images, images, axis=0)
    other_rows = lax.dynamic_slice_in_dim(silu_terms, (1 - pair_index) * images, images, axis=0)
    silu_sums = own_rows + lax.ppermute(other_rows, "zl", [(0, 1), (1, 0)])
    condition_grad = silu_sums * sigmoid * (1.0 + cond_full * (1.0 - sigmoid))
    dp_count = lax.axis_size(DP)
    row_block = width // dp_count
    silu_parts = silu_pair.reshape(-1, dp_count, row_block).transpose(1, 0, 2)
    silu_parts = jnp.pad(silu_parts, ((0, 0), (0, 0), (0, 128 - row_block)))
    payload = jnp.concatenate(
        [jnp.broadcast_to(modulation_cols[None], (dp_count,) + modulation_cols.shape), silu_parts], axis=2
    )
    factors = lax.all_to_all(payload, DP, 0, 0, tiled=False)
    mod_all = factors[:, :, : modulation_cols.shape[1]].reshape(-1, modulation_cols.shape[1])
    silu_rows = factors[:, :, modulation_cols.shape[1] : modulation_cols.shape[1] + row_block]
    silu_rows = silu_rows.reshape(-1, row_block)
    dp_index = lax.axis_index(DP)
    modulation_weight_grad = left_trans(silu_rows, mod_all)
    bias_all = jnp.sum(mod_all.astype(jnp.float32), axis=0).reshape(-1, width)
    modulation_bias_grad = lax.dynamic_slice_in_dim(bias_all, dp_index * row_block, row_block, axis=1)
    chain_a = reduce_rest(chain_a, STAGES[2:])
    chain_b, mod_all = lax.optimization_barrier((chain_b, mod_all))
    chain_b = reduce_rest(chain_b, STAGES_B[2:])
    three = input_weight.shape[1]
    fw = expand_weight.shape[1]
    input_weight_grad = chain_b[:, :three]
    output_weight_grad = chain_b[:, three : three + width]
    qb_grad = chain_b[:, three + width]
    vb_grad = chain_b[:, three + width + 1]
    ob_grad = chain_b[:, three + width + 2]
    expand_weight_grad = chain_a[:, :fw]
    contract_weight_grad = chain_a[:, fw : fw + split * width].reshape(-1, split, width)
    contract_weight_grad = contract_weight_grad.transpose(1, 0, 2).reshape(-1, width)
    cb_grad = chain_b[:, three + width + 3]
    eb_grad = chain_b[:, three + width + 4 : three + width + 4 + split].T.reshape(-1)
    summed = (
        input_weight_grad,
        qb_grad,
        vb_grad,
        output_weight_grad,
        ob_grad,
        expand_weight_grad,
        eb_grad,
        contract_weight_grad,
        cb_grad,
    )
    return (
        layer_out,
        tokens_grad,
        condition_grad,
        modulation_weight_grad,
        modulation_bias_grad,
        *summed,
    )


def solution(mesh):
    dp_size, mod_size = mesh.devices.shape
    rest = dp_size // 4
    side = int(round(rest ** 0.5))
    shape = (side, 2, rest // side, 2, mod_size)
    sizes = dict(zip(AXES, shape))
    physical = Mesh(np.asarray(mesh.devices).reshape(shape), AXES)
    ALL = AXES
    placed = (
        P(ALL, None, None),
        P(ALL, None),
        P(ALL),
        P(None, "zl"),
        P("zl", None),
        P(),
        P(),
        P(),
        P(),
        P(),
        P(),
        P(),
        P(),
        P(),
        P(ALL, None, None),
    )
    return jax.shard_map(
        functools.partial(per_device, sizes),
        mesh=physical,
        in_specs=placed,
        out_specs=(
            P(ALL, None, None),
            P(ALL, None, None),
            P(ALL, None),
            P(DP, "zl"),
            P("zl", DP),
            P(ALL, None),
            P(ALL),
            P(ALL),
            P(ALL, None),
            P(ALL),
            P(ALL, None),
            P(ALL),
            P(ALL, None),
            P(ALL),
        ),
        check_vma=False,
    )
```

```python
import functools

import jax
import jax.numpy as jnp
import numpy as np
from jax import lax
from jax.experimental import pallas as pl
from jax.experimental.pallas import tpu as pltpu
from jax.sharding import Mesh
from jax.sharding import PartitionSpec as P

HEAD_DIM = 64
LANES = 128


def _nt(a, b):
    return lax.dot_general(a, b, (((1,), (1,)), ((), ())), preferred_element_type=jnp.float32)


def _tn(a, b):
    return lax.dot_general(a, b, (((0,), (0,)), ((), ())), preferred_element_type=jnp.float32)


def _probs(q, k, head, factor):
    lane = lax.broadcasted_iota(jnp.int32, (1, LANES), 1)
    mine = (lane // HEAD_DIM) == head
    qh = jnp.where(mine, q, jnp.zeros_like(q))
    scores = _nt(qh, k) * factor
    weights = jnp.exp(scores - jnp.max(scores, axis=-1, keepdims=True))
    return mine, qh, weights / jnp.sum(weights, axis=-1, keepdims=True)


def _fwd_kernel(factor, q_ref, k_ref, v_ref, o_ref):
    def pair(j, carry):
        cols = pl.ds(pl.multiple_of(j * LANES, LANES), LANES)
        q = q_ref[:, cols]
        k = k_ref[:, cols]
        v = v_ref[:, cols]
        out = jnp.zeros((q.shape[0], LANES), jnp.float32)
        for head in range(LANES // HEAD_DIM):
            mine, _, probs = _probs(q, k, head, factor)
            vh = jnp.where(mine, v, jnp.zeros_like(v))
            out = out + jnp.dot(probs.astype(v.dtype), vh, preferred_element_type=jnp.float32)
        o_ref[:, cols] = out.astype(o_ref.dtype)
        return carry

    lax.fori_loop(0, o_ref.shape[1] // LANES, pair, 0, unroll=4)


def _bwd_kernel(factor, q_ref, k_ref, v_ref, d_ref, dq_ref, dk_ref, dv_ref):
    def pair(j, carry):
        cols = pl.ds(pl.multiple_of(j * LANES, LANES), LANES)
        q = q_ref[:, cols]
        k = k_ref[:, cols]
        v = v_ref[:, cols]
        d = d_ref[:, cols]
        dq = jnp.zeros((q.shape[0], LANES), jnp.float32)
        dk = jnp.zeros((q.shape[0], LANES), jnp.float32)
        dv = jnp.zeros((q.shape[0], LANES), jnp.float32)
        for head in range(LANES // HEAD_DIM):
            mine, qh, probs = _probs(q, k, head, factor)
            dh = jnp.where(mine, d, jnp.zeros_like(d))
            kh = jnp.where(mine, k, jnp.zeros_like(k))
            dprobs = _nt(dh, v)
            dv = dv + _tn(probs.astype(d.dtype), dh)
            inner = jnp.sum(dprobs * probs, axis=-1, keepdims=True)
            dscores = (probs * (dprobs - inner)).astype(q.dtype)
            dq = dq + jnp.dot(dscores, kh, preferred_element_type=jnp.float32)
            dk = dk + _tn(dscores, qh)
        dq_ref[:, cols] = (dq * factor).astype(dq_ref.dtype)
        dk_ref[:, cols] = (dk * factor).astype(dk_ref.dtype)
        dv_ref[:, cols] = dv.astype(dv_ref.dtype)
        return carry

    lax.fori_loop(0, dq_ref.shape[1] // LANES, pair, 0, unroll=4)


def _wgrad_kernel(expand_tiles, modb_ref, du_ref, act_ref, dz_ref, out_ref):
    j = pl.program_id(0)

    @pl.when(j < expand_tiles)
    def _():
        out_ref[...] = jnp.dot(
            modb_ref[...], du_ref[...], preferred_element_type=jnp.float32
        ).astype(out_ref.dtype)

    @pl.when(j >= expand_tiles)
    def _():
        out_ref[...] = jnp.dot(
            act_ref[...], dz_ref[...], preferred_element_type=jnp.float32
        ).astype(out_ref.dtype)


def ffn_weight_grads(mod_t, grad_exp, act_t, grad_branch, tile=1024):
    width, tokens = mod_t.shape
    ff = grad_exp.shape[1]
    expand_tiles = ff // tile
    per_part = width // tile
    tiles = expand_tiles + (ff // width) * per_part

    def act_index(j):
        return (jnp.maximum(j - expand_tiles, 0) // per_part, 0)

    def dz_index(j):
        return (0, jnp.maximum(j - expand_tiles, 0) % per_part)

    return pl.pallas_call(
        functools.partial(_wgrad_kernel, expand_tiles),
        out_shape=jax.ShapeDtypeStruct((width, tiles * tile), jnp.bfloat16),
        grid=(tiles,),
        in_specs=[
            pl.BlockSpec((width, tokens), lambda j: (0, 0)),
            pl.BlockSpec((tokens, tile), lambda j: (0, jnp.minimum(j, expand_tiles - 1))),
            pl.BlockSpec((width, tokens), act_index),
            pl.BlockSpec((tokens, tile), dz_index),
        ],
        out_specs=pl.BlockSpec((width, tile), lambda j: (0, j)),
        compiler_params=pltpu.CompilerParams(dimension_semantics=("arbitrary",)),
        cost_estimate=pl.CostEstimate(
            flops=2 * tokens * width * tiles * tile,
            transcendentals=0,
            bytes_accessed=2 * (tokens * (width + 2 * ff + width) + width * tiles * tile),
        ),
    )(mod_t, grad_exp, act_t, grad_branch)

def attention_forward(projected, images):
    tokens, three = projected.shape
    rows, width = tokens // images, three // 3
    pairs = width // LANES
    factor = HEAD_DIM ** (-0.5)

    def part(offset):
        return pl.BlockSpec((rows, width), lambda b: (b, offset))

    flops = 2 * 2 * images * (width // HEAD_DIM) * rows * rows * LANES
    return pl.pallas_call(
        functools.partial(_fwd_kernel, factor),
        out_shape=jax.ShapeDtypeStruct((tokens, width), projected.dtype),
        grid=(images,),
        in_specs=[part(0), part(1), part(2)],
        out_specs=part(0),
        compiler_params=pltpu.CompilerParams(dimension_semantics=("parallel",)),
        cost_estimate=pl.CostEstimate(
            flops=flops, transcendentals=images * (width // HEAD_DIM) * rows * rows,
            bytes_accessed=2 * tokens * (three + width),
        ),
    )(projected, projected, projected)


def attention_backward(projected, grad_attended, images):
    tokens, three = projected.shape
    rows, width = tokens // images, three // 3
    pairs = width // LANES
    factor = HEAD_DIM ** (-0.5)

    def part(offset):
        return pl.BlockSpec((rows, width), lambda b: (b, offset))

    out = jax.ShapeDtypeStruct((tokens, width), projected.dtype)
    flops = 5 * 2 * 2 * images * (width // HEAD_DIM) * rows * rows * LANES
    dq, dk, dv = pl.pallas_call(
        functools.partial(_bwd_kernel, factor),
        out_shape=(out, out, out),
        grid=(images,),
        in_specs=[part(0), part(1), part(2), part(0)],
        out_specs=[part(0)] * 3,
        compiler_params=pltpu.CompilerParams(dimension_semantics=("parallel",)),
        cost_estimate=pl.CostEstimate(
            flops=flops, transcendentals=images * (width // HEAD_DIM) * rows * rows,
            bytes_accessed=2 * tokens * (three + 4 * width),
        ),
    )(projected, projected, projected, grad_attended)
    return jnp.concatenate([dq, dk, dv], axis=1)


EPS = 1e-06
GELU_C = 0.7978845608028654

AXES = ("y", "zh", "x", "c", "zl")
DP = ("y", "zh", "x", "c")
STAGES = ("c", "x", "y", "zh", "zl")
STAGES_B = ("c", "y", "x", "zh", "zl")


def matmul(left, right):
    return jnp.dot(left, right, preferred_element_type=jnp.float32)


def left_trans(left, right):
    return lax.dot_general(
        left, right, (((0,), (0,)), ((), ())), preferred_element_type=jnp.float32
    )


def right_trans(left, right):
    return lax.dot_general(
        left, right, (((1,), (1,)), ((), ())), preferred_element_type=jnp.float32
    )


def normalize(values):
    centre = values - jnp.mean(values, axis=-1, keepdims=True)
    inverse = lax.rsqrt(jnp.mean(centre * centre, axis=-1, keepdims=True) + EPS)
    return (centre * inverse, inverse)


def norm_back(grad, normed, inverse):
    return inverse * (
        grad
        - jnp.mean(grad, axis=-1, keepdims=True)
        - normed * jnp.mean(grad * normed, axis=-1, keepdims=True)
    )


def stage_order(values, sizes, inner, stages=STAGES):
    lead = values.shape[:-1]
    shape = [sizes[a] for a in AXES]
    values = values.reshape(*lead, *shape, inner)
    n = len(lead)
    order = list(range(n)) + [n + AXES.index(a) for a in stages] + [n + len(AXES)]
    return jnp.transpose(values, order).reshape(*lead, -1)


def reduce_stages(packed, stages):
    for a in stages:
        packed = lax.psum_scatter(packed, a, scatter_dimension=0, tiled=True)
    return packed


def reduce_pair(packed, axis):
    half = packed.shape[0] // 2
    index = lax.axis_index(axis)
    keep = lax.dynamic_slice_in_dim(packed, index * half, half, axis=0)
    send = lax.dynamic_slice_in_dim(packed, (1 - index) * half, half, axis=0)
    got = lax.ppermute(send, axis, [(0, 1), (1, 0)])
    return (keep.astype(jnp.float32) + got.astype(jnp.float32)).astype(packed.dtype)


def reduce_rest(packed, axes):
    count = 1
    for a in axes:
        count *= lax.axis_size(a)
    chunks = packed.reshape(count, packed.shape[0] // count, packed.shape[1])
    chunks = lax.all_to_all(chunks, axes, 0, 0, tiled=False)
    return jnp.sum(chunks.astype(jnp.float32), axis=0)


def bias_columns(columns, rows):
    block = jnp.stack(columns, axis=1)
    return jnp.pad(block, ((0, 0), (0, 128 - block.shape[1]))).astype(jnp.bfloat16)


def gather_dp(values):
    count = 1
    for a in DP:
        count *= lax.axis_size(a)
    copies = jnp.broadcast_to(values[None], (count,) + values.shape)
    return lax.all_to_all(copies, DP, 0, 0, tiled=False).reshape(-1, values.shape[1])


def per_device(
    sizes,
    tokens,
    condition,
    occupied,
    modulation_weight,
    modulation_bias,
    input_weight,
    query_bias,
    value_bias,
    output_weight,
    output_bias,
    expand_weight,
    expand_bias,
    contract_weight,
    contract_bias,
    cotangent,
):
    images, rows, width = tokens.shape
    heads = width // HEAD_DIM
    flat = images * rows
    factor = HEAD_DIM ** (-0.5)
    cond_full = condition.astype(jnp.float32)
    sigmoid = jax.nn.sigmoid(cond_full)
    silu_b = (cond_full * sigmoid).astype(jnp.bfloat16)
    swap = [(0, 1), (1, 0)]
    first = lax.axis_index("zl") == 0
    silu_other = lax.ppermute(silu_b, "zl", swap)
    silu_pair = jnp.where(
        first,
        jnp.concatenate([silu_b, silu_other], axis=0),
        jnp.concatenate([silu_other, silu_b], axis=0),
    )
    mod_cols = matmul(silu_pair, modulation_weight) + modulation_bias.reshape(1, -1)
    own_cols = jnp.where(first, mod_cols[:images], mod_cols[images:])
    sent_cols = jnp.where(first, mod_cols[images:], mod_cols[:images])
    other_cols = lax.ppermute(sent_cols, "zl", swap)
    modulation = jnp.where(
        first,
        jnp.concatenate([own_cols, other_cols], axis=1),
        jnp.concatenate([other_cols, own_cols], axis=1),
    ).reshape(images, 6, 1, width)
    shift_a = modulation[:, 0]
    scale_a = modulation[:, 1]
    gate_a = modulation[:, 2]
    shift_b = modulation[:, 3]
    scale_b = modulation[:, 4]
    gate_b = modulation[:, 5]
    inputs = tokens.astype(jnp.float32)
    normed_a, inverse_a = normalize(inputs)
    mod_a = (normed_a * (1.0 + scale_a) + shift_a).astype(jnp.bfloat16).reshape(flat, width)
    qkv_bias = jnp.concatenate([query_bias, jnp.zeros_like(query_bias), value_bias])
    projected = (matmul(mod_a, input_weight) + qkv_bias).astype(jnp.bfloat16)
    attended_b = attention_forward(projected, images)
    branch_a = (matmul(attended_b, output_weight) + output_bias).reshape(images, rows, width)
    middle = inputs + gate_a * branch_a
    normed_b, inverse_b = normalize(middle)
    mod_b = (normed_b * (1.0 + scale_b) + shift_b).astype(jnp.bfloat16).reshape(flat, width)
    expanded = matmul(mod_b, expand_weight) + expand_bias
    tanh_part = jnp.tanh(GELU_C * (expanded + 0.044715 * expanded * expanded * expanded))
    activated_b = (0.5 * expanded * (1.0 + tanh_part)).astype(jnp.bfloat16)
    branch_b = (matmul(activated_b, contract_weight) + contract_bias).reshape(images, rows, width)
    alive = occupied.astype(jnp.float32)[:, None, None]
    layer_out = (middle + gate_b * branch_b) * alive
    grad_out = cotangent.astype(jnp.float32) * alive
    grad_gate_b = jnp.sum(grad_out * branch_b, axis=1)
    grad_branch_b = (grad_out * gate_b).astype(jnp.bfloat16).reshape(flat, width)
    blocks = 1
    for a in AXES:
        blocks *= sizes[a]
    ff = activated_b.shape[1]
    split = ff // width
    act_perm = stage_order(
        activated_b.reshape(flat, blocks, split, width // blocks)
        .transpose(0, 2, 1, 3)
        .reshape(flat, split, width),
        sizes,
        width // blocks,
    )
    contract_bias_grad = stage_order(
        jnp.sum(grad_branch_b.astype(jnp.float32), axis=0), sizes, width // blocks, STAGES_B
    )
    grad_act = right_trans(grad_branch_b, contract_weight)
    slope = 0.5 * (1.0 + tanh_part) + 0.5 * expanded * (1.0 - tanh_part * tanh_part) * GELU_C * (
        1.0 + 3.0 * 0.044715 * expanded * expanded
    )
    grad_exp_b = (grad_act * slope).astype(jnp.bfloat16)
    expand_bias_grad = stage_order(
        jnp.sum(grad_exp_b.astype(jnp.float32), axis=0)
        .reshape(blocks, split, width // blocks)
        .transpose(1, 0, 2)
        .reshape(split, width),
        sizes,
        width // blocks,
        STAGES_B,
    )
    packed_a = ffn_weight_grads(
        stage_order(mod_b, sizes, width // blocks).T, grad_exp_b, act_perm.reshape(flat, -1).T, grad_branch_b
    )
    packed_a, grad_exp_b = lax.optimization_barrier((packed_a, grad_exp_b))
    chain_a = reduce_stages(packed_a, STAGES[:1])
    grad_mod_b = right_trans(grad_exp_b, expand_weight).reshape(images, rows, width)
    grad_shift_b = jnp.sum(grad_mod_b, axis=1)
    grad_scale_b = jnp.sum(grad_mod_b * normed_b, axis=1)
    grad_middle = grad_out + norm_back(grad_mod_b * (1.0 + scale_b), normed_b, inverse_b)
    grad_gate_a = jnp.sum(grad_middle * branch_a, axis=1)
    grad_branch_a = (grad_middle * gate_a).astype(jnp.bfloat16).reshape(flat, width)
    output_grad = left_trans(stage_order(attended_b, sizes, width // blocks, STAGES_B), grad_branch_a).astype(
        jnp.bfloat16
    )
    output_bias_grad = stage_order(
        jnp.sum(grad_branch_a.astype(jnp.float32), axis=0), sizes, width // blocks, STAGES_B
    )
    grad_att_b = right_trans(grad_branch_a, output_weight).astype(jnp.bfloat16)
    chain_a, grad_att_b = lax.optimization_barrier((chain_a, grad_att_b))
    chain_a = reduce_stages(chain_a, STAGES[1:2])
    grad_proj_b = attention_backward(projected, grad_att_b, images)
    input_grad = left_trans(stage_order(mod_a, sizes, width // blocks, STAGES_B), grad_proj_b).astype(
        jnp.bfloat16
    )
    bias_sums = jnp.sum(grad_proj_b.astype(jnp.float32), axis=0)
    query_bias_grad = stage_order(bias_sums[:width], sizes, width // blocks, STAGES_B)
    value_bias_grad = stage_order(bias_sums[2 * width :], sizes, width // blocks, STAGES_B)
    chain_b = reduce_pair(
        jnp.concatenate(
            [
                input_grad,
                output_grad,
                bias_columns(
                [query_bias_grad, value_bias_grad, output_bias_grad, contract_bias_grad]
                + [expand_bias_grad[q] for q in range(split)],
                width,
            ),
            ],
            axis=1,
        ),
        STAGES_B[0],
    )
    chain_a, chain_b = lax.optimization_barrier((chain_a, chain_b))
    chain_b = reduce_stages(chain_b, STAGES_B[1:2])
    grad_mod_a = right_trans(grad_proj_b, input_weight).reshape(images, rows, width)
    grad_shift_a = jnp.sum(grad_mod_a, axis=1)
    grad_scale_a = jnp.sum(grad_mod_a * normed_a, axis=1)
    tokens_grad = grad_middle + norm_back(grad_mod_a * (1.0 + scale_a), normed_a, inverse_a)
    modulation_terms = jnp.stack(
        [grad_shift_a, grad_scale_a, grad_gate_a, grad_shift_b, grad_scale_b, grad_gate_b], axis=1
    ).reshape(images, 6 * width)
    modulation_own = modulation_terms.astype(jnp.bfloat16)
    modulation_cols = lax.all_to_all(modulation_own, "zl", split_axis=1, concat_axis=0, tiled=True)
    silu_terms = right_trans(modulation_cols, modulation_weight)
    pair_index = lax.axis_index("zl")
    own_rows = lax.dynamic_slice_in_dim(silu_terms, pair_index * images, images, axis=0)
    other_rows = lax.dynamic_slice_in_dim(silu_terms, (1 - pair_index) * images, images, axis=0)
    silu_sums = own_rows + lax.ppermute(other_rows, "zl", [(0, 1), (1, 0)])
    condition_grad = silu_sums * sigmoid * (1.0 + cond_full * (1.0 - sigmoid))
    dp_count = lax.axis_size(DP)
    row_block = width // dp_count
    silu_parts = silu_pair.reshape(-1, dp_count, row_block).transpose(1, 0, 2)
    silu_parts = jnp.pad(silu_parts, ((0, 0), (0, 0), (0, 128 - row_block)))
    payload = jnp.concatenate(
        [jnp.broadcast_to(modulation_cols[None], (dp_count,) + modulation_cols.shape), silu_parts], axis=2
    )
    factors = lax.all_to_all(payload, DP, 0, 0, tiled=False)
    mod_all = factors[:, :, : modulation_cols.shape[1]].reshape(-1, modulation_cols.shape[1])
    silu_rows = factors[:, :, modulation_cols.shape[1] : modulation_cols.shape[1] + row_block]
    silu_rows = silu_rows.reshape(-1, row_block)
    dp_index = lax.axis_index(DP)
    modulation_weight_grad = left_trans(silu_rows, mod_all)
    bias_all = jnp.sum(mod_all.astype(jnp.float32), axis=0).reshape(-1, width)
    modulation_bias_grad = lax.dynamic_slice_in_dim(bias_all, dp_index * row_block, row_block, axis=1)
    chain_a = reduce_rest(chain_a, STAGES[2:])
    chain_b, mod_all = lax.optimization_barrier((chain_b, mod_all))
    chain_b = reduce_rest(chain_b, STAGES_B[2:])
    three = input_weight.shape[1]
    fw = expand_weight.shape[1]
    input_weight_grad = chain_b[:, :three]
    output_weight_grad = chain_b[:, three : three + width]
    qb_grad = chain_b[:, three + width]
    vb_grad = chain_b[:, three + width + 1]
    ob_grad = chain_b[:, three + width + 2]
    expand_weight_grad = chain_a[:, :fw]
    contract_weight_grad = chain_a[:, fw : fw + split * width].reshape(-1, split, width)
    contract_weight_grad = contract_weight_grad.transpose(1, 0, 2).reshape(-1, width)
    cb_grad = chain_b[:, three + width + 3]
    eb_grad = chain_b[:, three + width + 4 : three + width + 4 + split].T.reshape(-1)
    summed = (
        input_weight_grad,
        qb_grad,
        vb_grad,
        output_weight_grad,
        ob_grad,
        expand_weight_grad,
        eb_grad,
        contract_weight_grad,
        cb_grad,
    )
    return (
        layer_out,
        tokens_grad,
        condition_grad,
        modulation_weight_grad,
        modulation_bias_grad,
        *summed,
    )


def solution(mesh):
    dp_size, mod_size = mesh.devices.shape
    rest = dp_size // 4
    side = int(round(rest ** 0.5))
    shape = (side, 2, rest // side, 2, mod_size)
    sizes = dict(zip(AXES, shape))
    physical = Mesh(np.asarray(mesh.devices).reshape(shape), AXES)
    ALL = AXES
    placed = (
        P(ALL, None, None),
        P(ALL, None),
        P(ALL),
        P(None, "zl"),
        P("zl", None),
        P(),
        P(),
        P(),
        P(),
        P(),
        P(),
        P(),
        P(),
        P(),
        P(ALL, None, None),
    )
    return jax.shard_map(
        functools.partial(per_device, sizes),
        mesh=physical,
        in_specs=placed,
        out_specs=(
            P(ALL, None, None),
            P(ALL, None, None),
            P(ALL, None),
            P(DP, "zl"),
            P("zl", DP),
            P(ALL, None),
            P(ALL),
            P(ALL),
            P(ALL, None),
            P(ALL),
            P(ALL, None),
            P(ALL),
            P(ALL, None),
            P(ALL),
        ),
        check_vma=False,
    )
```

```python
import functools

import jax
import jax.numpy as jnp
import numpy as np
from jax import lax
from jax.experimental import pallas as pl
from jax.experimental.pallas import tpu as pltpu
from jax.sharding import Mesh
from jax.sharding import PartitionSpec as P

HEAD_DIM = 64
LANES = 128


def _nt(a, b):
    return lax.dot_general(a, b, (((1,), (1,)), ((), ())), preferred_element_type=jnp.float32)


def _tn(a, b):
    return lax.dot_general(a, b, (((0,), (0,)), ((), ())), preferred_element_type=jnp.float32)


def _probs(q, k, head, factor):
    lane = lax.broadcasted_iota(jnp.int32, (1, LANES), 1)
    mine = (lane // HEAD_DIM) == head
    qh = jnp.where(mine, q, jnp.zeros_like(q))
    scores = _nt(qh, k) * factor
    weights = jnp.exp(scores - jnp.max(scores, axis=-1, keepdims=True))
    return mine, qh, weights / jnp.sum(weights, axis=-1, keepdims=True)


def _fwd_kernel(factor, q_ref, k_ref, v_ref, o_ref):
    def pair(j, carry):
        cols = pl.ds(pl.multiple_of(j * LANES, LANES), LANES)
        q = q_ref[:, cols]
        k = k_ref[:, cols]
        v = v_ref[:, cols]
        out = jnp.zeros((q.shape[0], LANES), jnp.float32)
        for head in range(LANES // HEAD_DIM):
            mine, _, probs = _probs(q, k, head, factor)
            vh = jnp.where(mine, v, jnp.zeros_like(v))
            out = out + jnp.dot(probs.astype(v.dtype), vh, preferred_element_type=jnp.float32)
        o_ref[:, cols] = out.astype(o_ref.dtype)
        return carry

    lax.fori_loop(0, o_ref.shape[1] // LANES, pair, 0, unroll=4)


def _bwd_kernel(factor, q_ref, k_ref, v_ref, d_ref, dq_ref, dk_ref, dv_ref):
    def pair(j, carry):
        cols = pl.ds(pl.multiple_of(j * LANES, LANES), LANES)
        q = q_ref[:, cols]
        k = k_ref[:, cols]
        v = v_ref[:, cols]
        d = d_ref[:, cols]
        dq = jnp.zeros((q.shape[0], LANES), jnp.float32)
        dk = jnp.zeros((q.shape[0], LANES), jnp.float32)
        dv = jnp.zeros((q.shape[0], LANES), jnp.float32)
        for head in range(LANES // HEAD_DIM):
            mine, qh, probs = _probs(q, k, head, factor)
            dh = jnp.where(mine, d, jnp.zeros_like(d))
            kh = jnp.where(mine, k, jnp.zeros_like(k))
            dprobs = _nt(dh, v)
            dv = dv + _tn(probs.astype(d.dtype), dh)
            inner = jnp.sum(dprobs * probs, axis=-1, keepdims=True)
            dscores = (probs * (dprobs - inner)).astype(q.dtype)
            dq = dq + jnp.dot(dscores, kh, preferred_element_type=jnp.float32)
            dk = dk + _tn(dscores, qh)
        dq_ref[:, cols] = (dq * factor).astype(dq_ref.dtype)
        dk_ref[:, cols] = (dk * factor).astype(dk_ref.dtype)
        dv_ref[:, cols] = dv.astype(dv_ref.dtype)
        return carry

    lax.fori_loop(0, dq_ref.shape[1] // LANES, pair, 0, unroll=4)


def _wgrad_kernel(expand_tiles, modb_ref, du_ref, act_ref, dz_ref, out_ref):
    j = pl.program_id(0)

    @pl.when(j < expand_tiles)
    def _():
        out_ref[...] = jnp.dot(
            modb_ref[...], du_ref[...], preferred_element_type=jnp.float32
        ).astype(out_ref.dtype)

    @pl.when(j >= expand_tiles)
    def _():
        out_ref[...] = jnp.dot(
            act_ref[...], dz_ref[...], preferred_element_type=jnp.float32
        ).astype(out_ref.dtype)


def ffn_weight_grads(mod_t, grad_exp, act_t, grad_branch, tile=1024):
    width, tokens = mod_t.shape
    ff = grad_exp.shape[1]
    expand_tiles = ff // tile
    per_part = width // tile
    tiles = expand_tiles + (ff // width) * per_part

    def act_index(j):
        return (jnp.maximum(j - expand_tiles, 0) // per_part, 0)

    def dz_index(j):
        return (0, jnp.maximum(j - expand_tiles, 0) % per_part)

    return pl.pallas_call(
        functools.partial(_wgrad_kernel, expand_tiles),
        out_shape=jax.ShapeDtypeStruct((width, tiles * tile), jnp.bfloat16),
        grid=(tiles,),
        in_specs=[
            pl.BlockSpec((width, tokens), lambda j: (0, 0)),
            pl.BlockSpec((tokens, tile), lambda j: (0, jnp.minimum(j, expand_tiles - 1))),
            pl.BlockSpec((width, tokens), act_index),
            pl.BlockSpec((tokens, tile), dz_index),
        ],
        out_specs=pl.BlockSpec((width, tile), lambda j: (0, j)),
        compiler_params=pltpu.CompilerParams(dimension_semantics=("arbitrary",)),
        cost_estimate=pl.CostEstimate(
            flops=2 * tokens * width * tiles * tile,
            transcendentals=0,
            bytes_accessed=2 * (tokens * (width + 2 * ff + width) + width * tiles * tile),
        ),
    )(mod_t, grad_exp, act_t, grad_branch)

def attention_forward(projected, images):
    tokens, three = projected.shape
    rows, width = tokens // images, three // 3
    pairs = width // LANES
    factor = HEAD_DIM ** (-0.5)

    def part(offset):
        return pl.BlockSpec((rows, width), lambda b: (b, offset))

    flops = 2 * 2 * images * (width // HEAD_DIM) * rows * rows * LANES
    return pl.pallas_call(
        functools.partial(_fwd_kernel, factor),
        out_shape=jax.ShapeDtypeStruct((tokens, width), projected.dtype),
        grid=(images,),
        in_specs=[part(0), part(1), part(2)],
        out_specs=part(0),
        compiler_params=pltpu.CompilerParams(dimension_semantics=("parallel",)),
        cost_estimate=pl.CostEstimate(
            flops=flops, transcendentals=images * (width // HEAD_DIM) * rows * rows,
            bytes_accessed=2 * tokens * (three + width),
        ),
    )(projected, projected, projected)


def attention_backward(projected, grad_attended, images):
    tokens, three = projected.shape
    rows, width = tokens // images, three // 3
    pairs = width // LANES
    factor = HEAD_DIM ** (-0.5)

    def part(offset):
        return pl.BlockSpec((rows, width), lambda b: (b, offset))

    out = jax.ShapeDtypeStruct((tokens, width), projected.dtype)
    flops = 5 * 2 * 2 * images * (width // HEAD_DIM) * rows * rows * LANES
    dq, dk, dv = pl.pallas_call(
        functools.partial(_bwd_kernel, factor),
        out_shape=(out, out, out),
        grid=(images,),
        in_specs=[part(0), part(1), part(2), part(0)],
        out_specs=[part(0)] * 3,
        compiler_params=pltpu.CompilerParams(dimension_semantics=("parallel",)),
        cost_estimate=pl.CostEstimate(
            flops=flops, transcendentals=images * (width // HEAD_DIM) * rows * rows,
            bytes_accessed=2 * tokens * (three + 4 * width),
        ),
    )(projected, projected, projected, grad_attended)
    return jnp.concatenate([dq, dk, dv], axis=1)


EPS = 1e-06
GELU_C = 0.7978845608028654

AXES = ("y", "zh", "x", "c", "zl")
DP = ("y", "zh", "x", "c")
STAGES = ("c", "x", "y", "zh", "zl")
STAGES_B = ("c", "y", "x", "zh", "zl")


def matmul(left, right):
    return jnp.dot(left, right, preferred_element_type=jnp.float32)


def left_trans(left, right):
    return lax.dot_general(
        left, right, (((0,), (0,)), ((), ())), preferred_element_type=jnp.float32
    )


def right_trans(left, right):
    return lax.dot_general(
        left, right, (((1,), (1,)), ((), ())), preferred_element_type=jnp.float32
    )


def normalize(values):
    centre = values - jnp.mean(values, axis=-1, keepdims=True)
    inverse = lax.rsqrt(jnp.mean(centre * centre, axis=-1, keepdims=True) + EPS)
    return (centre * inverse, inverse)


def norm_back(grad, normed, inverse):
    return inverse * (
        grad
        - jnp.mean(grad, axis=-1, keepdims=True)
        - normed * jnp.mean(grad * normed, axis=-1, keepdims=True)
    )


def stage_order(values, sizes, inner, stages=STAGES):
    lead = values.shape[:-1]
    shape = [sizes[a] for a in AXES]
    values = values.reshape(*lead, *shape, inner)
    n = len(lead)
    order = list(range(n)) + [n + AXES.index(a) for a in stages] + [n + len(AXES)]
    return jnp.transpose(values, order).reshape(*lead, -1)


def reduce_stages(packed, stages):
    for a in stages:
        packed = lax.psum_scatter(packed, a, scatter_dimension=0, tiled=True)
    return packed


def reduce_pair(packed, axis):
    half = packed.shape[0] // 2
    index = lax.axis_index(axis)
    keep = lax.dynamic_slice_in_dim(packed, index * half, half, axis=0)
    send = lax.dynamic_slice_in_dim(packed, (1 - index) * half, half, axis=0)
    got = lax.ppermute(send, axis, [(0, 1), (1, 0)])
    return (keep.astype(jnp.float32) + got.astype(jnp.float32)).astype(packed.dtype)


def reduce_rest(packed, axes):
    count = 1
    for a in axes:
        count *= lax.axis_size(a)
    chunks = packed.reshape(count, packed.shape[0] // count, packed.shape[1])
    chunks = lax.all_to_all(chunks, axes, 0, 0, tiled=False)
    return jnp.sum(chunks.astype(jnp.float32), axis=0)


def bias_columns(columns, rows):
    block = jnp.stack(columns, axis=1)
    return jnp.pad(block, ((0, 0), (0, 128 - block.shape[1]))).astype(jnp.bfloat16)


def gather_dp(values):
    count = 1
    for a in DP:
        count *= lax.axis_size(a)
    copies = jnp.broadcast_to(values[None], (count,) + values.shape)
    return lax.all_to_all(copies, DP, 0, 0, tiled=False).reshape(-1, values.shape[1])


def per_device(
    sizes,
    tokens,
    condition,
    occupied,
    modulation_weight,
    modulation_bias,
    input_weight,
    query_bias,
    value_bias,
    output_weight,
    output_bias,
    expand_weight,
    expand_bias,
    contract_weight,
    contract_bias,
    cotangent,
):
    images, rows, width = tokens.shape
    heads = width // HEAD_DIM
    flat = images * rows
    factor = HEAD_DIM ** (-0.5)
    cond_full = condition.astype(jnp.float32)
    sigmoid = jax.nn.sigmoid(cond_full)
    silu_b = (cond_full * sigmoid).astype(jnp.bfloat16)
    swap = [(0, 1), (1, 0)]
    first = lax.axis_index("zl") == 0
    silu_other = lax.ppermute(silu_b, "zl", swap)
    silu_pair = jnp.where(
        first,
        jnp.concatenate([silu_b, silu_other], axis=0),
        jnp.concatenate([silu_other, silu_b], axis=0),
    )
    mod_cols = matmul(silu_pair, modulation_weight) + modulation_bias.reshape(1, -1)
    own_cols = jnp.where(first, mod_cols[:images], mod_cols[images:])
    sent_cols = jnp.where(first, mod_cols[images:], mod_cols[:images])
    other_cols = lax.ppermute(sent_cols, "zl", swap)
    modulation = jnp.where(
        first,
        jnp.concatenate([own_cols, other_cols], axis=1),
        jnp.concatenate([other_cols, own_cols], axis=1),
    ).reshape(images, 6, 1, width)
    shift_a = modulation[:, 0]
    scale_a = modulation[:, 1]
    gate_a = modulation[:, 2]
    shift_b = modulation[:, 3]
    scale_b = modulation[:, 4]
    gate_b = modulation[:, 5]
    inputs = tokens.astype(jnp.float32)
    normed_a, inverse_a = normalize(inputs)
    mod_a = (normed_a * (1.0 + scale_a) + shift_a).astype(jnp.bfloat16).reshape(flat, width)
    qkv_bias = jnp.concatenate([query_bias, jnp.zeros_like(query_bias), value_bias])
    projected = (matmul(mod_a, input_weight) + qkv_bias).astype(jnp.bfloat16)
    attended_b = attention_forward(projected, images)
    branch_a = (matmul(attended_b, output_weight) + output_bias).reshape(images, rows, width)
    middle = inputs + gate_a * branch_a
    normed_b, inverse_b = normalize(middle)
    mod_b = (normed_b * (1.0 + scale_b) + shift_b).astype(jnp.bfloat16).reshape(flat, width)
    expanded = matmul(mod_b, expand_weight) + expand_bias
    tanh_part = jnp.tanh(GELU_C * (expanded + 0.044715 * expanded * expanded * expanded))
    activated_b = (0.5 * expanded * (1.0 + tanh_part)).astype(jnp.bfloat16)
    branch_b = (matmul(activated_b, contract_weight) + contract_bias).reshape(images, rows, width)
    alive = occupied.astype(jnp.float32)[:, None, None]
    layer_out = (middle + gate_b * branch_b) * alive
    grad_out = cotangent.astype(jnp.float32) * alive
    grad_gate_b = jnp.sum(grad_out * branch_b, axis=1)
    grad_branch_b = (grad_out * gate_b).astype(jnp.bfloat16).reshape(flat, width)
    blocks = 1
    for a in AXES:
        blocks *= sizes[a]
    ff = activated_b.shape[1]
    split = ff // width
    act_perm = stage_order(
        activated_b.reshape(flat, blocks, split, width // blocks)
        .transpose(0, 2, 1, 3)
        .reshape(flat, split, width),
        sizes,
        width // blocks,
    )
    contract_bias_grad = stage_order(
        jnp.sum(grad_branch_b.astype(jnp.float32), axis=0), sizes, width // blocks, STAGES_B
    )
    grad_act = right_trans(grad_branch_b, contract_weight)
    slope = 0.5 * (1.0 + tanh_part) + 0.5 * expanded * (1.0 - tanh_part * tanh_part) * GELU_C * (
        1.0 + 3.0 * 0.044715 * expanded * expanded
    )
    grad_exp_b = (grad_act * slope).astype(jnp.bfloat16)
    expand_bias_grad = stage_order(
        jnp.sum(grad_exp_b.astype(jnp.float32), axis=0)
        .reshape(blocks, split, width // blocks)
        .transpose(1, 0, 2)
        .reshape(split, width),
        sizes,
        width // blocks,
        STAGES_B,
    )
    packed_a = ffn_weight_grads(
        stage_order(mod_b, sizes, width // blocks).T, grad_exp_b, act_perm.reshape(flat, -1).T, grad_branch_b
    )
    packed_a, grad_exp_b = lax.optimization_barrier((packed_a, grad_exp_b))
    chain_a = reduce_stages(packed_a, STAGES[:1])
    grad_mod_b = right_trans(grad_exp_b, expand_weight).reshape(images, rows, width)
    grad_shift_b = jnp.sum(grad_mod_b, axis=1)
    grad_scale_b = jnp.sum(grad_mod_b * normed_b, axis=1)
    grad_middle = grad_out + norm_back(grad_mod_b * (1.0 + scale_b), normed_b, inverse_b)
    grad_gate_a = jnp.sum(grad_middle * branch_a, axis=1)
    grad_branch_a = (grad_middle * gate_a).astype(jnp.bfloat16).reshape(flat, width)
    output_grad = left_trans(stage_order(attended_b, sizes, width // blocks, STAGES_B), grad_branch_a).astype(
        jnp.bfloat16
    )
    output_bias_grad = stage_order(
        jnp.sum(grad_branch_a.astype(jnp.float32), axis=0), sizes, width // blocks, STAGES_B
    )
    grad_att_b = right_trans(grad_branch_a, output_weight).astype(jnp.bfloat16)
    chain_a, grad_att_b = lax.optimization_barrier((chain_a, grad_att_b))
    chain_a = reduce_stages(chain_a, STAGES[1:2])
    grad_proj_b = attention_backward(projected, grad_att_b, images)
    input_grad = left_trans(stage_order(mod_a, sizes, width // blocks, STAGES_B), grad_proj_b).astype(
        jnp.bfloat16
    )
    bias_sums = jnp.sum(grad_proj_b.astype(jnp.float32), axis=0)
    query_bias_grad = stage_order(bias_sums[:width], sizes, width // blocks, STAGES_B)
    value_bias_grad = stage_order(bias_sums[2 * width :], sizes, width // blocks, STAGES_B)
    chain_b = reduce_pair(
        jnp.concatenate(
            [
                input_grad,
                output_grad,
                bias_columns(
                [query_bias_grad, value_bias_grad, output_bias_grad, contract_bias_grad]
                + [expand_bias_grad[q] for q in range(split)],
                width,
            ),
            ],
            axis=1,
        ),
        STAGES_B[0],
    )
    chain_a, chain_b = lax.optimization_barrier((chain_a, chain_b))
    chain_b = reduce_stages(chain_b, STAGES_B[1:2])
    grad_mod_a = right_trans(grad_proj_b, input_weight).reshape(images, rows, width)
    grad_shift_a = jnp.sum(grad_mod_a, axis=1)
    grad_scale_a = jnp.sum(grad_mod_a * normed_a, axis=1)
    tokens_grad = grad_middle + norm_back(grad_mod_a * (1.0 + scale_a), normed_a, inverse_a)
    modulation_terms = jnp.stack(
        [grad_shift_a, grad_scale_a, grad_gate_a, grad_shift_b, grad_scale_b, grad_gate_b], axis=1
    ).reshape(images, 6 * width)
    modulation_own = modulation_terms.astype(jnp.bfloat16)
    half = modulation_own.shape[1] // 2
    keep_cols = jnp.where(first, modulation_own[:, :half], modulation_own[:, half:])
    give_cols = jnp.where(first, modulation_own[:, half:], modulation_own[:, :half])
    got_cols = lax.ppermute(give_cols, "zl", swap)
    modulation_cols = jnp.where(
        first,
        jnp.concatenate([keep_cols, got_cols], axis=0),
        jnp.concatenate([got_cols, keep_cols], axis=0),
    )
    silu_terms = right_trans(modulation_cols, modulation_weight)
    pair_index = lax.axis_index("zl")
    own_rows = lax.dynamic_slice_in_dim(silu_terms, pair_index * images, images, axis=0)
    other_rows = lax.dynamic_slice_in_dim(silu_terms, (1 - pair_index) * images, images, axis=0)
    silu_sums = own_rows + lax.ppermute(other_rows, "zl", [(0, 1), (1, 0)])
    condition_grad = silu_sums * sigmoid * (1.0 + cond_full * (1.0 - sigmoid))
    dp_count = lax.axis_size(DP)
    row_block = width // dp_count
    silu_parts = silu_pair.reshape(-1, dp_count, row_block).transpose(1, 0, 2)
    silu_parts = jnp.pad(silu_parts, ((0, 0), (0, 0), (0, 128 - row_block)))
    payload = jnp.concatenate(
        [jnp.broadcast_to(modulation_cols[None], (dp_count,) + modulation_cols.shape), silu_parts], axis=2
    )
    factors = lax.all_to_all(payload, DP, 0, 0, tiled=False)
    mod_all = factors[:, :, : modulation_cols.shape[1]].reshape(-1, modulation_cols.shape[1])
    silu_rows = factors[:, :, modulation_cols.shape[1] : modulation_cols.shape[1] + row_block]
    silu_rows = silu_rows.reshape(-1, row_block)
    dp_index = lax.axis_index(DP)
    modulation_weight_grad = left_trans(silu_rows, mod_all)
    bias_all = jnp.sum(mod_all.astype(jnp.float32), axis=0).reshape(-1, width)
    modulation_bias_grad = lax.dynamic_slice_in_dim(bias_all, dp_index * row_block, row_block, axis=1)
    chain_a = reduce_rest(chain_a, STAGES[2:])
    chain_b, mod_all = lax.optimization_barrier((chain_b, mod_all))
    chain_b = reduce_rest(chain_b, STAGES_B[2:])
    three = input_weight.shape[1]
    fw = expand_weight.shape[1]
    input_weight_grad = chain_b[:, :three]
    output_weight_grad = chain_b[:, three : three + width]
    qb_grad = chain_b[:, three + width]
    vb_grad = chain_b[:, three + width + 1]
    ob_grad = chain_b[:, three + width + 2]
    expand_weight_grad = chain_a[:, :fw]
    contract_weight_grad = chain_a[:, fw : fw + split * width].reshape(-1, split, width)
    contract_weight_grad = contract_weight_grad.transpose(1, 0, 2).reshape(-1, width)
    cb_grad = chain_b[:, three + width + 3]
    eb_grad = chain_b[:, three + width + 4 : three + width + 4 + split].T.reshape(-1)
    summed = (
        input_weight_grad,
        qb_grad,
        vb_grad,
        output_weight_grad,
        ob_grad,
        expand_weight_grad,
        eb_grad,
        contract_weight_grad,
        cb_grad,
    )
    return (
        layer_out,
        tokens_grad,
        condition_grad,
        modulation_weight_grad,
        modulation_bias_grad,
        *summed,
    )


def solution(mesh):
    dp_size, mod_size = mesh.devices.shape
    rest = dp_size // 4
    side = int(round(rest ** 0.5))
    shape = (side, 2, rest // side, 2, mod_size)
    sizes = dict(zip(AXES, shape))
    physical = Mesh(np.asarray(mesh.devices).reshape(shape), AXES)
    ALL = AXES
    placed = (
        P(ALL, None, None),
        P(ALL, None),
        P(ALL),
        P(None, "zl"),
        P("zl", None),
        P(),
        P(),
        P(),
        P(),
        P(),
        P(),
        P(),
        P(),
        P(),
        P(ALL, None, None),
    )
    return jax.shard_map(
        functools.partial(per_device, sizes),
        mesh=physical,
        in_specs=placed,
        out_specs=(
            P(ALL, None, None),
            P(ALL, None, None),
            P(ALL, None),
            P(DP, "zl"),
            P("zl", DP),
            P(ALL, None),
            P(ALL),
            P(ALL),
            P(ALL, None),
            P(ALL),
            P(ALL, None),
            P(ALL),
            P(ALL, None),
            P(ALL),
        ),
        check_vma=False,
    )
```

```python
import functools

import jax
import jax.numpy as jnp
import numpy as np
from jax import lax
from jax.experimental import pallas as pl
from jax.experimental.pallas import tpu as pltpu
from jax.sharding import Mesh
from jax.sharding import PartitionSpec as P

HEAD_DIM = 64
LANES = 128


def _nt(a, b):
    return lax.dot_general(a, b, (((1,), (1,)), ((), ())), preferred_element_type=jnp.float32)


def _tn(a, b):
    return lax.dot_general(a, b, (((0,), (0,)), ((), ())), preferred_element_type=jnp.float32)


def _probs(q, k, head, factor):
    lane = lax.broadcasted_iota(jnp.int32, (1, LANES), 1)
    mine = (lane // HEAD_DIM) == head
    qh = jnp.where(mine, q, jnp.zeros_like(q))
    scores = _nt(qh, k) * factor
    weights = jnp.exp(scores - jnp.max(scores, axis=-1, keepdims=True))
    return mine, qh, weights / jnp.sum(weights, axis=-1, keepdims=True)


def _fwd_kernel(factor, q_ref, k_ref, v_ref, o_ref):
    def pair(j, carry):
        cols = pl.ds(pl.multiple_of(j * LANES, LANES), LANES)
        q = q_ref[:, cols]
        k = k_ref[:, cols]
        v = v_ref[:, cols]
        out = jnp.zeros((q.shape[0], LANES), jnp.float32)
        for head in range(LANES // HEAD_DIM):
            mine, _, probs = _probs(q, k, head, factor)
            vh = jnp.where(mine, v, jnp.zeros_like(v))
            out = out + jnp.dot(probs.astype(v.dtype), vh, preferred_element_type=jnp.float32)
        o_ref[:, cols] = out.astype(o_ref.dtype)
        return carry

    lax.fori_loop(0, o_ref.shape[1] // LANES, pair, 0, unroll=True)


def _bwd_kernel(factor, q_ref, k_ref, v_ref, d_ref, dq_ref, dk_ref, dv_ref):
    def pair(j, carry):
        cols = pl.ds(pl.multiple_of(j * LANES, LANES), LANES)
        q = q_ref[:, cols]
        k = k_ref[:, cols]
        v = v_ref[:, cols]
        d = d_ref[:, cols]
        dq = jnp.zeros((q.shape[0], LANES), jnp.float32)
        dk = jnp.zeros((q.shape[0], LANES), jnp.float32)
        dv = jnp.zeros((q.shape[0], LANES), jnp.float32)
        for head in range(LANES // HEAD_DIM):
            mine, qh, probs = _probs(q, k, head, factor)
            dh = jnp.where(mine, d, jnp.zeros_like(d))
            kh = jnp.where(mine, k, jnp.zeros_like(k))
            dprobs = _nt(dh, v)
            dv = dv + _tn(probs.astype(d.dtype), dh)
            inner = jnp.sum(dprobs * probs, axis=-1, keepdims=True)
            dscores = (probs * (dprobs - inner)).astype(q.dtype)
            dq = dq + jnp.dot(dscores, kh, preferred_element_type=jnp.float32)
            dk = dk + _tn(dscores, qh)
        dq_ref[:, cols] = (dq * factor).astype(dq_ref.dtype)
        dk_ref[:, cols] = (dk * factor).astype(dk_ref.dtype)
        dv_ref[:, cols] = dv.astype(dv_ref.dtype)
        return carry

    lax.fori_loop(0, dq_ref.shape[1] // LANES, pair, 0, unroll=4)


def _wgrad_kernel(expand_tiles, modb_ref, du_ref, act_ref, dz_ref, out_ref):
    j = pl.program_id(0)

    @pl.when(j < expand_tiles)
    def _():
        out_ref[...] = jnp.dot(
            modb_ref[...], du_ref[...], preferred_element_type=jnp.float32
        ).astype(out_ref.dtype)

    @pl.when(j >= expand_tiles)
    def _():
        out_ref[...] = jnp.dot(
            act_ref[...], dz_ref[...], preferred_element_type=jnp.float32
        ).astype(out_ref.dtype)


def ffn_weight_grads(mod_t, grad_exp, act_t, grad_branch, tile=1024):
    width, tokens = mod_t.shape
    ff = grad_exp.shape[1]
    expand_tiles = ff // tile
    per_part = width // tile
    tiles = expand_tiles + (ff // width) * per_part

    def act_index(j):
        return (jnp.maximum(j - expand_tiles, 0) // per_part, 0)

    def dz_index(j):
        return (0, jnp.maximum(j - expand_tiles, 0) % per_part)

    return pl.pallas_call(
        functools.partial(_wgrad_kernel, expand_tiles),
        out_shape=jax.ShapeDtypeStruct((width, tiles * tile), jnp.bfloat16),
        grid=(tiles,),
        in_specs=[
            pl.BlockSpec((width, tokens), lambda j: (0, 0)),
            pl.BlockSpec((tokens, tile), lambda j: (0, jnp.minimum(j, expand_tiles - 1))),
            pl.BlockSpec((width, tokens), act_index),
            pl.BlockSpec((tokens, tile), dz_index),
        ],
        out_specs=pl.BlockSpec((width, tile), lambda j: (0, j)),
        compiler_params=pltpu.CompilerParams(dimension_semantics=("arbitrary",)),
        cost_estimate=pl.CostEstimate(
            flops=2 * tokens * width * tiles * tile,
            transcendentals=0,
            bytes_accessed=2 * (tokens * (width + 2 * ff + width) + width * tiles * tile),
        ),
    )(mod_t, grad_exp, act_t, grad_branch)

def attention_forward(projected, images):
    tokens, three = projected.shape
    rows, width = tokens // images, three // 3
    pairs = width // LANES
    factor = HEAD_DIM ** (-0.5)

    def part(offset):
        return pl.BlockSpec((rows, width), lambda b: (b, offset))

    flops = 2 * 2 * images * (width // HEAD_DIM) * rows * rows * LANES
    return pl.pallas_call(
        functools.partial(_fwd_kernel, factor),
        out_shape=jax.ShapeDtypeStruct((tokens, width), projected.dtype),
        grid=(images,),
        in_specs=[part(0), part(1), part(2)],
        out_specs=part(0),
        compiler_params=pltpu.CompilerParams(dimension_semantics=("parallel",)),
        cost_estimate=pl.CostEstimate(
            flops=flops, transcendentals=images * (width // HEAD_DIM) * rows * rows,
            bytes_accessed=2 * tokens * (three + width),
        ),
    )(projected, projected, projected)


def attention_backward(projected, grad_attended, images):
    tokens, three = projected.shape
    rows, width = tokens // images, three // 3
    pairs = width // LANES
    factor = HEAD_DIM ** (-0.5)

    def part(offset):
        return pl.BlockSpec((rows, width), lambda b: (b, offset))

    out = jax.ShapeDtypeStruct((tokens, width), projected.dtype)
    flops = 5 * 2 * 2 * images * (width // HEAD_DIM) * rows * rows * LANES
    dq, dk, dv = pl.pallas_call(
        functools.partial(_bwd_kernel, factor),
        out_shape=(out, out, out),
        grid=(images,),
        in_specs=[part(0), part(1), part(2), part(0)],
        out_specs=[part(0)] * 3,
        compiler_params=pltpu.CompilerParams(dimension_semantics=("parallel",)),
        cost_estimate=pl.CostEstimate(
            flops=flops, transcendentals=images * (width // HEAD_DIM) * rows * rows,
            bytes_accessed=2 * tokens * (three + 4 * width),
        ),
    )(projected, projected, projected, grad_attended)
    return jnp.concatenate([dq, dk, dv], axis=1)


EPS = 1e-06
GELU_C = 0.7978845608028654

AXES = ("y", "zh", "x", "c", "zl")
DP = ("y", "zh", "x", "c")
STAGES = ("c", "x", "y", "zh", "zl")
STAGES_B = ("c", "y", "x", "zh", "zl")


def matmul(left, right):
    return jnp.dot(left, right, preferred_element_type=jnp.float32)


def left_trans(left, right):
    return lax.dot_general(
        left, right, (((0,), (0,)), ((), ())), preferred_element_type=jnp.float32
    )


def right_trans(left, right):
    return lax.dot_general(
        left, right, (((1,), (1,)), ((), ())), preferred_element_type=jnp.float32
    )


def normalize(values):
    centre = values - jnp.mean(values, axis=-1, keepdims=True)
    inverse = lax.rsqrt(jnp.mean(centre * centre, axis=-1, keepdims=True) + EPS)
    return (centre * inverse, inverse)


def norm_back(grad, normed, inverse):
    return inverse * (
        grad
        - jnp.mean(grad, axis=-1, keepdims=True)
        - normed * jnp.mean(grad * normed, axis=-1, keepdims=True)
    )


def stage_order(values, sizes, inner, stages=STAGES):
    lead = values.shape[:-1]
    shape = [sizes[a] for a in AXES]
    values = values.reshape(*lead, *shape, inner)
    n = len(lead)
    order = list(range(n)) + [n + AXES.index(a) for a in stages] + [n + len(AXES)]
    return jnp.transpose(values, order).reshape(*lead, -1)


def reduce_stages(packed, stages):
    for a in stages:
        packed = lax.psum_scatter(packed, a, scatter_dimension=0, tiled=True)
    return packed


def reduce_pair(packed, axis):
    half = packed.shape[0] // 2
    index = lax.axis_index(axis)
    keep = lax.dynamic_slice_in_dim(packed, index * half, half, axis=0)
    send = lax.dynamic_slice_in_dim(packed, (1 - index) * half, half, axis=0)
    got = lax.ppermute(send, axis, [(0, 1), (1, 0)])
    return (keep.astype(jnp.float32) + got.astype(jnp.float32)).astype(packed.dtype)


def reduce_rest(packed, axes):
    count = 1
    for a in axes:
        count *= lax.axis_size(a)
    chunks = packed.reshape(count, packed.shape[0] // count, packed.shape[1])
    chunks = lax.all_to_all(chunks, axes, 0, 0, tiled=False)
    return jnp.sum(chunks.astype(jnp.float32), axis=0)


def bias_columns(columns, rows):
    block = jnp.stack(columns, axis=1)
    return jnp.pad(block, ((0, 0), (0, 128 - block.shape[1]))).astype(jnp.bfloat16)


def gather_dp(values):
    count = 1
    for a in DP:
        count *= lax.axis_size(a)
    copies = jnp.broadcast_to(values[None], (count,) + values.shape)
    return lax.all_to_all(copies, DP, 0, 0, tiled=False).reshape(-1, values.shape[1])


def per_device(
    sizes,
    tokens,
    condition,
    occupied,
    modulation_weight,
    modulation_bias,
    input_weight,
    query_bias,
    value_bias,
    output_weight,
    output_bias,
    expand_weight,
    expand_bias,
    contract_weight,
    contract_bias,
    cotangent,
):
    images, rows, width = tokens.shape
    heads = width // HEAD_DIM
    flat = images * rows
    factor = HEAD_DIM ** (-0.5)
    cond_full = condition.astype(jnp.float32)
    sigmoid = jax.nn.sigmoid(cond_full)
    silu_b = (cond_full * sigmoid).astype(jnp.bfloat16)
    swap = [(0, 1), (1, 0)]
    first = lax.axis_index("zl") == 0
    silu_other = lax.ppermute(silu_b, "zl", swap)
    silu_pair = jnp.where(
        first,
        jnp.concatenate([silu_b, silu_other], axis=0),
        jnp.concatenate([silu_other, silu_b], axis=0),
    )
    mod_cols = matmul(silu_pair, modulation_weight) + modulation_bias.reshape(1, -1)
    own_cols = jnp.where(first, mod_cols[:images], mod_cols[images:])
    sent_cols = jnp.where(first, mod_cols[images:], mod_cols[:images])
    other_cols = lax.ppermute(sent_cols, "zl", swap)
    modulation = jnp.where(
        first,
        jnp.concatenate([own_cols, other_cols], axis=1),
        jnp.concatenate([other_cols, own_cols], axis=1),
    ).reshape(images, 6, 1, width)
    shift_a = modulation[:, 0]
    scale_a = modulation[:, 1]
    gate_a = modulation[:, 2]
    shift_b = modulation[:, 3]
    scale_b = modulation[:, 4]
    gate_b = modulation[:, 5]
    inputs = tokens.astype(jnp.float32)
    normed_a, inverse_a = normalize(inputs)
    mod_a = (normed_a * (1.0 + scale_a) + shift_a).astype(jnp.bfloat16).reshape(flat, width)
    qkv_bias = jnp.concatenate([query_bias, jnp.zeros_like(query_bias), value_bias])
    projected = (matmul(mod_a, input_weight) + qkv_bias).astype(jnp.bfloat16)
    attended_b = attention_forward(projected, images)
    branch_a = (matmul(attended_b, output_weight) + output_bias).reshape(images, rows, width)
    middle = inputs + gate_a * branch_a
    normed_b, inverse_b = normalize(middle)
    mod_b = (normed_b * (1.0 + scale_b) + shift_b).astype(jnp.bfloat16).reshape(flat, width)
    expanded = matmul(mod_b, expand_weight) + expand_bias
    tanh_part = jnp.tanh(GELU_C * (expanded + 0.044715 * expanded * expanded * expanded))
    activated_b = (0.5 * expanded * (1.0 + tanh_part)).astype(jnp.bfloat16)
    branch_b = (matmul(activated_b, contract_weight) + contract_bias).reshape(images, rows, width)
    alive = occupied.astype(jnp.float32)[:, None, None]
    layer_out = (middle + gate_b * branch_b) * alive
    grad_out = cotangent.astype(jnp.float32) * alive
    grad_gate_b = jnp.sum(grad_out * branch_b, axis=1)
    grad_branch_b = (grad_out * gate_b).astype(jnp.bfloat16).reshape(flat, width)
    blocks = 1
    for a in AXES:
        blocks *= sizes[a]
    ff = activated_b.shape[1]
    split = ff // width
    act_perm = stage_order(
        activated_b.reshape(flat, blocks, split, width // blocks)
        .transpose(0, 2, 1, 3)
        .reshape(flat, split, width),
        sizes,
        width // blocks,
    )
    contract_bias_grad = stage_order(
        jnp.sum(grad_branch_b.astype(jnp.float32), axis=0), sizes, width // blocks, STAGES_B
    )
    grad_act = right_trans(grad_branch_b, contract_weight)
    slope = 0.5 * (1.0 + tanh_part) + 0.5 * expanded * (1.0 - tanh_part * tanh_part) * GELU_C * (
        1.0 + 3.0 * 0.044715 * expanded * expanded
    )
    grad_exp_b = (grad_act * slope).astype(jnp.bfloat16)
    expand_bias_grad = stage_order(
        jnp.sum(grad_exp_b.astype(jnp.float32), axis=0)
        .reshape(blocks, split, width // blocks)
        .transpose(1, 0, 2)
        .reshape(split, width),
        sizes,
        width // blocks,
        STAGES_B,
    )
    packed_a = ffn_weight_grads(
        stage_order(mod_b, sizes, width // blocks).T, grad_exp_b, act_perm.reshape(flat, -1).T, grad_branch_b
    )
    packed_a, grad_exp_b = lax.optimization_barrier((packed_a, grad_exp_b))
    chain_a = reduce_stages(packed_a, STAGES[:1])
    grad_mod_b = right_trans(grad_exp_b, expand_weight).reshape(images, rows, width)
    grad_shift_b = jnp.sum(grad_mod_b, axis=1)
    grad_scale_b = jnp.sum(grad_mod_b * normed_b, axis=1)
    grad_middle = grad_out + norm_back(grad_mod_b * (1.0 + scale_b), normed_b, inverse_b)
    grad_gate_a = jnp.sum(grad_middle * branch_a, axis=1)
    grad_branch_a = (grad_middle * gate_a).astype(jnp.bfloat16).reshape(flat, width)
    output_grad = left_trans(stage_order(attended_b, sizes, width // blocks, STAGES_B), grad_branch_a).astype(
        jnp.bfloat16
    )
    output_bias_grad = stage_order(
        jnp.sum(grad_branch_a.astype(jnp.float32), axis=0), sizes, width // blocks, STAGES_B
    )
    grad_att_b = right_trans(grad_branch_a, output_weight).astype(jnp.bfloat16)
    chain_a, grad_att_b = lax.optimization_barrier((chain_a, grad_att_b))
    chain_a = reduce_stages(chain_a, STAGES[1:2])
    grad_proj_b = attention_backward(projected, grad_att_b, images)
    input_grad = left_trans(stage_order(mod_a, sizes, width // blocks, STAGES_B), grad_proj_b).astype(
        jnp.bfloat16
    )
    bias_sums = jnp.sum(grad_proj_b.astype(jnp.float32), axis=0)
    query_bias_grad = stage_order(bias_sums[:width], sizes, width // blocks, STAGES_B)
    value_bias_grad = stage_order(bias_sums[2 * width :], sizes, width // blocks, STAGES_B)
    chain_b = reduce_pair(
        jnp.concatenate(
            [
                input_grad,
                output_grad,
                bias_columns(
                [query_bias_grad, value_bias_grad, output_bias_grad, contract_bias_grad]
                + [expand_bias_grad[q] for q in range(split)],
                width,
            ),
            ],
            axis=1,
        ),
        STAGES_B[0],
    )
    chain_a, chain_b = lax.optimization_barrier((chain_a, chain_b))
    chain_b = reduce_stages(chain_b, STAGES_B[1:2])
    grad_mod_a = right_trans(grad_proj_b, input_weight).reshape(images, rows, width)
    grad_shift_a = jnp.sum(grad_mod_a, axis=1)
    grad_scale_a = jnp.sum(grad_mod_a * normed_a, axis=1)
    tokens_grad = grad_middle + norm_back(grad_mod_a * (1.0 + scale_a), normed_a, inverse_a)
    modulation_terms = jnp.stack(
        [grad_shift_a, grad_scale_a, grad_gate_a, grad_shift_b, grad_scale_b, grad_gate_b], axis=1
    ).reshape(images, 6 * width)
    modulation_own = modulation_terms.astype(jnp.bfloat16)
    half = modulation_own.shape[1] // 2
    keep_cols = jnp.where(first, modulation_own[:, :half], modulation_own[:, half:])
    give_cols = jnp.where(first, modulation_own[:, half:], modulation_own[:, :half])
    got_cols = lax.ppermute(give_cols, "zl", swap)
    modulation_cols = jnp.where(
        first,
        jnp.concatenate([keep_cols, got_cols], axis=0),
        jnp.concatenate([got_cols, keep_cols], axis=0),
    )
    silu_terms = right_trans(modulation_cols, modulation_weight)
    pair_index = lax.axis_index("zl")
    own_rows = lax.dynamic_slice_in_dim(silu_terms, pair_index * images, images, axis=0)
    other_rows = lax.dynamic_slice_in_dim(silu_terms, (1 - pair_index) * images, images, axis=0)
    silu_sums = own_rows + lax.ppermute(other_rows, "zl", [(0, 1), (1, 0)])
    condition_grad = silu_sums * sigmoid * (1.0 + cond_full * (1.0 - sigmoid))
    dp_count = lax.axis_size(DP)
    row_block = width // dp_count
    silu_parts = silu_pair.reshape(-1, dp_count, row_block).transpose(1, 0, 2)
    silu_parts = jnp.pad(silu_parts, ((0, 0), (0, 0), (0, 128 - row_block)))
    payload = jnp.concatenate(
        [jnp.broadcast_to(modulation_cols[None], (dp_count,) + modulation_cols.shape), silu_parts], axis=2
    )
    factors = lax.all_to_all(payload, DP, 0, 0, tiled=False)
    mod_all = factors[:, :, : modulation_cols.shape[1]].reshape(-1, modulation_cols.shape[1])
    silu_rows = factors[:, :, modulation_cols.shape[1] : modulation_cols.shape[1] + row_block]
    silu_rows = silu_rows.reshape(-1, row_block)
    dp_index = lax.axis_index(DP)
    modulation_weight_grad = left_trans(silu_rows, mod_all)
    bias_all = jnp.sum(mod_all.astype(jnp.float32), axis=0).reshape(-1, width)
    modulation_bias_grad = lax.dynamic_slice_in_dim(bias_all, dp_index * row_block, row_block, axis=1)
    chain_a = reduce_rest(chain_a, STAGES[2:])
    chain_b, mod_all = lax.optimization_barrier((chain_b, mod_all))
    chain_b = reduce_rest(chain_b, STAGES_B[2:])
    three = input_weight.shape[1]
    fw = expand_weight.shape[1]
    input_weight_grad = chain_b[:, :three]
    output_weight_grad = chain_b[:, three : three + width]
    qb_grad = chain_b[:, three + width]
    vb_grad = chain_b[:, three + width + 1]
    ob_grad = chain_b[:, three + width + 2]
    expand_weight_grad = chain_a[:, :fw]
    contract_weight_grad = chain_a[:, fw : fw + split * width].reshape(-1, split, width)
    contract_weight_grad = contract_weight_grad.transpose(1, 0, 2).reshape(-1, width)
    cb_grad = chain_b[:, three + width + 3]
    eb_grad = chain_b[:, three + width + 4 : three + width + 4 + split].T.reshape(-1)
    summed = (
        input_weight_grad,
        qb_grad,
        vb_grad,
        output_weight_grad,
        ob_grad,
        expand_weight_grad,
        eb_grad,
        contract_weight_grad,
        cb_grad,
    )
    return (
        layer_out,
        tokens_grad,
        condition_grad,
        modulation_weight_grad,
        modulation_bias_grad,
        *summed,
    )


def solution(mesh):
    dp_size, mod_size = mesh.devices.shape
    rest = dp_size // 4
    side = int(round(rest ** 0.5))
    shape = (side, 2, rest // side, 2, mod_size)
    sizes = dict(zip(AXES, shape))
    physical = Mesh(np.asarray(mesh.devices).reshape(shape), AXES)
    ALL = AXES
    placed = (
        P(ALL, None, None),
        P(ALL, None),
        P(ALL),
        P(None, "zl"),
        P("zl", None),
        P(),
        P(),
        P(),
        P(),
        P(),
        P(),
        P(),
        P(),
        P(),
        P(ALL, None, None),
    )
    return jax.shard_map(
        functools.partial(per_device, sizes),
        mesh=physical,
        in_specs=placed,
        out_specs=(
            P(ALL, None, None),
            P(ALL, None, None),
            P(ALL, None),
            P(DP, "zl"),
            P("zl", DP),
            P(ALL, None),
            P(ALL),
            P(ALL),
            P(ALL, None),
            P(ALL),
            P(ALL, None),
            P(ALL),
            P(ALL, None),
            P(ALL),
        ),
        check_vma=False,
    )
```

```python
import functools

import jax
import jax.numpy as jnp
import numpy as np
from jax import lax
from jax.experimental import pallas as pl
from jax.experimental.pallas import tpu as pltpu
from jax.sharding import Mesh
from jax.sharding import PartitionSpec as P

HEAD_DIM = 64
LANES = 128


def _nt(a, b):
    return lax.dot_general(a, b, (((1,), (1,)), ((), ())), preferred_element_type=jnp.float32)


def _tn(a, b):
    return lax.dot_general(a, b, (((0,), (0,)), ((), ())), preferred_element_type=jnp.float32)


def _probs(q, k, head, factor):
    lane = lax.broadcasted_iota(jnp.int32, (1, LANES), 1)
    mine = (lane // HEAD_DIM) == head
    qh = jnp.where(mine, q, jnp.zeros_like(q))
    scores = _nt(qh, k) * factor
    weights = jnp.exp(scores - jnp.max(scores, axis=-1, keepdims=True))
    return mine, qh, weights / jnp.sum(weights, axis=-1, keepdims=True)


def _fwd_kernel(factor, q_ref, k_ref, v_ref, o_ref):
    def pair(j, carry):
        cols = pl.ds(pl.multiple_of(j * LANES, LANES), LANES)
        q = q_ref[:, cols]
        k = k_ref[:, cols]
        v = v_ref[:, cols]
        out = jnp.zeros((q.shape[0], LANES), jnp.float32)
        for head in range(LANES // HEAD_DIM):
            mine, _, probs = _probs(q, k, head, factor)
            vh = jnp.where(mine, v, jnp.zeros_like(v))
            out = out + jnp.dot(probs.astype(v.dtype), vh, preferred_element_type=jnp.float32)
        o_ref[:, cols] = out.astype(o_ref.dtype)
        return carry

    lax.fori_loop(0, o_ref.shape[1] // LANES, pair, 0, unroll=4)


def _bwd_kernel(factor, q_ref, k_ref, v_ref, d_ref, dq_ref, dk_ref, dv_ref):
    def pair(j, carry):
        cols = pl.ds(pl.multiple_of(j * LANES, LANES), LANES)
        q = q_ref[:, cols]
        k = k_ref[:, cols]
        v = v_ref[:, cols]
        d = d_ref[:, cols]
        dq = jnp.zeros((q.shape[0], LANES), jnp.float32)
        dk = jnp.zeros((q.shape[0], LANES), jnp.float32)
        dv = jnp.zeros((q.shape[0], LANES), jnp.float32)
        for head in range(LANES // HEAD_DIM):
            mine, qh, probs = _probs(q, k, head, factor)
            dh = jnp.where(mine, d, jnp.zeros_like(d))
            kh = jnp.where(mine, k, jnp.zeros_like(k))
            dprobs = _nt(dh, v)
            dv = dv + _tn(probs.astype(d.dtype), dh)
            inner = jnp.sum(dprobs * probs, axis=-1, keepdims=True)
            dscores = (probs * (dprobs - inner)).astype(q.dtype)
            dq = dq + jnp.dot(dscores, kh, preferred_element_type=jnp.float32)
            dk = dk + _tn(dscores, qh)
        dq_ref[:, cols] = (dq * factor).astype(dq_ref.dtype)
        dk_ref[:, cols] = (dk * factor).astype(dk_ref.dtype)
        dv_ref[:, cols] = dv.astype(dv_ref.dtype)
        return carry

    lax.fori_loop(0, dq_ref.shape[1] // LANES, pair, 0, unroll=4)


def _wgrad_kernel(expand_tiles, modb_ref, du_ref, act_ref, dz_ref, out_ref):
    j = pl.program_id(0)

    @pl.when(j < expand_tiles)
    def _():
        out_ref[...] = jnp.dot(
            modb_ref[...], du_ref[...], preferred_element_type=jnp.float32
        ).astype(out_ref.dtype)

    @pl.when(j >= expand_tiles)
    def _():
        out_ref[...] = jnp.dot(
            act_ref[...], dz_ref[...], preferred_element_type=jnp.float32
        ).astype(out_ref.dtype)


def ffn_weight_grads(mod_t, grad_exp, act_t, grad_branch, tile=1024):
    width, tokens = mod_t.shape
    ff = grad_exp.shape[1]
    expand_tiles = ff // tile
    per_part = width // tile
    tiles = expand_tiles + (ff // width) * per_part

    def act_index(j):
        return (jnp.maximum(j - expand_tiles, 0) // per_part, 0)

    def dz_index(j):
        return (0, jnp.maximum(j - expand_tiles, 0) % per_part)

    return pl.pallas_call(
        functools.partial(_wgrad_kernel, expand_tiles),
        out_shape=jax.ShapeDtypeStruct((width, tiles * tile), jnp.bfloat16),
        grid=(tiles,),
        in_specs=[
            pl.BlockSpec((width, tokens), lambda j: (0, 0)),
            pl.BlockSpec((tokens, tile), lambda j: (0, jnp.minimum(j, expand_tiles - 1))),
            pl.BlockSpec((width, tokens), act_index),
            pl.BlockSpec((tokens, tile), dz_index),
        ],
        out_specs=pl.BlockSpec((width, tile), lambda j: (0, j)),
        compiler_params=pltpu.CompilerParams(dimension_semantics=("arbitrary",)),
        cost_estimate=pl.CostEstimate(
            flops=2 * tokens * width * tiles * tile,
            transcendentals=0,
            bytes_accessed=2 * (tokens * (width + 2 * ff + width) + width * tiles * tile),
        ),
    )(mod_t, grad_exp, act_t, grad_branch)

def attention_forward(projected, images):
    tokens, three = projected.shape
    rows, width = tokens // images, three // 3
    pairs = width // LANES
    factor = HEAD_DIM ** (-0.5)

    def part(offset):
        return pl.BlockSpec((rows, width), lambda b: (b, offset))

    flops = 2 * 2 * images * (width // HEAD_DIM) * rows * rows * LANES
    return pl.pallas_call(
        functools.partial(_fwd_kernel, factor),
        out_shape=jax.ShapeDtypeStruct((tokens, width), projected.dtype),
        grid=(images,),
        in_specs=[part(0), part(1), part(2)],
        out_specs=part(0),
        compiler_params=pltpu.CompilerParams(dimension_semantics=("parallel",)),
        cost_estimate=pl.CostEstimate(
            flops=flops, transcendentals=images * (width // HEAD_DIM) * rows * rows,
            bytes_accessed=2 * tokens * (three + width),
        ),
    )(projected, projected, projected)


def attention_backward(projected, grad_attended, images):
    tokens, three = projected.shape
    rows, width = tokens // images, three // 3
    pairs = width // LANES
    factor = HEAD_DIM ** (-0.5)

    def part(offset):
        return pl.BlockSpec((rows, width), lambda b: (b, offset))

    out = jax.ShapeDtypeStruct((tokens, width), projected.dtype)
    flops = 5 * 2 * 2 * images * (width // HEAD_DIM) * rows * rows * LANES
    dq, dk, dv = pl.pallas_call(
        functools.partial(_bwd_kernel, factor),
        out_shape=(out, out, out),
        grid=(images,),
        in_specs=[part(0), part(1), part(2), part(0)],
        out_specs=[part(0)] * 3,
        compiler_params=pltpu.CompilerParams(dimension_semantics=("parallel",)),
        cost_estimate=pl.CostEstimate(
            flops=flops, transcendentals=images * (width // HEAD_DIM) * rows * rows,
            bytes_accessed=2 * tokens * (three + 4 * width),
        ),
    )(projected, projected, projected, grad_attended)
    return jnp.concatenate([dq, dk, dv], axis=1)


EPS = 1e-06
GELU_C = 0.7978845608028654

AXES = ("y", "zh", "x", "c", "zl")
DP = ("y", "zh", "x", "c")
STAGES = ("c", "x", "y", "zh", "zl")
STAGES_B = ("c", "y", "x", "zh", "zl")


def matmul(left, right):
    return jnp.dot(left, right, preferred_element_type=jnp.float32)


def left_trans(left, right):
    return lax.dot_general(
        left, right, (((0,), (0,)), ((), ())), preferred_element_type=jnp.float32
    )


def right_trans(left, right):
    return lax.dot_general(
        left, right, (((1,), (1,)), ((), ())), preferred_element_type=jnp.float32
    )


def normalize(values):
    centre = values - jnp.mean(values, axis=-1, keepdims=True)
    inverse = lax.rsqrt(jnp.mean(centre * centre, axis=-1, keepdims=True) + EPS)
    return (centre * inverse, inverse)


def norm_back(grad, normed, inverse):
    return inverse * (
        grad
        - jnp.mean(grad, axis=-1, keepdims=True)
        - normed * jnp.mean(grad * normed, axis=-1, keepdims=True)
    )


def stage_order(values, sizes, inner, stages=STAGES):
    lead = values.shape[:-1]
    shape = [sizes[a] for a in AXES]
    values = values.reshape(*lead, *shape, inner)
    n = len(lead)
    order = list(range(n)) + [n + AXES.index(a) for a in stages] + [n + len(AXES)]
    return jnp.transpose(values, order).reshape(*lead, -1)


def reduce_stages(packed, stages):
    for a in stages:
        packed = lax.psum_scatter(packed, a, scatter_dimension=0, tiled=True)
    return packed


def reduce_pair(packed, axis):
    half = packed.shape[0] // 2
    index = lax.axis_index(axis)
    keep = lax.dynamic_slice_in_dim(packed, index * half, half, axis=0)
    send = lax.dynamic_slice_in_dim(packed, (1 - index) * half, half, axis=0)
    got = lax.ppermute(send, axis, [(0, 1), (1, 0)])
    return (keep.astype(jnp.float32) + got.astype(jnp.float32)).astype(packed.dtype)


def reduce_rest(packed, axes):
    count = 1
    for a in axes:
        count *= lax.axis_size(a)
    chunks = packed.reshape(count, packed.shape[0] // count, packed.shape[1])
    chunks = lax.all_to_all(chunks, axes, 0, 0, tiled=False)
    return jnp.sum(chunks.astype(jnp.float32), axis=0)


def bias_columns(columns, rows):
    block = jnp.stack(columns, axis=1)
    return jnp.pad(block, ((0, 0), (0, 128 - block.shape[1]))).astype(jnp.bfloat16)


def gather_dp(values):
    count = 1
    for a in DP:
        count *= lax.axis_size(a)
    copies = jnp.broadcast_to(values[None], (count,) + values.shape)
    return lax.all_to_all(copies, DP, 0, 0, tiled=False).reshape(-1, values.shape[1])


def per_device(
    sizes,
    tokens,
    condition,
    occupied,
    modulation_weight,
    modulation_bias,
    input_weight,
    query_bias,
    value_bias,
    output_weight,
    output_bias,
    expand_weight,
    expand_bias,
    contract_weight,
    contract_bias,
    cotangent,
):
    images, rows, width = tokens.shape
    heads = width // HEAD_DIM
    flat = images * rows
    factor = HEAD_DIM ** (-0.5)
    cond_full = condition.astype(jnp.float32)
    sigmoid = jax.nn.sigmoid(cond_full)
    silu_b = (cond_full * sigmoid).astype(jnp.bfloat16)
    swap = [(0, 1), (1, 0)]
    first = lax.axis_index("zl") == 0
    silu_other = lax.ppermute(silu_b, "zl", swap)
    silu_pair = jnp.where(
        first,
        jnp.concatenate([silu_b, silu_other], axis=0),
        jnp.concatenate([silu_other, silu_b], axis=0),
    )
    mod_cols = matmul(silu_pair, modulation_weight) + modulation_bias.reshape(1, -1)
    own_cols = jnp.where(first, mod_cols[:images], mod_cols[images:])
    sent_cols = jnp.where(first, mod_cols[images:], mod_cols[:images])
    other_cols = lax.ppermute(sent_cols, "zl", swap)
    modulation = jnp.where(
        first,
        jnp.concatenate([own_cols, other_cols], axis=1),
        jnp.concatenate([other_cols, own_cols], axis=1),
    ).reshape(images, 6, 1, width)
    shift_a = modulation[:, 0]
    scale_a = modulation[:, 1]
    gate_a = modulation[:, 2]
    shift_b = modulation[:, 3]
    scale_b = modulation[:, 4]
    gate_b = modulation[:, 5]
    inputs = tokens.astype(jnp.float32)
    normed_a, inverse_a = normalize(inputs)
    mod_a = (normed_a * (1.0 + scale_a) + shift_a).astype(jnp.bfloat16).reshape(flat, width)
    qkv_bias = jnp.concatenate([query_bias, jnp.zeros_like(query_bias), value_bias])
    projected = (matmul(mod_a, input_weight) + qkv_bias).astype(jnp.bfloat16)
    attended_b = attention_forward(projected, images)
    branch_a = (matmul(attended_b, output_weight) + output_bias).reshape(images, rows, width)
    middle = inputs + gate_a * branch_a
    normed_b, inverse_b = normalize(middle)
    mod_b = (normed_b * (1.0 + scale_b) + shift_b).astype(jnp.bfloat16).reshape(flat, width)
    expanded = matmul(mod_b, expand_weight) + expand_bias
    tanh_part = jnp.tanh(GELU_C * (expanded + 0.044715 * expanded * expanded * expanded))
    activated_b = (0.5 * expanded * (1.0 + tanh_part)).astype(jnp.bfloat16)
    branch_b = (matmul(activated_b, contract_weight) + contract_bias).reshape(images, rows, width)
    alive = occupied.astype(jnp.float32)[:, None, None]
    layer_out = (middle + gate_b * branch_b) * alive
    grad_out = cotangent.astype(jnp.float32) * alive
    grad_gate_b = jnp.sum(grad_out * branch_b, axis=1)
    grad_branch_b = (grad_out * gate_b).astype(jnp.bfloat16).reshape(flat, width)
    blocks = 1
    for a in AXES:
        blocks *= sizes[a]
    ff = activated_b.shape[1]
    split = ff // width
    act_perm = stage_order(
        activated_b.reshape(flat, blocks, split, width // blocks)
        .transpose(0, 2, 1, 3)
        .reshape(flat, split, width),
        sizes,
        width // blocks,
    )
    contract_bias_grad = stage_order(
        jnp.sum(grad_branch_b.astype(jnp.float32), axis=0), sizes, width // blocks, STAGES_B
    )
    grad_act = right_trans(grad_branch_b, contract_weight)
    slope = 0.5 * (1.0 + tanh_part) + 0.5 * expanded * (1.0 - tanh_part * tanh_part) * GELU_C * (
        1.0 + 3.0 * 0.044715 * expanded * expanded
    )
    grad_exp_b = (grad_act * slope).astype(jnp.bfloat16)
    expand_bias_grad = stage_order(
        jnp.sum(grad_exp_b.astype(jnp.float32), axis=0)
        .reshape(blocks, split, width // blocks)
        .transpose(1, 0, 2)
        .reshape(split, width),
        sizes,
        width // blocks,
        STAGES_B,
    )
    packed_a = ffn_weight_grads(
        stage_order(mod_b, sizes, width // blocks).T, grad_exp_b, act_perm.reshape(flat, -1).T, grad_branch_b
    )
    packed_a, grad_exp_b = lax.optimization_barrier((packed_a, grad_exp_b))
    chain_a = reduce_stages(packed_a, STAGES[:1])
    grad_mod_b = right_trans(grad_exp_b, expand_weight).reshape(images, rows, width)
    grad_shift_b = jnp.sum(grad_mod_b, axis=1)
    grad_scale_b = jnp.sum(grad_mod_b * normed_b, axis=1)
    grad_middle = grad_out + norm_back(grad_mod_b * (1.0 + scale_b), normed_b, inverse_b)
    grad_gate_a = jnp.sum(grad_middle * branch_a, axis=1)
    grad_branch_a = (grad_middle * gate_a).astype(jnp.bfloat16).reshape(flat, width)
    output_grad = left_trans(stage_order(attended_b, sizes, width // blocks, STAGES_B), grad_branch_a).astype(
        jnp.bfloat16
    )
    output_bias_grad = stage_order(
        jnp.sum(grad_branch_a.astype(jnp.float32), axis=0), sizes, width // blocks, STAGES_B
    )
    grad_att_b = right_trans(grad_branch_a, output_weight).astype(jnp.bfloat16)
    chain_a, grad_att_b = lax.optimization_barrier((chain_a, grad_att_b))
    chain_a = reduce_stages(chain_a, STAGES[1:2])
    grad_proj_b = attention_backward(projected, grad_att_b, images)
    input_grad = left_trans(stage_order(mod_a, sizes, width // blocks, STAGES_B), grad_proj_b).astype(
        jnp.bfloat16
    )
    bias_sums = jnp.sum(grad_proj_b.astype(jnp.float32), axis=0)
    query_bias_grad = stage_order(bias_sums[:width], sizes, width // blocks, STAGES_B)
    value_bias_grad = stage_order(bias_sums[2 * width :], sizes, width // blocks, STAGES_B)
    chain_b = reduce_pair(
        jnp.concatenate(
            [
                input_grad,
                output_grad,
                bias_columns(
                [query_bias_grad, value_bias_grad, output_bias_grad, contract_bias_grad]
                + [expand_bias_grad[q] for q in range(split)],
                width,
            ),
            ],
            axis=1,
        ),
        STAGES_B[0],
    )
    chain_a, chain_b = lax.optimization_barrier((chain_a, chain_b))
    chain_b = reduce_stages(chain_b, STAGES_B[1:2])
    grad_mod_a = right_trans(grad_proj_b, input_weight).reshape(images, rows, width)
    grad_shift_a = jnp.sum(grad_mod_a, axis=1)
    grad_scale_a = jnp.sum(grad_mod_a * normed_a, axis=1)
    tokens_grad = grad_middle + norm_back(grad_mod_a * (1.0 + scale_a), normed_a, inverse_a)
    modulation_terms = jnp.stack(
        [grad_shift_a, grad_scale_a, grad_gate_a, grad_shift_b, grad_scale_b, grad_gate_b], axis=1
    ).reshape(images, 6 * width)
    modulation_own = modulation_terms.astype(jnp.bfloat16)
    half = modulation_own.shape[1] // 2
    keep_cols = jnp.where(first, modulation_own[:, :half], modulation_own[:, half:])
    give_cols = jnp.where(first, modulation_own[:, half:], modulation_own[:, :half])
    got_cols = lax.ppermute(give_cols, "zl", swap)
    modulation_cols = jnp.where(
        first,
        jnp.concatenate([keep_cols, got_cols], axis=0),
        jnp.concatenate([got_cols, keep_cols], axis=0),
    )
    silu_terms = right_trans(modulation_cols, modulation_weight)
    pair_index = lax.axis_index("zl")
    own_rows = lax.dynamic_slice_in_dim(silu_terms, pair_index * images, images, axis=0)
    other_rows = lax.dynamic_slice_in_dim(silu_terms, (1 - pair_index) * images, images, axis=0)
    silu_sums = own_rows + lax.ppermute(other_rows, "zl", [(0, 1), (1, 0)])
    condition_grad = silu_sums * sigmoid * (1.0 + cond_full * (1.0 - sigmoid))
    dp_count = lax.axis_size(DP)
    cores = lax.axis_size("c")
    peers = dp_count // cores
    row_block = width // dp_count
    cols = modulation_cols.shape[1]
    silu_parts = silu_pair.reshape(-1, peers, cores * row_block).transpose(1, 0, 2)
    silu_parts = jnp.pad(silu_parts, ((0, 0), (0, 0), (0, 128 - cores * row_block)))
    payload = jnp.concatenate(
        [jnp.broadcast_to(modulation_cols[None], (peers,) + modulation_cols.shape), silu_parts], axis=2
    )
    near = lax.all_to_all(payload, ("y", "zh", "x"), 0, 0, tiled=False)
    far = lax.ppermute(near, "c", [(0, 1), (1, 0)])
    factors = jnp.concatenate([near, far], axis=0)
    mod_all = factors[:, :, :cols].reshape(-1, cols)
    silu_rows = lax.dynamic_slice_in_dim(
        factors[:, :, cols : cols + cores * row_block], lax.axis_index("c") * row_block, row_block, axis=2
    ).reshape(-1, row_block)
    dp_index = lax.axis_index(DP)
    modulation_weight_grad = left_trans(silu_rows, mod_all)
    bias_all = jnp.sum(mod_all.astype(jnp.float32), axis=0).reshape(-1, width)
    modulation_bias_grad = lax.dynamic_slice_in_dim(bias_all, dp_index * row_block, row_block, axis=1)
    chain_a = reduce_rest(chain_a, STAGES[2:])
    chain_b, mod_all = lax.optimization_barrier((chain_b, mod_all))
    chain_b = reduce_rest(chain_b, STAGES_B[2:])
    three = input_weight.shape[1]
    fw = expand_weight.shape[1]
    input_weight_grad = chain_b[:, :three]
    output_weight_grad = chain_b[:, three : three + width]
    qb_grad = chain_b[:, three + width]
    vb_grad = chain_b[:, three + width + 1]
    ob_grad = chain_b[:, three + width + 2]
    expand_weight_grad = chain_a[:, :fw]
    contract_weight_grad = chain_a[:, fw : fw + split * width].reshape(-1, split, width)
    contract_weight_grad = contract_weight_grad.transpose(1, 0, 2).reshape(-1, width)
    cb_grad = chain_b[:, three + width + 3]
    eb_grad = chain_b[:, three + width + 4 : three + width + 4 + split].T.reshape(-1)
    summed = (
        input_weight_grad,
        qb_grad,
        vb_grad,
        output_weight_grad,
        ob_grad,
        expand_weight_grad,
        eb_grad,
        contract_weight_grad,
        cb_grad,
    )
    return (
        layer_out,
        tokens_grad,
        condition_grad,
        modulation_weight_grad,
        modulation_bias_grad,
        *summed,
    )


def solution(mesh):
    dp_size, mod_size = mesh.devices.shape
    rest = dp_size // 4
    side = int(round(rest ** 0.5))
    shape = (side, 2, rest // side, 2, mod_size)
    sizes = dict(zip(AXES, shape))
    physical = Mesh(np.asarray(mesh.devices).reshape(shape), AXES)
    ALL = AXES
    placed = (
        P(ALL, None, None),
        P(ALL, None),
        P(ALL),
        P(None, "zl"),
        P("zl", None),
        P(),
        P(),
        P(),
        P(),
        P(),
        P(),
        P(),
        P(),
        P(),
        P(ALL, None, None),
    )
    return jax.shard_map(
        functools.partial(per_device, sizes),
        mesh=physical,
        in_specs=placed,
        out_specs=(
            P(ALL, None, None),
            P(ALL, None, None),
            P(ALL, None),
            P(DP, "zl"),
            P("zl", DP),
            P(ALL, None),
            P(ALL),
            P(ALL),
            P(ALL, None),
            P(ALL),
            P(ALL, None),
            P(ALL),
            P(ALL, None),
            P(ALL),
        ),
        check_vma=False,
    )
```

```python
import functools

import jax
import jax.numpy as jnp
import numpy as np
from jax import lax
from jax.experimental import pallas as pl
from jax.experimental.pallas import tpu as pltpu
from jax.sharding import Mesh
from jax.sharding import PartitionSpec as P

HEAD_DIM = 64
LANES = 128


def _nt(a, b):
    return lax.dot_general(a, b, (((1,), (1,)), ((), ())), preferred_element_type=jnp.float32)


def _tn(a, b):
    return lax.dot_general(a, b, (((0,), (0,)), ((), ())), preferred_element_type=jnp.float32)


def _probs(q, k, head, factor):
    lane = lax.broadcasted_iota(jnp.int32, (1, LANES), 1)
    mine = (lane // HEAD_DIM) == head
    qh = jnp.where(mine, q, jnp.zeros_like(q))
    scores = _nt(qh, k) * factor
    weights = jnp.exp(scores - jnp.max(scores, axis=-1, keepdims=True))
    return mine, qh, weights / jnp.sum(weights, axis=-1, keepdims=True)


def _fwd_kernel(factor, q_ref, k_ref, v_ref, o_ref):
    def pair(j, carry):
        cols = pl.ds(pl.multiple_of(j * LANES, LANES), LANES)
        q = q_ref[:, cols]
        k = k_ref[:, cols]
        v = v_ref[:, cols]
        out = jnp.zeros((q.shape[0], LANES), jnp.float32)
        for head in range(LANES // HEAD_DIM):
            mine, _, probs = _probs(q, k, head, factor)
            vh = jnp.where(mine, v, jnp.zeros_like(v))
            out = out + jnp.dot(probs.astype(v.dtype), vh, preferred_element_type=jnp.float32)
        o_ref[:, cols] = out.astype(o_ref.dtype)
        return carry

    lax.fori_loop(0, o_ref.shape[1] // LANES, pair, 0, unroll=4)


def _bwd_kernel(factor, q_ref, k_ref, v_ref, d_ref, dq_ref, dk_ref, dv_ref):
    def pair(j, carry):
        cols = pl.ds(pl.multiple_of(j * LANES, LANES), LANES)
        q = q_ref[:, cols]
        k = k_ref[:, cols]
        v = v_ref[:, cols]
        d = d_ref[:, cols]
        dq = jnp.zeros((q.shape[0], LANES), jnp.float32)
        dk = jnp.zeros((q.shape[0], LANES), jnp.float32)
        dv = jnp.zeros((q.shape[0], LANES), jnp.float32)
        for head in range(LANES // HEAD_DIM):
            mine, qh, probs = _probs(q, k, head, factor)
            dh = jnp.where(mine, d, jnp.zeros_like(d))
            kh = jnp.where(mine, k, jnp.zeros_like(k))
            dprobs = _nt(dh, v)
            dv = dv + _tn(probs.astype(d.dtype), dh)
            inner = jnp.sum(dprobs * probs, axis=-1, keepdims=True)
            dscores = (probs * (dprobs - inner)).astype(q.dtype)
            dq = dq + jnp.dot(dscores, kh, preferred_element_type=jnp.float32)
            dk = dk + _tn(dscores, qh)
        dq_ref[:, cols] = (dq * factor).astype(dq_ref.dtype)
        dk_ref[:, cols] = (dk * factor).astype(dk_ref.dtype)
        dv_ref[:, cols] = dv.astype(dv_ref.dtype)
        return carry

    lax.fori_loop(0, dq_ref.shape[1] // LANES, pair, 0, unroll=4)


def _wgrad_kernel(expand_tiles, modb_ref, du_ref, act_ref, dz_ref, out_ref):
    j = pl.program_id(0)

    @pl.when(j < expand_tiles)
    def _():
        out_ref[...] = jnp.dot(
            modb_ref[...], du_ref[...], preferred_element_type=jnp.float32
        ).astype(out_ref.dtype)

    @pl.when(j >= expand_tiles)
    def _():
        out_ref[...] = jnp.dot(
            act_ref[...], dz_ref[...], preferred_element_type=jnp.float32
        ).astype(out_ref.dtype)


def ffn_weight_grads(mod_t, grad_exp, act_t, grad_branch, tile=1024):
    width, tokens = mod_t.shape
    ff = grad_exp.shape[1]
    expand_tiles = ff // tile
    per_part = width // tile
    tiles = expand_tiles + (ff // width) * per_part

    def act_index(j):
        return (jnp.maximum(j - expand_tiles, 0) // per_part, 0)

    def dz_index(j):
        return (0, jnp.maximum(j - expand_tiles, 0) % per_part)

    return pl.pallas_call(
        functools.partial(_wgrad_kernel, expand_tiles),
        out_shape=jax.ShapeDtypeStruct((width, tiles * tile), jnp.bfloat16),
        grid=(tiles,),
        in_specs=[
            pl.BlockSpec((width, tokens), lambda j: (0, 0)),
            pl.BlockSpec((tokens, tile), lambda j: (0, jnp.minimum(j, expand_tiles - 1))),
            pl.BlockSpec((width, tokens), act_index),
            pl.BlockSpec((tokens, tile), dz_index),
        ],
        out_specs=pl.BlockSpec((width, tile), lambda j: (0, j)),
        compiler_params=pltpu.CompilerParams(dimension_semantics=("arbitrary",)),
        cost_estimate=pl.CostEstimate(
            flops=2 * tokens * width * tiles * tile,
            transcendentals=0,
            bytes_accessed=2 * (tokens * (width + 2 * ff + width) + width * tiles * tile),
        ),
    )(mod_t, grad_exp, act_t, grad_branch)

def attention_forward(projected, images):
    tokens, three = projected.shape
    rows, width = tokens // images, three // 3
    pairs = width // LANES
    factor = HEAD_DIM ** (-0.5)

    def part(offset):
        return pl.BlockSpec((rows, width), lambda b: (b, offset))

    flops = 2 * 2 * images * (width // HEAD_DIM) * rows * rows * LANES
    return pl.pallas_call(
        functools.partial(_fwd_kernel, factor),
        out_shape=jax.ShapeDtypeStruct((tokens, width), projected.dtype),
        grid=(images,),
        in_specs=[part(0), part(1), part(2)],
        out_specs=part(0),
        compiler_params=pltpu.CompilerParams(dimension_semantics=("parallel",)),
        cost_estimate=pl.CostEstimate(
            flops=flops, transcendentals=images * (width // HEAD_DIM) * rows * rows,
            bytes_accessed=2 * tokens * (three + width),
        ),
    )(projected, projected, projected)


def attention_backward(projected, grad_attended, images):
    tokens, three = projected.shape
    rows, width = tokens // images, three // 3
    pairs = width // LANES
    factor = HEAD_DIM ** (-0.5)

    def part(offset):
        return pl.BlockSpec((rows, width), lambda b: (b, offset))

    out = jax.ShapeDtypeStruct((tokens, width), projected.dtype)
    flops = 5 * 2 * 2 * images * (width // HEAD_DIM) * rows * rows * LANES
    dq, dk, dv = pl.pallas_call(
        functools.partial(_bwd_kernel, factor),
        out_shape=(out, out, out),
        grid=(images,),
        in_specs=[part(0), part(1), part(2), part(0)],
        out_specs=[part(0)] * 3,
        compiler_params=pltpu.CompilerParams(dimension_semantics=("parallel",)),
        cost_estimate=pl.CostEstimate(
            flops=flops, transcendentals=images * (width // HEAD_DIM) * rows * rows,
            bytes_accessed=2 * tokens * (three + 4 * width),
        ),
    )(projected, projected, projected, grad_attended)
    return jnp.concatenate([dq, dk, dv], axis=1)


EPS = 1e-06
GELU_C = 0.7978845608028654

AXES = ("y", "zh", "x", "c", "zl")
DP = ("y", "zh", "x", "c")
STAGES = ("c", "x", "y", "zh", "zl")
STAGES_B = STAGES


def matmul(left, right):
    return jnp.dot(left, right, preferred_element_type=jnp.float32)


def left_trans(left, right):
    return lax.dot_general(
        left, right, (((0,), (0,)), ((), ())), preferred_element_type=jnp.float32
    )


def right_trans(left, right):
    return lax.dot_general(
        left, right, (((1,), (1,)), ((), ())), preferred_element_type=jnp.float32
    )


def normalize(values):
    centre = values - jnp.mean(values, axis=-1, keepdims=True)
    inverse = lax.rsqrt(jnp.mean(centre * centre, axis=-1, keepdims=True) + EPS)
    return (centre * inverse, inverse)


def norm_back(grad, normed, inverse):
    return inverse * (
        grad
        - jnp.mean(grad, axis=-1, keepdims=True)
        - normed * jnp.mean(grad * normed, axis=-1, keepdims=True)
    )


def stage_order(values, sizes, inner, stages=STAGES):
    lead = values.shape[:-1]
    shape = [sizes[a] for a in AXES]
    values = values.reshape(*lead, *shape, inner)
    n = len(lead)
    order = list(range(n)) + [n + AXES.index(a) for a in stages] + [n + len(AXES)]
    return jnp.transpose(values, order).reshape(*lead, -1)


def reduce_stages(packed, stages):
    for a in stages:
        packed = lax.psum_scatter(packed, a, scatter_dimension=0, tiled=True)
    return packed


def reduce_pair(packed, axis):
    half = packed.shape[0] // 2
    index = lax.axis_index(axis)
    keep = lax.dynamic_slice_in_dim(packed, index * half, half, axis=0)
    send = lax.dynamic_slice_in_dim(packed, (1 - index) * half, half, axis=0)
    got = lax.ppermute(send, axis, [(0, 1), (1, 0)])
    return (keep.astype(jnp.float32) + got.astype(jnp.float32)).astype(packed.dtype)


def reduce_rest(packed, axes):
    count = 1
    for a in axes:
        count *= lax.axis_size(a)
    chunks = packed.reshape(count, packed.shape[0] // count, packed.shape[1])
    chunks = lax.all_to_all(chunks, axes, 0, 0, tiled=False)
    return jnp.sum(chunks.astype(jnp.float32), axis=0)


def bias_columns(columns, rows):
    block = jnp.stack(columns, axis=1)
    return jnp.pad(block, ((0, 0), (0, 128 - block.shape[1]))).astype(jnp.bfloat16)


def gather_dp(values):
    count = 1
    for a in DP:
        count *= lax.axis_size(a)
    copies = jnp.broadcast_to(values[None], (count,) + values.shape)
    return lax.all_to_all(copies, DP, 0, 0, tiled=False).reshape(-1, values.shape[1])


def per_device(
    sizes,
    tokens,
    condition,
    occupied,
    modulation_weight,
    modulation_bias,
    input_weight,
    query_bias,
    value_bias,
    output_weight,
    output_bias,
    expand_weight,
    expand_bias,
    contract_weight,
    contract_bias,
    cotangent,
):
    images, rows, width = tokens.shape
    heads = width // HEAD_DIM
    flat = images * rows
    factor = HEAD_DIM ** (-0.5)
    cond_full = condition.astype(jnp.float32)
    sigmoid = jax.nn.sigmoid(cond_full)
    silu_b = (cond_full * sigmoid).astype(jnp.bfloat16)
    swap = [(0, 1), (1, 0)]
    first = lax.axis_index("zl") == 0
    silu_other = lax.ppermute(silu_b, "zl", swap)
    silu_pair = jnp.where(
        first,
        jnp.concatenate([silu_b, silu_other], axis=0),
        jnp.concatenate([silu_other, silu_b], axis=0),
    )
    mod_cols = matmul(silu_pair, modulation_weight) + modulation_bias.reshape(1, -1)
    own_cols = jnp.where(first, mod_cols[:images], mod_cols[images:])
    sent_cols = jnp.where(first, mod_cols[images:], mod_cols[:images])
    other_cols = lax.ppermute(sent_cols, "zl", swap)
    modulation = jnp.where(
        first,
        jnp.concatenate([own_cols, other_cols], axis=1),
        jnp.concatenate([other_cols, own_cols], axis=1),
    ).reshape(images, 6, 1, width)
    shift_a = modulation[:, 0]
    scale_a = modulation[:, 1]
    gate_a = modulation[:, 2]
    shift_b = modulation[:, 3]
    scale_b = modulation[:, 4]
    gate_b = modulation[:, 5]
    inputs = tokens.astype(jnp.float32)
    normed_a, inverse_a = normalize(inputs)
    mod_a = (normed_a * (1.0 + scale_a) + shift_a).astype(jnp.bfloat16).reshape(flat, width)
    qkv_bias = jnp.concatenate([query_bias, jnp.zeros_like(query_bias), value_bias])
    projected = (matmul(mod_a, input_weight) + qkv_bias).astype(jnp.bfloat16)
    attended_b = attention_forward(projected, images)
    branch_a = (matmul(attended_b, output_weight) + output_bias).reshape(images, rows, width)
    middle = inputs + gate_a * branch_a
    normed_b, inverse_b = normalize(middle)
    mod_b = (normed_b * (1.0 + scale_b) + shift_b).astype(jnp.bfloat16).reshape(flat, width)
    expanded = matmul(mod_b, expand_weight) + expand_bias
    tanh_part = jnp.tanh(GELU_C * (expanded + 0.044715 * expanded * expanded * expanded))
    activated_b = (0.5 * expanded * (1.0 + tanh_part)).astype(jnp.bfloat16)
    branch_b = (matmul(activated_b, contract_weight) + contract_bias).reshape(images, rows, width)
    alive = occupied.astype(jnp.float32)[:, None, None]
    layer_out = (middle + gate_b * branch_b) * alive
    grad_out = cotangent.astype(jnp.float32) * alive
    grad_gate_b = jnp.sum(grad_out * branch_b, axis=1)
    grad_branch_b = (grad_out * gate_b).astype(jnp.bfloat16).reshape(flat, width)
    blocks = 1
    for a in AXES:
        blocks *= sizes[a]
    ff = activated_b.shape[1]
    split = ff // width
    act_perm = stage_order(
        activated_b.reshape(flat, blocks, split, width // blocks)
        .transpose(0, 2, 1, 3)
        .reshape(flat, split, width),
        sizes,
        width // blocks,
    )
    contract_bias_grad = stage_order(
        jnp.sum(grad_branch_b.astype(jnp.float32), axis=0), sizes, width // blocks, STAGES_B
    )
    grad_act = right_trans(grad_branch_b, contract_weight)
    slope = 0.5 * (1.0 + tanh_part) + 0.5 * expanded * (1.0 - tanh_part * tanh_part) * GELU_C * (
        1.0 + 3.0 * 0.044715 * expanded * expanded
    )
    grad_exp_b = (grad_act * slope).astype(jnp.bfloat16)
    expand_bias_grad = stage_order(
        jnp.sum(grad_exp_b.astype(jnp.float32), axis=0)
        .reshape(blocks, split, width // blocks)
        .transpose(1, 0, 2)
        .reshape(split, width),
        sizes,
        width // blocks,
        STAGES_B,
    )
    packed_a = ffn_weight_grads(
        stage_order(mod_b, sizes, width // blocks).T, grad_exp_b, act_perm.reshape(flat, -1).T, grad_branch_b
    )
    packed_a, grad_exp_b = lax.optimization_barrier((packed_a, grad_exp_b))
    chain_a = reduce_stages(packed_a, STAGES[:1])
    grad_mod_b = right_trans(grad_exp_b, expand_weight).reshape(images, rows, width)
    grad_shift_b = jnp.sum(grad_mod_b, axis=1)
    grad_scale_b = jnp.sum(grad_mod_b * normed_b, axis=1)
    grad_middle = grad_out + norm_back(grad_mod_b * (1.0 + scale_b), normed_b, inverse_b)
    grad_gate_a = jnp.sum(grad_middle * branch_a, axis=1)
    grad_branch_a = (grad_middle * gate_a).astype(jnp.bfloat16).reshape(flat, width)
    output_grad = left_trans(stage_order(attended_b, sizes, width // blocks, STAGES_B), grad_branch_a).astype(
        jnp.bfloat16
    )
    output_bias_grad = stage_order(
        jnp.sum(grad_branch_a.astype(jnp.float32), axis=0), sizes, width // blocks, STAGES_B
    )
    grad_att_b = right_trans(grad_branch_a, output_weight).astype(jnp.bfloat16)
    chain_a, grad_att_b = lax.optimization_barrier((chain_a, grad_att_b))
    chain_a = reduce_stages(chain_a, STAGES[1:2])
    grad_proj_b = attention_backward(projected, grad_att_b, images)
    input_grad = left_trans(stage_order(mod_a, sizes, width // blocks, STAGES_B), grad_proj_b).astype(
        jnp.bfloat16
    )
    bias_sums = jnp.sum(grad_proj_b.astype(jnp.float32), axis=0)
    query_bias_grad = stage_order(bias_sums[:width], sizes, width // blocks, STAGES_B)
    value_bias_grad = stage_order(bias_sums[2 * width :], sizes, width // blocks, STAGES_B)
    chain_b = reduce_pair(
        jnp.concatenate(
            [
                input_grad,
                output_grad,
                bias_columns(
                [query_bias_grad, value_bias_grad, output_bias_grad, contract_bias_grad]
                + [expand_bias_grad[q] for q in range(split)],
                width,
            ),
            ],
            axis=1,
        ),
        STAGES_B[0],
    )
    chain_a, chain_b = lax.optimization_barrier((chain_a, chain_b))
    chain_b = reduce_stages(chain_b, STAGES_B[1:2])
    grad_mod_a = right_trans(grad_proj_b, input_weight).reshape(images, rows, width)
    grad_shift_a = jnp.sum(grad_mod_a, axis=1)
    grad_scale_a = jnp.sum(grad_mod_a * normed_a, axis=1)
    tokens_grad = grad_middle + norm_back(grad_mod_a * (1.0 + scale_a), normed_a, inverse_a)
    modulation_terms = jnp.stack(
        [grad_shift_a, grad_scale_a, grad_gate_a, grad_shift_b, grad_scale_b, grad_gate_b], axis=1
    ).reshape(images, 6 * width)
    modulation_own = modulation_terms.astype(jnp.bfloat16)
    half = modulation_own.shape[1] // 2
    keep_cols = jnp.where(first, modulation_own[:, :half], modulation_own[:, half:])
    give_cols = jnp.where(first, modulation_own[:, half:], modulation_own[:, :half])
    got_cols = lax.ppermute(give_cols, "zl", swap)
    modulation_cols = jnp.where(
        first,
        jnp.concatenate([keep_cols, got_cols], axis=0),
        jnp.concatenate([got_cols, keep_cols], axis=0),
    )
    silu_terms = right_trans(modulation_cols, modulation_weight)
    pair_index = lax.axis_index("zl")
    own_rows = lax.dynamic_slice_in_dim(silu_terms, pair_index * images, images, axis=0)
    other_rows = lax.dynamic_slice_in_dim(silu_terms, (1 - pair_index) * images, images, axis=0)
    silu_sums = own_rows + lax.ppermute(other_rows, "zl", [(0, 1), (1, 0)])
    condition_grad = silu_sums * sigmoid * (1.0 + cond_full * (1.0 - sigmoid))
    dp_count = lax.axis_size(DP)
    cores = lax.axis_size("c")
    peers = dp_count // cores
    row_block = width // dp_count
    cols = modulation_cols.shape[1]
    silu_parts = silu_pair.reshape(-1, peers, cores * row_block).transpose(1, 0, 2)
    silu_parts = jnp.pad(silu_parts, ((0, 0), (0, 0), (0, 128 - cores * row_block)))
    payload = jnp.concatenate(
        [jnp.broadcast_to(modulation_cols[None], (peers,) + modulation_cols.shape), silu_parts], axis=2
    )
    near = lax.all_to_all(payload, ("y", "zh", "x"), 0, 0, tiled=False)
    far = lax.ppermute(near, "c", [(0, 1), (1, 0)])
    factors = jnp.concatenate([near, far], axis=0)
    mod_all = factors[:, :, :cols].reshape(-1, cols)
    silu_rows = lax.dynamic_slice_in_dim(
        factors[:, :, cols : cols + cores * row_block], lax.axis_index("c") * row_block, row_block, axis=2
    ).reshape(-1, row_block)
    dp_index = lax.axis_index(DP)
    modulation_weight_grad = left_trans(silu_rows, mod_all)
    bias_all = jnp.sum(mod_all.astype(jnp.float32), axis=0).reshape(-1, width)
    modulation_bias_grad = lax.dynamic_slice_in_dim(bias_all, dp_index * row_block, row_block, axis=1)
    chain_b, mod_all = lax.optimization_barrier((chain_b, mod_all))
    rest = reduce_rest(jnp.concatenate([chain_a, chain_b], axis=1), STAGES[2:])
    chain_a = rest[:, : chain_a.shape[1]]
    chain_b = rest[:, chain_a.shape[1] :]
    three = input_weight.shape[1]
    fw = expand_weight.shape[1]
    input_weight_grad = chain_b[:, :three]
    output_weight_grad = chain_b[:, three : three + width]
    qb_grad = chain_b[:, three + width]
    vb_grad = chain_b[:, three + width + 1]
    ob_grad = chain_b[:, three + width + 2]
    expand_weight_grad = chain_a[:, :fw]
    contract_weight_grad = chain_a[:, fw : fw + split * width].reshape(-1, split, width)
    contract_weight_grad = contract_weight_grad.transpose(1, 0, 2).reshape(-1, width)
    cb_grad = chain_b[:, three + width + 3]
    eb_grad = chain_b[:, three + width + 4 : three + width + 4 + split].T.reshape(-1)
    summed = (
        input_weight_grad,
        qb_grad,
        vb_grad,
        output_weight_grad,
        ob_grad,
        expand_weight_grad,
        eb_grad,
        contract_weight_grad,
        cb_grad,
    )
    return (
        layer_out,
        tokens_grad,
        condition_grad,
        modulation_weight_grad,
        modulation_bias_grad,
        *summed,
    )


def solution(mesh):
    dp_size, mod_size = mesh.devices.shape
    rest = dp_size // 4
    side = int(round(rest ** 0.5))
    shape = (side, 2, rest // side, 2, mod_size)
    sizes = dict(zip(AXES, shape))
    physical = Mesh(np.asarray(mesh.devices).reshape(shape), AXES)
    ALL = AXES
    placed = (
        P(ALL, None, None),
        P(ALL, None),
        P(ALL),
        P(None, "zl"),
        P("zl", None),
        P(),
        P(),
        P(),
        P(),
        P(),
        P(),
        P(),
        P(),
        P(),
        P(ALL, None, None),
    )
    return jax.shard_map(
        functools.partial(per_device, sizes),
        mesh=physical,
        in_specs=placed,
        out_specs=(
            P(ALL, None, None),
            P(ALL, None, None),
            P(ALL, None),
            P(DP, "zl"),
            P("zl", DP),
            P(ALL, None),
            P(ALL),
            P(ALL),
            P(ALL, None),
            P(ALL),
            P(ALL, None),
            P(ALL),
            P(ALL, None),
            P(ALL),
        ),
        check_vma=False,
    )
```
